32 devices in a mesh: dp: 8 (over z, x), tensor: 4 (over y, core).
Axes of the slice: x: 2, y: 2, z: 4, core: 2. Of those that a mesh axis runs over, the one named last changes fastest.
Arguments:
- tokens: bfloat16 [20480, 768], P(('dp', 'tensor')), may hold values from -6 to 6
- lengths: int32 [8, 5], P('dp'), may hold values from 1 to 32, 40 in all within a row
- in_gain: float32 [768], replicated, may hold values from 0.25 to 1.75
- qkv_weight: bfloat16 [768, 2304], P(None, 'tensor'), may hold values from -0.21875 to 0.21875
- attn_gain: float32 [768], P('tensor'), may hold values from 0.25 to 1.75
- out_weight: bfloat16 [768, 768], P('tensor'), may hold values from -0.21875 to 0.21875
- ffn_gain: float32 [768], replicated, may hold values from 0.25 to 1.75
- up_weight: bfloat16 [768, 3072], P(None, 'tensor'), may hold values from -0.21875 to 0.21875
- hidden_gain: float32 [3072], P('tensor'), may hold values from 0.25 to 1.75
- down_weight: bfloat16 [3072, 768], P('tensor'), may hold values from -0.109375 to 0.109375
- out_grad: bfloat16 [20480, 768], P(('dp', 'tensor')), may hold values from -6 to 6
Outputs:
- output: bfloat16 [20480, 768], P(('dp', 'tensor'))
- in_grad: float32 [20480, 768], P(('dp', 'tensor'))
- grad_in_gain: float32 [768], replicated
- grad_qkv: float32 [768, 2304], P(None, 'tensor')
- grad_attn_gain: float32 [768], P('tensor')
- grad_out: float32 [768, 768], P('tensor')
- grad_ffn_gain: float32 [768], replicated
- grad_up: float32 [768, 3072], P(None, 'tensor')
- grad_hidden_gain: float32 [3072], P('tensor')
- grad_down: float32 [3072, 768], P('tensor')
The draws below stay inside these ranges and needn't reach their ends.
Inputs may be any that keep to these rules, and one draw needn't show every extreme that they name: Each row of lengths sums to 40, and its largest entry is exactly 32.
All inputs are finite; a program needn't handle non-finite values.
Results may differ from the reference program's by a relative error of at most 0.015.
Values may be sent and summed in bfloat16 or wider, within the bound.
A program may use at most 192 MiB of HBM per device.

```python
import math
import jax
import jax.numpy as jnp
import numpy as np
from jax import lax

D = 768
HEADS = 12
HEAD_DIM = 64
FF = 3072
UNIT = 64
MAXLEN = 2048
QB = 512
TOK_GROUP = 2560
SEQS = 5
TOKENS = 20480
N_DP = 8


def levels(stream_key, dims, shards, least, top_value):
    def one(dim, blocks):
        heights = jax.random.uniform(jax.random.fold_in(jax.random.fold_in(stream_key, 6), dim), (blocks,), jnp.float32, least / len(shards), top_value / len(shards))
        return jnp.repeat(jnp.exp(heights), dims[dim] // blocks).reshape((-1,) + (1,) * (len(dims) - dim - 1))

    level = one(*shards[0])
    for cut in shards[1:]:
        level = level * one(*cut)
    return level


def split_up(number_of, total, most, lean):
    portions = [(1 << 20) // math.isqrt(rank ** lean) + 1 for rank in range(2, number_of + 1)]
    rest, given = total - most - (number_of - 1), [1] * (number_of - 1)
    while rest > 0:
        free = [i for i in range(number_of - 1) if given[i] < most]
        whole, left = sum([portions[i] for i in free]), rest
        for i in free:
            extra = min(most - given[i], max(1, left * portions[i] // whole), rest)
            given[i] = given[i] + extra
            rest = rest - extra
    return np.array([most] + given)


def ragged(key, amount, total, bound, skew):
    if amount == 2:
        one = jax.random.randint(key, (), max(1, total - bound), min(bound, total - 1) + 1)
        return jnp.stack([one, total - one])
    sizes = jnp.asarray(split_up(amount, total, bound, skew), jnp.int32)
    pairs = (amount - 1) // 2
    source_of, taker = sizes[1:1 + 2 * pairs:2], sizes[2:2 + 2 * pairs:2]
    slack = jnp.minimum(source_of - 1, bound - taker)
    shifted = jax.random.randint(jax.random.fold_in(key, 1), (pairs,), 0, 1 << 20) % (slack + 1)
    sizes = sizes.at[1:1 + 2 * pairs:2].set(source_of - shifted).at[2:2 + 2 * pairs:2].set(taker + shifted)
    return sizes[jax.random.permutation(jax.random.fold_in(key, 2), amount)]


def bell_draw(rng, shape, scale, reach, cuts=(), kind=jnp.bfloat16):
    loudness = levels(rng, shape, cuts, -0.22, 0.18) if cuts else 1.0
    values = jax.random.normal(rng, shape, jnp.float32) * scale * loudness
    return jnp.minimum(jnp.maximum(values, -reach), reach).astype(kind)


def setup_inputs(seed: int = 0) -> dict:
    seeds = jax.random.split(jax.random.key(seed), 12)
    return {
        "tokens": bell_draw(seeds[0], (TOKENS, D), 1.0, 6.0, ((0, 32),)),
        "lengths": jax.vmap(lambda own: ragged(own, SEQS, TOK_GROUP // UNIT, MAXLEN // UNIT, 2))(jax.random.split(seeds[1], N_DP)).reshape((N_DP, SEQS)).astype(jnp.int32),
        "in_gain": jnp.clip(1.0 + 0.15 * jax.random.normal(seeds[2], (D,), jnp.float32), 0.25, 1.75),
        "qkv_weight": bell_draw(seeds[3], (D, 3 * D), D ** -0.5, 0.21875, ((1, 4),)),
        "attn_gain": jnp.clip(1.0 + 0.15 * jax.random.normal(seeds[4], (D,), jnp.float32), 0.25, 1.75),
        "out_weight": bell_draw(seeds[5], (D, D), D ** -0.5, 0.21875, ((0, 4),)),
        "ffn_gain": jnp.clip(1.0 + 0.15 * jax.random.normal(seeds[6], (D,), jnp.float32), 0.25, 1.75),
        "up_weight": bell_draw(seeds[7], (D, FF), D ** -0.5, 0.21875, ((1, 4),)),
        "hidden_gain": jnp.clip(1.0 + 0.15 * jax.random.normal(seeds[8], (FF,), jnp.float32), 0.25, 1.75),
        "down_weight": bell_draw(seeds[9], (FF, D), FF ** -0.5, 0.109375, ((0, 4),)),
        "out_grad": bell_draw(seeds[10], (TOKENS, D), 1.0, 6.0, ((0, 32),)),
    }


@jax.custom_vjp
def low(v):
    return lax.optimization_barrier(v.astype(jnp.bfloat16)).astype(jnp.float32)

@jax.custom_vjp
def low_back(v):
    return v

def low_keep(v):
    return (low(v), None)

def low_pass(kept, grad):
    return (grad,)

def back_keep(v):
    return (v, None)

def back_low(kept, grad):
    return (low(grad),)
low.defvjp(low_keep, low_pass)
low_back.defvjp(back_keep, back_low)
EPS = 1e-05
HIGHEST = lax.Precision.HIGHEST

def product(left, right):
    return jnp.dot(left, right, precision=HIGHEST, preferred_element_type=jnp.float32)

def norm_rows(values, gain):
    row_mean = lax.optimization_barrier(jnp.mean(values, axis=-1, keepdims=True))
    row_square = lax.optimization_barrier(jnp.mean(values * values, axis=-1, keepdims=True))
    return (values - row_mean) * lax.rsqrt(row_square - row_mean * row_mean + EPS) * gain

def segment_ids(counts, row_count):
    ends = jnp.cumsum(counts * UNIT).astype(jnp.int32)
    positions = jnp.arange(row_count, dtype=jnp.int32)
    return lax.optimization_barrier(jnp.sum((positions[:, None] >= ends[None, :]).astype(jnp.int32), axis=1))

def attend(queries, keys, values, segment):
    row_count = queries.shape[0]
    width = MAXLEN + QB
    scale = 1.0 / float(HEAD_DIM) ** 0.5

    def one_block(block_index):
        first_row = block_index * QB
        key_start = jnp.clip(first_row + QB - width, 0, row_count - width)
        query_block = lax.dynamic_slice_in_dim(queries, first_row, QB, 0)
        key_window = lax.dynamic_slice_in_dim(keys, key_start, width, 0)
        value_window = lax.dynamic_slice_in_dim(values, key_start, width, 0)
        query_segment = lax.dynamic_slice_in_dim(segment, first_row, QB, 0)
        key_segment = lax.dynamic_slice_in_dim(segment, key_start, width, 0)
        query_pos = first_row + jnp.arange(QB, dtype=jnp.int32)
        key_pos = key_start + jnp.arange(width, dtype=jnp.int32)
        allowed = (query_segment[:, None] == key_segment[None, :]) & (key_pos[None, :] <= query_pos[:, None])
        score = jnp.einsum('qhe,khe->hqk', query_block, key_window, precision=HIGHEST) * scale
        score = low_back(score)
        score = jnp.where(allowed[None], score, -1000000000.0)
        weights = low(jax.nn.softmax(score, axis=-1))
        return low_back(jnp.einsum('hqk,khe->qhe', weights, value_window, precision=HIGHEST))
    blocks = lax.map(jax.checkpoint(one_block), jnp.arange(row_count // QB, dtype=jnp.int32))
    return blocks.reshape(row_count, HEADS * HEAD_DIM)

def layer_forward(tokens, in_gain, qkv_weight, attn_gain, out_weight, ffn_gain, up_weight, hidden_gain, down_weight, segment):
    row_count = tokens.shape[0]
    normed_in = low(norm_rows(tokens, in_gain))
    packed = low(low_back(product(normed_in, qkv_weight)))
    heads_view = packed.reshape(row_count, HEADS, 3, HEAD_DIM)
    attended = attend(heads_view[:, :, 0], heads_view[:, :, 1], heads_view[:, :, 2], segment)
    normed_att = low(norm_rows(attended, attn_gain))
    middle = tokens + low_back(product(normed_att, out_weight))
    normed_mid = low(norm_rows(middle, ffn_gain))
    hidden = jax.nn.gelu(low_back(product(normed_mid, up_weight)), approximate=True)
    normed_hidden = low(norm_rows(hidden, hidden_gain))
    return middle + low_back(product(normed_hidden, down_weight))

def reference(tokens, lengths, in_gain, qkv_weight, attn_gain, out_weight, ffn_gain, up_weight, hidden_gain, down_weight, out_grad):
    params = tuple((item.astype(jnp.float32) for item in (in_gain, qkv_weight, attn_gain, out_weight, ffn_gain, up_weight, hidden_gain, down_weight)))
    inputs = tokens.astype(jnp.float32).reshape(N_DP, TOK_GROUP, D)
    cotangent = out_grad.astype(jnp.float32).reshape(N_DP, TOK_GROUP, D)

    def group_step(totals, item):
        group_in, group_cot, group_len = item
        segment = segment_ids(group_len, TOK_GROUP)

        def forward(values, *weights):
            return layer_forward(values, *weights, segment)
        result, pull = jax.vjp(forward, group_in, *params)
        grads = pull(group_cot)
        totals = tuple((total + grad for total, grad in zip(totals, grads[1:])))
        return (totals, (result.astype(jnp.bfloat16), grads[0]))
    zeros = tuple((jnp.zeros_like(item) for item in params))
    totals, (outputs, in_grads) = lax.scan(group_step, zeros, (inputs, cotangent, lengths))
    return (outputs.reshape(TOKENS, D), in_grads.reshape(TOKENS, D), totals[0], totals[1], totals[2], totals[3], totals[4], totals[5], totals[6], totals[7])
```

```python
from functools import partial

import jax
import jax.numpy as jnp
from jax import lax
from jax.experimental import pallas as pl
from jax.experimental.pallas import tpu as pltpu
from jax.sharding import PartitionSpec as P

D = 768
HEAD_DIM = 64
FF = 3072
UNIT = 64


EPS = 1e-05


def contract_rows(left, right):
    return lax.dot_general(
        left, right, (((0,), (0,)), ((), ())), preferred_element_type=jnp.float32
    )


def contract_cols(left, right):
    return lax.dot_general(
        left, right, (((1,), (1,)), ((), ())), preferred_element_type=jnp.float32
    )


def normalize(values, gain):
    row_mean = jnp.mean(values, axis=1, keepdims=True)
    row_square = jnp.mean(values * values, axis=1, keepdims=True)
    inv_scale = lax.rsqrt(row_square - row_mean * row_mean + EPS)
    unit_rows = (values - row_mean) * inv_scale
    return (unit_rows, inv_scale, unit_rows * gain)


def norm_back(grad_normed, unit_rows, inv_scale, gain):
    weighted = grad_normed * gain
    first_mean = jnp.mean(weighted, axis=1, keepdims=True)
    second = jnp.mean(weighted * unit_rows, axis=1, keepdims=True)
    return (
        inv_scale * (weighted - first_mean - unit_rows * second),
        jnp.sum(grad_normed * unit_rows, axis=0),
    )


NEG = -1e30
def seq_bounds(len_ref):
    ends, total = [], 0
    for s in range(len_ref.shape[1]):
        total = total + len_ref[0, s] * UNIT
        ends.append(total)
    return ends


def start_of(ends, row):
    at = 0
    for end in ends:
        at = jnp.where(row >= end, end, at)
    return at


def end_of(ends, row):
    at = ends[-1]
    for end in reversed(ends):
        at = jnp.where(row < end, end, at)
    return at


def dot(a, b):
    return lax.dot_general(a, b, (((1,), (0,)), ((), ())), preferred_element_type=jnp.float32)


def fwd_kernel(bq, bk, len_ref, qkv_ref, o_ref, lse_ref, k_s, qt_s, vt_s, acc_s, m_s):
    rows = qkv_ref.shape[0]
    heads = k_s.shape[0]
    ends = seq_bounds(len_ref)
    ones = (lax.broadcasted_iota(jnp.int32, (16, bq), 0) == 0).astype(jnp.float32).astype(jnp.bfloat16)

    def stage(i, _):
        at = pl.ds(pl.multiple_of(i * bq, bq), bq)
        x = qkv_ref[at, :]
        for h in range(heads):
            base = h * 3 * HEAD_DIM
            q = x[:, base : base + HEAD_DIM] * jnp.bfloat16(0.125)
            qt_s[h, :, at] = q.T
            k_s[h, at, :] = x[:, base + HEAD_DIM : base + 2 * HEAD_DIM]
            vt_s[h, :HEAD_DIM, at] = x[:, base + 2 * HEAD_DIM : base + 3 * HEAD_DIM].T
            vt_s[h, HEAD_DIM:, at] = ones
        return 0

    lax.fori_loop(0, rows // bq, stage, 0)

    def query_block(i, _):
        first = pl.multiple_of(i * bq, bq)
        at = pl.ds(first, bq)
        q_pos = first + lax.broadcasted_iota(jnp.int32, (1, bq), 1)
        q_start = start_of(ends, q_pos)
        lo = start_of(ends, first)
        hi = start_of(ends, first + bq - 1)
        for h in range(heads):
            acc_s[h] = jnp.zeros_like(acc_s[h])
            m_s[h] = jnp.full_like(m_s[h], NEG)

        def step(masked, c, _):
            c0 = pl.multiple_of(c * bk, bk)
            for h in range(heads):
                s = dot(k_s[h, pl.ds(c0, bk), :], qt_s[h, :, at])
                if masked:
                    k_pos = c0 + lax.broadcasted_iota(jnp.int32, (bk, 1), 0)
                    s = jnp.where((k_pos <= q_pos) & (k_pos >= q_start), s, NEG)
                old = m_s[h]
                new = jnp.maximum(old, jnp.max(s, axis=0, keepdims=True))
                p = jnp.exp(s - new).astype(jnp.bfloat16)
                m_s[h] = new
                acc_s[h] = acc_s[h] * jnp.exp(old - new) + dot(vt_s[h, :, pl.ds(c0, bk)], p)
            return 0

        c_lo = lo // bk
        c_diag = first // bk
        c_end = (first + bq - 1) // bk + 1
        c_int = jnp.minimum((hi + bk - 1) // bk, c_diag)
        lax.fori_loop(c_lo, c_int, partial(step, True), 0)
        lax.fori_loop(c_int, c_diag, partial(step, False), 0)
        lax.fori_loop(jnp.maximum(c_diag, c_lo), c_end, partial(step, True), 0)
        outs = []
        for h in range(heads):
            acc = acc_s[h]
            total = acc[HEAD_DIM : HEAD_DIM + 1, :]
            outs.append((acc[:HEAD_DIM, :] / total).T)
            lse_ref[h : h + 1, at] = m_s[h] + jnp.log(total)
        o_ref[at, :] = jnp.concatenate(outs, axis=1).astype(o_ref.dtype)
        return 0

    lax.fori_loop(0, rows // bq, query_block, 0)


def attn_fwd(packed, lengths, bq=256, bk=256, out_dtype=jnp.float32):
    rows = packed.shape[0]
    heads = packed.shape[1] // (3 * HEAD_DIM)
    return pl.pallas_call(
        partial(fwd_kernel, bq, bk),
        out_shape=(
            jax.ShapeDtypeStruct((rows, heads * HEAD_DIM), out_dtype),
            jax.ShapeDtypeStruct((8, rows), jnp.float32),
        ),
        in_specs=[pl.BlockSpec(memory_space=pltpu.SMEM), pl.BlockSpec(memory_space=pltpu.VMEM)],
        out_specs=[pl.BlockSpec(memory_space=pltpu.VMEM)] * 2,
        scratch_shapes=[
            pltpu.VMEM((heads, rows, HEAD_DIM), jnp.bfloat16),
            pltpu.VMEM((heads, HEAD_DIM, rows), jnp.bfloat16),
            pltpu.VMEM((heads, HEAD_DIM + 16, rows), jnp.bfloat16),
            pltpu.VMEM((heads, HEAD_DIM + 16, bq), jnp.float32),
            pltpu.VMEM((heads, 1, bq), jnp.float32),
        ],
        compiler_params=pltpu.CompilerParams(vmem_limit_bytes=48 << 20),
        name="attn_fwd",
    )(lengths, packed)


def bwd_kernel(bq, bk, len_ref, qkv_ref, o_ref, lse_ref, do_ref, out_ref,
               q_s, k_s, v_s, do_s, qt_s, kt_s, dot_s, d_s, dqt_s, dk_s, dv_s):
    rows = qkv_ref.shape[0]
    heads = k_s.shape[0]
    ends = seq_bounds(len_ref)
    scale = jnp.bfloat16(0.125)

    def stage(i, _):
        at = pl.ds(pl.multiple_of(i * bq, bq), bq)
        x = qkv_ref[at, :]
        g = do_ref[at, :]
        prod = g.astype(jnp.float32) * o_ref[at, :].astype(jnp.float32)
        for h in range(heads):
            base = h * 3 * HEAD_DIM
            q = x[:, base : base + HEAD_DIM] * scale
            k = x[:, base + HEAD_DIM : base + 2 * HEAD_DIM]
            d = g[:, h * HEAD_DIM : (h + 1) * HEAD_DIM]
            q_s[h, at, :] = q
            k_s[h, at, :] = k
            v_s[h, at, :] = x[:, base + 2 * HEAD_DIM : base + 3 * HEAD_DIM]
            do_s[h, at, :] = d
            qt_s[h, :, at] = q.T
            kt_s[h, :, at] = (k * scale).T
            dot_s[h, :, at] = d.T
            d_s[h, :, at] = jnp.sum(prod[:, h * HEAD_DIM : (h + 1) * HEAD_DIM].T, axis=0, keepdims=True)
            dqt_s[h, :, at] = jnp.zeros((HEAD_DIM, bq), jnp.float32)
        return 0

    lax.fori_loop(0, rows // bq, stage, 0)

    def key_block(j, _):
        c0 = pl.multiple_of(j * bk, bk)
        kat = pl.ds(c0, bk)
        for h in range(heads):
            dk_s[h, kat, :] = jnp.zeros((bk, HEAD_DIM), jnp.float32)
            dv_s[h, kat, :] = jnp.zeros((bk, HEAD_DIM), jnp.float32)

        def step(masked, i, _):
            first = pl.multiple_of(i * bq, bq)
            at = pl.ds(first, bq)
            if masked:
                q_pos = first + lax.broadcasted_iota(jnp.int32, (1, bq), 1)
                q_start = start_of(ends, q_pos)
                k_pos = c0 + lax.broadcasted_iota(jnp.int32, (bk, 1), 0)
                keep = (k_pos <= q_pos) & (k_pos >= q_start)
            for h in range(heads):
                s = dot(k_s[h, kat, :], qt_s[h, :, at]) - lse_ref[h : h + 1, at]
                if masked:
                    s = jnp.where(keep, s, NEG)
                p = jnp.exp(s)
                dp = dot(v_s[h, kat, :], dot_s[h, :, at])
                ds = (p * (dp - d_s[h, :, at])).astype(jnp.bfloat16)
                dv_s[h, kat, :] += dot(p.astype(jnp.bfloat16), do_s[h, at, :])
                dk_s[h, kat, :] += dot(ds, q_s[h, at, :])
                dqt_s[h, :, at] += dot(kt_s[h, :, kat], ds)
            return 0

        i_diag = c0 // bq
        i_after = (c0 + bk - 1) // bq + 1
        i_end = (end_of(ends, c0 + bk - 1) + bq - 1) // bq
        i_int = jnp.maximum(end_of(ends, c0) // bq, i_after)
        i_int = jnp.minimum(i_int, i_end)
        lax.fori_loop(i_diag, i_after, partial(step, True), 0)
        lax.fori_loop(i_after, i_int, partial(step, False), 0)
        lax.fori_loop(i_int, i_end, partial(step, True), 0)
        return 0

    lax.fori_loop(0, rows // bk, key_block, 0)

    def finish(i, _):
        at = pl.ds(pl.multiple_of(i * bq, bq), bq)
        parts = []
        for h in range(heads):
            parts += [dqt_s[h, :, at].T, dk_s[h, at, :], dv_s[h, at, :]]
        out_ref[at, :] = jnp.concatenate(parts, axis=1).astype(out_ref.dtype)
        return 0

    lax.fori_loop(0, rows // bq, finish, 0)


def attn_bwd(packed, lengths, att, lse, d_att, bq=256, bk=256):
    rows = packed.shape[0]
    heads = packed.shape[1] // (3 * HEAD_DIM)
    row_major = pltpu.VMEM((heads, rows, HEAD_DIM), jnp.bfloat16)
    col_major = pltpu.VMEM((heads, HEAD_DIM, rows), jnp.bfloat16)
    return pl.pallas_call(
        partial(bwd_kernel, bq, bk),
        out_shape=jax.ShapeDtypeStruct(packed.shape, jnp.bfloat16),
        in_specs=[pl.BlockSpec(memory_space=pltpu.SMEM)] + [pl.BlockSpec(memory_space=pltpu.VMEM)] * 4,
        out_specs=pl.BlockSpec(memory_space=pltpu.VMEM),
        scratch_shapes=[row_major] * 4 + [col_major] * 3 + [
            pltpu.VMEM((heads, 1, rows), jnp.float32),
            pltpu.VMEM((heads, HEAD_DIM, rows), jnp.float32),
            pltpu.VMEM((heads, rows, HEAD_DIM), jnp.float32),
            pltpu.VMEM((heads, rows, HEAD_DIM), jnp.float32),
        ],
        compiler_params=pltpu.CompilerParams(vmem_limit_bytes=56 << 20),
        name="attn_bwd",
    )(lengths, packed, att, lse, d_att)


def ffn_totals(grad_up, grad_down, grad_hidden):
    return lax.psum((grad_up, grad_down, grad_hidden), "dp")


def local(
    tokens,
    lengths,
    in_gain,
    qkv_weight,
    attn_gain,
    out_weight,
    ffn_gain,
    up_weight,
    hidden_gain,
    down_weight,
    out_grad,
):
    tensor_size = lax.axis_size("tensor")
    own_rows = tokens.shape[0]
    group_rows = own_rows * tensor_size
    residual = tokens.astype(jnp.float32)
    in_unit, in_scale, in_normed = normalize(residual, in_gain)
    gathered_in, gathered_grad = (
        lax.all_gather(in_normed.astype(jnp.bfloat16), "tensor", axis=0, tiled=True),
        lax.all_gather(out_grad, "tensor", axis=0, tiled=True),
    )
    packed = jnp.dot(gathered_in, qkv_weight, preferred_element_type=jnp.float32).astype(
        jnp.bfloat16
    )
    attended, log_total = attn_fwd(packed, lengths, 512, 512)
    att_sum, att_square = lax.psum(
        (jnp.sum(attended, axis=1), jnp.sum(attended * attended, axis=1)), "tensor"
    )
    att_mean = att_sum / D
    att_scale = lax.rsqrt(att_square / D - att_mean * att_mean + EPS)
    att_unit = (attended - att_mean[:, None]) * att_scale[:, None]
    att_low = (att_unit * attn_gain).astype(jnp.bfloat16)
    middle = residual + lax.psum_scatter(
        jnp.dot(att_low, out_weight, preferred_element_type=jnp.float32),
        "tensor",
        scatter_dimension=0,
        tiled=True,
    )
    mid_unit, mid_scale, mid_normed = normalize(middle, ffn_gain)
    mid_low = mid_normed.astype(jnp.bfloat16)
    gathered_mid = lax.all_gather(mid_low, "tensor", axis=0, tiled=True)
    pre_act = jnp.dot(gathered_mid, up_weight, preferred_element_type=jnp.float32)
    activated, gelu_pull = jax.vjp(partial(jax.nn.gelu, approximate=True), pre_act)
    act_sum, act_square = lax.psum(
        (jnp.sum(activated, axis=1), jnp.sum(activated * activated, axis=1)), "tensor"
    )
    act_mean = act_sum / FF
    act_scale = lax.rsqrt(act_square / FF - act_mean * act_mean + EPS)
    act_unit = (activated - act_mean[:, None]) * act_scale[:, None]
    act_low = (act_unit * hidden_gain).astype(jnp.bfloat16)
    result = (
        middle
        + lax.psum_scatter(
            jnp.dot(
                lax.slice_in_dim(act_low, 0, lax.axis_size("tensor") * own_rows, axis=0),
                down_weight,
                preferred_element_type=jnp.float32,
            ).astype(jnp.bfloat16),
            "tensor",
            scatter_dimension=0,
            tiled=True,
        ).astype(jnp.float32)
    ).astype(jnp.bfloat16)
    grad_down = contract_rows(act_low, gathered_grad)
    grad_act_low = contract_cols(gathered_grad, down_weight)
    weighted_act = grad_act_low * hidden_gain
    grad_hidden = jnp.sum(grad_act_low * act_unit, axis=0)
    first_sum, second_sum = lax.psum(
        (jnp.sum(weighted_act, axis=1), jnp.sum(weighted_act * act_unit, axis=1)), "tensor"
    )
    grad_act = act_scale[:, None] * (
        weighted_act - (first_sum / FF)[:, None] - act_unit * (second_sum / FF)[:, None]
    )
    grad_pre = gelu_pull(grad_act)[0].astype(jnp.bfloat16)
    grad_up = contract_rows(gathered_mid, grad_pre)
    grad_mid_normed = lax.psum_scatter(
        contract_cols(grad_pre, up_weight), "tensor", scatter_dimension=0, tiled=True
    )
    grad_mid_part, grad_ffn_gain_part = norm_back(grad_mid_normed, mid_unit, mid_scale, ffn_gain)
    grad_middle = out_grad.astype(jnp.float32) + grad_mid_part
    gathered_back = lax.all_gather(grad_middle.astype(jnp.bfloat16), "tensor", axis=0, tiled=True)
    grad_out_part = contract_rows(att_low, gathered_back)
    grad_att_low = contract_cols(gathered_back, out_weight)
    weighted_att = grad_att_low * attn_gain
    grad_attn_gain_part = jnp.sum(grad_att_low * att_unit, axis=0)
    first_att, second_att, grad_ffn_gain_group = lax.psum(
        (
            jnp.sum(weighted_att, axis=1),
            jnp.sum(weighted_att * att_unit, axis=1),
            grad_ffn_gain_part,
        ),
        "tensor",
    )
    grad_attended = (
        att_scale[:, None]
        * (weighted_att - (first_att / D)[:, None] - att_unit * (second_att / D)[:, None])
    ).astype(jnp.bfloat16)
    grad_packed = attn_bwd(packed, lengths, attended, log_total, grad_attended, 512, 256)
    grad_qkv_part = contract_rows(gathered_in, grad_packed)
    grad_in_normed = lax.psum_scatter(
        contract_cols(grad_packed, qkv_weight).astype(jnp.bfloat16),
        "tensor",
        scatter_dimension=0,
        tiled=True,
    ).astype(jnp.float32)
    grad_in_part, grad_in_gain_part = norm_back(grad_in_normed, in_unit, in_scale, in_gain)
    in_grad = grad_middle + grad_in_part
    ffn_sums = ffn_totals(grad_up, grad_down, grad_hidden)
    attn_sums = lax.psum(
        (grad_qkv_part, grad_out_part, grad_attn_gain_part, grad_ffn_gain_group), "dp"
    )
    grad_in_gain = lax.psum(grad_in_gain_part, ("dp", "tensor"))
    return (
        result,
        in_grad,
        grad_in_gain,
        attn_sums[0],
        attn_sums[2],
        attn_sums[1],
        attn_sums[3],
        ffn_sums[0],
        ffn_sums[2],
        ffn_sums[1],
    )


def solution(mesh):
    return jax.shard_map(
        local,
        mesh=mesh,
        in_specs=(
            P(("dp", "tensor"), None),
            P("dp", None),
            P(),
            P(None, "tensor"),
            P("tensor"),
            P("tensor", None),
            P(),
            P(None, "tensor"),
            P("tensor"),
            P("tensor", None),
            P(("dp", "tensor"), None),
        ),
        out_specs=(
            P(("dp", "tensor"), None),
            P(("dp", "tensor"), None),
            P(),
            P(None, "tensor"),
            P("tensor"),
            P("tensor", None),
            P(),
            P(None, "tensor"),
            P("tensor"),
            P("tensor", None),
        ),
        check_vma=False,
    )
```

```python
from functools import partial

import jax
import jax.numpy as jnp
from jax import lax
from jax.experimental import pallas as pl
from jax.experimental.pallas import tpu as pltpu
from jax.sharding import PartitionSpec as P

D = 768
HEAD_DIM = 64
FF = 3072
UNIT = 64


EPS = 1e-05


def contract_rows(left, right):
    return lax.dot_general(
        left, right, (((0,), (0,)), ((), ())), preferred_element_type=jnp.float32
    )


def contract_cols(left, right):
    return lax.dot_general(
        left, right, (((1,), (1,)), ((), ())), preferred_element_type=jnp.float32
    )


def normalize(values, gain):
    row_mean = jnp.mean(values, axis=1, keepdims=True)
    row_square = jnp.mean(values * values, axis=1, keepdims=True)
    inv_scale = lax.rsqrt(row_square - row_mean * row_mean + EPS)
    unit_rows = (values - row_mean) * inv_scale
    return (unit_rows, inv_scale, unit_rows * gain)


def norm_back(grad_normed, unit_rows, inv_scale, gain):
    weighted = grad_normed * gain
    first_mean = jnp.mean(weighted, axis=1, keepdims=True)
    second = jnp.mean(weighted * unit_rows, axis=1, keepdims=True)
    return (
        inv_scale * (weighted - first_mean - unit_rows * second),
        jnp.sum(grad_normed * unit_rows, axis=0),
    )


NEG = -1e30
def seq_bounds(len_ref):
    ends, total = [], 0
    for s in range(len_ref.shape[1]):
        total = total + len_ref[0, s] * UNIT
        ends.append(total)
    return ends


def start_of(ends, row):
    at = 0
    for end in ends:
        at = jnp.where(row >= end, end, at)
    return at


def end_of(ends, row):
    at = ends[-1]
    for end in reversed(ends):
        at = jnp.where(row < end, end, at)
    return at


def dot(a, b):
    return lax.dot_general(a, b, (((1,), (0,)), ((), ())), preferred_element_type=jnp.float32)


def fwd_kernel(bq, bk, len_ref, qkv_ref, o_ref, lse_ref, k_s, qt_s, vt_s, acc_s, m_s):
    rows = qkv_ref.shape[0]
    heads = k_s.shape[0]
    ends = seq_bounds(len_ref)
    ones = (lax.broadcasted_iota(jnp.int32, (16, bq), 0) == 0).astype(jnp.float32).astype(jnp.bfloat16)

    def stage(i, _):
        at = pl.ds(pl.multiple_of(i * bq, bq), bq)
        x = qkv_ref[at, :]
        for h in range(heads):
            base = h * 3 * HEAD_DIM
            q = x[:, base : base + HEAD_DIM] * jnp.bfloat16(0.125)
            qt_s[h, :, at] = q.T
            k_s[h, at, :] = x[:, base + HEAD_DIM : base + 2 * HEAD_DIM]
            vt_s[h, :HEAD_DIM, at] = x[:, base + 2 * HEAD_DIM : base + 3 * HEAD_DIM].T
            vt_s[h, HEAD_DIM:, at] = ones
        return 0

    lax.fori_loop(0, rows // bq, stage, 0)

    def query_block(i, _):
        first = pl.multiple_of(i * bq, bq)
        at = pl.ds(first, bq)
        q_pos = first + lax.broadcasted_iota(jnp.int32, (1, bq), 1)
        q_start = start_of(ends, q_pos)
        lo = start_of(ends, first)
        hi = start_of(ends, first + bq - 1)
        for h in range(heads):
            acc_s[h] = jnp.zeros_like(acc_s[h])
            m_s[h] = jnp.full_like(m_s[h], NEG)

        def step(masked, c, _):
            c0 = pl.multiple_of(c * bk, bk)
            for h in range(heads):
                s = dot(k_s[h, pl.ds(c0, bk), :], qt_s[h, :, at])
                if masked:
                    k_pos = c0 + lax.broadcasted_iota(jnp.int32, (bk, 1), 0)
                    s = jnp.where((k_pos <= q_pos) & (k_pos >= q_start), s, NEG)
                old = m_s[h]
                new = jnp.maximum(old, jnp.max(s, axis=0, keepdims=True))
                p = jnp.exp(s - new).astype(jnp.bfloat16)
                m_s[h] = new
                acc_s[h] = acc_s[h] * jnp.exp(old - new) + dot(vt_s[h, :, pl.ds(c0, bk)], p)
            return 0

        c_lo = lo // bk
        c_diag = first // bk
        c_end = (first + bq - 1) // bk + 1
        c_int = jnp.minimum((hi + bk - 1) // bk, c_diag)
        lax.fori_loop(c_lo, c_int, partial(step, True), 0)
        lax.fori_loop(c_int, c_diag, partial(step, False), 0)
        lax.fori_loop(jnp.maximum(c_diag, c_lo), c_end, partial(step, True), 0)
        outs = []
        for h in range(heads):
            acc = acc_s[h]
            total = acc[HEAD_DIM : HEAD_DIM + 1, :]
            outs.append((acc[:HEAD_DIM, :] / total).T)
            lse_ref[h : h + 1, at] = m_s[h] + jnp.log(total)
        o_ref[at, :] = jnp.concatenate(outs, axis=1).astype(o_ref.dtype)
        return 0

    lax.fori_loop(0, rows // bq, query_block, 0)


def attn_fwd(packed, lengths, bq=256, bk=256, out_dtype=jnp.float32):
    rows = packed.shape[0]
    heads = packed.shape[1] // (3 * HEAD_DIM)
    return pl.pallas_call(
        partial(fwd_kernel, bq, bk),
        out_shape=(
            jax.ShapeDtypeStruct((rows, heads * HEAD_DIM), out_dtype),
            jax.ShapeDtypeStruct((8, rows), jnp.float32),
        ),
        in_specs=[pl.BlockSpec(memory_space=pltpu.SMEM), pl.BlockSpec(memory_space=pltpu.VMEM)],
        out_specs=[pl.BlockSpec(memory_space=pltpu.VMEM)] * 2,
        scratch_shapes=[
            pltpu.VMEM((heads, rows, HEAD_DIM), jnp.bfloat16),
            pltpu.VMEM((heads, HEAD_DIM, rows), jnp.bfloat16),
            pltpu.VMEM((heads, HEAD_DIM + 16, rows), jnp.bfloat16),
            pltpu.VMEM((heads, HEAD_DIM + 16, bq), jnp.float32),
            pltpu.VMEM((heads, 1, bq), jnp.float32),
        ],
        compiler_params=pltpu.CompilerParams(vmem_limit_bytes=48 << 20),
        name="attn_fwd",
    )(lengths, packed)


def bwd_kernel(bq, bk, len_ref, qkv_ref, o_ref, lse_ref, do_ref, out_ref,
               q_s, k_s, v_s, do_s, qt_s, kt_s, dot_s, d_s, dqt_s, dk_s, dv_s):
    rows = qkv_ref.shape[0]
    heads = k_s.shape[0]
    ends = seq_bounds(len_ref)
    scale = jnp.bfloat16(0.125)

    def stage(i, _):
        at = pl.ds(pl.multiple_of(i * bq, bq), bq)
        x = qkv_ref[at, :]
        g = do_ref[at, :]
        prod = g.astype(jnp.float32) * o_ref[at, :].astype(jnp.float32)
        for h in range(heads):
            base = h * 3 * HEAD_DIM
            q = x[:, base : base + HEAD_DIM] * scale
            k = x[:, base + HEAD_DIM : base + 2 * HEAD_DIM]
            d = g[:, h * HEAD_DIM : (h + 1) * HEAD_DIM]
            q_s[h, at, :] = q
            k_s[h, at, :] = k
            v_s[h, at, :] = x[:, base + 2 * HEAD_DIM : base + 3 * HEAD_DIM]
            do_s[h, at, :] = d
            qt_s[h, :, at] = q.T
            kt_s[h, :, at] = (k * scale).T
            dot_s[h, :, at] = d.T
            d_s[h, :, at] = jnp.sum(prod[:, h * HEAD_DIM : (h + 1) * HEAD_DIM].T, axis=0, keepdims=True)
            dqt_s[h, :, at] = jnp.zeros((HEAD_DIM, bq), jnp.float32)
        return 0

    lax.fori_loop(0, rows // bq, stage, 0)

    def key_block(j, _):
        c0 = pl.multiple_of(j * bk, bk)
        kat = pl.ds(c0, bk)
        for h in range(heads):
            dk_s[h, kat, :] = jnp.zeros((bk, HEAD_DIM), jnp.float32)
            dv_s[h, kat, :] = jnp.zeros((bk, HEAD_DIM), jnp.float32)

        def step(masked, i, _):
            first = pl.multiple_of(i * bq, bq)
            at = pl.ds(first, bq)
            if masked:
                q_pos = first + lax.broadcasted_iota(jnp.int32, (1, bq), 1)
                q_start = start_of(ends, q_pos)
                k_pos = c0 + lax.broadcasted_iota(jnp.int32, (bk, 1), 0)
                keep = (k_pos <= q_pos) & (k_pos >= q_start)
            for h in range(heads):
                s = dot(k_s[h, kat, :], qt_s[h, :, at]) - lse_ref[h : h + 1, at]
                if masked:
                    s = jnp.where(keep, s, NEG)
                p = jnp.exp(s)
                dp = dot(v_s[h, kat, :], dot_s[h, :, at])
                ds = (p * (dp - d_s[h, :, at])).astype(jnp.bfloat16)
                dv_s[h, kat, :] += dot(p.astype(jnp.bfloat16), do_s[h, at, :])
                dk_s[h, kat, :] += dot(ds, q_s[h, at, :])
                dqt_s[h, :, at] += dot(kt_s[h, :, kat], ds)
            return 0

        i_diag = c0 // bq
        i_after = (c0 + bk - 1) // bq + 1
        i_end = (end_of(ends, c0 + bk - 1) + bq - 1) // bq
        i_int = jnp.maximum(end_of(ends, c0) // bq, i_after)
        i_int = jnp.minimum(i_int, i_end)
        lax.fori_loop(i_diag, i_after, partial(step, True), 0)
        lax.fori_loop(i_after, i_int, partial(step, False), 0)
        lax.fori_loop(i_int, i_end, partial(step, True), 0)
        return 0

    lax.fori_loop(0, rows // bk, key_block, 0)

    def finish(i, _):
        at = pl.ds(pl.multiple_of(i * bq, bq), bq)
        parts = []
        for h in range(heads):
            parts += [dqt_s[h, :, at].T, dk_s[h, at, :], dv_s[h, at, :]]
        out_ref[at, :] = jnp.concatenate(parts, axis=1).astype(out_ref.dtype)
        return 0

    lax.fori_loop(0, rows // bq, finish, 0)


def attn_bwd(packed, lengths, att, lse, d_att, bq=256, bk=256):
    rows = packed.shape[0]
    heads = packed.shape[1] // (3 * HEAD_DIM)
    row_major = pltpu.VMEM((heads, rows, HEAD_DIM), jnp.bfloat16)
    col_major = pltpu.VMEM((heads, HEAD_DIM, rows), jnp.bfloat16)
    return pl.pallas_call(
        partial(bwd_kernel, bq, bk),
        out_shape=jax.ShapeDtypeStruct(packed.shape, jnp.bfloat16),
        in_specs=[pl.BlockSpec(memory_space=pltpu.SMEM)] + [pl.BlockSpec(memory_space=pltpu.VMEM)] * 4,
        out_specs=pl.BlockSpec(memory_space=pltpu.VMEM),
        scratch_shapes=[row_major] * 4 + [col_major] * 3 + [
            pltpu.VMEM((heads, 1, rows), jnp.float32),
            pltpu.VMEM((heads, HEAD_DIM, rows), jnp.float32),
            pltpu.VMEM((heads, rows, HEAD_DIM), jnp.float32),
            pltpu.VMEM((heads, rows, HEAD_DIM), jnp.float32),
        ],
        compiler_params=pltpu.CompilerParams(vmem_limit_bytes=56 << 20),
        name="attn_bwd",
    )(lengths, packed, att, lse, d_att)


def local(
    tokens,
    lengths,
    in_gain,
    qkv_weight,
    attn_gain,
    out_weight,
    ffn_gain,
    up_weight,
    hidden_gain,
    down_weight,
    out_grad,
):
    parts = lax.axis_size("tensor")
    own_rows, width = tokens.shape
    group_rows = own_rows * parts
    head_width = attn_gain.shape[0]

    def gather(values):
        return lax.all_gather(values, "tensor", axis=0, tiled=True)

    def to_rows(values):
        blocks = values.reshape(parts, own_rows, head_width)
        moved = lax.all_to_all(blocks, "tensor", 0, 0, tiled=True)
        return moved.transpose(1, 0, 2).reshape(own_rows, width)

    def to_heads(values):
        blocks = values.reshape(own_rows, parts, head_width).transpose(1, 0, 2)
        return lax.all_to_all(blocks, "tensor", 0, 0, tiled=True).reshape(group_rows, head_width)

    residual = tokens.astype(jnp.float32)
    in_unit, in_scale, in_normed = normalize(residual, in_gain)
    gathered_in = gather(in_normed.astype(jnp.bfloat16))
    full_out, full_up, full_down = gather(out_weight), gather(up_weight), gather(down_weight)
    full_gains = gather(jnp.concatenate((attn_gain, hidden_gain))).reshape(parts, -1)
    full_attn_gain = full_gains[:, :head_width].reshape(-1)
    full_hidden_gain = full_gains[:, head_width:].reshape(-1)
    full_up = full_up.reshape(parts, width, -1)
    packed = jnp.dot(gathered_in, qkv_weight, preferred_element_type=jnp.float32).astype(
        jnp.bfloat16
    )
    attended, log_total = attn_fwd(packed, lengths, 512, 512)
    own_att = to_rows(attended.astype(jnp.bfloat16)).astype(jnp.float32)

    att_unit, att_scale, att_normed = normalize(own_att, full_attn_gain)
    att_low = att_normed.astype(jnp.bfloat16)
    middle = residual + jnp.dot(att_low, full_out, preferred_element_type=jnp.float32)
    mid_unit, mid_scale, mid_normed = normalize(middle, ffn_gain)
    mid_low = mid_normed.astype(jnp.bfloat16)
    pre_act = jnp.einsum("rk,tkn->rtn", mid_low, full_up, preferred_element_type=jnp.float32)
    pre_act = pre_act.reshape(own_rows, -1)
    activated, gelu_pull = jax.vjp(partial(jax.nn.gelu, approximate=True), pre_act)
    act_unit, act_scale, act_normed = normalize(activated, full_hidden_gain)
    act_low = act_normed.astype(jnp.bfloat16)
    result = (middle + jnp.dot(act_low, full_down, preferred_element_type=jnp.float32)).astype(
        jnp.bfloat16
    )
    grad_down = contract_rows(act_low, out_grad)
    grad_act_low = contract_cols(out_grad, full_down)
    grad_act, grad_hidden = norm_back(grad_act_low, act_unit, act_scale, full_hidden_gain)
    grad_pre = gelu_pull(grad_act)[0].astype(jnp.bfloat16).reshape(own_rows, parts, -1)
    grad_up = jnp.einsum("rk,rtn->tkn", mid_low, grad_pre, preferred_element_type=jnp.float32)
    grad_mid_normed = jnp.einsum(
        "rtn,tkn->rk", grad_pre, full_up, preferred_element_type=jnp.float32
    )
    grad_mid_part, grad_ffn_gain = norm_back(grad_mid_normed, mid_unit, mid_scale, ffn_gain)
    grad_middle = out_grad.astype(jnp.float32) + grad_mid_part
    grad_mid_low = grad_middle.astype(jnp.bfloat16)
    grad_out = contract_rows(att_low, grad_mid_low)
    grad_att_low = contract_cols(grad_mid_low, full_out)
    grad_att, grad_attn_gain = norm_back(grad_att_low, att_unit, att_scale, full_attn_gain)
    grad_attended = to_heads(grad_att.astype(jnp.bfloat16))

    def scatter(values):
        return lax.psum_scatter(
            values.astype(jnp.bfloat16), "tensor", scatter_dimension=0, tiled=True
        )

    def total(values):
        return lax.psum(values, "dp")

    down_sum = total(scatter(grad_down).astype(jnp.float32))
    up_sum = total(scatter(grad_up.reshape(parts * width, -1)).astype(jnp.float32))
    out_sum = total(scatter(grad_out).astype(jnp.float32))

    grad_packed = attn_bwd(packed, lengths, attended, log_total, grad_attended, 512, 256)
    qkv_sum = total(contract_rows(gathered_in, grad_packed))
    grad_in_normed = scatter(contract_cols(grad_packed, qkv_weight)).astype(jnp.float32)
    grad_in_part, grad_in_gain = norm_back(grad_in_normed, in_unit, in_scale, in_gain)
    in_grad = grad_middle + grad_in_part
    gains = lax.psum(
        jnp.concatenate((grad_in_gain, grad_ffn_gain, grad_attn_gain, grad_hidden)),
        ("dp", "tensor"),
    )
    me = lax.axis_index("tensor")
    hidden = hidden_gain.shape[0]
    return (
        result,
        in_grad,
        gains[:width],
        qkv_sum,
        lax.dynamic_slice_in_dim(gains, 2 * width + me * head_width, head_width),
        out_sum,
        gains[width : 2 * width],
        up_sum,
        lax.dynamic_slice_in_dim(gains, 3 * width + me * hidden, hidden),
        down_sum,
    )


def solution(mesh):
    return jax.shard_map(
        local,
        mesh=mesh,
        in_specs=(
            P(("dp", "tensor"), None),
            P("dp", None),
            P(),
            P(None, "tensor"),
            P("tensor"),
            P("tensor", None),
            P(),
            P(None, "tensor"),
            P("tensor"),
            P("tensor", None),
            P(("dp", "tensor"), None),
        ),
        out_specs=(
            P(("dp", "tensor"), None),
            P(("dp", "tensor"), None),
            P(),
            P(None, "tensor"),
            P("tensor"),
            P("tensor", None),
            P(),
            P(None, "tensor"),
            P("tensor"),
            P("tensor", None),
        ),
        check_vma=False,
    )
```

```python
from functools import partial

import jax
import jax.numpy as jnp
from jax import lax
from jax.experimental import pallas as pl
from jax.experimental.pallas import tpu as pltpu
from jax.sharding import PartitionSpec as P

D = 768
HEAD_DIM = 64
FF = 3072
UNIT = 64


EPS = 1e-05


def contract_rows(left, right):
    return lax.dot_general(
        left, right, (((0,), (0,)), ((), ())), preferred_element_type=jnp.float32
    )


def contract_cols(left, right):
    return lax.dot_general(
        left, right, (((1,), (1,)), ((), ())), preferred_element_type=jnp.float32
    )


def normalize(values, gain):
    row_mean = jnp.mean(values, axis=1, keepdims=True)
    row_square = jnp.mean(values * values, axis=1, keepdims=True)
    inv_scale = lax.rsqrt(row_square - row_mean * row_mean + EPS)
    unit_rows = (values - row_mean) * inv_scale
    return (unit_rows, inv_scale, unit_rows * gain)


def norm_back(grad_normed, unit_rows, inv_scale, gain):
    weighted = grad_normed * gain
    first_mean = jnp.mean(weighted, axis=1, keepdims=True)
    second = jnp.mean(weighted * unit_rows, axis=1, keepdims=True)
    return (
        inv_scale * (weighted - first_mean - unit_rows * second),
        jnp.sum(grad_normed * unit_rows, axis=0),
    )


NEG = -1e30
def seq_bounds(len_ref):
    ends, total = [], 0
    for s in range(len_ref.shape[1]):
        total = total + len_ref[0, s] * UNIT
        ends.append(total)
    return ends


def start_of(ends, row):
    at = 0
    for end in ends:
        at = jnp.where(row >= end, end, at)
    return at


def end_of(ends, row):
    at = ends[-1]
    for end in reversed(ends):
        at = jnp.where(row < end, end, at)
    return at


def dot(a, b):
    return lax.dot_general(a, b, (((1,), (0,)), ((), ())), preferred_element_type=jnp.float32)


def fwd_kernel(bq, bk, len_ref, qkv_ref, o_ref, lse_ref, k_s, qt_s, vt_s, acc_s, m_s):
    rows = qkv_ref.shape[0]
    heads = k_s.shape[0]
    ends = seq_bounds(len_ref)
    ones = (lax.broadcasted_iota(jnp.int32, (16, bq), 0) == 0).astype(jnp.float32).astype(jnp.bfloat16)

    def stage(i, _):
        at = pl.ds(pl.multiple_of(i * bq, bq), bq)
        x = qkv_ref[at, :]
        for h in range(heads):
            base = h * 3 * HEAD_DIM
            q = x[:, base : base + HEAD_DIM] * jnp.bfloat16(0.125)
            qt_s[h, :, at] = q.T
            k_s[h, at, :] = x[:, base + HEAD_DIM : base + 2 * HEAD_DIM]
            vt_s[h, :HEAD_DIM, at] = x[:, base + 2 * HEAD_DIM : base + 3 * HEAD_DIM].T
            vt_s[h, HEAD_DIM:, at] = ones
        return 0

    lax.fori_loop(0, rows // bq, stage, 0)

    def query_block(i, _):
        first = pl.multiple_of(i * bq, bq)
        at = pl.ds(first, bq)
        q_pos = first + lax.broadcasted_iota(jnp.int32, (1, bq), 1)
        q_start = start_of(ends, q_pos)
        lo = start_of(ends, first)
        hi = start_of(ends, first + bq - 1)
        for h in range(heads):
            acc_s[h] = jnp.zeros_like(acc_s[h])
            m_s[h] = jnp.full_like(m_s[h], NEG)

        def step(masked, c, _):
            c0 = pl.multiple_of(c * bk, bk)
            for h in range(heads):
                s = dot(k_s[h, pl.ds(c0, bk), :], qt_s[h, :, at])
                if masked:
                    k_pos = c0 + lax.broadcasted_iota(jnp.int32, (bk, 1), 0)
                    s = jnp.where((k_pos <= q_pos) & (k_pos >= q_start), s, NEG)
                old = m_s[h]
                new = jnp.maximum(old, jnp.max(s, axis=0, keepdims=True))
                p = jnp.exp(s - new).astype(jnp.bfloat16)
                m_s[h] = new
                acc_s[h] = acc_s[h] * jnp.exp(old - new) + dot(vt_s[h, :, pl.ds(c0, bk)], p)
            return 0

        c_lo = lo // bk
        c_diag = first // bk
        c_end = (first + bq - 1) // bk + 1
        c_int = jnp.minimum((hi + bk - 1) // bk, c_diag)
        lax.fori_loop(c_lo, c_int, partial(step, True), 0)
        lax.fori_loop(c_int, c_diag, partial(step, False), 0)
        lax.fori_loop(jnp.maximum(c_diag, c_lo), c_end, partial(step, True), 0)
        outs = []
        for h in range(heads):
            acc = acc_s[h]
            total = acc[HEAD_DIM : HEAD_DIM + 1, :]
            outs.append((acc[:HEAD_DIM, :] / total).T)
            lse_ref[h : h + 1, at] = m_s[h] + jnp.log(total)
        o_ref[at, :] = jnp.concatenate(outs, axis=1).astype(o_ref.dtype)
        return 0

    lax.fori_loop(0, rows // bq, query_block, 0)


def attn_fwd(packed, lengths, bq=256, bk=256, out_dtype=jnp.float32):
    rows = packed.shape[0]
    heads = packed.shape[1] // (3 * HEAD_DIM)
    return pl.pallas_call(
        partial(fwd_kernel, bq, bk),
        out_shape=(
            jax.ShapeDtypeStruct((rows, heads * HEAD_DIM), out_dtype),
            jax.ShapeDtypeStruct((8, rows), jnp.float32),
        ),
        in_specs=[pl.BlockSpec(memory_space=pltpu.SMEM), pl.BlockSpec(memory_space=pltpu.VMEM)],
        out_specs=[pl.BlockSpec(memory_space=pltpu.VMEM)] * 2,
        scratch_shapes=[
            pltpu.VMEM((heads, rows, HEAD_DIM), jnp.bfloat16),
            pltpu.VMEM((heads, HEAD_DIM, rows), jnp.bfloat16),
            pltpu.VMEM((heads, HEAD_DIM + 16, rows), jnp.bfloat16),
            pltpu.VMEM((heads, HEAD_DIM + 16, bq), jnp.float32),
            pltpu.VMEM((heads, 1, bq), jnp.float32),
        ],
        compiler_params=pltpu.CompilerParams(vmem_limit_bytes=48 << 20),
        name="attn_fwd",
    )(lengths, packed)


def bwd_kernel(bq, bk, len_ref, qkv_ref, o_ref, lse_ref, do_ref, out_ref,
               q_s, k_s, v_s, do_s, qt_s, kt_s, dot_s, d_s, dqt_s, dk_s, dv_s):
    rows = qkv_ref.shape[0]
    heads = k_s.shape[0]
    ends = seq_bounds(len_ref)
    scale = jnp.bfloat16(0.125)

    def stage(i, _):
        at = pl.ds(pl.multiple_of(i * bq, bq), bq)
        x = qkv_ref[at, :]
        g = do_ref[at, :]
        prod = g.astype(jnp.float32) * o_ref[at, :].astype(jnp.float32)
        for h in range(heads):
            base = h * 3 * HEAD_DIM
            q = x[:, base : base + HEAD_DIM] * scale
            k = x[:, base + HEAD_DIM : base + 2 * HEAD_DIM]
            d = g[:, h * HEAD_DIM : (h + 1) * HEAD_DIM]
            q_s[h, at, :] = q
            k_s[h, at, :] = k
            v_s[h, at, :] = x[:, base + 2 * HEAD_DIM : base + 3 * HEAD_DIM]
            do_s[h, at, :] = d
            qt_s[h, :, at] = q.T
            kt_s[h, :, at] = (k * scale).T
            dot_s[h, :, at] = d.T
            d_s[h, :, at] = jnp.sum(prod[:, h * HEAD_DIM : (h + 1) * HEAD_DIM].T, axis=0, keepdims=True)
            dqt_s[h, :, at] = jnp.zeros((HEAD_DIM, bq), jnp.float32)
        return 0

    lax.fori_loop(0, rows // bq, stage, 0)

    def key_block(j, _):
        c0 = pl.multiple_of(j * bk, bk)
        kat = pl.ds(c0, bk)
        for h in range(heads):
            dk_s[h, kat, :] = jnp.zeros((bk, HEAD_DIM), jnp.float32)
            dv_s[h, kat, :] = jnp.zeros((bk, HEAD_DIM), jnp.float32)

        def step(masked, i, _):
            first = pl.multiple_of(i * bq, bq)
            at = pl.ds(first, bq)
            if masked:
                q_pos = first + lax.broadcasted_iota(jnp.int32, (1, bq), 1)
                q_start = start_of(ends, q_pos)
                k_pos = c0 + lax.broadcasted_iota(jnp.int32, (bk, 1), 0)
                keep = (k_pos <= q_pos) & (k_pos >= q_start)
            for h in range(heads):
                s = dot(k_s[h, kat, :], qt_s[h, :, at]) - lse_ref[h : h + 1, at]
                if masked:
                    s = jnp.where(keep, s, NEG)
                p = jnp.exp(s)
                dp = dot(v_s[h, kat, :], dot_s[h, :, at])
                ds = (p * (dp - d_s[h, :, at])).astype(jnp.bfloat16)
                dv_s[h, kat, :] += dot(p.astype(jnp.bfloat16), do_s[h, at, :])
                dk_s[h, kat, :] += dot(ds, q_s[h, at, :])
                dqt_s[h, :, at] += dot(kt_s[h, :, kat], ds)
            return 0

        i_diag = c0 // bq
        i_after = (c0 + bk - 1) // bq + 1
        i_end = (end_of(ends, c0 + bk - 1) + bq - 1) // bq
        i_int = jnp.maximum(end_of(ends, c0) // bq, i_after)
        i_int = jnp.minimum(i_int, i_end)
        lax.fori_loop(i_diag, i_after, partial(step, True), 0)
        lax.fori_loop(i_after, i_int, partial(step, False), 0)
        lax.fori_loop(i_int, i_end, partial(step, True), 0)
        return 0

    lax.fori_loop(0, rows // bk, key_block, 0)

    def finish(i, _):
        at = pl.ds(pl.multiple_of(i * bq, bq), bq)
        parts = []
        for h in range(heads):
            parts += [dqt_s[h, :, at].T, dk_s[h, at, :], dv_s[h, at, :]]
        out_ref[at, :] = jnp.concatenate(parts, axis=1).astype(out_ref.dtype)
        return 0

    lax.fori_loop(0, rows // bq, finish, 0)


def attn_bwd(packed, lengths, att, lse, d_att, bq=256, bk=256):
    rows = packed.shape[0]
    heads = packed.shape[1] // (3 * HEAD_DIM)
    row_major = pltpu.VMEM((heads, rows, HEAD_DIM), jnp.bfloat16)
    col_major = pltpu.VMEM((heads, HEAD_DIM, rows), jnp.bfloat16)
    return pl.pallas_call(
        partial(bwd_kernel, bq, bk),
        out_shape=jax.ShapeDtypeStruct(packed.shape, jnp.bfloat16),
        in_specs=[pl.BlockSpec(memory_space=pltpu.SMEM)] + [pl.BlockSpec(memory_space=pltpu.VMEM)] * 4,
        out_specs=pl.BlockSpec(memory_space=pltpu.VMEM),
        scratch_shapes=[row_major] * 4 + [col_major] * 3 + [
            pltpu.VMEM((heads, 1, rows), jnp.float32),
            pltpu.VMEM((heads, HEAD_DIM, rows), jnp.float32),
            pltpu.VMEM((heads, rows, HEAD_DIM), jnp.float32),
            pltpu.VMEM((heads, rows, HEAD_DIM), jnp.float32),
        ],
        compiler_params=pltpu.CompilerParams(vmem_limit_bytes=56 << 20),
        name="attn_bwd",
    )(lengths, packed, att, lse, d_att)


MESH = pl.DeviceIdType.MESH
CHUNK = 192


def flip(index, bit):
    return index + bit - 2 * bit * ((index // bit) % 2)


def peers_of(parts, groups):
    steps, bit = [], 1
    while bit < parts:
        steps.append(("tensor", bit))
        bit *= 2
    bit = 1
    while bit < groups:
        steps.append(("dp", bit))
        bit *= 2
    return steps


def at_peer(axis, bit):
    return {axis: flip(lax.axis_index(axis), bit)}


def greet(steps):
    barrier = pltpu.get_barrier_semaphore()
    for axis, bit in steps:
        pl.semaphore_signal(barrier, inc=1, device_id=at_peer(axis, bit), device_id_type=MESH)
    pl.semaphore_wait(barrier, len(steps))


def remote(src, dst, send, recv, axis, bit):
    copy = pltpu.make_async_remote_copy(
        src_ref=src,
        dst_ref=dst,
        send_sem=send,
        recv_sem=recv,
        device_id=at_peer(axis, bit),
        device_id_type=MESH,
    )
    copy.start()
    return copy


def rounded(values):
    return values.astype(jnp.bfloat16)


def sync_kernel(groups, sizes, out_ref, up_ref, down_ref, gains_ref, sum_ref, gains_sum_ref,
                own, first, second, acc, to_y, to_x, from_x, to_z, from_z, to_w, from_w,
                more_to, more_from, gain_at, send, recv, local_sem, gain_send, gain_recv):
    steps = peers_of(4, groups)
    me, dp = lax.axis_index("tensor"), lax.axis_index("dp")
    cols = out_ref.shape[1]
    half, rows2, rows4 = cols // 2, CHUNK // 2, CHUNK // 4
    b0, b1, b2 = dp % 2, (dp // 2) % 2, (dp // 4) % 2
    chunks = []
    for ref, size in zip((down_ref, up_ref, out_ref), sizes):
        for at in range(0, size, CHUNK):
            chunks.append((ref, size, at))
    far = steps[5:]
    flight = {}
    sends = []

    def take(ref, size, shard, at):
        return ref.at[pl.ds(pl.multiple_of(shard * size + at, 16), CHUNK), :]

    def go(c, s, src, dst, axis, bit):
        copy = remote(src, dst, send.at[c, s], recv.at[c, s], axis, bit)
        flight[c, s] = copy
        sends.append(copy)

    def col(b):
        return pl.ds(pl.multiple_of(b * half, 128), half)

    def row2(b):
        return pl.ds(pl.multiple_of(b * rows2, 16), rows2)

    def row4(b, bb):
        return pl.ds(pl.multiple_of(b * rows2 + bb * rows4, 16), rows4)

    def pair(c):
        ref, size, at = chunks[c]
        go(c, 0, take(ref, size, flip(me, 1), at), first.at[c, 0], "tensor", 1)
        go(c, 1, take(ref, size, flip(flip(me, 1), 2), at), first.at[c, 1], "tensor", 1)
        for k, shard in enumerate((me, flip(me, 2))):
            copy = pltpu.make_async_copy(take(ref, size, shard, at), own.at[c, k], local_sem.at[c, k])
            copy.start()
            flight[c, "own", k] = copy

    def chip(c):
        flight[c, "own", 1].wait()
        flight[c, 1].wait_recv()
        to_y[c] = rounded(own[c, 1].astype(jnp.float32) + first[c, 1].astype(jnp.float32))
        go(c, 2, to_y.at[c], second.at[c], "tensor", 2)
        flight[c, "own", 0].wait()
        flight[c, 0].wait_recv()
        acc[c] = own[c, 0].astype(jnp.float32) + first[c, 0].astype(jnp.float32)

    def x_half(c):
        flight[c, 2].wait_recv()
        acc[c] += second[c].astype(jnp.float32)
        to_x[c] = rounded(acc[c, :, col(1 - b0)])
        go(c, 3, to_x.at[c], from_x.at[c], "dp", 1)

    def z_half(c):
        flight[c, 3].wait_recv()
        acc[c, :, col(b0)] += from_x[c].astype(jnp.float32)
        to_z[c] = rounded(acc[c, row2(1 - b1), col(b0)])
        go(c, 4, to_z.at[c], from_z.at[c], "dp", 2)

    def z_quarter(c):
        flight[c, 4].wait_recv()
        acc[c, row2(b1), col(b0)] += from_z[c].astype(jnp.float32)
        to_w[c] = rounded(acc[c, row4(b1, 1 - b2), col(b0)])
        go(c, 5, to_w.at[c], from_w.at[c], "dp", 4)

    def settle(c):
        flight[c, 5].wait_recv()
        mine = acc[c, row4(b1, b2), col(b0)] + from_w[c].astype(jnp.float32)
        for n, (axis, bit) in enumerate(far):
            more_to[c, n] = rounded(mine)
            go(c, 9 + n, more_to.at[c, n], more_from.at[c, n], axis, bit)
            flight[c, 9 + n].wait_recv()
            mine = rounded(mine).astype(jnp.float32) + more_from[c, n].astype(jnp.float32)
        sum_ref[c, row4(b1, b2), col(b0)] = rounded(mine)
        piece = sum_ref.at[c, row4(b1, b2), col(b0)]
        go(c, 6, piece, piece, "dp", 4)

    def z_share(c):
        flight[c, 6].wait_recv()
        piece = sum_ref.at[c, row2(b1), col(b0)]
        go(c, 7, piece, piece, "dp", 2)

    def x_share(c):
        flight[c, 7].wait_recv()
        piece = sum_ref.at[c, :, col(b0)]
        go(c, 8, piece, piece, "dp", 1)

    def end(c):
        flight[c, 8].wait_recv()

    stages = (pair, chip, x_half, z_half, z_quarter, settle, z_share, x_share, end)

    def gain_start(n):
        axis, bit = steps[n]
        copy = remote(gain_at.at[0, n], gain_at.at[1, n], gain_send.at[n], gain_recv.at[n], axis, bit)
        flight["gain", n] = copy
        sends.append(copy)

    greet(steps)
    gain_at[0, 0] = gains_ref[...]
    gain_start(0)
    gain_turn = 0
    for turn in range(len(chunks) + len(stages) - 1):
        for s in reversed(range(len(stages))):
            if 0 <= turn - s < len(chunks):
                stages[s](turn - s)
        if gain_turn < len(steps):
            flight["gain", gain_turn].wait_recv()
            now = gain_at[0, gain_turn] + gain_at[1, gain_turn]
            gain_turn += 1
            if gain_turn < len(steps):
                gain_at[0, gain_turn] = now
                gain_start(gain_turn)
            else:
                gains_sum_ref[...] = now
    for copy in sends:
        copy.wait_send()


def grad_sync(groups, grad_out, grad_up, grad_down, gains):
    width = grad_out.shape[1]
    sizes = tuple(g.shape[0] // 4 for g in (grad_down, grad_up, grad_out))
    n = sum(sizes) // CHUNK
    steps = len(peers_of(4, groups))
    extra = max(steps - 5, 1)
    bf16 = lambda *shape: pltpu.VMEM(shape, jnp.bfloat16)
    anywhere, vmem = pl.BlockSpec(memory_space=pl.ANY), pl.BlockSpec(memory_space=pltpu.VMEM)
    return pl.pallas_call(
        partial(sync_kernel, groups, sizes),
        out_shape=(
            jax.ShapeDtypeStruct((n, CHUNK, width), jnp.bfloat16),
            jax.ShapeDtypeStruct(gains.shape, jnp.float32),
        ),
        in_specs=[anywhere] * 3 + [vmem],
        out_specs=[vmem, vmem],
        scratch_shapes=[
            bf16(n, 2, CHUNK, width),
            bf16(n, 2, CHUNK, width),
            bf16(n, CHUNK, width),
            pltpu.VMEM((n, CHUNK, width), jnp.float32),
            bf16(n, CHUNK, width),
            bf16(n, CHUNK, width // 2),
            bf16(n, CHUNK, width // 2),
            bf16(n, CHUNK // 2, width // 2),
            bf16(n, CHUNK // 2, width // 2),
            bf16(n, CHUNK // 4, width // 2),
            bf16(n, CHUNK // 4, width // 2),
            bf16(n, extra, CHUNK // 4, width // 2),
            bf16(n, extra, CHUNK // 4, width // 2),
            pltpu.VMEM((2, steps) + gains.shape, jnp.float32),
            pltpu.SemaphoreType.DMA((n, 9 + extra)),
            pltpu.SemaphoreType.DMA((n, 9 + extra)),
            pltpu.SemaphoreType.DMA((n, 2)),
            pltpu.SemaphoreType.DMA((steps,)),
            pltpu.SemaphoreType.DMA((steps,)),
        ],
        compiler_params=pltpu.CompilerParams(
            collective_id=0, has_side_effects=True, vmem_limit_bytes=56 << 20
        ),
        name="grad_sync",
    )(grad_out, grad_up, grad_down, gains)


def local(
    tokens,
    lengths,
    in_gain,
    qkv_weight,
    attn_gain,
    out_weight,
    ffn_gain,
    up_weight,
    hidden_gain,
    down_weight,
    out_grad,
):
    parts = lax.axis_size("tensor")
    own_rows, width = tokens.shape
    group_rows = own_rows * parts
    head_width = attn_gain.shape[0]

    def gather(values):
        return lax.all_gather(values, "tensor", axis=0, tiled=True)

    def to_rows(values):
        blocks = values.reshape(parts, own_rows, head_width)
        moved = lax.all_to_all(blocks, "tensor", 0, 0, tiled=True)
        return moved.transpose(1, 0, 2).reshape(own_rows, width)

    def to_heads(values):
        blocks = values.reshape(own_rows, parts, head_width).transpose(1, 0, 2)
        return lax.all_to_all(blocks, "tensor", 0, 0, tiled=True).reshape(group_rows, head_width)

    residual = tokens.astype(jnp.float32)
    in_unit, in_scale, in_normed = normalize(residual, in_gain)
    gathered_in = gather(in_normed.astype(jnp.bfloat16))
    full_out, full_up, full_down = gather(out_weight), gather(up_weight), gather(down_weight)
    full_gains = gather(jnp.concatenate((attn_gain, hidden_gain))).reshape(parts, -1)
    full_attn_gain = full_gains[:, :head_width].reshape(-1)
    full_hidden_gain = full_gains[:, head_width:].reshape(-1)
    full_up = full_up.reshape(parts, width, -1)
    packed = jnp.dot(gathered_in, qkv_weight, preferred_element_type=jnp.float32).astype(
        jnp.bfloat16
    )
    attended, log_total = attn_fwd(packed, lengths, 512, 512)
    own_att = to_rows(attended.astype(jnp.bfloat16)).astype(jnp.float32)

    att_unit, att_scale, att_normed = normalize(own_att, full_attn_gain)
    att_low = att_normed.astype(jnp.bfloat16)
    middle = residual + jnp.dot(att_low, full_out, preferred_element_type=jnp.float32)
    mid_unit, mid_scale, mid_normed = normalize(middle, ffn_gain)
    mid_low = mid_normed.astype(jnp.bfloat16)
    pre_act = jnp.einsum("rk,tkn->rtn", mid_low, full_up, preferred_element_type=jnp.float32)
    pre_act = pre_act.reshape(own_rows, -1)
    activated, gelu_pull = jax.vjp(partial(jax.nn.gelu, approximate=True), pre_act)
    act_unit, act_scale, act_normed = normalize(activated, full_hidden_gain)
    act_low = act_normed.astype(jnp.bfloat16)
    result = (middle + jnp.dot(act_low, full_down, preferred_element_type=jnp.float32)).astype(
        jnp.bfloat16
    )
    grad_down = contract_rows(act_low, out_grad)
    grad_act_low = contract_cols(out_grad, full_down)
    grad_act, grad_hidden = norm_back(grad_act_low, act_unit, act_scale, full_hidden_gain)
    grad_pre = gelu_pull(grad_act)[0].astype(jnp.bfloat16).reshape(own_rows, parts, -1)
    grad_up = jnp.einsum("rk,rtn->tkn", mid_low, grad_pre, preferred_element_type=jnp.float32)
    grad_mid_normed = jnp.einsum(
        "rtn,tkn->rk", grad_pre, full_up, preferred_element_type=jnp.float32
    )
    grad_mid_part, grad_ffn_gain = norm_back(grad_mid_normed, mid_unit, mid_scale, ffn_gain)
    grad_middle = out_grad.astype(jnp.float32) + grad_mid_part
    grad_mid_low = grad_middle.astype(jnp.bfloat16)
    grad_out = contract_rows(att_low, grad_mid_low)
    grad_att_low = contract_cols(grad_mid_low, full_out)
    grad_att, grad_attn_gain = norm_back(grad_att_low, att_unit, att_scale, full_attn_gain)
    grad_attended = to_heads(grad_att.astype(jnp.bfloat16))

    grad_packed = attn_bwd(packed, lengths, attended, log_total, grad_attended, 512, 256)
    qkv_sum = lax.psum(contract_rows(gathered_in, grad_packed), "dp")
    grad_in_normed = lax.psum_scatter(
        contract_cols(grad_packed, qkv_weight).astype(jnp.bfloat16),
        "tensor",
        scatter_dimension=0,
        tiled=True,
    ).astype(jnp.float32)
    grad_in_part, grad_in_gain = norm_back(grad_in_normed, in_unit, in_scale, in_gain)
    in_grad = grad_middle + grad_in_part
    gain_parts = jnp.concatenate((grad_in_gain, grad_ffn_gain, grad_attn_gain, grad_hidden))
    sums, gains = grad_sync(
        lax.axis_size("dp"),
        rounded(grad_out),
        rounded(grad_up.reshape(parts * width, -1)),
        rounded(grad_down),
        gain_parts.reshape(-1, 128),
    )
    gains = gains.reshape(-1)
    me = lax.axis_index("tensor")
    hidden = hidden_gain.shape[0]
    sums = sums.reshape(-1, width).astype(jnp.float32)
    down_sum, up_sum, out_sum = sums[:hidden], sums[hidden : hidden + width], sums[hidden + width :]
    return (
        result,
        in_grad,
        gains[:width],
        qkv_sum,
        lax.dynamic_slice_in_dim(gains, 2 * width + me * head_width, head_width),
        out_sum,
        gains[width : 2 * width],
        up_sum,
        lax.dynamic_slice_in_dim(gains, 3 * width + me * hidden, hidden),
        down_sum,
    )


def solution(mesh):
    return jax.shard_map(
        local,
        mesh=mesh,
        in_specs=(
            P(("dp", "tensor"), None),
            P("dp", None),
            P(),
            P(None, "tensor"),
            P("tensor"),
            P("tensor", None),
            P(),
            P(None, "tensor"),
            P("tensor"),
            P("tensor", None),
            P(("dp", "tensor"), None),
        ),
        out_specs=(
            P(("dp", "tensor"), None),
            P(("dp", "tensor"), None),
            P(),
            P(None, "tensor"),
            P("tensor"),
            P("tensor", None),
            P(),
            P(None, "tensor"),
            P("tensor"),
            P("tensor", None),
        ),
        check_vma=False,
    )
```

```python
from functools import partial

import jax
import jax.numpy as jnp
from jax import lax
from jax.experimental import pallas as pl
from jax.experimental.pallas import tpu as pltpu
from jax.sharding import PartitionSpec as P

HEAD_DIM = 64
UNIT = 64
EPS = 1e-05


def contract_rows(left, right):
    return lax.dot_general(
        left, right, (((0,), (0,)), ((), ())), preferred_element_type=jnp.float32
    )


def contract_cols(left, right):
    return lax.dot_general(
        left, right, (((1,), (1,)), ((), ())), preferred_element_type=jnp.float32
    )


NEG = -1e30


def seq_bounds(len_ref):
    ends, total = [], 0
    for s in range(len_ref.shape[1]):
        total = total + len_ref[0, s] * UNIT
        ends.append(total)
    return ends


def start_of(ends, row):
    at = 0
    for end in ends:
        at = jnp.where(row >= end, end, at)
    return at


def end_of(ends, row):
    at = ends[-1]
    for end in reversed(ends):
        at = jnp.where(row < end, end, at)
    return at


def dot(a, b):
    return lax.dot_general(a, b, (((1,), (0,)), ((), ())), preferred_element_type=jnp.float32)


def fwd_kernel(bq, bk, len_ref, qkv_ref, o_ref, lse_ref, k_s, qt_s, vt_s, acc_s, m_s):
    rows = qkv_ref.shape[0]
    heads = k_s.shape[0]
    ends = seq_bounds(len_ref)
    ones = (lax.broadcasted_iota(jnp.int32, (16, bq), 0) == 0).astype(jnp.float32).astype(jnp.bfloat16)

    def stage(i, _):
        at = pl.ds(pl.multiple_of(i * bq, bq), bq)
        x = qkv_ref[at, :]
        for h in range(heads):
            base = h * 3 * HEAD_DIM
            q = x[:, base : base + HEAD_DIM] * jnp.bfloat16(0.125)
            qt_s[h, :, at] = q.T
            k_s[h, at, :] = x[:, base + HEAD_DIM : base + 2 * HEAD_DIM]
            vt_s[h, :HEAD_DIM, at] = x[:, base + 2 * HEAD_DIM : base + 3 * HEAD_DIM].T
            vt_s[h, HEAD_DIM:, at] = ones
        return 0

    lax.fori_loop(0, rows // bq, stage, 0)

    def query_block(i, _):
        first = pl.multiple_of(i * bq, bq)
        at = pl.ds(first, bq)
        q_pos = first + lax.broadcasted_iota(jnp.int32, (1, bq), 1)
        q_start = start_of(ends, q_pos)
        lo = start_of(ends, first)
        hi = start_of(ends, first + bq - 1)
        for h in range(heads):
            acc_s[h] = jnp.zeros_like(acc_s[h])
            m_s[h] = jnp.full_like(m_s[h], NEG)

        def step(masked, c, _):
            c0 = pl.multiple_of(c * bk, bk)
            for h in range(heads):
                s = dot(k_s[h, pl.ds(c0, bk), :], qt_s[h, :, at])
                if masked:
                    k_pos = c0 + lax.broadcasted_iota(jnp.int32, (bk, 1), 0)
                    s = jnp.where((k_pos <= q_pos) & (k_pos >= q_start), s, NEG)
                old = m_s[h]
                new = jnp.maximum(old, jnp.max(s, axis=0, keepdims=True))
                p = jnp.exp(s - new).astype(jnp.bfloat16)
                m_s[h] = new
                acc_s[h] = acc_s[h] * jnp.exp(old - new) + dot(vt_s[h, :, pl.ds(c0, bk)], p)
            return 0

        c_lo = lo // bk
        c_diag = first // bk
        c_end = (first + bq - 1) // bk + 1
        c_int = jnp.minimum((hi + bk - 1) // bk, c_diag)
        lax.fori_loop(c_lo, c_int, partial(step, True), 0)
        lax.fori_loop(c_int, c_diag, partial(step, False), 0)
        lax.fori_loop(jnp.maximum(c_diag, c_lo), c_end, partial(step, True), 0)
        outs = []
        for h in range(heads):
            acc = acc_s[h]
            total = acc[HEAD_DIM : HEAD_DIM + 1, :]
            outs.append((acc[:HEAD_DIM, :] / total).T)
            lse_ref[h : h + 1, at] = m_s[h] + jnp.log(total)
        o_ref[at, :] = jnp.concatenate(outs, axis=1).astype(o_ref.dtype)
        return 0

    lax.fori_loop(0, rows // bq, query_block, 0)


def attn_fwd(packed, lengths, bq=256, bk=256, out_dtype=jnp.float32):
    rows = packed.shape[0]
    heads = packed.shape[1] // (3 * HEAD_DIM)
    return pl.pallas_call(
        partial(fwd_kernel, bq, bk),
        out_shape=(
            jax.ShapeDtypeStruct((rows, heads * HEAD_DIM), out_dtype),
            jax.ShapeDtypeStruct((8, rows), jnp.float32),
        ),
        in_specs=[pl.BlockSpec(memory_space=pltpu.SMEM), pl.BlockSpec(memory_space=pltpu.VMEM)],
        out_specs=[pl.BlockSpec(memory_space=pltpu.VMEM)] * 2,
        scratch_shapes=[
            pltpu.VMEM((heads, rows, HEAD_DIM), jnp.bfloat16),
            pltpu.VMEM((heads, HEAD_DIM, rows), jnp.bfloat16),
            pltpu.VMEM((heads, HEAD_DIM + 16, rows), jnp.bfloat16),
            pltpu.VMEM((heads, HEAD_DIM + 16, bq), jnp.float32),
            pltpu.VMEM((heads, 1, bq), jnp.float32),
        ],
        compiler_params=pltpu.CompilerParams(vmem_limit_bytes=48 << 20),
        name="attn_fwd",
    )(lengths, packed)


def bwd_kernel(bq, bk, len_ref, qkv_ref, o_ref, lse_ref, do_ref, out_ref,
               q_s, k_s, v_s, do_s, qt_s, kt_s, dot_s, d_s, dqt_s, dk_s, dv_s):
    rows = qkv_ref.shape[0]
    heads = k_s.shape[0]
    ends = seq_bounds(len_ref)
    scale = jnp.bfloat16(0.125)

    def stage(i, _):
        at = pl.ds(pl.multiple_of(i * bq, bq), bq)
        x = qkv_ref[at, :]
        g = do_ref[at, :]
        prod = g.astype(jnp.float32) * o_ref[at, :].astype(jnp.float32)
        for h in range(heads):
            base = h * 3 * HEAD_DIM
            q = x[:, base : base + HEAD_DIM] * scale
            k = x[:, base + HEAD_DIM : base + 2 * HEAD_DIM]
            d = g[:, h * HEAD_DIM : (h + 1) * HEAD_DIM]
            q_s[h, at, :] = q
            k_s[h, at, :] = k
            v_s[h, at, :] = x[:, base + 2 * HEAD_DIM : base + 3 * HEAD_DIM]
            do_s[h, at, :] = d
            qt_s[h, :, at] = q.T
            kt_s[h, :, at] = (k * scale).T
            dot_s[h, :, at] = d.T
            d_s[h, :, at] = jnp.sum(prod[:, h * HEAD_DIM : (h + 1) * HEAD_DIM].T, axis=0, keepdims=True)
            dqt_s[h, :, at] = jnp.zeros((HEAD_DIM, bq), jnp.float32)
        return 0

    lax.fori_loop(0, rows // bq, stage, 0)

    def key_block(j, _):
        c0 = pl.multiple_of(j * bk, bk)
        kat = pl.ds(c0, bk)
        for h in range(heads):
            dk_s[h, kat, :] = jnp.zeros((bk, HEAD_DIM), jnp.float32)
            dv_s[h, kat, :] = jnp.zeros((bk, HEAD_DIM), jnp.float32)

        def step(masked, i, _):
            first = pl.multiple_of(i * bq, bq)
            at = pl.ds(first, bq)
            if masked:
                q_pos = first + lax.broadcasted_iota(jnp.int32, (1, bq), 1)
                q_start = start_of(ends, q_pos)
                k_pos = c0 + lax.broadcasted_iota(jnp.int32, (bk, 1), 0)
                keep = (k_pos <= q_pos) & (k_pos >= q_start)
            for h in range(heads):
                s = dot(k_s[h, kat, :], qt_s[h, :, at]) - lse_ref[h : h + 1, at]
                if masked:
                    s = jnp.where(keep, s, NEG)
                p = jnp.exp(s)
                dp = dot(v_s[h, kat, :], dot_s[h, :, at])
                ds = (p * (dp - d_s[h, :, at])).astype(jnp.bfloat16)
                dv_s[h, kat, :] += dot(p.astype(jnp.bfloat16), do_s[h, at, :])
                dk_s[h, kat, :] += dot(ds, q_s[h, at, :])
                dqt_s[h, :, at] += dot(kt_s[h, :, kat], ds)
            return 0

        i_diag = c0 // bq
        i_after = (c0 + bk - 1) // bq + 1
        i_end = (end_of(ends, c0 + bk - 1) + bq - 1) // bq
        i_int = jnp.maximum(end_of(ends, c0) // bq, i_after)
        i_int = jnp.minimum(i_int, i_end)
        lax.fori_loop(i_diag, i_after, partial(step, True), 0)
        lax.fori_loop(i_after, i_int, partial(step, False), 0)
        lax.fori_loop(i_int, i_end, partial(step, True), 0)
        return 0

    lax.fori_loop(0, rows // bk, key_block, 0)

    def finish(i, _):
        at = pl.ds(pl.multiple_of(i * bq, bq), bq)
        parts = []
        for h in range(heads):
            parts += [dqt_s[h, :, at].T, dk_s[h, at, :], dv_s[h, at, :]]
        out_ref[at, :] = jnp.concatenate(parts, axis=1).astype(out_ref.dtype)
        return 0

    lax.fori_loop(0, rows // bq, finish, 0)


def attn_bwd(packed, lengths, att, lse, d_att, bq=256, bk=256):
    rows = packed.shape[0]
    heads = packed.shape[1] // (3 * HEAD_DIM)
    row_major = pltpu.VMEM((heads, rows, HEAD_DIM), jnp.bfloat16)
    col_major = pltpu.VMEM((heads, HEAD_DIM, rows), jnp.bfloat16)
    return pl.pallas_call(
        partial(bwd_kernel, bq, bk),
        out_shape=jax.ShapeDtypeStruct(packed.shape, jnp.bfloat16),
        in_specs=[pl.BlockSpec(memory_space=pltpu.SMEM)] + [pl.BlockSpec(memory_space=pltpu.VMEM)] * 4,
        out_specs=pl.BlockSpec(memory_space=pltpu.VMEM),
        scratch_shapes=[row_major] * 4 + [col_major] * 3 + [
            pltpu.VMEM((heads, 1, rows), jnp.float32),
            pltpu.VMEM((heads, HEAD_DIM, rows), jnp.float32),
            pltpu.VMEM((heads, rows, HEAD_DIM), jnp.float32),
            pltpu.VMEM((heads, rows, HEAD_DIM), jnp.float32),
        ],
        compiler_params=pltpu.CompilerParams(vmem_limit_bytes=56 << 20),
        name="attn_bwd",
    )(lengths, packed, att, lse, d_att)


MESH = pl.DeviceIdType.MESH
CHUNK = 192


def flip(index, bit):
    return index + bit - 2 * bit * ((index // bit) % 2)


def peers_of(parts, groups):
    steps, bit = [], 1
    while bit < parts:
        steps.append(("tensor", bit))
        bit *= 2
    bit = 1
    while bit < groups:
        steps.append(("dp", bit))
        bit *= 2
    return steps


def at_peer(axis, bit):
    return {axis: flip(lax.axis_index(axis), bit)}


def greet(steps):
    barrier = pltpu.get_barrier_semaphore()
    for axis, bit in steps:
        pl.semaphore_signal(barrier, inc=1, device_id=at_peer(axis, bit), device_id_type=MESH)
    pl.semaphore_wait(barrier, len(steps))


def remote(src, dst, send, recv, axis, bit):
    copy = pltpu.make_async_remote_copy(
        src_ref=src,
        dst_ref=dst,
        send_sem=send,
        recv_sem=recv,
        device_id=at_peer(axis, bit),
        device_id_type=MESH,
    )
    copy.start()
    return copy


def rounded(values):
    return values.astype(jnp.bfloat16)


def sync_kernel(groups, grads_ref, gains_ref, sum_ref, gains_sum_ref,
                own, first, second, acc, to_y, to_x, from_x, to_z, from_z, to_w, from_w,
                more_to, more_from, gain_at, send, recv, local_sem, gain_send, gain_recv):
    steps = peers_of(4, groups)
    me, dp = lax.axis_index("tensor"), lax.axis_index("dp")
    cols = grads_ref.shape[2]
    half, rows2, rows4 = cols // 2, CHUNK // 2, CHUNK // 4
    b0, b1, b2 = dp % 2, (dp // 2) % 2, (dp // 4) % 2
    chunks = range(grads_ref.shape[1] // CHUNK)
    far = steps[5:]
    flight = {}
    sends = []

    def take(c, shard):
        return grads_ref.at[shard, pl.ds(c * CHUNK, CHUNK), :]

    def go(c, s, src, dst, axis, bit):
        copy = remote(src, dst, send.at[c, s], recv.at[c, s], axis, bit)
        flight[c, s] = copy
        sends.append(copy)

    def col(b):
        return pl.ds(pl.multiple_of(b * half, 128), half)

    def row2(b):
        return pl.ds(pl.multiple_of(b * rows2, 16), rows2)

    def row4(b, bb):
        return pl.ds(pl.multiple_of(b * rows2 + bb * rows4, 16), rows4)

    def pair(c):
        go(c, 0, take(c, flip(me, 1)), first.at[c, 0], "tensor", 1)
        go(c, 1, take(c, flip(flip(me, 1), 2)), first.at[c, 1], "tensor", 1)
        for k, shard in enumerate((me, flip(me, 2))):
            copy = pltpu.make_async_copy(take(c, shard), own.at[c, k], local_sem.at[c, k])
            copy.start()
            flight[c, "own", k] = copy

    def chip(c):
        flight[c, "own", 1].wait()
        flight[c, 1].wait_recv()
        to_y[c] = rounded(own[c, 1].astype(jnp.float32) + first[c, 1].astype(jnp.float32))
        go(c, 2, to_y.at[c], second.at[c], "tensor", 2)
        flight[c, "own", 0].wait()
        flight[c, 0].wait_recv()
        acc[c] = own[c, 0].astype(jnp.float32) + first[c, 0].astype(jnp.float32)

    def x_half(c):
        flight[c, 2].wait_recv()
        acc[c] += second[c].astype(jnp.float32)
        to_x[c] = rounded(acc[c, :, col(1 - b0)])
        go(c, 3, to_x.at[c], from_x.at[c], "dp", 1)

    def z_half(c):
        flight[c, 3].wait_recv()
        acc[c, :, col(b0)] += from_x[c].astype(jnp.float32)
        to_z[c] = rounded(acc[c, row2(1 - b1), col(b0)])
        go(c, 4, to_z.at[c], from_z.at[c], "dp", 2)

    def z_quarter(c):
        flight[c, 4].wait_recv()
        acc[c, row2(b1), col(b0)] += from_z[c].astype(jnp.float32)
        to_w[c] = rounded(acc[c, row4(b1, 1 - b2), col(b0)])
        go(c, 5, to_w.at[c], from_w.at[c], "dp", 4)

    def settle(c):
        flight[c, 5].wait_recv()
        mine = acc[c, row4(b1, b2), col(b0)] + from_w[c].astype(jnp.float32)
        for n, (axis, bit) in enumerate(far):
            more_to[c, n] = rounded(mine)
            go(c, 9 + n, more_to.at[c, n], more_from.at[c, n], axis, bit)
            flight[c, 9 + n].wait_recv()
            mine = rounded(mine).astype(jnp.float32) + more_from[c, n].astype(jnp.float32)
        sum_ref[c, row4(b1, b2), col(b0)] = rounded(mine)
        piece = sum_ref.at[c, row4(b1, b2), col(b0)]
        go(c, 6, piece, piece, "dp", 4)

    def z_share(c):
        flight[c, 6].wait_recv()
        piece = sum_ref.at[c, row2(b1), col(b0)]
        go(c, 7, piece, piece, "dp", 2)

    def x_share(c):
        flight[c, 7].wait_recv()
        piece = sum_ref.at[c, :, col(b0)]
        go(c, 8, piece, piece, "dp", 1)

    def end(c):
        flight[c, 8].wait_recv()

    stages = (pair, chip, x_half, z_half, z_quarter, settle, z_share, x_share, end)

    def gain_start(n):
        axis, bit = steps[n]
        copy = remote(gain_at.at[0, n], gain_at.at[1, n], gain_send.at[n], gain_recv.at[n], axis, bit)
        flight["gain", n] = copy
        sends.append(copy)

    greet(steps)
    gain_at[0, 0] = gains_ref[...]
    gain_start(0)
    gain_turn = 0
    for turn in range(len(chunks) + len(stages) - 1):
        for s in reversed(range(len(stages))):
            if 0 <= turn - s < len(chunks):
                stages[s](turn - s)
        if gain_turn < len(steps):
            flight["gain", gain_turn].wait_recv()
            now = gain_at[0, gain_turn] + gain_at[1, gain_turn]
            gain_turn += 1
            if gain_turn < len(steps):
                gain_at[0, gain_turn] = now
                gain_start(gain_turn)
            else:
                gains_sum_ref[...] = now
    for copy in sends:
        copy.wait_send()


def grad_sync(groups, grads, gains):
    width = grads.shape[2]
    n = grads.shape[1] // CHUNK
    steps = len(peers_of(4, groups))
    extra = max(steps - 5, 1)
    bf16 = lambda *shape: pltpu.VMEM(shape, jnp.bfloat16)
    anywhere, vmem = pl.BlockSpec(memory_space=pl.ANY), pl.BlockSpec(memory_space=pltpu.VMEM)
    return pl.pallas_call(
        partial(sync_kernel, groups),
        out_shape=(
            jax.ShapeDtypeStruct((n, CHUNK, width), jnp.bfloat16),
            jax.ShapeDtypeStruct(gains.shape, jnp.float32),
        ),
        in_specs=[anywhere, vmem],
        out_specs=[vmem, vmem],
        scratch_shapes=[
            bf16(n, 2, CHUNK, width),
            bf16(n, 2, CHUNK, width),
            bf16(n, CHUNK, width),
            pltpu.VMEM((n, CHUNK, width), jnp.float32),
            bf16(n, CHUNK, width),
            bf16(n, CHUNK, width // 2),
            bf16(n, CHUNK, width // 2),
            bf16(n, CHUNK // 2, width // 2),
            bf16(n, CHUNK // 2, width // 2),
            bf16(n, CHUNK // 4, width // 2),
            bf16(n, CHUNK // 4, width // 2),
            bf16(n, extra, CHUNK // 4, width // 2),
            bf16(n, extra, CHUNK // 4, width // 2),
            pltpu.VMEM((2, steps) + gains.shape, jnp.float32),
            pltpu.SemaphoreType.DMA((n, 9 + extra)),
            pltpu.SemaphoreType.DMA((n, 9 + extra)),
            pltpu.SemaphoreType.DMA((n, 2)),
            pltpu.SemaphoreType.DMA((steps,)),
            pltpu.SemaphoreType.DMA((steps,)),
        ],
        compiler_params=pltpu.CompilerParams(
            collective_id=0, has_side_effects=True, vmem_limit_bytes=56 << 20
        ),
        name="grad_sync",
    )(grads, gains)


def spread(me):
    return flip(me, 1), flip(me, 2), flip(flip(me, 1), 2)


def greet_tensor(ids):
    barrier = pltpu.get_barrier_semaphore()
    for peer in ids:
        pl.semaphore_signal(barrier, inc=1, device_id={"tensor": peer}, device_id_type=MESH)
    pl.semaphore_wait(barrier, len(ids))


def push(src, dst, send, recv, peer):
    copy = pltpu.make_async_remote_copy(
        src_ref=src,
        dst_ref=dst,
        send_sem=send,
        recv_sem=recv,
        device_id={"tensor": peer},
        device_id_type=MESH,
    )
    copy.start()
    return copy


def intake_kernel(tok_ref, gain_ref, w_ref, own_gain_ref, all_ref, packed_ref, gains_ref,
                  send, recv, gain_send, gain_recv):
    me = lax.axis_index("tensor")
    core, chip, cross = spread(me)
    rows, width = tok_ref.shape
    pieces = (send.shape[0] - 1) // 2
    piece = rows // pieces
    f32 = jnp.float32
    values = tok_ref[...].astype(f32)
    mu = jnp.sum(values, axis=1, keepdims=True) / width
    ms = jnp.sum(values * values, axis=1, keepdims=True) / width
    normed = (values - mu) * lax.rsqrt(ms - mu * mu + EPS) * gain_ref[...]
    all_ref[me] = normed.astype(jnp.bfloat16)
    gains_ref[me] = own_gain_ref[...]
    greet_tensor((core, chip))

    def span(c):
        return pl.ds(c * piece, piece)

    def block(c, owner):
        return all_ref.at[owner, span(c), :]

    to_chip = [push(block(c, me), block(c, me), send.at[c], recv.at[c], chip) for c in range(pieces)]
    gain_chip = push(gains_ref.at[me], gains_ref.at[me], gain_send.at[0], gain_recv.at[0], chip)
    to_core = push(all_ref.at[me], all_ref.at[me], send.at[2 * pieces], recv.at[2 * pieces], core)
    gain_core = push(gains_ref.at[me], gains_ref.at[me], gain_send.at[1], gain_recv.at[1], core)

    def project(owner, c):
        product = jnp.dot(all_ref[owner, span(c), :], w_ref[...], preferred_element_type=f32)
        packed_ref[owner, span(c), :] = product.astype(jnp.bfloat16)

    for c in range(pieces):
        project(me, c)
    to_core.wait_recv()
    for c in range(pieces):
        project(core, c)
    gain_chip.wait_recv()
    gain_far = push(gains_ref.at[chip], gains_ref.at[chip], gain_send.at[2], gain_recv.at[2], core)
    far = []
    for c in range(pieces):
        to_chip[c].wait_recv()
        far.append(push(block(c, chip), block(c, chip), send.at[pieces + c], recv.at[pieces + c], core))
        project(chip, c)
    for c in range(pieces):
        far[c].wait_recv()
        project(cross, c)
    gain_core.wait_recv()
    gain_far.wait_recv()
    for copy in [*to_chip, to_core, *far, gain_chip, gain_core, gain_far]:
        copy.wait_send()


def intake(tokens, gain, weight, own_gains, pieces=5):
    rows, width = tokens.shape
    vmem = pl.BlockSpec(memory_space=pltpu.VMEM)
    return pl.pallas_call(
        intake_kernel,
        out_shape=(
            jax.ShapeDtypeStruct((4, rows, width), jnp.bfloat16),
            jax.ShapeDtypeStruct((4, rows, weight.shape[1]), jnp.bfloat16),
            jax.ShapeDtypeStruct((4,) + own_gains.shape, jnp.float32),
        ),
        in_specs=[vmem] * 4,
        out_specs=[vmem] * 3,
        scratch_shapes=[
            pltpu.SemaphoreType.DMA((2 * pieces + 1,)),
            pltpu.SemaphoreType.DMA((2 * pieces + 1,)),
            pltpu.SemaphoreType.DMA((3,)),
            pltpu.SemaphoreType.DMA((3,)),
        ],
        compiler_params=pltpu.CompilerParams(
            collective_id=1, has_side_effects=True, vmem_limit_bytes=40 << 20
        ),
        name="intake",
    )(tokens, gain.reshape(1, -1), weight, own_gains)


def exchange_kernel(in_ref, out_ref, send, recv, local_sem):
    me = lax.axis_index("tensor")
    peers = spread(me)
    greet_tensor(peers)
    moves = []
    for n, peer in reversed(list(enumerate(peers))):
        moves.append(push(in_ref.at[peer], out_ref.at[me], send.at[n], recv.at[n], peer))
    own = pltpu.make_async_copy(in_ref.at[me], out_ref.at[me], local_sem)
    own.start()
    own.wait()
    for move in moves:
        move.wait()


def exchange(blocks, number):
    anywhere = pl.BlockSpec(memory_space=pltpu.VMEM)
    return pl.pallas_call(
        exchange_kernel,
        out_shape=jax.ShapeDtypeStruct(blocks.shape, blocks.dtype),
        in_specs=[anywhere],
        out_specs=anywhere,
        scratch_shapes=[
            pltpu.SemaphoreType.DMA((3,)),
            pltpu.SemaphoreType.DMA((3,)),
            pltpu.SemaphoreType.DMA,
        ],
        compiler_params=pltpu.CompilerParams(
            collective_id=number, has_side_effects=True, vmem_limit_bytes=24 << 20
        ),
        name="exchange",
    )(blocks)


def dot_nt(a, b):
    return lax.dot_general(a, b, (((1,), (1,)), ((), ())), preferred_element_type=jnp.float32)


def dot_tn(a, b):
    return lax.dot_general(a, b, (((0,), (0,)), ((), ())), preferred_element_type=jnp.float32)


GELU_A = 0.7978845608028654
GELU_B = 0.044715


def rows_kernel(tile, att_ref, tok_ref, og_ref, again_ref, fgain_ref, hgain_ref, wout_hbm, wup_hbm, wdown_hbm,
                res_ref, gm_ref, datt_ref, g_hbm, gsum_ref,
                wout, wup, wdown, x_s, mid_s, low_att, low_mid, act_s, slope_s, wide_s, low_act, big_s, acc_s,
                mu_s, rs_s, mu4_s, rs4_s, one_s, two_s, stage, w_sem, g_sem):
    parts, rows, head_width = att_ref.shape
    width = tok_ref.shape[1]
    hidden = width * hgain_ref.shape[0]
    n_tiles = rows // tile
    f32 = jnp.float32

    loads = [pltpu.make_async_copy(wout_hbm, wout, w_sem.at[0])]
    for t in range(parts):
        loads.append(pltpu.make_async_copy(wup_hbm.at[t], wup.at[t], w_sem.at[1 + t]))
    for t in range(parts):
        loads.append(pltpu.make_async_copy(wdown_hbm.at[t], wdown.at[t], w_sem.at[1 + parts + t]))
    for copy in loads:
        copy.start()

    def at(i):
        return pl.ds(pl.multiple_of(i * tile, tile), tile)

    def fold(v):
        return jnp.sum(v.reshape(tile // 8, 8, width), axis=0)

    def tiles(body, init=0):
        return lax.fori_loop(0, n_tiles, body, init)

    def stats(v, n):
        mu = jnp.sum(v, axis=1, keepdims=True) / n
        ms = jnp.sum(v * v, axis=1, keepdims=True) / n
        return mu, lax.rsqrt(ms - mu * mu + EPS)

    def save(slot, block, shard, row, n):
        copy = pltpu.make_async_copy(
            stage.at[slot, pl.ds(0, n), :], g_hbm.at[shard, pl.ds(row, n), :], g_sem.at[slot]
        )
        return copy

    again = again_ref[...]
    fgain = fgain_ref[...]

    def first(i, _):
        v = jnp.concatenate([att_ref[t, at(i), :] for t in range(parts)], axis=1).astype(f32)
        x_s[at(i), :] = v
        mu, rs = stats(v, width)
        mu_s[at(i), :] = mu
        rs_s[at(i), :] = rs
        low_att[at(i), :] = ((v - mu) * rs * again).astype(jnp.bfloat16)
        return 0

    tiles(first)
    loads[0].wait()
    big_s[...] = jnp.dot(low_att[...], wout[...], preferred_element_type=f32)

    def second(i, _):
        v = tok_ref[at(i), :].astype(f32) + big_s[at(i), :]
        mid_s[at(i), :] = v
        mu, rs = stats(v, width)
        low_mid[at(i), :] = ((v - mu) * rs * fgain).astype(jnp.bfloat16)
        one_s[at(i), :] = jnp.zeros((tile, 1), f32)
        two_s[at(i), :] = jnp.zeros((tile, 1), f32)
        acc_s[at(i), :] = v
        return 0

    tiles(second)

    for copy in loads[1:]:
        copy.wait()

    def up_block(t, _):
        big_s[...] = jnp.dot(low_mid[...], wup[t], preferred_element_type=f32)

        def body(i, _):
            v = big_s[at(i), :]
            sq = v * v
            th = jnp.tanh(v * (GELU_A + (GELU_A * GELU_B) * sq))
            half = 0.5 * th + 0.5
            act = v * half
            act_s[t, at(i), :] = act
            slope = half + (0.5 * v) * (1.0 - th * th) * (GELU_A + (3.0 * GELU_A * GELU_B) * sq)
            slope_s[t, at(i), :] = slope.astype(jnp.bfloat16)
            one_s[at(i), :] += jnp.sum(act, axis=1, keepdims=True)
            two_s[at(i), :] += jnp.sum(act * act, axis=1, keepdims=True)
            return 0

        tiles(body)
        return 0

    lax.fori_loop(0, parts, up_block, 0)

    def third(i, _):
        mu = one_s[at(i), :] / hidden
        mu4_s[at(i), :] = mu
        rs4_s[at(i), :] = lax.rsqrt(two_s[at(i), :] / hidden - mu * mu + EPS)
        one_s[at(i), :] = jnp.zeros((tile, 1), f32)
        two_s[at(i), :] = jnp.zeros((tile, 1), f32)
        return 0

    tiles(third)

    def down_block(t, _):
        hg = hgain_ref[t]
        big_s[...] = dot_nt(og_ref[...], wdown[t])

        def body(i, part):
            unit = (act_s[t, at(i), :] - mu4_s[at(i), :]) * rs4_s[at(i), :]
            act_s[t, at(i), :] = unit
            low_act[at(i), :] = (unit * hg).astype(jnp.bfloat16)
            d4 = big_s[at(i), :]
            wide = d4 * hg
            wide_s[t, at(i), :] = wide
            one_s[at(i), :] += jnp.sum(wide, axis=1, keepdims=True)
            two_s[at(i), :] += jnp.sum(wide * unit, axis=1, keepdims=True)
            return part + fold(d4 * unit)

        part = tiles(body, jnp.zeros((8, width), f32))
        gsum_ref[pl.ds(2 + t, 1), :] = jnp.sum(part, axis=0, keepdims=True)
        acc_s[...] += jnp.dot(low_act[...], wdown[t], preferred_element_type=f32)
        slot = t % 2

        @pl.when(t >= 2)
        def _():
            save(slot, None, t, 0, width).wait()

        stage[slot] = dot_tn(low_act[...], og_ref[...]).astype(jnp.bfloat16)
        save(slot, None, t, 0, width).start()
        return 0

    lax.fori_loop(0, parts, down_block, 0)

    def fourth(i, _):
        res_ref[at(i), :] = acc_s[at(i), :].astype(jnp.bfloat16)
        one_s[at(i), :] = one_s[at(i), :] / hidden
        two_s[at(i), :] = two_s[at(i), :] / hidden
        acc_s[at(i), :] = jnp.zeros((tile, width), f32)
        return 0

    tiles(fourth)

    def back_block(t, _):
        def body(i, _):
            d_act = rs4_s[at(i), :] * (wide_s[t, at(i), :] - one_s[at(i), :] - act_s[t, at(i), :] * two_s[at(i), :])
            low_act[at(i), :] = (d_act * slope_s[t, at(i), :].astype(f32)).astype(jnp.bfloat16)
            return 0

        tiles(body)
        acc_s[...] += dot_nt(low_act[...], wup[t])
        slot = t % 2
        save(slot, None, t, 0, width).wait()
        stage[slot] = dot_tn(low_mid[...], low_act[...]).astype(jnp.bfloat16)
        save(slot, None, t, width, width).start()
        return 0

    lax.fori_loop(0, parts, back_block, 0)

    def fifth(i, part):
        v = mid_s[at(i), :]
        mu, rs = stats(v, width)
        unit = (v - mu) * rs
        d3 = acc_s[at(i), :]
        wide = d3 * fgain
        m1 = jnp.sum(wide, axis=1, keepdims=True) / width
        m2 = jnp.sum(wide * unit, axis=1, keepdims=True) / width
        d_mid = og_ref[at(i), :].astype(f32) + rs * (wide - m1 - unit * m2)
        gm_ref[at(i), :] = d_mid
        low_act[at(i), :] = d_mid.astype(jnp.bfloat16)
        return part + fold(d3 * unit)

    part = tiles(fifth, jnp.zeros((8, width), f32))
    gsum_ref[0:1, :] = jnp.sum(part, axis=0, keepdims=True)
    big_s[...] = dot_nt(low_act[...], wout[...])
    for slot in range(2):
        save(slot, None, slot, width, width).wait()
    stage[0] = dot_tn(low_att[...], low_act[...]).astype(jnp.bfloat16)
    last = []
    for t in range(parts):
        copy = pltpu.make_async_copy(
            stage.at[0, pl.ds(t * head_width, head_width), :],
            g_hbm.at[t, pl.ds(2 * width, head_width), :],
            w_sem.at[t],
        )
        copy.start()
        last.append(copy)

    def sixth(i, part):
        mu, rs = mu_s[at(i), :], rs_s[at(i), :]
        unit = (x_s[at(i), :] - mu) * rs
        d2 = big_s[at(i), :]
        wide = d2 * again
        m1 = jnp.sum(wide, axis=1, keepdims=True) / width
        m2 = jnp.sum(wide * unit, axis=1, keepdims=True) / width
        d_att = (rs * (wide - m1 - unit * m2)).astype(jnp.bfloat16)
        for t in range(parts):
            datt_ref[t, at(i), :] = d_att[:, t * head_width : (t + 1) * head_width]
        return part + fold(d2 * unit)

    part = tiles(sixth, jnp.zeros((8, width), f32))
    gsum_ref[1:2, :] = jnp.sum(part, axis=0, keepdims=True)
    gsum_ref[pl.ds(2 + parts, 8 - 2 - parts), :] = jnp.zeros((8 - 2 - parts, width), f32)
    for copy in last:
        copy.wait()


def rows_pass(att, tokens, out_grad, attn_gain, ffn_gain, hidden_gain, w_out, w_up, w_down, tile=32):
    parts, rows, head_width = att.shape
    width = tokens.shape[1]
    bf16, f32 = jnp.bfloat16, jnp.float32
    vmem = pl.BlockSpec(memory_space=pltpu.VMEM)
    anywhere = pl.BlockSpec(memory_space=pl.ANY)
    column = pltpu.VMEM((rows, 1), f32)
    return pl.pallas_call(
        partial(rows_kernel, tile),
        out_shape=(
            jax.ShapeDtypeStruct((rows, width), bf16),
            jax.ShapeDtypeStruct((rows, width), f32),
            jax.ShapeDtypeStruct(att.shape, bf16),
            jax.ShapeDtypeStruct((parts, 2 * width + head_width, width), bf16),
            jax.ShapeDtypeStruct((8, width), f32),
        ),
        in_specs=[vmem] * 6 + [anywhere] * 3,
        out_specs=[vmem] * 3 + [anywhere, vmem],
        scratch_shapes=[
            pltpu.VMEM((width, width), bf16),
            pltpu.VMEM((parts, width, width), bf16),
            pltpu.VMEM((parts, width, width), bf16),
            pltpu.VMEM((rows, width), f32),
            pltpu.VMEM((rows, width), f32),
            pltpu.VMEM((rows, width), bf16),
            pltpu.VMEM((rows, width), bf16),
            pltpu.VMEM((parts, rows, width), f32),
            pltpu.VMEM((parts, rows, width), bf16),
            pltpu.VMEM((parts, rows, width), f32),
            pltpu.VMEM((rows, width), bf16),
            pltpu.VMEM((rows, width), f32),
            pltpu.VMEM((rows, width), f32),
        ] + [column] * 6 + [
            pltpu.VMEM((2, width, width), bf16),
            pltpu.SemaphoreType.DMA((1 + 2 * parts,)),
            pltpu.SemaphoreType.DMA((2,)),
        ],
        compiler_params=pltpu.CompilerParams(vmem_limit_bytes=60 << 20),
        cost_estimate=pl.CostEstimate(flops=20 * 10**9, bytes_accessed=40 << 20, transcendentals=2 * 10**6),
        name="rows_pass",
    )(att, tokens, out_grad, attn_gain.reshape(1, -1), ffn_gain.reshape(1, -1),
      hidden_gain.reshape(parts, 1, -1), w_out, w_up, w_down)


def local(
    tokens,
    lengths,
    in_gain,
    qkv_weight,
    attn_gain,
    out_weight,
    ffn_gain,
    up_weight,
    hidden_gain,
    down_weight,
    out_grad,
):
    parts = lax.axis_size("tensor")
    own_rows, width = tokens.shape
    head_width, hidden = attn_gain.shape[0], hidden_gain.shape[0]

    def gather(values):
        return lax.all_gather(values, "tensor", axis=0)

    full_out, full_up, full_down = gather(out_weight), gather(up_weight), gather(down_weight)
    pad = -(head_width + hidden) % 1024
    own_gains = jnp.concatenate((attn_gain, hidden_gain, jnp.zeros((pad,), jnp.float32)))
    gathered_in, packed, gains = intake(tokens, in_gain, qkv_weight, own_gains.reshape(8, -1))
    gathered_in = gathered_in.reshape(parts * own_rows, width)
    packed = packed.reshape(parts * own_rows, -1)
    gains = gains.reshape(parts, -1)
    full_attn_gain = gains[:, :head_width].reshape(-1)
    full_hidden_gain = gains[:, head_width : head_width + hidden].reshape(-1)

    attended, log_total = attn_fwd(packed, lengths, 512, 512)
    own_att = exchange(attended.astype(jnp.bfloat16).reshape(parts, own_rows, head_width), 2)
    result, grad_middle, grad_att, grads, gain_parts = rows_pass(
        own_att,
        tokens,
        out_grad,
        full_attn_gain,
        ffn_gain,
        full_hidden_gain,
        full_out.reshape(width, width),
        full_up,
        full_down,
        own_rows,
    )
    grad_attended = exchange(grad_att, 3).reshape(parts * own_rows, head_width)

    grad_packed = attn_bwd(packed, lengths, attended, log_total, grad_attended, 512, 256)
    grad_qkv = contract_rows(gathered_in, grad_packed)
    qkv_sum = lax.psum(grad_qkv, "dp")
    grad_in_normed = lax.psum_scatter(
        contract_cols(grad_packed, qkv_weight).astype(jnp.bfloat16),
        "tensor",
        scatter_dimension=0,
        tiled=True,
    ).astype(jnp.float32)
    in_gain_part = jnp.sum(qkv_weight.astype(jnp.float32) * grad_qkv, axis=1) / in_gain
    gain_parts = gain_parts.at[2 + parts].set(in_gain_part)
    sums, gains = grad_sync(lax.axis_size("dp"), grads, gain_parts)

    residual = tokens.astype(jnp.float32)
    mean = jnp.mean(residual, axis=1, keepdims=True)
    square = jnp.mean(residual * residual, axis=1, keepdims=True)
    scale = lax.rsqrt(square - mean * mean + EPS)
    unit = (residual - mean) * scale
    weighted = grad_in_normed * in_gain
    first = jnp.mean(weighted, axis=1, keepdims=True)
    second = jnp.mean(weighted * unit, axis=1, keepdims=True)
    in_grad = grad_middle + scale * (weighted - first - unit * second)

    me = lax.axis_index("tensor")
    sums = sums.reshape(-1, width).astype(jnp.float32)
    return (
        result,
        in_grad,
        gains[2 + parts],
        qkv_sum,
        lax.dynamic_slice_in_dim(gains[1], me * head_width, head_width),
        sums[hidden + width : hidden + width + head_width],
        gains[0],
        sums[hidden : hidden + width],
        lax.dynamic_index_in_dim(gains, 2 + me, 0, keepdims=False),
        sums[:hidden],
    )


def solution(mesh):
    return jax.shard_map(
        local,
        mesh=mesh,
        in_specs=(
            P(("dp", "tensor"), None),
            P("dp", None),
            P(),
            P(None, "tensor"),
            P("tensor"),
            P("tensor", None),
            P(),
            P(None, "tensor"),
            P("tensor"),
            P("tensor", None),
            P(("dp", "tensor"), None),
        ),
        out_specs=(
            P(("dp", "tensor"), None),
            P(("dp", "tensor"), None),
            P(),
            P(None, "tensor"),
            P("tensor"),
            P("tensor", None),
            P(),
            P(None, "tensor"),
            P("tensor"),
            P("tensor", None),
        ),
        check_vma=False,
    )
```

```python
from functools import partial

import jax
import jax.numpy as jnp
from jax import lax
from jax.experimental import pallas as pl
from jax.experimental.pallas import tpu as pltpu
from jax.sharding import PartitionSpec as P

HEAD_DIM = 64
UNIT = 64
EPS = 1e-05


def contract_rows(left, right):
    return lax.dot_general(
        left, right, (((0,), (0,)), ((), ())), preferred_element_type=jnp.float32
    )


def contract_cols(left, right):
    return lax.dot_general(
        left, right, (((1,), (1,)), ((), ())), preferred_element_type=jnp.float32
    )


NEG = -1e30


def seq_bounds(len_ref):
    ends, total = [], 0
    for s in range(len_ref.shape[1]):
        total = total + len_ref[0, s] * UNIT
        ends.append(total)
    return ends


def start_of(ends, row):
    at = 0
    for end in ends:
        at = jnp.where(row >= end, end, at)
    return at


def end_of(ends, row):
    at = ends[-1]
    for end in reversed(ends):
        at = jnp.where(row < end, end, at)
    return at


def dot(a, b):
    return lax.dot_general(a, b, (((1,), (0,)), ((), ())), preferred_element_type=jnp.float32)


def fwd_kernel(bq, bk, len_ref, qkv_ref, o_ref, lse_ref, k_s, qt_s, vt_s, acc_s, m_s):
    rows = qkv_ref.shape[0]
    heads = k_s.shape[0]
    ends = seq_bounds(len_ref)
    ones = (lax.broadcasted_iota(jnp.int32, (16, bq), 0) == 0).astype(jnp.float32).astype(jnp.bfloat16)

    def stage(i, _):
        at = pl.ds(pl.multiple_of(i * bq, bq), bq)
        x = qkv_ref[at, :]
        for h in range(heads):
            base = h * 3 * HEAD_DIM
            q = x[:, base : base + HEAD_DIM] * jnp.bfloat16(0.125)
            qt_s[h, :, at] = q.T
            k_s[h, at, :] = x[:, base + HEAD_DIM : base + 2 * HEAD_DIM]
            vt_s[h, :HEAD_DIM, at] = x[:, base + 2 * HEAD_DIM : base + 3 * HEAD_DIM].T
            vt_s[h, HEAD_DIM:, at] = ones
        return 0

    lax.fori_loop(0, rows // bq, stage, 0)

    def query_block(i, _):
        first = pl.multiple_of(i * bq, bq)
        at = pl.ds(first, bq)
        q_pos = first + lax.broadcasted_iota(jnp.int32, (1, bq), 1)
        q_start = start_of(ends, q_pos)
        lo = start_of(ends, first)
        hi = start_of(ends, first + bq - 1)
        for h in range(heads):
            acc_s[h] = jnp.zeros_like(acc_s[h])
            m_s[h] = jnp.full_like(m_s[h], NEG)

        def step(masked, c, _):
            c0 = pl.multiple_of(c * bk, bk)
            for h in range(heads):
                s = dot(k_s[h, pl.ds(c0, bk), :], qt_s[h, :, at])
                if masked:
                    k_pos = c0 + lax.broadcasted_iota(jnp.int32, (bk, 1), 0)
                    s = jnp.where((k_pos <= q_pos) & (k_pos >= q_start), s, NEG)
                old = m_s[h]
                new = jnp.maximum(old, jnp.max(s, axis=0, keepdims=True))
                p = jnp.exp(s - new).astype(jnp.bfloat16)
                m_s[h] = new
                acc_s[h] = acc_s[h] * jnp.exp(old - new) + dot(vt_s[h, :, pl.ds(c0, bk)], p)
            return 0

        c_lo = lo // bk
        c_diag = first // bk
        c_end = (first + bq - 1) // bk + 1
        c_int = jnp.minimum((hi + bk - 1) // bk, c_diag)
        lax.fori_loop(c_lo, c_int, partial(step, True), 0)
        lax.fori_loop(c_int, c_diag, partial(step, False), 0)
        lax.fori_loop(jnp.maximum(c_diag, c_lo), c_end, partial(step, True), 0)
        outs = []
        for h in range(heads):
            acc = acc_s[h]
            total = acc[HEAD_DIM : HEAD_DIM + 1, :]
            outs.append((acc[:HEAD_DIM, :] / total).T)
            lse_ref[h : h + 1, at] = m_s[h] + jnp.log(total)
        o_ref[at, :] = jnp.concatenate(outs, axis=1).astype(o_ref.dtype)
        return 0

    lax.fori_loop(0, rows // bq, query_block, 0)


def attn_fwd(packed, lengths, bq=256, bk=256, out_dtype=jnp.bfloat16):
    rows = packed.shape[0]
    heads = packed.shape[1] // (3 * HEAD_DIM)
    return pl.pallas_call(
        partial(fwd_kernel, bq, bk),
        out_shape=(
            jax.ShapeDtypeStruct((rows, heads * HEAD_DIM), out_dtype),
            jax.ShapeDtypeStruct((8, rows), jnp.float32),
        ),
        in_specs=[pl.BlockSpec(memory_space=pltpu.SMEM), pl.BlockSpec(memory_space=pltpu.VMEM)],
        out_specs=[pl.BlockSpec(memory_space=pltpu.VMEM)] * 2,
        scratch_shapes=[
            pltpu.VMEM((heads, rows, HEAD_DIM), jnp.bfloat16),
            pltpu.VMEM((heads, HEAD_DIM, rows), jnp.bfloat16),
            pltpu.VMEM((heads, HEAD_DIM + 16, rows), jnp.bfloat16),
            pltpu.VMEM((heads, HEAD_DIM + 16, bq), jnp.float32),
            pltpu.VMEM((heads, 1, bq), jnp.float32),
        ],
        compiler_params=pltpu.CompilerParams(vmem_limit_bytes=48 << 20),
        name="attn_fwd",
    )(lengths, packed)


MESH = pl.DeviceIdType.MESH


def flip(index, bit):
    return index + bit - 2 * bit * ((index // bit) % 2)


def peers_of(parts, groups):
    steps, bit = [], 1
    while bit < parts:
        steps.append(("tensor", bit))
        bit *= 2
    bit = 1
    while bit < groups:
        steps.append(("dp", bit))
        bit *= 2
    return steps


def at_peer(axis, bit):
    return {axis: flip(lax.axis_index(axis), bit)}


def greet(steps, *more):
    barrier = pltpu.get_barrier_semaphore()
    for axis, bit in steps:
        pl.semaphore_signal(barrier, inc=1, device_id=at_peer(axis, bit), device_id_type=MESH)
    for peer in more:
        pl.semaphore_signal(barrier, inc=1, device_id={"tensor": peer}, device_id_type=MESH)
    pl.semaphore_wait(barrier, len(steps) + len(more))


def remote(src, dst, send, recv, axis, bit):
    copy = pltpu.make_async_remote_copy(
        src_ref=src,
        dst_ref=dst,
        send_sem=send,
        recv_sem=recv,
        device_id=at_peer(axis, bit),
        device_id_type=MESH,
    )
    copy.start()
    return copy


def rounded(values):
    return values.astype(jnp.bfloat16)


def spread(me):
    return flip(me, 1), flip(me, 2), flip(flip(me, 1), 2)


def greet_tensor(ids):
    barrier = pltpu.get_barrier_semaphore()
    for peer in ids:
        pl.semaphore_signal(barrier, inc=1, device_id={"tensor": peer}, device_id_type=MESH)
    pl.semaphore_wait(barrier, len(ids))


def push(src, dst, send, recv, peer):
    copy = pltpu.make_async_remote_copy(
        src_ref=src,
        dst_ref=dst,
        send_sem=send,
        recv_sem=recv,
        device_id={"tensor": peer},
        device_id_type=MESH,
    )
    copy.start()
    return copy


def intake_kernel(tok_ref, gain_ref, w_ref, own_gain_ref, all_ref, packed_ref, gains_ref,
                  send, recv, gain_send, gain_recv):
    me = lax.axis_index("tensor")
    core, chip, cross = spread(me)
    rows, width = tok_ref.shape
    pieces = (send.shape[0] - 1) // 2
    piece = rows // pieces
    f32 = jnp.float32
    values = tok_ref[...].astype(f32)
    mu = jnp.sum(values, axis=1, keepdims=True) / width
    ms = jnp.sum(values * values, axis=1, keepdims=True) / width
    normed = (values - mu) * lax.rsqrt(ms - mu * mu + EPS) * gain_ref[...]
    all_ref[me] = normed.astype(jnp.bfloat16)
    gains_ref[me] = own_gain_ref[...]
    greet_tensor((core, chip))

    def span(c):
        return pl.ds(c * piece, piece)

    def block(c, owner):
        return all_ref.at[owner, span(c), :]

    to_chip = [push(block(c, me), block(c, me), send.at[c], recv.at[c], chip) for c in range(pieces)]
    gain_chip = push(gains_ref.at[me], gains_ref.at[me], gain_send.at[0], gain_recv.at[0], chip)
    to_core = push(all_ref.at[me], all_ref.at[me], send.at[2 * pieces], recv.at[2 * pieces], core)
    gain_core = push(gains_ref.at[me], gains_ref.at[me], gain_send.at[1], gain_recv.at[1], core)

    def project(owner, c):
        product = jnp.dot(all_ref[owner, span(c), :], w_ref[...], preferred_element_type=f32)
        packed_ref[owner, span(c), :] = product.astype(jnp.bfloat16)

    for c in range(pieces):
        project(me, c)
    to_core.wait_recv()
    for c in range(pieces):
        project(core, c)
    gain_chip.wait_recv()
    gain_far = push(gains_ref.at[chip], gains_ref.at[chip], gain_send.at[2], gain_recv.at[2], core)
    far = []
    for c in range(pieces):
        to_chip[c].wait_recv()
        far.append(push(block(c, chip), block(c, chip), send.at[pieces + c], recv.at[pieces + c], core))
        project(chip, c)
    for c in range(pieces):
        far[c].wait_recv()
        project(cross, c)
    gain_core.wait_recv()
    gain_far.wait_recv()
    for copy in [*to_chip, to_core, *far, gain_chip, gain_core, gain_far]:
        copy.wait_send()


def intake(tokens, gain, weight, own_gains, pieces=5):
    rows, width = tokens.shape
    vmem = pl.BlockSpec(memory_space=pltpu.VMEM)
    return pl.pallas_call(
        intake_kernel,
        out_shape=(
            jax.ShapeDtypeStruct((4, rows, width), jnp.bfloat16),
            jax.ShapeDtypeStruct((4, rows, weight.shape[1]), jnp.bfloat16),
            jax.ShapeDtypeStruct((4,) + own_gains.shape, jnp.float32),
        ),
        in_specs=[vmem] * 4,
        out_specs=[vmem] * 3,
        scratch_shapes=[
            pltpu.SemaphoreType.DMA((2 * pieces + 1,)),
            pltpu.SemaphoreType.DMA((2 * pieces + 1,)),
            pltpu.SemaphoreType.DMA((3,)),
            pltpu.SemaphoreType.DMA((3,)),
        ],
        compiler_params=pltpu.CompilerParams(
            collective_id=1, has_side_effects=True, vmem_limit_bytes=40 << 20
        ),
        name="intake",
    )(tokens, gain.reshape(1, -1), weight, own_gains)


def exchange_kernel(in_ref, out_ref, send, recv, local_sem):
    me = lax.axis_index("tensor")
    peers = spread(me)
    greet_tensor(peers)
    moves = []
    for n, peer in reversed(list(enumerate(peers))):
        moves.append(push(in_ref.at[peer], out_ref.at[me], send.at[n], recv.at[n], peer))
    own = pltpu.make_async_copy(in_ref.at[me], out_ref.at[me], local_sem)
    own.start()
    own.wait()
    for move in moves:
        move.wait()


def exchange(blocks, number):
    anywhere = pl.BlockSpec(memory_space=pltpu.VMEM)
    return pl.pallas_call(
        exchange_kernel,
        out_shape=jax.ShapeDtypeStruct(blocks.shape, blocks.dtype),
        in_specs=[anywhere],
        out_specs=anywhere,
        scratch_shapes=[
            pltpu.SemaphoreType.DMA((3,)),
            pltpu.SemaphoreType.DMA((3,)),
            pltpu.SemaphoreType.DMA,
        ],
        compiler_params=pltpu.CompilerParams(
            collective_id=number, has_side_effects=True, vmem_limit_bytes=24 << 20
        ),
        name="exchange",
    )(blocks)


def dot_nt(a, b):
    return lax.dot_general(a, b, (((1,), (1,)), ((), ())), preferred_element_type=jnp.float32)


def dot_tn(a, b):
    return lax.dot_general(a, b, (((0,), (0,)), ((), ())), preferred_element_type=jnp.float32)


GELU_A = 0.7978845608028654
GELU_B = 0.044715


def rows_kernel(tile, att_ref, tok_ref, og_ref, again_ref, fgain_ref, hgain_ref, wout_hbm, wup_hbm, wdown_hbm,
                res_ref, gm_ref, datt_ref, g_hbm, gsum_ref,
                wout, wup, wdown, x_s, mid_s, low_att, low_mid, act_s, slope_s, wide_s, low_act, big_s, acc_s,
                mu_s, rs_s, mu4_s, rs4_s, one_s, two_s, stage, w_sem, g_sem):
    parts, rows, head_width = att_ref.shape
    width = tok_ref.shape[1]
    hidden = width * hgain_ref.shape[0]
    n_tiles = rows // tile
    f32 = jnp.float32

    loads = [pltpu.make_async_copy(wout_hbm, wout, w_sem.at[0])]
    for t in range(parts):
        loads.append(pltpu.make_async_copy(wup_hbm.at[t], wup.at[t], w_sem.at[1 + t]))
    for t in range(parts):
        loads.append(pltpu.make_async_copy(wdown_hbm.at[t], wdown.at[t], w_sem.at[1 + parts + t]))
    for copy in loads:
        copy.start()

    def at(i):
        return pl.ds(pl.multiple_of(i * tile, tile), tile)

    def fold(v):
        return jnp.sum(v.reshape(tile // 8, 8, width), axis=0)

    def tiles(body, init=0):
        return lax.fori_loop(0, n_tiles, body, init)

    def stats(v, n):
        mu = jnp.sum(v, axis=1, keepdims=True) / n
        ms = jnp.sum(v * v, axis=1, keepdims=True) / n
        return mu, lax.rsqrt(ms - mu * mu + EPS)

    def save(slot, block, shard, row, n):
        copy = pltpu.make_async_copy(
            stage.at[slot, pl.ds(0, n), :], g_hbm.at[shard, pl.ds(row, n), :], g_sem.at[slot]
        )
        return copy

    again = again_ref[...]
    fgain = fgain_ref[...]

    def first(i, _):
        v = jnp.concatenate([att_ref[t, at(i), :] for t in range(parts)], axis=1).astype(f32)
        x_s[at(i), :] = v
        mu, rs = stats(v, width)
        mu_s[at(i), :] = mu
        rs_s[at(i), :] = rs
        low_att[at(i), :] = ((v - mu) * rs * again).astype(jnp.bfloat16)
        return 0

    tiles(first)
    loads[0].wait()
    big_s[...] = jnp.dot(low_att[...], wout[...], preferred_element_type=f32)

    def second(i, _):
        v = tok_ref[at(i), :].astype(f32) + big_s[at(i), :]
        mid_s[at(i), :] = v
        mu, rs = stats(v, width)
        low_mid[at(i), :] = ((v - mu) * rs * fgain).astype(jnp.bfloat16)
        one_s[at(i), :] = jnp.zeros((tile, 1), f32)
        two_s[at(i), :] = jnp.zeros((tile, 1), f32)
        acc_s[at(i), :] = v
        return 0

    tiles(second)

    for copy in loads[1:]:
        copy.wait()

    def up_block(t, _):
        big_s[...] = jnp.dot(low_mid[...], wup[t], preferred_element_type=f32)

        def body(i, _):
            v = big_s[at(i), :]
            sq = v * v
            th = jnp.tanh(v * (GELU_A + (GELU_A * GELU_B) * sq))
            half = 0.5 * th + 0.5
            act = v * half
            act_s[t, at(i), :] = act
            slope = half + (0.5 * v) * (1.0 - th * th) * (GELU_A + (3.0 * GELU_A * GELU_B) * sq)
            slope_s[t, at(i), :] = slope.astype(jnp.bfloat16)
            one_s[at(i), :] += jnp.sum(act, axis=1, keepdims=True)
            two_s[at(i), :] += jnp.sum(act * act, axis=1, keepdims=True)
            return 0

        tiles(body)
        return 0

    lax.fori_loop(0, parts, up_block, 0)

    def third(i, _):
        mu = one_s[at(i), :] / hidden
        mu4_s[at(i), :] = mu
        rs4_s[at(i), :] = lax.rsqrt(two_s[at(i), :] / hidden - mu * mu + EPS)
        one_s[at(i), :] = jnp.zeros((tile, 1), f32)
        two_s[at(i), :] = jnp.zeros((tile, 1), f32)
        return 0

    tiles(third)

    def down_block(t, _):
        hg = hgain_ref[t]
        big_s[...] = dot_nt(og_ref[...], wdown[t])

        def body(i, part):
            unit = (act_s[t, at(i), :] - mu4_s[at(i), :]) * rs4_s[at(i), :]
            act_s[t, at(i), :] = unit
            low_act[at(i), :] = (unit * hg).astype(jnp.bfloat16)
            d4 = big_s[at(i), :]
            wide = d4 * hg
            wide_s[t, at(i), :] = wide
            one_s[at(i), :] += jnp.sum(wide, axis=1, keepdims=True)
            two_s[at(i), :] += jnp.sum(wide * unit, axis=1, keepdims=True)
            return part + fold(d4 * unit)

        part = tiles(body, jnp.zeros((8, width), f32))
        gsum_ref[pl.ds(2 + t, 1), :] = jnp.sum(part, axis=0, keepdims=True)
        acc_s[...] += jnp.dot(low_act[...], wdown[t], preferred_element_type=f32)
        slot = t % 2

        @pl.when(t >= 2)
        def _():
            save(slot, None, t, 0, width).wait()

        stage[slot] = dot_tn(low_act[...], og_ref[...]).astype(jnp.bfloat16)
        save(slot, None, t, 0, width).start()
        return 0

    lax.fori_loop(0, parts, down_block, 0)

    def fourth(i, _):
        res_ref[at(i), :] = acc_s[at(i), :].astype(jnp.bfloat16)
        one_s[at(i), :] = one_s[at(i), :] / hidden
        two_s[at(i), :] = two_s[at(i), :] / hidden
        acc_s[at(i), :] = jnp.zeros((tile, width), f32)
        return 0

    tiles(fourth)

    def back_block(t, _):
        def body(i, _):
            d_act = rs4_s[at(i), :] * (wide_s[t, at(i), :] - one_s[at(i), :] - act_s[t, at(i), :] * two_s[at(i), :])
            low_act[at(i), :] = (d_act * slope_s[t, at(i), :].astype(f32)).astype(jnp.bfloat16)
            return 0

        tiles(body)
        acc_s[...] += dot_nt(low_act[...], wup[t])
        slot = t % 2
        save(slot, None, t, 0, width).wait()
        stage[slot] = dot_tn(low_mid[...], low_act[...]).astype(jnp.bfloat16)
        save(slot, None, t, width, width).start()
        return 0

    lax.fori_loop(0, parts, back_block, 0)

    def fifth(i, part):
        v = mid_s[at(i), :]
        mu, rs = stats(v, width)
        unit = (v - mu) * rs
        d3 = acc_s[at(i), :]
        wide = d3 * fgain
        m1 = jnp.sum(wide, axis=1, keepdims=True) / width
        m2 = jnp.sum(wide * unit, axis=1, keepdims=True) / width
        d_mid = og_ref[at(i), :].astype(f32) + rs * (wide - m1 - unit * m2)
        gm_ref[at(i), :] = d_mid
        low_act[at(i), :] = d_mid.astype(jnp.bfloat16)
        return part + fold(d3 * unit)

    part = tiles(fifth, jnp.zeros((8, width), f32))
    gsum_ref[0:1, :] = jnp.sum(part, axis=0, keepdims=True)
    big_s[...] = dot_nt(low_act[...], wout[...])
    for slot in range(2):
        save(slot, None, slot, width, width).wait()
    stage[0] = dot_tn(low_att[...], low_act[...]).astype(jnp.bfloat16)
    last = []
    for t in range(parts):
        copy = pltpu.make_async_copy(
            stage.at[0, pl.ds(t * head_width, head_width), :],
            g_hbm.at[t, pl.ds(2 * width, head_width), :],
            w_sem.at[t],
        )
        copy.start()
        last.append(copy)

    def sixth(i, part):
        mu, rs = mu_s[at(i), :], rs_s[at(i), :]
        unit = (x_s[at(i), :] - mu) * rs
        d2 = big_s[at(i), :]
        wide = d2 * again
        m1 = jnp.sum(wide, axis=1, keepdims=True) / width
        m2 = jnp.sum(wide * unit, axis=1, keepdims=True) / width
        d_att = (rs * (wide - m1 - unit * m2)).astype(jnp.bfloat16)
        for t in range(parts):
            datt_ref[t, at(i), :] = d_att[:, t * head_width : (t + 1) * head_width]
        return part + fold(d2 * unit)

    part = tiles(sixth, jnp.zeros((8, width), f32))
    gsum_ref[1:2, :] = jnp.sum(part, axis=0, keepdims=True)
    gsum_ref[pl.ds(2 + parts, 8 - 2 - parts), :] = jnp.zeros((8 - 2 - parts, width), f32)
    for copy in last:
        copy.wait()


def rows_pass(att, tokens, out_grad, attn_gain, ffn_gain, hidden_gain, w_out, w_up, w_down, tile=32):
    parts, rows, head_width = att.shape
    width = tokens.shape[1]
    bf16, f32 = jnp.bfloat16, jnp.float32
    vmem = pl.BlockSpec(memory_space=pltpu.VMEM)
    anywhere = pl.BlockSpec(memory_space=pl.ANY)
    column = pltpu.VMEM((rows, 1), f32)
    return pl.pallas_call(
        partial(rows_kernel, tile),
        out_shape=(
            jax.ShapeDtypeStruct((rows, width), bf16),
            jax.ShapeDtypeStruct((rows, width), f32),
            jax.ShapeDtypeStruct(att.shape, bf16),
            jax.ShapeDtypeStruct((parts, 2 * width + head_width, width), bf16),
            jax.ShapeDtypeStruct((8, width), f32),
        ),
        in_specs=[vmem] * 6 + [anywhere] * 3,
        out_specs=[vmem] * 3 + [anywhere, vmem],
        scratch_shapes=[
            pltpu.VMEM((width, width), bf16),
            pltpu.VMEM((parts, width, width), bf16),
            pltpu.VMEM((parts, width, width), bf16),
            pltpu.VMEM((rows, width), f32),
            pltpu.VMEM((rows, width), f32),
            pltpu.VMEM((rows, width), bf16),
            pltpu.VMEM((rows, width), bf16),
            pltpu.VMEM((parts, rows, width), f32),
            pltpu.VMEM((parts, rows, width), bf16),
            pltpu.VMEM((parts, rows, width), f32),
            pltpu.VMEM((rows, width), bf16),
            pltpu.VMEM((rows, width), f32),
            pltpu.VMEM((rows, width), f32),
        ] + [column] * 6 + [
            pltpu.VMEM((2, width, width), bf16),
            pltpu.SemaphoreType.DMA((1 + 2 * parts,)),
            pltpu.SemaphoreType.DMA((2,)),
        ],
        compiler_params=pltpu.CompilerParams(vmem_limit_bytes=60 << 20),
        cost_estimate=pl.CostEstimate(flops=20 * 10**9, bytes_accessed=40 << 20, transcendentals=2 * 10**6),
        name="rows_pass",
    )(att, tokens, out_grad, attn_gain.reshape(1, -1), ffn_gain.reshape(1, -1),
      hidden_gain.reshape(parts, 1, -1), w_out, w_up, w_down)


def chunk_copy(c, s, src, dst, send, recv, axis, bit):
    return pltpu.make_async_remote_copy(
        src_ref=src,
        dst_ref=dst,
        send_sem=send.at[c, s],
        recv_sem=recv.at[c, s],
        device_id=at_peer(axis, bit),
        device_id_type=MESH,
    )


def back_kernel(groups, chunk, block, len_ref, datt_ref, packed_ref, att_ref, lse_ref, grads_ref, out_ref, sum_ref,
                do_s, kv_s, q_s, g_s, qt_s, gt_s, kt_s, d_s, dqt_s, acc_kv,
                own, first, second, acc, to_y, to_x, from_x, to_z, from_z, to_w, from_w, more_to, more_from,
                send, recv, local_sem, a2a_send, a2a_recv, a2a_local):
    f32, bf16 = jnp.float32, jnp.bfloat16
    steps = peers_of(4, groups)
    far = steps[5:]
    me, dp = lax.axis_index("tensor"), lax.axis_index("dp")
    core, chip, cross = spread(me)
    cols = grads_ref.shape[2]
    half, rows2, rows4 = cols // 2, chunk // 2, chunk // 4
    b0, b1, b2 = dp % 2, (dp // 2) % 2, (dp // 4) % 2
    n = grads_ref.shape[1] // chunk

    def take(c, shard):
        return grads_ref.at[shard, pl.ds(pl.multiple_of(c * chunk, 16), chunk), :]

    def col(b):
        return pl.ds(pl.multiple_of(b * half, 128), half)

    def row2(b):
        return pl.ds(pl.multiple_of(b * rows2, 16), rows2)

    def row4(b, bb):
        return pl.ds(pl.multiple_of(b * rows2 + bb * rows4, 16), rows4)

    def copy(c, s):
        if s == 0:
            return chunk_copy(c, 0, take(c, core), first.at[c, 0], send, recv, "tensor", 1)
        if s == 1:
            return chunk_copy(c, 1, take(c, cross), first.at[c, 1], send, recv, "tensor", 1)
        if s == 2:
            return chunk_copy(c, 2, to_y.at[c], second.at[c], send, recv, "tensor", 2)
        if s == 3:
            return chunk_copy(c, 3, to_x.at[c], from_x.at[c], send, recv, "dp", 1)
        if s == 4:
            return chunk_copy(c, 4, to_z.at[c], from_z.at[c], send, recv, "dp", 2)
        if s == 5:
            return chunk_copy(c, 5, to_w.at[c], from_w.at[c], send, recv, "dp", 4)
        if s == 6:
            piece = sum_ref.at[c, row4(b1, b2), col(b0)]
            return chunk_copy(c, 6, piece, piece, send, recv, "dp", 4)
        if s == 7:
            piece = sum_ref.at[c, row2(b1), col(b0)]
            return chunk_copy(c, 7, piece, piece, send, recv, "dp", 2)
        if s == 8:
            piece = sum_ref.at[c, :, col(b0)]
            return chunk_copy(c, 8, piece, piece, send, recv, "dp", 1)
        axis, bit = far[s - 9]
        return chunk_copy(c, s, more_to.at[c, s - 9], more_from.at[c, s - 9], send, recv, axis, bit)

    def arrived(c, s, piece=None):
        if piece is None:
            copy(c, s).wait_recv()
        else:
            axis, bit = {6: ("dp", 4), 7: ("dp", 2), 8: ("dp", 1)}[s]
            chunk_copy(c, s, piece, piece, send, recv, axis, bit).wait_recv()

    def mine(c, k):
        shard = (me, chip)[k]
        return pltpu.make_async_copy(take(c, shard), own.at[c % 3, k], local_sem.at[c % 3, k])

    def pair(c):
        copy(c, 1).start()
        copy(c, 0).start()
        mine(c, 1).start()
        mine(c, 0).start()

    def to_chip(c):
        mine(c, 1).wait()
        arrived(c, 1)
        to_y[c] = rounded(own[c % 3, 1].astype(f32) + first[c, 1].astype(f32))
        copy(c, 2).start()
        mine(c, 0).wait()
        arrived(c, 0)
        acc[c] = own[c % 3, 0].astype(f32) + first[c, 0].astype(f32)

    def x_half(c):
        arrived(c, 2)
        acc[c] += second[c].astype(f32)
        to_x[c] = rounded(acc[c, :, col(1 - b0)])
        copy(c, 3).start()

    def z_half(c):
        arrived(c, 3)
        acc[c, :, col(b0)] += from_x[c].astype(f32)
        to_z[c] = rounded(acc[c, row2(1 - b1), col(b0)])
        copy(c, 4).start()

    def z_quarter(c):
        arrived(c, 4)
        acc[c, row2(b1), col(b0)] += from_z[c].astype(f32)
        to_w[c] = rounded(acc[c, row4(b1, 1 - b2), col(b0)])
        copy(c, 5).start()

    def settle(c):
        arrived(c, 5)
        total = acc[c, row4(b1, b2), col(b0)] + from_w[c].astype(f32)
        for m in range(len(far)):
            more_to[c, m] = rounded(total)
            copy(c, 9 + m).start()
            arrived(c, 9 + m)
            total = rounded(total).astype(f32) + more_from[c, m].astype(f32)
        sum_ref[c, row4(b1, b2), col(b0)] = rounded(total)
        copy(c, 6).start()

    def z_share(c):
        arrived(c, 6, sum_ref.at[c, row4(b1, 1 - b2), col(b0)])
        copy(c, 7).start()

    def x_share(c):
        arrived(c, 7, sum_ref.at[c, row2(1 - b1), col(b0)])
        copy(c, 8).start()

    def end(c):
        arrived(c, 8, sum_ref.at[c, :, col(1 - b0)])

    stages = (pair, to_chip, x_half, z_half, z_quarter, settle, z_share, x_share, end)

    def turn(at):
        for s in reversed(range(len(stages))):
            c = at - s

            @pl.when((c >= 0) & (c < n))
            def _():
                stages[s](c)

    rows = packed_ref.shape[0]
    heads = acc_kv.shape[0]
    own_rows = datt_ref.shape[1]
    ends = seq_bounds(len_ref)
    scale = jnp.bfloat16(0.125)
    greet(steps, cross)

    def a2a(k, peer):
        return pltpu.make_async_remote_copy(
            src_ref=datt_ref.at[peer],
            dst_ref=do_s.at[me],
            send_sem=a2a_send.at[k],
            recv_sem=a2a_recv.at[k],
            device_id={"tensor": peer},
            device_id_type=MESH,
        )

    moves = [a2a(k, peer) for k, peer in reversed(list(enumerate((core, chip, cross))))]
    for move in moves:
        move.start()
    keep = pltpu.make_async_copy(datt_ref.at[me], do_s.at[me], a2a_local)
    keep.start()
    turn(jnp.int32(0))

    def stage_qkv(i, _):
        at = pl.ds(pl.multiple_of(i * 256, 256), 256)
        x = packed_ref[at, :]
        blank = jnp.zeros((256, HEAD_DIM), bf16)
        blank_t = jnp.zeros((HEAD_DIM, 256), bf16)
        for h in range(heads):
            base = h * 3 * HEAD_DIM
            q = x[:, base : base + HEAD_DIM] * scale
            k = x[:, base + HEAD_DIM : base + 2 * HEAD_DIM]
            v = x[:, base + 2 * HEAD_DIM : base + 3 * HEAD_DIM]
            kv_s[h, at, :] = jnp.concatenate([k, v], axis=1)
            q_s[h, at, :] = jnp.concatenate([q, blank], axis=1)
            qt_s[h, :HEAD_DIM, at] = q.T
            qt_s[h, HEAD_DIM:, at] = blank_t
            kt_s[h, :, at] = (k * scale).T
            dqt_s[h, :, at] = jnp.zeros((HEAD_DIM, 256), f32)
            acc_kv[h, at, :] = jnp.zeros((256, 2 * HEAD_DIM), f32)
        return 0

    lax.fori_loop(0, rows // 256, stage_qkv, 0)
    keep.wait()
    for move in moves:
        move.wait()
    turn(jnp.int32(1))
    piece = own_rows // 5

    def stage_grad(i, _):
        owner, part = i // 5, i % 5
        inner = pl.ds(pl.multiple_of(part * piece, piece), piece)
        at = pl.ds(pl.multiple_of(owner * own_rows + part * piece, piece), piece)
        g = do_s[owner, inner, :]
        prod = g.astype(f32) * att_ref[at, :].astype(f32)
        blank = jnp.zeros((piece, HEAD_DIM), bf16)
        blank_t = jnp.zeros((HEAD_DIM, piece), bf16)
        for h in range(heads):
            d = g[:, h * HEAD_DIM : (h + 1) * HEAD_DIM]
            g_s[h, at, :] = jnp.concatenate([blank, d], axis=1)
            gt_s[h, HEAD_DIM:, at] = d.T
            gt_s[h, :HEAD_DIM, at] = blank_t
            d_s[h, :, at] = jnp.sum(prod[:, h * HEAD_DIM : (h + 1) * HEAD_DIM].T, axis=0, keepdims=True)
        return 0

    lax.fori_loop(0, rows // piece, stage_grad, 0)

    def body(i, j):
        q0 = pl.multiple_of(i * block, block)
        k0 = pl.multiple_of(j * block, block)
        at, kat = pl.ds(q0, block), pl.ds(k0, block)
        q_pos = q0 + lax.broadcasted_iota(jnp.int32, (1, block), 1)
        q_start = start_of(ends, q_pos)
        k_pos = k0 + lax.broadcasted_iota(jnp.int32, (block, 1), 0)
        keep = (k_pos <= q_pos) & (k_pos >= q_start)
        for h in range(heads):
            kv = kv_s[h, kat, :]
            s = dot(kv, qt_s[h, :, at]) - lse_ref[h : h + 1, at]
            p = jnp.exp(jnp.where(keep, s, NEG))
            dp_t = dot(kv, gt_s[h, :, at])
            ds = (p * (dp_t - d_s[h, :, at])).astype(bf16)
            acc_kv[h, kat, :] += dot(p.astype(bf16), g_s[h, at, :]) + dot(ds, q_s[h, at, :])
            dqt_s[h, :, at] += dot(kt_s[h, :, kat], ds)

    count = rows // block
    done = 2
    for g in range(count // 2 + 1):
        length = count - g

        def one(p, _, length=length, g=g, done=done):
            wrap = p // length
            i = (length - 1) - wrap * (length - g)
            j = p - wrap * length
            body(i, j)
            turn(p + done)
            return 0

        bodies = count if g else count
        lax.fori_loop(0, bodies, one, 0)
        done += bodies

    def finish(i, _):
        at = pl.ds(pl.multiple_of(i * 256, 256), 256)
        pieces = []
        for h in range(heads):
            pieces += [dqt_s[h, :, at].T, acc_kv[h, at, :]]
        out_ref[at, :] = jnp.concatenate(pieces, axis=1).astype(out_ref.dtype)
        return 0

    lax.fori_loop(0, rows // 256, finish, 0)

    def rest(at, _):
        turn(at)
        return 0

    lax.fori_loop(done, n + len(stages) - 1, rest, 0)

    def sent(c, _):
        for s in range(9 + len(far)):
            copy(c, s).wait_send()
        return 0

    lax.fori_loop(0, n, sent, 0)


def back_pass(groups, lengths, grad_att, packed, att, lse, grads, chunk=192, block=512):
    rows = packed.shape[0]
    parts, own_rows, head_width = grad_att.shape
    heads = head_width // HEAD_DIM
    width = grads.shape[2]
    n = grads.shape[1] // chunk
    extra = max(len(peers_of(4, groups)) - 5, 1)
    bf16 = lambda *shape: pltpu.VMEM(shape, jnp.bfloat16)
    f32 = lambda *shape: pltpu.VMEM(shape, jnp.float32)
    vmem = pl.BlockSpec(memory_space=pltpu.VMEM)
    sems = pltpu.SemaphoreType.DMA
    wide = 2 * HEAD_DIM
    return pl.pallas_call(
        partial(back_kernel, groups, chunk, block),
        out_shape=(
            jax.ShapeDtypeStruct(packed.shape, jnp.bfloat16),
            jax.ShapeDtypeStruct((n, chunk, width), jnp.bfloat16),
        ),
        in_specs=[pl.BlockSpec(memory_space=pltpu.SMEM)] + [vmem] * 4 + [pl.BlockSpec(memory_space=pl.ANY)],
        out_specs=[vmem, vmem],
        scratch_shapes=[
            bf16(parts, own_rows, head_width),
            bf16(heads, rows, wide),
            bf16(heads, rows, wide),
            bf16(heads, rows, wide),
            bf16(heads, wide, rows),
            bf16(heads, wide, rows),
            bf16(heads, HEAD_DIM, rows),
            f32(heads, 1, rows),
            f32(heads, HEAD_DIM, rows),
            f32(heads, rows, wide),
            bf16(3, 2, chunk, width),
            bf16(n, 2, chunk, width),
            bf16(n, chunk, width),
            f32(n, chunk, width),
            bf16(n, chunk, width),
            bf16(n, chunk, width // 2),
            bf16(n, chunk, width // 2),
            bf16(n, chunk // 2, width // 2),
            bf16(n, chunk // 2, width // 2),
            bf16(n, chunk // 4, width // 2),
            bf16(n, chunk // 4, width // 2),
            bf16(n, extra, chunk // 4, width // 2),
            bf16(n, extra, chunk // 4, width // 2),
            sems((n, 9 + extra)),
            sems((n, 9 + extra)),
            sems((3, 2)),
            sems((3,)),
            sems((3,)),
            sems,
        ],
        compiler_params=pltpu.CompilerParams(
            collective_id=0, has_side_effects=True, vmem_limit_bytes=60 << 20
        ),
        name="back_pass",
    )(lengths, grad_att, packed, att, lse, grads)


def close_kernel(groups, pieces, split, d1_ref, qkv_ref, gains_ref, in_sum, qkv_sum, gains_sum,
                 first, second, to_y, acc, send, recv,
                 qacc, to_x, from_x, to_z, from_z, to_w, from_w, more_to, more_from, qsend, qrecv,
                 gain_at, gain_send, gain_recv):
    f32 = jnp.float32
    steps = peers_of(4, groups)
    far = steps[5:]
    me, dp = lax.axis_index("tensor"), lax.axis_index("dp")
    core, chip, cross = spread(me)
    b0, b1, b2 = dp % 2, (dp // 2) % 2, (dp // 4) % 2
    piece = d1_ref.shape[1] // pieces
    part = qkv_ref.shape[0] // split
    r2, r4, r8 = part // 2, part // 4, part // 8
    flight, sends = {}, []

    def go(key, src, dst, ssem, rsem, axis, bit):
        flight[key] = remote(src, dst, ssem, rsem, axis, bit)
        sends.append(flight[key])

    def span(c):
        return pl.ds(c * piece, piece)

    def pair(c):
        go(("d", c, 1), d1_ref.at[cross, span(c)], first.at[1, span(c)], send.at[c, 1], recv.at[c, 1], "tensor", 1)
        go(("d", c, 0), d1_ref.at[core, span(c)], first.at[0, span(c)], send.at[c, 0], recv.at[c, 0], "tensor", 1)

    def across(c):
        flight["d", c, 1].wait_recv()
        to_y[span(c)] = rounded(d1_ref[chip, span(c), :].astype(f32) + first[1, span(c), :].astype(f32))
        go(("d", c, 2), to_y.at[span(c)], second.at[span(c)], send.at[c, 2], recv.at[c, 2], "tensor", 2)
        flight["d", c, 0].wait_recv()
        acc[span(c)] = d1_ref[me, span(c), :].astype(f32) + first[0, span(c), :].astype(f32)

    def settle_rows(c):
        flight["d", c, 2].wait_recv()
        in_sum[span(c)] = acc[span(c)] + second[span(c)].astype(f32)

    def row(c, *bits):
        at, size = c * part, part
        for b in bits:
            size = size // 2
            at = at + b * size
        return pl.ds(pl.multiple_of(at, 16), size)

    def q_go(c, s, src, dst, axis, bit):
        go(("q", c, s), src, dst, qsend.at[c, s], qrecv.at[c, s], axis, bit)

    def q_x(c):
        to_x[c] = rounded(qkv_ref[row(c, 1 - b0), :])
        q_go(c, 0, to_x.at[c], from_x.at[c], "dp", 1)

    def q_z(c):
        flight["q", c, 0].wait_recv()
        qacc[c] = qkv_ref[row(c, b0), :] + from_x[c].astype(f32)
        to_z[c] = rounded(qacc[c, pl.ds(pl.multiple_of((1 - b1) * r4, 16), r4), :])
        q_go(c, 1, to_z.at[c], from_z.at[c], "dp", 2)

    def q_w(c):
        flight["q", c, 1].wait_recv()
        low = pl.ds(pl.multiple_of(b1 * r4, 16), r4)
        qacc[c, low, :] += from_z[c].astype(f32)
        to_w[c] = rounded(qacc[c, pl.ds(pl.multiple_of(b1 * r4 + (1 - b2) * r8, 16), r8), :])
        q_go(c, 2, to_w.at[c], from_w.at[c], "dp", 4)

    def q_settle(c):
        flight["q", c, 2].wait_recv()
        total = qacc[c, pl.ds(pl.multiple_of(b1 * r4 + b2 * r8, 16), r8), :] + from_w[c].astype(f32)
        for m, (axis, bit) in enumerate(far):
            more_to[c, m] = rounded(total)
            q_go(c, 6 + m, more_to.at[c, m], more_from.at[c, m], axis, bit)
            flight["q", c, 6 + m].wait_recv()
            total = rounded(total).astype(f32) + more_from[c, m].astype(f32)
        qkv_sum[row(c, b0, b1, b2), :] = rounded(total)
        spot = qkv_sum.at[row(c, b0, b1, b2), :]
        q_go(c, 3, spot, spot, "dp", 4)

    def q_share(c):
        flight["q", c, 3].wait_recv()
        spot = qkv_sum.at[row(c, b0, b1), :]
        q_go(c, 4, spot, spot, "dp", 2)

    def q_more(c):
        flight["q", c, 4].wait_recv()
        spot = qkv_sum.at[row(c, b0), :]
        q_go(c, 5, spot, spot, "dp", 1)

    def q_end(c):
        flight["q", c, 5].wait_recv()

    def gain_start(m):
        axis, bit = steps[m]
        go(("g", m), gain_at.at[0, m], gain_at.at[1, m], gain_send.at[m], gain_recv.at[m], axis, bit)

    greet(steps)
    q_stages = (q_x, q_z, q_w, q_settle, q_share, q_more, q_end)
    d_stages = (pair, across, settle_rows)
    gain_at[0, 0] = gains_ref[...]
    gain_start(0)
    gain_turn = 0
    for turn in range(max(split + len(q_stages), pieces + len(d_stages)) - 1):
        for s in reversed(range(len(d_stages))):
            if 0 <= turn - s < pieces:
                d_stages[s](turn - s)
        for s in reversed(range(len(q_stages))):
            if 0 <= turn - s < split:
                q_stages[s](turn - s)
        if gain_turn < len(steps):
            flight["g", gain_turn].wait_recv()
            now = gain_at[0, gain_turn] + gain_at[1, gain_turn]
            gain_turn += 1
            if gain_turn < len(steps):
                gain_at[0, gain_turn] = now
                gain_start(gain_turn)
            else:
                gains_sum[...] = now
    for copy in sends:
        copy.wait_send()


def close_pass(groups, d1, grad_qkv, gains, pieces=5, split=3):
    parts, own_rows, width = d1.shape
    rows, qcols = grad_qkv.shape
    part = rows // split
    steps = len(peers_of(4, groups))
    extra = max(steps - 5, 1)
    bf16 = lambda *shape: pltpu.VMEM(shape, jnp.bfloat16)
    f32 = lambda *shape: pltpu.VMEM(shape, jnp.float32)
    sems = pltpu.SemaphoreType.DMA
    vmem = pl.BlockSpec(memory_space=pltpu.VMEM)
    return pl.pallas_call(
        partial(close_kernel, groups, pieces, split),
        out_shape=(
            jax.ShapeDtypeStruct((own_rows, width), jnp.float32),
            jax.ShapeDtypeStruct((rows, qcols), jnp.bfloat16),
            jax.ShapeDtypeStruct(gains.shape, jnp.float32),
        ),
        in_specs=[vmem] * 3,
        out_specs=[vmem] * 3,
        scratch_shapes=[
            bf16(2, own_rows, width),
            bf16(own_rows, width),
            bf16(own_rows, width),
            f32(own_rows, width),
            sems((pieces, 3)),
            sems((pieces, 3)),
            f32(split, part // 2, qcols),
            bf16(split, part // 2, qcols),
            bf16(split, part // 2, qcols),
            bf16(split, part // 4, qcols),
            bf16(split, part // 4, qcols),
            bf16(split, part // 8, qcols),
            bf16(split, part // 8, qcols),
            bf16(split, extra, part // 8, qcols),
            bf16(split, extra, part // 8, qcols),
            sems((split, 6 + extra)),
            sems((split, 6 + extra)),
            pltpu.VMEM((2, steps) + gains.shape, jnp.float32),
            sems((steps,)),
            sems((steps,)),
        ],
        compiler_params=pltpu.CompilerParams(
            collective_id=4, has_side_effects=True, vmem_limit_bytes=40 << 20
        ),
        name="close_pass",
    )(d1, grad_qkv, gains)


def local(
    tokens,
    lengths,
    in_gain,
    qkv_weight,
    attn_gain,
    out_weight,
    ffn_gain,
    up_weight,
    hidden_gain,
    down_weight,
    out_grad,
):
    parts = lax.axis_size("tensor")
    own_rows, width = tokens.shape
    head_width, hidden = attn_gain.shape[0], hidden_gain.shape[0]

    def gather(values):
        return lax.all_gather(values, "tensor", axis=0)

    full_out, full_up, full_down = gather(out_weight), gather(up_weight), gather(down_weight)
    pad = -(head_width + hidden) % 1024
    own_gains = jnp.concatenate((attn_gain, hidden_gain, jnp.zeros((pad,), jnp.float32)))
    gathered_in, packed, gains = intake(tokens, in_gain, qkv_weight, own_gains.reshape(8, -1))
    gathered_in = gathered_in.reshape(parts * own_rows, width)
    packed = packed.reshape(parts * own_rows, -1)
    gains = gains.reshape(parts, -1)
    full_attn_gain = gains[:, :head_width].reshape(-1)
    full_hidden_gain = gains[:, head_width : head_width + hidden].reshape(-1)

    attended, log_total = attn_fwd(packed, lengths, 512, 512)
    own_att = exchange(attended.reshape(parts, own_rows, head_width), 2)
    result, grad_middle, grad_att, grads, gain_parts = rows_pass(
        own_att,
        tokens,
        out_grad,
        full_attn_gain,
        ffn_gain,
        full_hidden_gain,
        full_out.reshape(width, width),
        full_up,
        full_down,
        own_rows,
    )
    groups = lax.axis_size("dp")
    grad_packed, sums = back_pass(groups, lengths, grad_att, packed, attended, log_total, grads)
    grad_qkv = contract_rows(gathered_in, grad_packed)
    grad_in_parts = contract_cols(grad_packed, qkv_weight).astype(jnp.bfloat16)
    in_gain_part = jnp.sum(qkv_weight.astype(jnp.float32) * grad_qkv, axis=1) / in_gain
    gain_parts = gain_parts.at[2 + parts].set(in_gain_part)
    grad_in_normed, qkv_sum, gains = close_pass(
        groups, grad_in_parts.reshape(parts, own_rows, width), grad_qkv, gain_parts
    )

    residual = tokens.astype(jnp.float32)
    mean = jnp.mean(residual, axis=1, keepdims=True)
    square = jnp.mean(residual * residual, axis=1, keepdims=True)
    scale = lax.rsqrt(square - mean * mean + EPS)
    unit = (residual - mean) * scale
    weighted = grad_in_normed * in_gain
    first = jnp.mean(weighted, axis=1, keepdims=True)
    second = jnp.mean(weighted * unit, axis=1, keepdims=True)
    in_grad = grad_middle + scale * (weighted - first - unit * second)

    me = lax.axis_index("tensor")
    sums = sums.reshape(-1, width).astype(jnp.float32)
    return (
        result,
        in_grad,
        gains[2 + parts],
        qkv_sum.astype(jnp.float32),
        lax.dynamic_slice_in_dim(gains[1], me * head_width, head_width),
        sums[hidden + width : hidden + width + head_width],
        gains[0],
        sums[hidden : hidden + width],
        lax.dynamic_index_in_dim(gains, 2 + me, 0, keepdims=False),
        sums[:hidden],
    )


def solution(mesh):
    return jax.shard_map(
        local,
        mesh=mesh,
        in_specs=(
            P(("dp", "tensor"), None),
            P("dp", None),
            P(),
            P(None, "tensor"),
            P("tensor"),
            P("tensor", None),
            P(),
            P(None, "tensor"),
            P("tensor"),
            P("tensor", None),
            P(("dp", "tensor"), None),
        ),
        out_specs=(
            P(("dp", "tensor"), None),
            P(("dp", "tensor"), None),
            P(),
            P(None, "tensor"),
            P("tensor"),
            P("tensor", None),
            P(),
            P(None, "tensor"),
            P("tensor"),
            P("tensor", None),
        ),
        check_vma=False,
    )
```

```python
from functools import partial

import jax
import jax.numpy as jnp
from jax import lax
from jax.experimental import pallas as pl
from jax.experimental.pallas import tpu as pltpu
from jax.sharding import PartitionSpec as P

HEAD_DIM = 64
UNIT = 64
EPS = 1e-05


def contract_rows(left, right):
    return lax.dot_general(
        left, right, (((0,), (0,)), ((), ())), preferred_element_type=jnp.float32
    )


def contract_cols(left, right):
    return lax.dot_general(
        left, right, (((1,), (1,)), ((), ())), preferred_element_type=jnp.float32
    )


NEG = -1e30


def seq_bounds(len_ref):
    ends, total = [], 0
    for s in range(len_ref.shape[1]):
        total = total + len_ref[0, s] * UNIT
        ends.append(total)
    return ends


def start_of(ends, row):
    at = 0
    for end in ends:
        at = jnp.where(row >= end, end, at)
    return at


def end_of(ends, row):
    at = ends[-1]
    for end in reversed(ends):
        at = jnp.where(row < end, end, at)
    return at


def dot(a, b):
    return lax.dot_general(a, b, (((1,), (0,)), ((), ())), preferred_element_type=jnp.float32)


def fwd_kernel(bq, bk, len_ref, qkv_ref, o_ref, lse_ref, k_s, qt_s, vt_s, acc_s, m_s):
    rows = qkv_ref.shape[0]
    heads = k_s.shape[0]
    ends = seq_bounds(len_ref)
    ones = (lax.broadcasted_iota(jnp.int32, (16, bq), 0) == 0).astype(jnp.float32).astype(jnp.bfloat16)

    def stage(i, _):
        at = pl.ds(pl.multiple_of(i * bq, bq), bq)
        x = qkv_ref[at, :]
        for h in range(heads):
            base = h * 3 * HEAD_DIM
            q = x[:, base : base + HEAD_DIM] * jnp.bfloat16(0.125)
            qt_s[h, :, at] = q.T
            k_s[h, at, :] = x[:, base + HEAD_DIM : base + 2 * HEAD_DIM]
            vt_s[h, :HEAD_DIM, at] = x[:, base + 2 * HEAD_DIM : base + 3 * HEAD_DIM].T
            vt_s[h, HEAD_DIM:, at] = ones
        return 0

    lax.fori_loop(0, rows // bq, stage, 0)

    def query_block(i, _):
        first = pl.multiple_of(i * bq, bq)
        at = pl.ds(first, bq)
        q_pos = first + lax.broadcasted_iota(jnp.int32, (1, bq), 1)
        q_start = start_of(ends, q_pos)
        lo = start_of(ends, first)
        hi = start_of(ends, first + bq - 1)
        for h in range(heads):
            acc_s[h] = jnp.zeros_like(acc_s[h])
            m_s[h] = jnp.full_like(m_s[h], NEG)

        def step(masked, c, _):
            c0 = pl.multiple_of(c * bk, bk)
            for h in range(heads):
                s = dot(k_s[h, pl.ds(c0, bk), :], qt_s[h, :, at])
                if masked:
                    k_pos = c0 + lax.broadcasted_iota(jnp.int32, (bk, 1), 0)
                    s = jnp.where((k_pos <= q_pos) & (k_pos >= q_start), s, NEG)
                old = m_s[h]
                new = jnp.maximum(old, jnp.max(s, axis=0, keepdims=True))
                p = jnp.exp(s - new).astype(jnp.bfloat16)
                m_s[h] = new
                acc_s[h] = acc_s[h] * jnp.exp(old - new) + dot(vt_s[h, :, pl.ds(c0, bk)], p)
            return 0

        c_lo = lo // bk
        c_diag = first // bk
        c_end = (first + bq - 1) // bk + 1
        c_int = jnp.minimum((hi + bk - 1) // bk, c_diag)
        lax.fori_loop(c_lo, c_int, partial(step, True), 0)
        lax.fori_loop(c_int, c_diag, partial(step, False), 0)
        lax.fori_loop(jnp.maximum(c_diag, c_lo), c_end, partial(step, True), 0)
        outs = []
        for h in range(heads):
            acc = acc_s[h]
            total = acc[HEAD_DIM : HEAD_DIM + 1, :]
            outs.append((acc[:HEAD_DIM, :] / total).T)
            lse_ref[h : h + 1, at] = m_s[h] + jnp.log(total)
        o_ref[at, :] = jnp.concatenate(outs, axis=1).astype(o_ref.dtype)
        return 0

    lax.fori_loop(0, rows // bq, query_block, 0)


def attn_fwd(packed, lengths, bq=256, bk=256, out_dtype=jnp.bfloat16):
    rows = packed.shape[0]
    heads = packed.shape[1] // (3 * HEAD_DIM)
    return pl.pallas_call(
        partial(fwd_kernel, bq, bk),
        out_shape=(
            jax.ShapeDtypeStruct((rows, heads * HEAD_DIM), out_dtype),
            jax.ShapeDtypeStruct((8, rows), jnp.float32),
        ),
        in_specs=[pl.BlockSpec(memory_space=pltpu.SMEM), pl.BlockSpec(memory_space=pltpu.VMEM)],
        out_specs=[pl.BlockSpec(memory_space=pltpu.VMEM)] * 2,
        scratch_shapes=[
            pltpu.VMEM((heads, rows, HEAD_DIM), jnp.bfloat16),
            pltpu.VMEM((heads, HEAD_DIM, rows), jnp.bfloat16),
            pltpu.VMEM((heads, HEAD_DIM + 16, rows), jnp.bfloat16),
            pltpu.VMEM((heads, HEAD_DIM + 16, bq), jnp.float32),
            pltpu.VMEM((heads, 1, bq), jnp.float32),
        ],
        compiler_params=pltpu.CompilerParams(vmem_limit_bytes=48 << 20),
        name="attn_fwd",
    )(lengths, packed)


MESH = pl.DeviceIdType.MESH


def flip(index, bit):
    return index + bit - 2 * bit * ((index // bit) % 2)


def peers_of(parts, groups):
    steps, bit = [], 1
    while bit < parts:
        steps.append(("tensor", bit))
        bit *= 2
    bit = 1
    while bit < groups:
        steps.append(("dp", bit))
        bit *= 2
    return steps


def at_peer(axis, bit):
    return {axis: flip(lax.axis_index(axis), bit)}


def greet(steps, *more):
    barrier = pltpu.get_barrier_semaphore()
    for axis, bit in steps:
        pl.semaphore_signal(barrier, inc=1, device_id=at_peer(axis, bit), device_id_type=MESH)
    for peer in more:
        pl.semaphore_signal(barrier, inc=1, device_id={"tensor": peer}, device_id_type=MESH)
    pl.semaphore_wait(barrier, len(steps) + len(more))


def remote(src, dst, send, recv, axis, bit):
    copy = pltpu.make_async_remote_copy(
        src_ref=src,
        dst_ref=dst,
        send_sem=send,
        recv_sem=recv,
        device_id=at_peer(axis, bit),
        device_id_type=MESH,
    )
    copy.start()
    return copy


def rounded(values):
    return values.astype(jnp.bfloat16)


def spread(me):
    return flip(me, 1), flip(me, 2), flip(flip(me, 1), 2)


def greet_tensor(ids):
    barrier = pltpu.get_barrier_semaphore()
    for peer in ids:
        pl.semaphore_signal(barrier, inc=1, device_id={"tensor": peer}, device_id_type=MESH)
    pl.semaphore_wait(barrier, len(ids))


def push(src, dst, send, recv, peer):
    copy = pltpu.make_async_remote_copy(
        src_ref=src,
        dst_ref=dst,
        send_sem=send,
        recv_sem=recv,
        device_id={"tensor": peer},
        device_id_type=MESH,
    )
    copy.start()
    return copy


def intake_kernel(tok_ref, gain_ref, w_ref, own_gain_ref, all_ref, packed_ref, gains_ref,
                  send, recv, gain_send, gain_recv):
    me = lax.axis_index("tensor")
    core, chip, cross = spread(me)
    rows, width = tok_ref.shape
    pieces = (send.shape[0] - 1) // 2
    piece = rows // pieces
    f32 = jnp.float32
    values = tok_ref[...].astype(f32)
    mu = jnp.sum(values, axis=1, keepdims=True) / width
    ms = jnp.sum(values * values, axis=1, keepdims=True) / width
    normed = (values - mu) * lax.rsqrt(ms - mu * mu + EPS) * gain_ref[...]
    all_ref[me] = normed.astype(jnp.bfloat16)
    gains_ref[me] = own_gain_ref[...]
    greet_tensor((core, chip))

    def span(c):
        return pl.ds(c * piece, piece)

    def block(c, owner):
        return all_ref.at[owner, span(c), :]

    to_chip = [push(block(c, me), block(c, me), send.at[c], recv.at[c], chip) for c in range(pieces)]
    gain_chip = push(gains_ref.at[me], gains_ref.at[me], gain_send.at[0], gain_recv.at[0], chip)
    to_core = push(all_ref.at[me], all_ref.at[me], send.at[2 * pieces], recv.at[2 * pieces], core)
    gain_core = push(gains_ref.at[me], gains_ref.at[me], gain_send.at[1], gain_recv.at[1], core)

    def project(owner, c):
        product = jnp.dot(all_ref[owner, span(c), :], w_ref[...], preferred_element_type=f32)
        packed_ref[owner, span(c), :] = product.astype(jnp.bfloat16)

    for c in range(pieces):
        project(me, c)
    to_core.wait_recv()
    for c in range(pieces):
        project(core, c)
    gain_chip.wait_recv()
    gain_far = push(gains_ref.at[chip], gains_ref.at[chip], gain_send.at[2], gain_recv.at[2], core)
    far = []
    for c in range(pieces):
        to_chip[c].wait_recv()
        far.append(push(block(c, chip), block(c, chip), send.at[pieces + c], recv.at[pieces + c], core))
        project(chip, c)
    for c in range(pieces):
        far[c].wait_recv()
        project(cross, c)
    gain_core.wait_recv()
    gain_far.wait_recv()
    for copy in [*to_chip, to_core, *far, gain_chip, gain_core, gain_far]:
        copy.wait_send()


def intake(tokens, gain, weight, own_gains, pieces=5):
    rows, width = tokens.shape
    vmem = pl.BlockSpec(memory_space=pltpu.VMEM)
    return pl.pallas_call(
        intake_kernel,
        out_shape=(
            jax.ShapeDtypeStruct((4, rows, width), jnp.bfloat16),
            jax.ShapeDtypeStruct((4, rows, weight.shape[1]), jnp.bfloat16),
            jax.ShapeDtypeStruct((4,) + own_gains.shape, jnp.float32),
        ),
        in_specs=[vmem] * 4,
        out_specs=[vmem] * 3,
        scratch_shapes=[
            pltpu.SemaphoreType.DMA((2 * pieces + 1,)),
            pltpu.SemaphoreType.DMA((2 * pieces + 1,)),
            pltpu.SemaphoreType.DMA((3,)),
            pltpu.SemaphoreType.DMA((3,)),
        ],
        compiler_params=pltpu.CompilerParams(
            collective_id=1, has_side_effects=True, vmem_limit_bytes=40 << 20
        ),
        name="intake",
    )(tokens, gain.reshape(1, -1), weight, own_gains)


def exchange_kernel(in_ref, out_ref, send, recv, local_sem):
    me = lax.axis_index("tensor")
    peers = spread(me)
    greet_tensor(peers)
    moves = []
    for n, peer in reversed(list(enumerate(peers))):
        moves.append(push(in_ref.at[peer], out_ref.at[me], send.at[n], recv.at[n], peer))
    own = pltpu.make_async_copy(in_ref.at[me], out_ref.at[me], local_sem)
    own.start()
    own.wait()
    for move in moves:
        move.wait()


def exchange(blocks, number):
    anywhere = pl.BlockSpec(memory_space=pltpu.VMEM)
    return pl.pallas_call(
        exchange_kernel,
        out_shape=jax.ShapeDtypeStruct(blocks.shape, blocks.dtype),
        in_specs=[anywhere],
        out_specs=anywhere,
        scratch_shapes=[
            pltpu.SemaphoreType.DMA((3,)),
            pltpu.SemaphoreType.DMA((3,)),
            pltpu.SemaphoreType.DMA,
        ],
        compiler_params=pltpu.CompilerParams(
            collective_id=number, has_side_effects=True, vmem_limit_bytes=24 << 20
        ),
        name="exchange",
    )(blocks)


def dot_nt(a, b):
    return lax.dot_general(a, b, (((1,), (1,)), ((), ())), preferred_element_type=jnp.float32)


def dot_tn(a, b):
    return lax.dot_general(a, b, (((0,), (0,)), ((), ())), preferred_element_type=jnp.float32)


GELU_A = 0.7978845608028654
GELU_B = 0.044715


def rows_kernel(tile, att_ref, tok_ref, og_ref, again_ref, fgain_ref, hgain_ref, wout_hbm, wup_hbm, wdown_hbm,
                res_ref, gm_ref, datt_ref, g_hbm, gsum_ref,
                wout, wup, wdown, x_s, mid_s, low_att, low_mid, act_s, slope_s, wide_s, low_act, big_s, acc_s,
                mu_s, rs_s, mu4_s, rs4_s, one_s, two_s, stage, w_sem, g_sem):
    parts, rows, head_width = att_ref.shape
    width = tok_ref.shape[1]
    hidden = width * hgain_ref.shape[0]
    n_tiles = rows // tile
    f32 = jnp.float32

    loads = [pltpu.make_async_copy(wout_hbm, wout, w_sem.at[0])]
    for t in range(parts):
        loads.append(pltpu.make_async_copy(wup_hbm.at[t], wup.at[t], w_sem.at[1 + t]))
    for t in range(parts):
        loads.append(pltpu.make_async_copy(wdown_hbm.at[t], wdown.at[t], w_sem.at[1 + parts + t]))
    for copy in loads:
        copy.start()

    def at(i):
        return pl.ds(pl.multiple_of(i * tile, tile), tile)

    def fold(v):
        return jnp.sum(v.reshape(tile // 8, 8, width), axis=0)

    def tiles(body, init=0):
        return lax.fori_loop(0, n_tiles, body, init)

    def stats(v, n):
        mu = jnp.sum(v, axis=1, keepdims=True) / n
        ms = jnp.sum(v * v, axis=1, keepdims=True) / n
        return mu, lax.rsqrt(ms - mu * mu + EPS)

    def save(slot, block, shard, row, n):
        copy = pltpu.make_async_copy(
            stage.at[slot, pl.ds(0, n), :], g_hbm.at[shard, pl.ds(row, n), :], g_sem.at[slot]
        )
        return copy

    again = again_ref[...]
    fgain = fgain_ref[...]

    def first(i, _):
        v = jnp.concatenate([att_ref[t, at(i), :] for t in range(parts)], axis=1).astype(f32)
        x_s[at(i), :] = v
        mu, rs = stats(v, width)
        mu_s[at(i), :] = mu
        rs_s[at(i), :] = rs
        low_att[at(i), :] = ((v - mu) * rs * again).astype(jnp.bfloat16)
        return 0

    tiles(first)
    loads[0].wait()
    big_s[...] = jnp.dot(low_att[...], wout[...], preferred_element_type=f32)

    def second(i, _):
        v = tok_ref[at(i), :].astype(f32) + big_s[at(i), :]
        mid_s[at(i), :] = v
        mu, rs = stats(v, width)
        low_mid[at(i), :] = ((v - mu) * rs * fgain).astype(jnp.bfloat16)
        one_s[at(i), :] = jnp.zeros((tile, 1), f32)
        two_s[at(i), :] = jnp.zeros((tile, 1), f32)
        acc_s[at(i), :] = v
        return 0

    tiles(second)

    for copy in loads[1:]:
        copy.wait()

    def up_block(t, _):
        big_s[...] = jnp.dot(low_mid[...], wup[t], preferred_element_type=f32)

        def body(i, _):
            v = big_s[at(i), :]
            sq = v * v
            th = jnp.tanh(v * (GELU_A + (GELU_A * GELU_B) * sq))
            half = 0.5 * th + 0.5
            act = v * half
            act_s[t, at(i), :] = act
            slope = half + (0.5 * v) * (1.0 - th * th) * (GELU_A + (3.0 * GELU_A * GELU_B) * sq)
            slope_s[t, at(i), :] = slope.astype(jnp.bfloat16)
            one_s[at(i), :] += jnp.sum(act, axis=1, keepdims=True)
            two_s[at(i), :] += jnp.sum(act * act, axis=1, keepdims=True)
            return 0

        tiles(body)
        return 0

    lax.fori_loop(0, parts, up_block, 0)

    def third(i, _):
        mu = one_s[at(i), :] / hidden
        mu4_s[at(i), :] = mu
        rs4_s[at(i), :] = lax.rsqrt(two_s[at(i), :] / hidden - mu * mu + EPS)
        one_s[at(i), :] = jnp.zeros((tile, 1), f32)
        two_s[at(i), :] = jnp.zeros((tile, 1), f32)
        return 0

    tiles(third)

    def down_block(t, _):
        hg = hgain_ref[t]
        big_s[...] = dot_nt(og_ref[...], wdown[t])

        def body(i, part):
            unit = (act_s[t, at(i), :] - mu4_s[at(i), :]) * rs4_s[at(i), :]
            act_s[t, at(i), :] = unit
            low_act[at(i), :] = (unit * hg).astype(jnp.bfloat16)
            d4 = big_s[at(i), :]
            wide = d4 * hg
            wide_s[t, at(i), :] = wide
            one_s[at(i), :] += jnp.sum(wide, axis=1, keepdims=True)
            two_s[at(i), :] += jnp.sum(wide * unit, axis=1, keepdims=True)
            return part + fold(d4 * unit)

        part = tiles(body, jnp.zeros((8, width), f32))
        gsum_ref[pl.ds(2 + t, 1), :] = jnp.sum(part, axis=0, keepdims=True)
        acc_s[...] += jnp.dot(low_act[...], wdown[t], preferred_element_type=f32)
        slot = t % 2

        @pl.when(t >= 2)
        def _():
            save(slot, None, t, 0, width).wait()

        stage[slot] = dot_tn(low_act[...], og_ref[...]).astype(jnp.bfloat16)
        save(slot, None, t, 0, width).start()
        return 0

    lax.fori_loop(0, parts, down_block, 0)

    def fourth(i, _):
        res_ref[at(i), :] = acc_s[at(i), :].astype(jnp.bfloat16)
        one_s[at(i), :] = one_s[at(i), :] / hidden
        two_s[at(i), :] = two_s[at(i), :] / hidden
        acc_s[at(i), :] = jnp.zeros((tile, width), f32)
        return 0

    tiles(fourth)

    def back_block(t, _):
        def body(i, _):
            d_act = rs4_s[at(i), :] * (wide_s[t, at(i), :] - one_s[at(i), :] - act_s[t, at(i), :] * two_s[at(i), :])
            low_act[at(i), :] = (d_act * slope_s[t, at(i), :].astype(f32)).astype(jnp.bfloat16)
            return 0

        tiles(body)
        acc_s[...] += dot_nt(low_act[...], wup[t])
        slot = t % 2
        save(slot, None, t, 0, width).wait()
        stage[slot] = dot_tn(low_mid[...], low_act[...]).astype(jnp.bfloat16)
        save(slot, None, t, width, width).start()
        return 0

    lax.fori_loop(0, parts, back_block, 0)

    def fifth(i, part):
        v = mid_s[at(i), :]
        mu, rs = stats(v, width)
        unit = (v - mu) * rs
        d3 = acc_s[at(i), :]
        wide = d3 * fgain
        m1 = jnp.sum(wide, axis=1, keepdims=True) / width
        m2 = jnp.sum(wide * unit, axis=1, keepdims=True) / width
        d_mid = og_ref[at(i), :].astype(f32) + rs * (wide - m1 - unit * m2)
        gm_ref[at(i), :] = d_mid
        low_act[at(i), :] = d_mid.astype(jnp.bfloat16)
        return part + fold(d3 * unit)

    part = tiles(fifth, jnp.zeros((8, width), f32))
    gsum_ref[0:1, :] = jnp.sum(part, axis=0, keepdims=True)
    big_s[...] = dot_nt(low_act[...], wout[...])
    for slot in range(2):
        save(slot, None, slot, width, width).wait()
    stage[0] = dot_tn(low_att[...], low_act[...]).astype(jnp.bfloat16)
    last = []
    for t in range(parts):
        copy = pltpu.make_async_copy(
            stage.at[0, pl.ds(t * head_width, head_width), :],
            g_hbm.at[t, pl.ds(2 * width, head_width), :],
            w_sem.at[t],
        )
        copy.start()
        last.append(copy)

    def sixth(i, part):
        mu, rs = mu_s[at(i), :], rs_s[at(i), :]
        unit = (x_s[at(i), :] - mu) * rs
        d2 = big_s[at(i), :]
        wide = d2 * again
        m1 = jnp.sum(wide, axis=1, keepdims=True) / width
        m2 = jnp.sum(wide * unit, axis=1, keepdims=True) / width
        d_att = (rs * (wide - m1 - unit * m2)).astype(jnp.bfloat16)
        for t in range(parts):
            datt_ref[t, at(i), :] = d_att[:, t * head_width : (t + 1) * head_width]
        return part + fold(d2 * unit)

    part = tiles(sixth, jnp.zeros((8, width), f32))
    gsum_ref[1:2, :] = jnp.sum(part, axis=0, keepdims=True)
    gsum_ref[pl.ds(2 + parts, 8 - 2 - parts), :] = jnp.zeros((8 - 2 - parts, width), f32)
    for copy in last:
        copy.wait()


def rows_pass(att, tokens, out_grad, attn_gain, ffn_gain, hidden_gain, w_out, w_up, w_down, tile=32):
    parts, rows, head_width = att.shape
    width = tokens.shape[1]
    bf16, f32 = jnp.bfloat16, jnp.float32
    vmem = pl.BlockSpec(memory_space=pltpu.VMEM)
    anywhere = pl.BlockSpec(memory_space=pl.ANY)
    column = pltpu.VMEM((rows, 1), f32)
    return pl.pallas_call(
        partial(rows_kernel, tile),
        out_shape=(
            jax.ShapeDtypeStruct((rows, width), bf16),
            jax.ShapeDtypeStruct((rows, width), f32),
            jax.ShapeDtypeStruct(att.shape, bf16),
            jax.ShapeDtypeStruct((parts, 2 * width + head_width, width), bf16),
            jax.ShapeDtypeStruct((8, width), f32),
        ),
        in_specs=[vmem] * 6 + [anywhere] * 3,
        out_specs=[vmem] * 3 + [anywhere, vmem],
        scratch_shapes=[
            pltpu.VMEM((width, width), bf16),
            pltpu.VMEM((parts, width, width), bf16),
            pltpu.VMEM((parts, width, width), bf16),
            pltpu.VMEM((rows, width), f32),
            pltpu.VMEM((rows, width), f32),
            pltpu.VMEM((rows, width), bf16),
            pltpu.VMEM((rows, width), bf16),
            pltpu.VMEM((parts, rows, width), f32),
            pltpu.VMEM((parts, rows, width), bf16),
            pltpu.VMEM((parts, rows, width), f32),
            pltpu.VMEM((rows, width), bf16),
            pltpu.VMEM((rows, width), f32),
            pltpu.VMEM((rows, width), f32),
        ] + [column] * 6 + [
            pltpu.VMEM((2, width, width), bf16),
            pltpu.SemaphoreType.DMA((1 + 2 * parts,)),
            pltpu.SemaphoreType.DMA((2,)),
        ],
        compiler_params=pltpu.CompilerParams(vmem_limit_bytes=60 << 20),
        cost_estimate=pl.CostEstimate(flops=20 * 10**9, bytes_accessed=40 << 20, transcendentals=2 * 10**6),
        name="rows_pass",
    )(att, tokens, out_grad, attn_gain.reshape(1, -1), ffn_gain.reshape(1, -1),
      hidden_gain.reshape(parts, 1, -1), w_out, w_up, w_down)


def chunk_copy(c, s, src, dst, send, recv, axis, bit):
    return pltpu.make_async_remote_copy(
        src_ref=src,
        dst_ref=dst,
        send_sem=send.at[c, s],
        recv_sem=recv.at[c, s],
        device_id=at_peer(axis, bit),
        device_id_type=MESH,
    )


def back_kernel(groups, chunk, block, pieces, split, len_ref, datt_ref, packed_ref, att_ref, lse_ref, grads_ref,
                h1_ref, w_ref, gains_ref, in_gain_ref,
                sum_ref, in_sum, qkv_sum, gains_sum,
                pq, do_s, own, first, second, acc, to_y, to_x, from_x, to_z, from_z, to_w, from_w, more_to, more_from,
                send, recv, local_sem, a2a_send, a2a_recv, a2a_local,
                d_first, d_second, d_send, d_recv, q_from_x, q_from_z, q_from_w, q_more_from, q_send, q_recv,
                gain_at, gain_send, gain_recv, load_sem):
    f32, bf16 = jnp.float32, jnp.bfloat16
    steps = peers_of(4, groups)
    far = steps[5:]
    me, dp = lax.axis_index("tensor"), lax.axis_index("dp")
    core, chip, cross = spread(me)
    cols = grads_ref.shape[2]
    half, rows2, rows4 = cols // 2, chunk // 2, chunk // 4
    b0, b1, b2 = dp % 2, (dp // 2) % 2, (dp // 4) % 2
    n = grads_ref.shape[1] // chunk

    def take(c, shard):
        return grads_ref.at[shard, pl.ds(pl.multiple_of(c * chunk, 16), chunk), :]

    def col(b):
        return pl.ds(pl.multiple_of(b * half, 128), half)

    def row2(b):
        return pl.ds(pl.multiple_of(b * rows2, 16), rows2)

    def row4(b, bb):
        return pl.ds(pl.multiple_of(b * rows2 + bb * rows4, 16), rows4)

    def copy(c, s):
        if s == 0:
            return chunk_copy(c, 0, take(c, core), first.at[c, 0], send, recv, "tensor", 1)
        if s == 1:
            return chunk_copy(c, 1, take(c, cross), first.at[c, 1], send, recv, "tensor", 1)
        if s == 2:
            return chunk_copy(c, 2, to_y.at[c % 3], second.at[c], send, recv, "tensor", 2)
        if s == 3:
            return chunk_copy(c, 3, to_x.at[c % 3], from_x.at[c], send, recv, "dp", 1)
        if s == 4:
            return chunk_copy(c, 4, to_z.at[c], from_z.at[c], send, recv, "dp", 2)
        if s == 5:
            return chunk_copy(c, 5, to_w.at[c], from_w.at[c], send, recv, "dp", 4)
        if s == 6:
            piece = sum_ref.at[c, row4(b1, b2), col(b0)]
            return chunk_copy(c, 6, piece, piece, send, recv, "dp", 4)
        if s == 7:
            piece = sum_ref.at[c, row2(b1), col(b0)]
            return chunk_copy(c, 7, piece, piece, send, recv, "dp", 2)
        if s == 8:
            piece = sum_ref.at[c, :, col(b0)]
            return chunk_copy(c, 8, piece, piece, send, recv, "dp", 1)
        axis, bit = far[s - 9]
        return chunk_copy(c, s, more_to.at[c, s - 9], more_from.at[c, s - 9], send, recv, axis, bit)

    def arrived(c, s, piece=None):
        if piece is None:
            copy(c, s).wait_recv()
        else:
            axis, bit = {6: ("dp", 4), 7: ("dp", 2), 8: ("dp", 1)}[s]
            chunk_copy(c, s, piece, piece, send, recv, axis, bit).wait_recv()

    def mine(c, k):
        shard = (me, chip)[k]
        return pltpu.make_async_copy(take(c, shard), own.at[c % 3, k], local_sem.at[c % 3, k])

    def pair(c):
        copy(c, 1).start()
        copy(c, 0).start()
        mine(c, 1).start()
        mine(c, 0).start()

    def to_chip(c):
        @pl.when(c >= 3)
        def _():
            copy(c - 3, 2).wait_send()

        mine(c, 1).wait()
        arrived(c, 1)
        to_y[c % 3] = rounded(own[c % 3, 1].astype(f32) + first[c, 1].astype(f32))
        copy(c, 2).start()

    def x_half(c):
        @pl.when(c >= 3)
        def _():
            copy(c - 3, 3).wait_send()

        mine(c, 0).wait()
        arrived(c, 0)
        arrived(c, 2)

        def total(b):
            whole = own[c % 3, 0, :, col(b)].astype(f32) + first[c, 0, :, col(b)].astype(f32)
            return whole + second[c, :, col(b)].astype(f32)

        to_x[c % 3] = rounded(total(1 - b0))
        copy(c, 3).start()
        acc[c] = total(b0)

    def z_half(c):
        arrived(c, 3)
        acc[c] += from_x[c].astype(f32)
        to_z[c] = rounded(acc[c, row2(1 - b1), :])
        copy(c, 4).start()

    def z_quarter(c):
        arrived(c, 4)
        acc[c, row2(b1), :] += from_z[c].astype(f32)
        to_w[c] = rounded(acc[c, row4(b1, 1 - b2), :])
        copy(c, 5).start()

    def settle(c):
        arrived(c, 5)
        total = acc[c, row4(b1, b2), :] + from_w[c].astype(f32)
        for m in range(len(far)):
            more_to[c, m] = rounded(total)
            copy(c, 9 + m).start()
            arrived(c, 9 + m)
            total = rounded(total).astype(f32) + more_from[c, m].astype(f32)
        sum_ref[c, row4(b1, b2), col(b0)] = rounded(total)
        copy(c, 6).start()

    def z_share(c):
        arrived(c, 6, sum_ref.at[c, row4(b1, 1 - b2), col(b0)])
        copy(c, 7).start()

    def x_share(c):
        arrived(c, 7, sum_ref.at[c, row2(1 - b1), col(b0)])
        copy(c, 8).start()

    def end(c):
        arrived(c, 8, sum_ref.at[c, :, col(1 - b0)])

    stages = (pair, to_chip, x_half, z_half, z_quarter, settle, z_share, x_share, end)

    def turn(at):
        for s in range(len(stages)):
            c = at - s

            @pl.when((c >= 0) & (c < n))
            def _():
                stages[s](c)

    rows = packed_ref.shape[0]
    heads = packed_ref.shape[1] // (3 * HEAD_DIM)
    own_rows = datt_ref.shape[1]
    width = h1_ref.shape[1]
    ends = seq_bounds(len_ref)
    scale = jnp.bfloat16(0.125)
    load = pltpu.make_async_copy(packed_ref, pq, load_sem.at[0])
    load.start()
    greet(steps, cross)

    def a2a(k, peer):
        return pltpu.make_async_remote_copy(
            src_ref=datt_ref.at[peer],
            dst_ref=do_s.at[me],
            send_sem=a2a_send.at[k],
            recv_sem=a2a_recv.at[k],
            device_id={"tensor": peer},
            device_id_type=MESH,
        )

    moves = [a2a(k, peer) for k, peer in reversed(list(enumerate((core, chip, cross))))]
    for move in moves:
        move.start()
    keep_own = pltpu.make_async_copy(datt_ref.at[me], do_s.at[me], a2a_local)
    keep_own.start()
    turn(jnp.int32(0))
    load.wait()

    def attention(kv_s, q_s, g_s, qt_s, gt_s, kt_s, d_s, dqt_s, acc_kv):
        def stage_qkv(i, _):
            at = pl.ds(pl.multiple_of(i * 256, 256), 256)
            x = pq[at, :]
            blank = jnp.zeros((256, HEAD_DIM), bf16)
            blank_t = jnp.zeros((HEAD_DIM, 256), bf16)
            for h in range(heads):
                base = h * 3 * HEAD_DIM
                q = x[:, base : base + HEAD_DIM] * scale
                k = x[:, base + HEAD_DIM : base + 2 * HEAD_DIM]
                v = x[:, base + 2 * HEAD_DIM : base + 3 * HEAD_DIM]
                kv_s[h, at, :] = jnp.concatenate([k, v], axis=1)
                q_s[h, at, :] = jnp.concatenate([q, blank], axis=1)
                qt_s[h, :HEAD_DIM, at] = q.T
                qt_s[h, HEAD_DIM:, at] = blank_t
                kt_s[h, :, at] = (k * scale).T
                dqt_s[h, :, at] = jnp.zeros((HEAD_DIM, 256), f32)
                acc_kv[h, at, :] = jnp.zeros((256, 2 * HEAD_DIM), f32)
            return 0

        lax.fori_loop(0, rows // 256, stage_qkv, 0)
        keep_own.wait()
        for move in moves:
            move.wait()
        piece = own_rows // 5

        def stage_grad(i, _):
            owner, part = i // 5, i % 5
            inner = pl.ds(pl.multiple_of(part * piece, piece), piece)
            at = pl.ds(pl.multiple_of(owner * own_rows + part * piece, piece), piece)
            g = do_s[owner, inner, :]
            prod = g.astype(f32) * att_ref[at, :].astype(f32)
            blank = jnp.zeros((piece, HEAD_DIM), bf16)
            blank_t = jnp.zeros((HEAD_DIM, piece), bf16)
            for h in range(heads):
                d = g[:, h * HEAD_DIM : (h + 1) * HEAD_DIM]
                g_s[h, at, :] = jnp.concatenate([blank, d], axis=1)
                gt_s[h, HEAD_DIM:, at] = d.T
                gt_s[h, :HEAD_DIM, at] = blank_t
                d_s[h, :, at] = jnp.sum(prod[:, h * HEAD_DIM : (h + 1) * HEAD_DIM].T, axis=0, keepdims=True)
            return 0

        lax.fori_loop(0, rows // piece, stage_grad, 0)

        def body(i, j):
            q0 = pl.multiple_of(i * block, block)
            k0 = pl.multiple_of(j * block, block)
            at, kat = pl.ds(q0, block), pl.ds(k0, block)
            q_pos = q0 + lax.broadcasted_iota(jnp.int32, (1, block), 1)
            q_start = start_of(ends, q_pos)
            k_pos = k0 + lax.broadcasted_iota(jnp.int32, (block, 1), 0)
            keep = (k_pos <= q_pos) & (k_pos >= q_start)
            for h in range(heads):
                kv = kv_s[h, kat, :]
                s = dot(kv, qt_s[h, :, at]) - lse_ref[h : h + 1, at]
                p = jnp.exp(jnp.where(keep, s, NEG))
                dp_t = dot(kv, gt_s[h, :, at])
                ds = (p * (dp_t - d_s[h, :, at])).astype(bf16)
                acc_kv[h, kat, :] += dot(p.astype(bf16), g_s[h, at, :]) + dot(ds, q_s[h, at, :])
                dqt_s[h, :, at] += dot(kt_s[h, :, kat], ds)

        count = rows // block
        done = 0
        for g in range(count // 2 + 1):
            length = count - g

            def one(p, _, length=length, g=g, done=done):
                wrap = p // length
                i = (length - 1) - wrap * (length - g)
                j = p - wrap * length
                body(i, j)
                b = p + done

                @pl.when(b % 2 == 1)
                def _():
                    turn((b + 1) // 2)

                return 0

            lax.fori_loop(0, count, one, 0)
            done += count

        def finish(i, _):
            at = pl.ds(pl.multiple_of(i * 256, 256), 256)
            parts_of = []
            for h in range(heads):
                parts_of += [dqt_s[h, :, at].T, acc_kv[h, at, :]]
            pq[at, :] = jnp.concatenate(parts_of, axis=1).astype(bf16)
            return 0

        lax.fori_loop(0, rows // 256, finish, 0)

    wide = 2 * HEAD_DIM
    pl.run_scoped(
        attention,
        pltpu.VMEM((heads, rows, wide), bf16),
        pltpu.VMEM((heads, rows, wide), bf16),
        pltpu.VMEM((heads, rows, wide), bf16),
        pltpu.VMEM((heads, wide, rows), bf16),
        pltpu.VMEM((heads, wide, rows), bf16),
        pltpu.VMEM((heads, HEAD_DIM, rows), bf16),
        pltpu.VMEM((heads, 1, rows), f32),
        pltpu.VMEM((heads, HEAD_DIM, rows), f32),
        pltpu.VMEM((heads, rows, wide), f32),
    )
    bodies = (rows // block) * (rows // block + 1) // 2
    next_turn = bodies // 2 + 1
    piece = own_rows // pieces
    parts = rows // own_rows
    qrows, qcols = w_ref.shape
    part = qrows // split
    r2, r4, r8 = part // 2, part // 4, part // 8

    def closing(h1_s, d1_s, d_to, gq, qacc, q_to_x, q_to_z, q_to_w, q_more_to):
        flight, sends = {}, []

        def go(key, src, dst, ssem, rsem, axis, bit):
            flight[key] = remote(src, dst, ssem, rsem, axis, bit)
            sends.append(flight[key])

        def owned(owner):
            return pl.ds(pl.multiple_of(owner * own_rows, own_rows), own_rows)

        fetch = [
            pltpu.make_async_copy(h1_ref.at[pl.ds(t * own_rows, own_rows), :], h1_s.at[t], load_sem.at[1 + t])
            for t in range(parts)
        ]
        for t in fetch:
            t.start()

        def span(c):
            return pl.ds(c * piece, piece)

        def product(slot, owner):
            d1_s[slot] = rounded(dot_nt(pq[owned(owner), :], w_ref[...]))

        def pair_rows(c):
            go(("d", c, 1), d1_s.at[0, span(c)], d_first.at[1, span(c)], d_send.at[c, 1], d_recv.at[c, 1], "tensor", 1)
            go(("d", c, 0), d1_s.at[1, span(c)], d_first.at[0, span(c)], d_send.at[c, 0], d_recv.at[c, 0], "tensor", 1)

        def across(c):
            flight["d", c, 1].wait_recv()
            d_to[span(c)] = rounded(d1_s[2, span(c), :].astype(f32) + d_first[1, span(c), :].astype(f32))
            go(("d", c, 2), d_to.at[span(c)], d_second.at[span(c)], d_send.at[c, 2], d_recv.at[c, 2], "tensor", 2)

        def settle_rows(c):
            flight["d", c, 0].wait_recv()
            flight["d", c, 2].wait_recv()
            near = d1_s[3, span(c), :].astype(f32) + d_first[0, span(c), :].astype(f32)
            in_sum[span(c)] = near + d_second[span(c)].astype(f32)

        def row(c, *bits):
            at, size = c * part, part
            for b in bits:
                size = size // 2
                at = at + b * size
            return pl.ds(pl.multiple_of(at, 16), size)

        def q_go(c, s, src, dst, axis, bit):
            go(("q", c, s), src, dst, q_send.at[c, s], q_recv.at[c, s], axis, bit)

        def q_x(c):
            q_to_x[c] = rounded(gq[row(c, 1 - b0), :])
            q_go(c, 0, q_to_x.at[c], q_from_x.at[c], "dp", 1)

        def q_z(c):
            flight["q", c, 0].wait_recv()
            qacc[c] = gq[row(c, b0), :] + q_from_x[c].astype(f32)
            q_to_z[c] = rounded(qacc[c, pl.ds(pl.multiple_of((1 - b1) * r4, 16), r4), :])
            q_go(c, 1, q_to_z.at[c], q_from_z.at[c], "dp", 2)

        def q_w(c):
            flight["q", c, 1].wait_recv()
            low = pl.ds(pl.multiple_of(b1 * r4, 16), r4)
            qacc[c, low, :] += q_from_z[c].astype(f32)
            q_to_w[c] = rounded(qacc[c, pl.ds(pl.multiple_of(b1 * r4 + (1 - b2) * r8, 16), r8), :])
            q_go(c, 2, q_to_w.at[c], q_from_w.at[c], "dp", 4)

        def q_settle(c):
            flight["q", c, 2].wait_recv()
            total = qacc[c, pl.ds(pl.multiple_of(b1 * r4 + b2 * r8, 16), r8), :] + q_from_w[c].astype(f32)
            for m, (axis, bit) in enumerate(far):
                q_more_to[c, m] = rounded(total)
                q_go(c, 6 + m, q_more_to.at[c, m], q_more_from.at[c, m], axis, bit)
                flight["q", c, 6 + m].wait_recv()
                total = rounded(total).astype(f32) + q_more_from[c, m].astype(f32)
            qkv_sum[row(c, b0, b1, b2), :] = rounded(total)
            spot = qkv_sum.at[row(c, b0, b1, b2), :]
            q_go(c, 3, spot, spot, "dp", 4)

        def q_share(c):
            flight["q", c, 3].wait_recv()
            spot = qkv_sum.at[row(c, b0, b1), :]
            q_go(c, 4, spot, spot, "dp", 2)

        def q_more(c):
            flight["q", c, 4].wait_recv()
            spot = qkv_sum.at[row(c, b0), :]
            q_go(c, 5, spot, spot, "dp", 1)

        def q_end(c):
            flight["q", c, 5].wait_recv()

        def gain_start(m):
            axis, bit = steps[m]
            go(("g", m), gain_at.at[0, m], gain_at.at[1, m], gain_send.at[m], gain_recv.at[m], axis, bit)

        def gain_step(m):
            flight["g", m].wait_recv()
            now = gain_at[0, m] + gain_at[1, m]
            if m + 1 < len(steps):
                gain_at[0, m + 1] = now
                gain_start(m + 1)
            else:
                gains_sum[...] = now

        last = n + len(stages) - 1
        turns = iter(range(next_turn, last))

        def main_turn():
            at = next(turns, None)
            if at is not None:
                turn(jnp.int32(at))

        main_turn()
        product(0, cross)
        product(1, core)
        for c in range(pieces):
            pair_rows(c)
        product(2, chip)
        product(3, me)
        main_turn()
        for t in fetch:
            t.wait()
        gq[...] = dot_tn(h1_s[0], pq[owned(0), :])
        for c in range(pieces):
            across(c)
        for t in range(1, parts):
            gq[...] += dot_tn(h1_s[t], pq[owned(t), :])
        for c in range(split):
            q_x(c)
        main_turn()
        gain_at[0, 0] = gains_ref[...]
        column = jnp.sum(w_ref[...].astype(f32) * gq[...], axis=1, keepdims=True)
        line = jnp.broadcast_to(column, (qrows, 128)).T
        gain_at[0, 0, 2 + parts : 3 + parts, :] = line[0:1, :] / in_gain_ref[...]
        gain_start(0)
        q_stages = (q_z, q_w, q_settle, q_share, q_more, q_end)
        settled = gained = 0
        for stage in q_stages:
            for c in range(split):
                stage(c)
            main_turn()
            if settled < pieces:
                settle_rows(settled)
                settled += 1
            if gained < len(steps):
                gain_step(gained)
                gained += 1
        while settled < pieces:
            settle_rows(settled)
            settled += 1
        while gained < len(steps):
            gain_step(gained)
            gained += 1
        for at in turns:
            turn(jnp.int32(at))
        for each in sends:
            each.wait_send()

    pl.run_scoped(
        closing,
        pltpu.VMEM((parts, own_rows, width), bf16),
        pltpu.VMEM((parts, own_rows, width), bf16),
        pltpu.VMEM((own_rows, width), bf16),
        pltpu.VMEM((qrows, qcols), f32),
        pltpu.VMEM((split, r2, qcols), f32),
        pltpu.VMEM((split, r2, qcols), bf16),
        pltpu.VMEM((split, r4, qcols), bf16),
        pltpu.VMEM((split, r8, qcols), bf16),
        pltpu.VMEM((split, max(len(far), 1), r8, qcols), bf16),
    )

    def sent(c, _):
        for s in range(9 + len(far)):
            if s in (2, 3):

                @pl.when(c >= n - 3)
                def _():
                    copy(c, s).wait_send()

            else:
                copy(c, s).wait_send()
        return 0

    lax.fori_loop(0, n, sent, 0)


def back_pass(groups, lengths, grad_att, packed, att, lse, grads, h1, weight, gains, in_gain,
              chunk=192, block=512, pieces=5, split=3):
    rows = packed.shape[0]
    parts, own_rows, head_width = grad_att.shape
    heads = head_width // HEAD_DIM
    width = grads.shape[2]
    n = grads.shape[1] // chunk
    steps = len(peers_of(4, groups))
    extra = max(steps - 5, 1)
    qrows, qcols = weight.shape
    part = qrows // split
    bf16 = lambda *shape: pltpu.VMEM(shape, jnp.bfloat16)
    f32 = lambda *shape: pltpu.VMEM(shape, jnp.float32)
    vmem, anywhere = pl.BlockSpec(memory_space=pltpu.VMEM), pl.BlockSpec(memory_space=pl.ANY)
    sems = pltpu.SemaphoreType.DMA
    return pl.pallas_call(
        partial(back_kernel, groups, chunk, block, pieces, split),
        out_shape=(
            jax.ShapeDtypeStruct((n, chunk, width), jnp.bfloat16),
            jax.ShapeDtypeStruct((own_rows, width), jnp.float32),
            jax.ShapeDtypeStruct((qrows, qcols), jnp.bfloat16),
            jax.ShapeDtypeStruct(gains.shape, jnp.float32),
        ),
        in_specs=[pl.BlockSpec(memory_space=pltpu.SMEM), anywhere, anywhere, vmem, vmem, anywhere,
                  anywhere, vmem, vmem, vmem],
        out_specs=[vmem] * 4,
        scratch_shapes=[
            bf16(rows, packed.shape[1]),
            bf16(parts, own_rows, head_width),
            bf16(3, 2, chunk, width),
            bf16(n, 2, chunk, width),
            bf16(n, chunk, width),
            f32(n, chunk, width // 2),
            bf16(3, chunk, width),
            bf16(3, chunk, width // 2),
            bf16(n, chunk, width // 2),
            bf16(n, chunk // 2, width // 2),
            bf16(n, chunk // 2, width // 2),
            bf16(n, chunk // 4, width // 2),
            bf16(n, chunk // 4, width // 2),
            bf16(n, extra, chunk // 4, width // 2),
            bf16(n, extra, chunk // 4, width // 2),
            sems((n, 9 + extra)),
            sems((n, 9 + extra)),
            sems((3, 2)),
            sems((3,)),
            sems((3,)),
            sems,
            bf16(2, own_rows, width),
            bf16(own_rows, width),
            sems((pieces, 3)),
            sems((pieces, 3)),
            bf16(split, part // 2, qcols),
            bf16(split, part // 4, qcols),
            bf16(split, part // 8, qcols),
            bf16(split, extra, part // 8, qcols),
            sems((split, 6 + extra)),
            sems((split, 6 + extra)),
            pltpu.VMEM((2, steps) + gains.shape, jnp.float32),
            sems((steps,)),
            sems((steps,)),
            sems((1 + parts,)),
        ],
        compiler_params=pltpu.CompilerParams(
            collective_id=0, has_side_effects=True, vmem_limit_bytes=60 << 20
        ),
        name="back_pass",
    )(lengths, grad_att, packed, att, lse, grads, h1, weight, gains, in_gain.reshape(1, -1))


def local(
    tokens,
    lengths,
    in_gain,
    qkv_weight,
    attn_gain,
    out_weight,
    ffn_gain,
    up_weight,
    hidden_gain,
    down_weight,
    out_grad,
):
    parts = lax.axis_size("tensor")
    own_rows, width = tokens.shape
    head_width, hidden = attn_gain.shape[0], hidden_gain.shape[0]

    def gather(values):
        return lax.all_gather(values, "tensor", axis=0)

    full_out, full_up, full_down = gather(out_weight), gather(up_weight), gather(down_weight)
    pad = -(head_width + hidden) % 1024
    own_gains = jnp.concatenate((attn_gain, hidden_gain, jnp.zeros((pad,), jnp.float32)))
    gathered_in, packed, gains = intake(tokens, in_gain, qkv_weight, own_gains.reshape(8, -1))
    gathered_in = gathered_in.reshape(parts * own_rows, width)
    packed = packed.reshape(parts * own_rows, -1)
    gains = gains.reshape(parts, -1)
    full_attn_gain = gains[:, :head_width].reshape(-1)
    full_hidden_gain = gains[:, head_width : head_width + hidden].reshape(-1)

    attended, log_total = attn_fwd(packed, lengths, 512, 512)
    own_att = exchange(attended.reshape(parts, own_rows, head_width), 2)
    result, grad_middle, grad_att, grads, gain_parts = rows_pass(
        own_att,
        tokens,
        out_grad,
        full_attn_gain,
        ffn_gain,
        full_hidden_gain,
        full_out.reshape(width, width),
        full_up,
        full_down,
        own_rows,
    )
    sums, grad_in_normed, qkv_sum, gains = back_pass(
        lax.axis_size("dp"),
        lengths,
        grad_att,
        packed,
        attended,
        log_total,
        grads,
        gathered_in,
        qkv_weight,
        gain_parts,
        in_gain,
    )

    residual = tokens.astype(jnp.float32)
    mean = jnp.mean(residual, axis=1, keepdims=True)
    square = jnp.mean(residual * residual, axis=1, keepdims=True)
    scale = lax.rsqrt(square - mean * mean + EPS)
    unit = (residual - mean) * scale
    weighted = grad_in_normed * in_gain
    first = jnp.mean(weighted, axis=1, keepdims=True)
    second = jnp.mean(weighted * unit, axis=1, keepdims=True)
    in_grad = grad_middle + scale * (weighted - first - unit * second)

    me = lax.axis_index("tensor")
    sums = sums.reshape(-1, width).astype(jnp.float32)
    return (
        result,
        in_grad,
        gains[2 + parts],
        qkv_sum.astype(jnp.float32),
        lax.dynamic_slice_in_dim(gains[1], me * head_width, head_width),
        sums[hidden + width : hidden + width + head_width],
        gains[0],
        sums[hidden : hidden + width],
        lax.dynamic_index_in_dim(gains, 2 + me, 0, keepdims=False),
        sums[:hidden],
    )


def solution(mesh):
    return jax.shard_map(
        local,
        mesh=mesh,
        in_specs=(
            P(("dp", "tensor"), None),
            P("dp", None),
            P(),
            P(None, "tensor"),
            P("tensor"),
            P("tensor", None),
            P(),
            P(None, "tensor"),
            P("tensor"),
            P("tensor", None),
            P(("dp", "tensor"), None),
        ),
        out_specs=(
            P(("dp", "tensor"), None),
            P(("dp", "tensor"), None),
            P(),
            P(None, "tensor"),
            P("tensor"),
            P("tensor", None),
            P(),
            P(None, "tensor"),
            P("tensor"),
            P("tensor", None),
        ),
        check_vma=False,
    )
```

```python
from functools import partial

import jax
import jax.numpy as jnp
from jax import lax
from jax.experimental import pallas as pl
from jax.experimental.pallas import tpu as pltpu
from jax.sharding import PartitionSpec as P

HEAD_DIM = 64
UNIT = 64
EPS = 1e-05


def contract_rows(left, right):
    return lax.dot_general(
        left, right, (((0,), (0,)), ((), ())), preferred_element_type=jnp.float32
    )


def contract_cols(left, right):
    return lax.dot_general(
        left, right, (((1,), (1,)), ((), ())), preferred_element_type=jnp.float32
    )


NEG = -1e30


def seq_bounds(len_ref):
    ends, total = [], 0
    for s in range(len_ref.shape[1]):
        total = total + len_ref[0, s] * UNIT
        ends.append(total)
    return ends


def start_of(ends, row):
    at = 0
    for end in ends:
        at = jnp.where(row >= end, end, at)
    return at


def end_of(ends, row):
    at = ends[-1]
    for end in reversed(ends):
        at = jnp.where(row < end, end, at)
    return at


def dot(a, b):
    return lax.dot_general(a, b, (((1,), (0,)), ((), ())), preferred_element_type=jnp.float32)


MESH = pl.DeviceIdType.MESH


def flip(index, bit):
    return index + bit - 2 * bit * ((index // bit) % 2)


def peers_of(parts, groups):
    steps, bit = [], 1
    while bit < parts:
        steps.append(("tensor", bit))
        bit *= 2
    bit = 1
    while bit < groups:
        steps.append(("dp", bit))
        bit *= 2
    return steps


def at_peer(axis, bit):
    return {axis: flip(lax.axis_index(axis), bit)}


def greet(steps, *more):
    barrier = pltpu.get_barrier_semaphore()
    for axis, bit in steps:
        pl.semaphore_signal(barrier, inc=1, device_id=at_peer(axis, bit), device_id_type=MESH)
    for peer in more:
        pl.semaphore_signal(barrier, inc=1, device_id={"tensor": peer}, device_id_type=MESH)
    pl.semaphore_wait(barrier, len(steps) + len(more))


def remote(src, dst, send, recv, axis, bit):
    copy = pltpu.make_async_remote_copy(
        src_ref=src,
        dst_ref=dst,
        send_sem=send,
        recv_sem=recv,
        device_id=at_peer(axis, bit),
        device_id_type=MESH,
    )
    copy.start()
    return copy


def rounded(values):
    return values.astype(jnp.bfloat16)


def spread(me):
    return flip(me, 1), flip(me, 2), flip(flip(me, 1), 2)


def dot_nt(a, b):
    return lax.dot_general(a, b, (((1,), (1,)), ((), ())), preferred_element_type=jnp.float32)


def dot_tn(a, b):
    return lax.dot_general(a, b, (((0,), (0,)), ((), ())), preferred_element_type=jnp.float32)


GELU_A = 0.7978845608028654
GELU_B = 0.044715


def rows_kernel(tile, att_ref, tok_ref, og_ref, again_ref, fgain_ref, hgain_ref, w_hbm,
                res_ref, gm_ref, datt_ref, g_hbm, gsum_ref,
                wout, wup, wdown, x_s, mid_s, low_att, low_mid, act_s, slope_s, wide_s, low_act, big_s, acc_s,
                mu_s, rs_s, mu4_s, rs4_s, one_s, two_s, stage, w_sem, g_sem):
    parts, rows, head_width = att_ref.shape
    width = tok_ref.shape[1]
    hidden = width * hgain_ref.shape[0]
    n_tiles = rows // tile
    f32 = jnp.float32

    loads = []
    for t in range(parts):
        loads.append(
            pltpu.make_async_copy(
                w_hbm.at[t, pl.ds(2 * width, head_width), :],
                wout.at[pl.ds(t * head_width, head_width), :],
                w_sem.at[2 * parts + t],
            )
        )
    for t in range(parts):
        loads.append(pltpu.make_async_copy(w_hbm.at[t, pl.ds(width, width), :], wup.at[t], w_sem.at[t]))
    for t in range(parts):
        loads.append(pltpu.make_async_copy(w_hbm.at[t, pl.ds(0, width), :], wdown.at[t], w_sem.at[parts + t]))
    for copy in loads:
        copy.start()

    def at(i):
        return pl.ds(pl.multiple_of(i * tile, tile), tile)

    def fold(v):
        return jnp.sum(v.reshape(tile // 8, 8, width), axis=0)

    def tiles(body, init=0):
        return lax.fori_loop(0, n_tiles, body, init)

    def stats(v, n):
        mu = jnp.sum(v, axis=1, keepdims=True) / n
        ms = jnp.sum(v * v, axis=1, keepdims=True) / n
        return mu, lax.rsqrt(ms - mu * mu + EPS)

    def save(slot, block, shard, row, n):
        copy = pltpu.make_async_copy(
            stage.at[slot, pl.ds(0, n), :], g_hbm.at[shard, pl.ds(row, n), :], g_sem.at[slot]
        )
        return copy

    again = again_ref[...]
    fgain = fgain_ref[...]

    def first(i, _):
        v = jnp.concatenate([att_ref[t, at(i), :] for t in range(parts)], axis=1).astype(f32)
        x_s[at(i), :] = v
        mu, rs = stats(v, width)
        mu_s[at(i), :] = mu
        rs_s[at(i), :] = rs
        low_att[at(i), :] = ((v - mu) * rs * again).astype(jnp.bfloat16)
        return 0

    tiles(first)
    for copy in loads[:parts]:
        copy.wait()
    big_s[...] = jnp.dot(low_att[...], wout[...], preferred_element_type=f32)

    def second(i, _):
        v = tok_ref[at(i), :].astype(f32) + big_s[at(i), :]
        mid_s[at(i), :] = v
        mu, rs = stats(v, width)
        low_mid[at(i), :] = ((v - mu) * rs * fgain).astype(jnp.bfloat16)
        one_s[at(i), :] = jnp.zeros((tile, 1), f32)
        two_s[at(i), :] = jnp.zeros((tile, 1), f32)
        acc_s[at(i), :] = v
        return 0

    tiles(second)

    for copy in loads[parts:]:
        copy.wait()

    def up_block(t, _):
        big_s[...] = jnp.dot(low_mid[...], wup[t], preferred_element_type=f32)

        def body(i, _):
            v = big_s[at(i), :]
            sq = v * v
            th = jnp.tanh(v * (GELU_A + (GELU_A * GELU_B) * sq))
            half = 0.5 * th + 0.5
            act = v * half
            act_s[t, at(i), :] = act
            slope = half + (0.5 * v) * (1.0 - th * th) * (GELU_A + (3.0 * GELU_A * GELU_B) * sq)
            slope_s[t, at(i), :] = slope.astype(jnp.bfloat16)
            one_s[at(i), :] += jnp.sum(act, axis=1, keepdims=True)
            two_s[at(i), :] += jnp.sum(act * act, axis=1, keepdims=True)
            return 0

        tiles(body)
        return 0

    lax.fori_loop(0, parts, up_block, 0)

    def third(i, _):
        mu = one_s[at(i), :] / hidden
        mu4_s[at(i), :] = mu
        rs4_s[at(i), :] = lax.rsqrt(two_s[at(i), :] / hidden - mu * mu + EPS)
        one_s[at(i), :] = jnp.zeros((tile, 1), f32)
        two_s[at(i), :] = jnp.zeros((tile, 1), f32)
        return 0

    tiles(third)

    def down_block(t, _):
        hg = hgain_ref[t]
        big_s[...] = dot_nt(og_ref[...], wdown[t])

        def body(i, part):
            unit = (act_s[t, at(i), :] - mu4_s[at(i), :]) * rs4_s[at(i), :]
            act_s[t, at(i), :] = unit
            low_act[at(i), :] = (unit * hg).astype(jnp.bfloat16)
            d4 = big_s[at(i), :]
            wide = d4 * hg
            wide_s[t, at(i), :] = wide
            one_s[at(i), :] += jnp.sum(wide, axis=1, keepdims=True)
            two_s[at(i), :] += jnp.sum(wide * unit, axis=1, keepdims=True)
            return part + fold(d4 * unit)

        part = tiles(body, jnp.zeros((8, width), f32))
        gsum_ref[pl.ds(2 + t, 1), :] = jnp.sum(part, axis=0, keepdims=True)
        acc_s[...] += jnp.dot(low_act[...], wdown[t], preferred_element_type=f32)
        slot = t % 2

        @pl.when(t >= 2)
        def _():
            save(slot, None, t, 0, width).wait()

        stage[slot] = dot_tn(low_act[...], og_ref[...]).astype(jnp.bfloat16)
        save(slot, None, t, 0, width).start()
        return 0

    lax.fori_loop(0, parts, down_block, 0)

    def fourth(i, _):
        res_ref[at(i), :] = acc_s[at(i), :].astype(jnp.bfloat16)
        one_s[at(i), :] = one_s[at(i), :] / hidden
        two_s[at(i), :] = two_s[at(i), :] / hidden
        acc_s[at(i), :] = jnp.zeros((tile, width), f32)
        return 0

    tiles(fourth)

    def back_block(t, _):
        def body(i, _):
            d_act = rs4_s[at(i), :] * (wide_s[t, at(i), :] - one_s[at(i), :] - act_s[t, at(i), :] * two_s[at(i), :])
            low_act[at(i), :] = (d_act * slope_s[t, at(i), :].astype(f32)).astype(jnp.bfloat16)
            return 0

        tiles(body)
        acc_s[...] += dot_nt(low_act[...], wup[t])
        slot = t % 2
        save(slot, None, t, 0, width).wait()
        stage[slot] = dot_tn(low_mid[...], low_act[...]).astype(jnp.bfloat16)
        save(slot, None, t, width, width).start()
        return 0

    lax.fori_loop(0, parts, back_block, 0)

    def fifth(i, part):
        v = mid_s[at(i), :]
        mu, rs = stats(v, width)
        unit = (v - mu) * rs
        d3 = acc_s[at(i), :]
        wide = d3 * fgain
        m1 = jnp.sum(wide, axis=1, keepdims=True) / width
        m2 = jnp.sum(wide * unit, axis=1, keepdims=True) / width
        d_mid = og_ref[at(i), :].astype(f32) + rs * (wide - m1 - unit * m2)
        gm_ref[at(i), :] = d_mid
        low_act[at(i), :] = d_mid.astype(jnp.bfloat16)
        return part + fold(d3 * unit)

    part = tiles(fifth, jnp.zeros((8, width), f32))
    gsum_ref[0:1, :] = jnp.sum(part, axis=0, keepdims=True)
    big_s[...] = dot_nt(low_act[...], wout[...])
    for slot in range(2):
        save(slot, None, slot, width, width).wait()
    stage[0] = dot_tn(low_att[...], low_act[...]).astype(jnp.bfloat16)
    last = []
    for t in range(parts):
        copy = pltpu.make_async_copy(
            stage.at[0, pl.ds(t * head_width, head_width), :],
            g_hbm.at[t, pl.ds(2 * width, head_width), :],
            w_sem.at[t],
        )
        copy.start()
        last.append(copy)

    def sixth(i, part):
        mu, rs = mu_s[at(i), :], rs_s[at(i), :]
        unit = (x_s[at(i), :] - mu) * rs
        d2 = big_s[at(i), :]
        wide = d2 * again
        m1 = jnp.sum(wide, axis=1, keepdims=True) / width
        m2 = jnp.sum(wide * unit, axis=1, keepdims=True) / width
        d_att = (rs * (wide - m1 - unit * m2)).astype(jnp.bfloat16)
        for t in range(parts):
            datt_ref[t, at(i), :] = d_att[:, t * head_width : (t + 1) * head_width]
        return part + fold(d2 * unit)

    part = tiles(sixth, jnp.zeros((8, width), f32))
    gsum_ref[1:2, :] = jnp.sum(part, axis=0, keepdims=True)
    gsum_ref[pl.ds(2 + parts, 8 - 2 - parts), :] = jnp.zeros((8 - 2 - parts, width), f32)
    for copy in last:
        copy.wait()


def rows_pass(att, tokens, out_grad, attn_gain, ffn_gain, hidden_gain, weights, tile):
    parts, rows, head_width = att.shape
    width = tokens.shape[1]
    bf16, f32 = jnp.bfloat16, jnp.float32
    vmem = pl.BlockSpec(memory_space=pltpu.VMEM)
    anywhere = pl.BlockSpec(memory_space=pl.ANY)
    column = pltpu.VMEM((rows, 1), f32)
    return pl.pallas_call(
        partial(rows_kernel, tile),
        out_shape=(
            jax.ShapeDtypeStruct((rows, width), bf16),
            jax.ShapeDtypeStruct((rows, width), f32),
            jax.ShapeDtypeStruct(att.shape, bf16),
            jax.ShapeDtypeStruct((parts, 2 * width + head_width, width), bf16),
            jax.ShapeDtypeStruct((8, width), f32),
        ),
        in_specs=[vmem] * 6 + [anywhere],
        out_specs=[vmem] * 3 + [anywhere, vmem],
        scratch_shapes=[
            pltpu.VMEM((width, width), bf16),
            pltpu.VMEM((parts, width, width), bf16),
            pltpu.VMEM((parts, width, width), bf16),
            pltpu.VMEM((rows, width), f32),
            pltpu.VMEM((rows, width), f32),
            pltpu.VMEM((rows, width), bf16),
            pltpu.VMEM((rows, width), bf16),
            pltpu.VMEM((parts, rows, width), f32),
            pltpu.VMEM((parts, rows, width), bf16),
            pltpu.VMEM((parts, rows, width), f32),
            pltpu.VMEM((rows, width), bf16),
            pltpu.VMEM((rows, width), f32),
            pltpu.VMEM((rows, width), f32),
        ] + [column] * 6 + [
            pltpu.VMEM((2, width, width), bf16),
            pltpu.SemaphoreType.DMA((3 * parts,)),
            pltpu.SemaphoreType.DMA((2,)),
        ],
        compiler_params=pltpu.CompilerParams(vmem_limit_bytes=60 << 20),
        cost_estimate=pl.CostEstimate(flops=20 * 10**9, bytes_accessed=40 << 20, transcendentals=2 * 10**6),
        name="rows_pass",
    )(att, tokens, out_grad, attn_gain.reshape(1, -1), ffn_gain.reshape(1, -1),
      hidden_gain.reshape(parts, 1, -1), weights)


def front_kernel(groups, pieces, chunk, len_ref, tok_ref, gain_ref, w_ref, own_gain_ref, down_ref, up_ref, out_ref,
                 all_ref, packed_ref, gains_ref, att_ref, own_ref, lse_ref, full_ref,
                 k_s, qt_s, vt_s, acc_s, m_s,
                 send, recv, gain_send, gain_recv, w_send, w_recv, w_local, a_send, a_recv, a_local):
    f32, bf16 = jnp.float32, jnp.bfloat16
    me, dp = lax.axis_index("tensor"), lax.axis_index("dp")
    core, chip, cross = spread(me)
    b0, b1, b2 = dp % 2, (dp // 2) % 2, (dp // 4) % 2
    rows, width = tok_ref.shape
    heads = k_s.shape[0]
    parts = all_ref.shape[0]
    piece = rows // pieces
    ends = seq_bounds(len_ref)
    half, rows2, rows4 = width // 2, chunk // 2, chunk // 4

    values = tok_ref[...].astype(f32)
    mu = jnp.sum(values, axis=1, keepdims=True) / width
    ms = jnp.sum(values * values, axis=1, keepdims=True) / width
    all_ref[me] = ((values - mu) * lax.rsqrt(ms - mu * mu + EPS) * gain_ref[...]).astype(bf16)
    gains_ref[me] = own_gain_ref[...]
    greet([("dp", 1), ("dp", 2), ("dp", 4)], core, chip, cross)

    def to_peer(src, dst, ssem, rsem, where):
        return pltpu.make_async_remote_copy(
            src_ref=src, dst_ref=dst, send_sem=ssem, recv_sem=rsem, device_id=where, device_id_type=MESH
        )

    def block(c, owner):
        return all_ref.at[owner, pl.ds(pl.multiple_of(c * piece, piece), piece), :]

    def to_chip(c):
        return to_peer(block(c, me), block(c, me), send.at[c], recv.at[c], {"tensor": chip})

    def to_far(c):
        return to_peer(block(c, chip), block(c, chip), send.at[pieces + c], recv.at[pieces + c], {"tensor": core})

    def to_core():
        return to_peer(all_ref.at[me], all_ref.at[me], send.at[2 * pieces], recv.at[2 * pieces], {"tensor": core})

    def gain_copy(k):
        owner, peer = ((me, chip), (me, core), (chip, core))[k]
        return to_peer(gains_ref.at[owner], gains_ref.at[owner], gain_send.at[k], gain_recv.at[k], {"tensor": peer})

    for c in range(pieces):
        to_chip(c).start()
    to_core().start()
    gain_copy(0).start()
    gain_copy(1).start()

    chunks = []
    for ref in (down_ref, up_ref, out_ref):
        for at in range(0, ref.shape[0], chunk):
            chunks.append((ref, at, len(chunks) * chunk))
    n = len(chunks)

    def spot(shard, c, row0, size, col0, span):
        row = chunks[c][2] + row0
        return full_ref.at[shard, pl.ds(pl.multiple_of(row, 16), size), pl.ds(pl.multiple_of(col0, 128), span)]

    def weight_copy(c, s):
        ref, at, _ = chunks[c]
        row4, row2, col = b1 * rows2 + b2 * rows4, b1 * rows2, b0 * half
        if s == 0:
            src = ref.at[pl.ds(pl.multiple_of(at + row4, 16), rows4), pl.ds(pl.multiple_of(col, 128), half)]
            dst, where = spot(me, c, row4, rows4, col, half), {"tensor": chip}
        elif s == 1:
            src = dst = spot(chip, c, row4, rows4, col, half)
            where = at_peer("dp", 4)
        elif s == 2:
            src = dst = spot(chip, c, row2, rows2, col, half)
            where = at_peer("dp", 2)
        elif s == 3:
            src = dst = spot(chip, c, 0, chunk, col, half)
            where = at_peer("dp", 1)
        elif s == 4:
            src = dst = spot(chip, c, 0, chunk, 0, width)
            where = {"tensor": core}
        else:
            src = ref.at[pl.ds(at, chunk), :]
            dst, where = spot(me, c, 0, chunk, 0, width), {"tensor": core}
        return to_peer(src, dst, w_send.at[c, s], w_recv.at[c, s], where)

    def own_weight(c):
        ref, at, _ = chunks[c]
        return pltpu.make_async_copy(ref.at[pl.ds(at, chunk), :], spot(me, c, 0, chunk, 0, width), w_local.at[c])

    order = list(reversed(range(n)))
    batches = [order[: n // 3], order[n // 3 : 2 * n // 3], order[2 * n // 3 :]]

    def weights(batch, s):
        for c in batches[batch]:
            if s:
                weight_copy(c, s - 1).wait_recv()
            if s < 5:
                weight_copy(c, s).start()

    scale = jnp.bfloat16(0.125)
    ones = (lax.broadcasted_iota(jnp.int32, (16, piece), 0) == 0).astype(f32).astype(bf16)

    def project(owner, c):
        span = pl.ds(pl.multiple_of(c * piece, piece), piece)
        at = pl.ds(pl.multiple_of(owner * rows + c * piece, piece), piece)
        x = jnp.dot(all_ref[owner, span, :], w_ref[...], preferred_element_type=f32).astype(bf16)
        packed_ref[owner, span, :] = x
        for h in range(heads):
            base = h * 3 * HEAD_DIM
            qt_s[h, :, at] = (x[:, base : base + HEAD_DIM] * scale).T
            k_s[h, at, :] = x[:, base + HEAD_DIM : base + 2 * HEAD_DIM]
            vt_s[h, :HEAD_DIM, at] = x[:, base + 2 * HEAD_DIM : base + 3 * HEAD_DIM].T
            vt_s[h, HEAD_DIM:, at] = ones

    def loop(body):
        def one(c, _):
            body(c)
            return 0

        lax.fori_loop(0, pieces, one, 0)

    weights(0, 0)
    loop(lambda c: project(me, c))
    to_core().wait_recv()
    weights(1, 0)
    loop(lambda c: project(core, c))
    weights(2, 0)
    for c in order:
        weight_copy(c, 5).start()
        own_weight(c).start()

    def from_chip(c):
        to_chip(c).wait_recv()
        to_far(c).start()
        project(chip, c)

    loop(from_chip)
    weights(0, 1)
    gain_copy(0).wait_recv()
    gain_copy(2).start()

    def from_far(c):
        to_far(c).wait_recv()
        project(cross, c)

    loop(from_far)
    weights(1, 1)
    weights(0, 2)
    weights(2, 1)

    def attend(o, later):
        first = o * rows
        at = pl.ds(first, rows)
        q_pos = first + lax.broadcasted_iota(jnp.int32, (1, rows), 1)
        q_start = start_of(ends, q_pos)
        for h in range(heads):
            acc_s[h] = jnp.zeros_like(acc_s[h])
            m_s[h] = jnp.full_like(m_s[h], NEG)

        def step(j, _):
            k0 = pl.multiple_of(j * rows, rows)
            kat = pl.ds(k0, rows)
            k_pos = k0 + lax.broadcasted_iota(jnp.int32, (rows, 1), 0)
            keep = (k_pos <= q_pos) & (k_pos >= q_start)
            for h in range(heads):
                s = jnp.where(keep, dot(k_s[h, kat, :], qt_s[h, :, at]), NEG)
                old = m_s[h]
                new = jnp.maximum(old, jnp.max(s, axis=0, keepdims=True))
                p = jnp.exp(s - new).astype(bf16)
                m_s[h] = new
                acc_s[h] = acc_s[h] * jnp.exp(old - new) + dot(vt_s[h, :, kat], p)
            return 0

        done = 0
        for stop, events in later:
            lax.fori_loop(done, stop, step, 0)
            for event in events:
                weights(*event)
            done = stop
        lax.fori_loop(done, o + 1, step, 0)
        outs = []
        for h in range(heads):
            acc = acc_s[h]
            total = acc[HEAD_DIM : HEAD_DIM + 1, :]
            outs.append((acc[:HEAD_DIM, :] / total).T)
            lse_ref[h : h + 1, at] = m_s[h] + jnp.log(total)
        att_ref[o] = jnp.concatenate(outs, axis=1).astype(bf16)

    def give(k):
        peer = (core, chip, cross)[k]
        return to_peer(att_ref.at[peer], own_ref.at[me], a_send.at[k], a_recv.at[k], {"tensor": peer})

    def keep_own():
        return pltpu.make_async_copy(att_ref.at[me], own_ref.at[me], a_local)

    plans = (
        [],
        [(1, [(0, 3), (1, 2)])],
        [(1, [(2, 2)]), (2, [(1, 3)])],
        [(1, [(0, 4)]), (2, [(2, 3)]), (3, [(1, 4)])],
    )
    for o in range(parts):
        attend(o, plans[o])

        for k, peer in enumerate((core, chip, cross)):

            @pl.when(peer == o)
            def _(k=k):
                give(k).start()

        @pl.when(me == o)
        def _():
            keep_own().start()

    weights(2, 4)
    gain_copy(1).wait_recv()
    gain_copy(2).wait_recv()
    for batch in range(3):
        weights(batch, 5)
    for c in order:
        weight_copy(c, 5).wait_recv()
        own_weight(c).wait()
    keep_own().wait()
    for k in range(3):
        give(k).wait()
    for c in range(pieces):
        to_chip(c).wait_send()
        to_far(c).wait_send()
    to_core().wait_send()
    for k in range(3):
        gain_copy(k).wait_send()
    for c in order:
        for s in range(6):
            weight_copy(c, s).wait_send()


def front_pass(groups, lengths, tokens, gain, weight, own_gains, w_down, w_up, w_out, pieces=5, chunk=192):
    rows, width = tokens.shape
    heads = weight.shape[1] // (3 * HEAD_DIM)
    parts = 4
    total = parts * rows
    n = (w_down.shape[0] + w_up.shape[0] + w_out.shape[0]) // chunk
    bf16, f32 = jnp.bfloat16, jnp.float32
    vmem, anywhere = pl.BlockSpec(memory_space=pltpu.VMEM), pl.BlockSpec(memory_space=pl.ANY)
    sems = pltpu.SemaphoreType.DMA
    shape = jax.ShapeDtypeStruct
    return pl.pallas_call(
        partial(front_kernel, groups, pieces, chunk),
        out_shape=(
            shape((parts, rows, width), bf16),
            shape((parts, rows, weight.shape[1]), bf16),
            shape((parts,) + own_gains.shape, f32),
            shape((parts, rows, heads * HEAD_DIM), bf16),
            shape((parts, rows, heads * HEAD_DIM), bf16),
            shape((8, total), f32),
            shape((parts, n * chunk, width), bf16),
        ),
        in_specs=[pl.BlockSpec(memory_space=pltpu.SMEM)] + [vmem] * 4 + [anywhere] * 3,
        out_specs=[vmem] * 6 + [anywhere],
        scratch_shapes=[
            pltpu.VMEM((heads, total, HEAD_DIM), bf16),
            pltpu.VMEM((heads, HEAD_DIM, total), bf16),
            pltpu.VMEM((heads, HEAD_DIM + 16, total), bf16),
            pltpu.VMEM((heads, HEAD_DIM + 16, rows), f32),
            pltpu.VMEM((heads, 1, rows), f32),
            sems((2 * pieces + 1,)),
            sems((2 * pieces + 1,)),
            sems((3,)),
            sems((3,)),
            sems((n, 6)),
            sems((n, 6)),
            sems((n,)),
            sems((3,)),
            sems((3,)),
            sems,
        ],
        compiler_params=pltpu.CompilerParams(
            collective_id=1, has_side_effects=True, vmem_limit_bytes=56 << 20
        ),
        name="front_pass",
    )(lengths, tokens, gain.reshape(1, -1), weight, own_gains, w_down, w_up, w_out)


def chunk_copy(c, s, src, dst, send, recv, axis, bit):
    return pltpu.make_async_remote_copy(
        src_ref=src,
        dst_ref=dst,
        send_sem=send.at[c, s],
        recv_sem=recv.at[c, s],
        device_id=at_peer(axis, bit),
        device_id_type=MESH,
    )


def back_kernel(groups, chunk, block, pieces, split, len_ref, datt_ref, packed_ref, att_ref, lse_ref, grads_ref,
                h1_ref, w_ref, gains_ref, in_gain_ref,
                sum_ref, in_sum, qkv_sum, gains_sum,
                pq, do_s, own, first, second, acc, to_y, to_x, from_x, to_z, from_z, to_w, from_w, more_to, more_from,
                send, recv, local_sem, a2a_send, a2a_recv, a2a_local,
                d_first, d_second, d_send, d_recv, q_from_x, q_from_z, q_from_w, q_more_from, q_send, q_recv,
                gain_at, gain_send, gain_recv, load_sem):
    f32, bf16 = jnp.float32, jnp.bfloat16
    steps = peers_of(4, groups)
    far = steps[5:]
    me, dp = lax.axis_index("tensor"), lax.axis_index("dp")
    core, chip, cross = spread(me)
    cols = grads_ref.shape[2]
    half, rows2, rows4 = cols // 2, chunk // 2, chunk // 4
    b0, b1, b2 = dp % 2, (dp // 2) % 2, (dp // 4) % 2
    n = grads_ref.shape[1] // chunk

    def take(c, shard):
        return grads_ref.at[shard, pl.ds(pl.multiple_of(c * chunk, 16), chunk), :]

    def col(b):
        return pl.ds(pl.multiple_of(b * half, 128), half)

    def row2(b):
        return pl.ds(pl.multiple_of(b * rows2, 16), rows2)

    def row4(b, bb):
        return pl.ds(pl.multiple_of(b * rows2 + bb * rows4, 16), rows4)

    def copy(c, s):
        if s == 0:
            return chunk_copy(c, 0, take(c, core), first.at[c, 0], send, recv, "tensor", 1)
        if s == 1:
            return chunk_copy(c, 1, take(c, cross), first.at[c, 1], send, recv, "tensor", 1)
        if s == 2:
            return chunk_copy(c, 2, to_y.at[c % 3], second.at[c], send, recv, "tensor", 2)
        if s == 3:
            return chunk_copy(c, 3, to_x.at[c % 3], from_x.at[c], send, recv, "dp", 1)
        if s == 4:
            return chunk_copy(c, 4, to_z.at[c], from_z.at[c], send, recv, "dp", 2)
        if s == 5:
            return chunk_copy(c, 5, to_w.at[c], from_w.at[c], send, recv, "dp", 4)
        if s == 6:
            piece = sum_ref.at[c, row4(b1, b2), col(b0)]
            return chunk_copy(c, 6, piece, piece, send, recv, "dp", 4)
        if s == 7:
            piece = sum_ref.at[c, row2(b1), col(b0)]
            return chunk_copy(c, 7, piece, piece, send, recv, "dp", 2)
        if s == 8:
            piece = sum_ref.at[c, :, col(b0)]
            return chunk_copy(c, 8, piece, piece, send, recv, "dp", 1)
        axis, bit = far[s - 9]
        return chunk_copy(c, s, more_to.at[c, s - 9], more_from.at[c, s - 9], send, recv, axis, bit)

    def arrived(c, s, piece=None):
        if piece is None:
            copy(c, s).wait_recv()
        else:
            axis, bit = {6: ("dp", 4), 7: ("dp", 2), 8: ("dp", 1)}[s]
            chunk_copy(c, s, piece, piece, send, recv, axis, bit).wait_recv()

    def mine(c, k):
        shard = (me, chip)[k]
        return pltpu.make_async_copy(take(c, shard), own.at[c % 3, k], local_sem.at[c % 3, k])

    def pair(c):
        copy(c, 1).start()
        copy(c, 0).start()
        mine(c, 1).start()
        mine(c, 0).start()

    def to_chip(c):
        @pl.when(c >= 3)
        def _():
            copy(c - 3, 2).wait_send()

        mine(c, 1).wait()
        arrived(c, 1)
        to_y[c % 3] = rounded(own[c % 3, 1].astype(f32) + first[c, 1].astype(f32))
        copy(c, 2).start()

    def x_half(c):
        @pl.when(c >= 3)
        def _():
            copy(c - 3, 3).wait_send()

        mine(c, 0).wait()
        arrived(c, 0)
        arrived(c, 2)

        def total(b):
            whole = own[c % 3, 0, :, col(b)].astype(f32) + first[c, 0, :, col(b)].astype(f32)
            return whole + second[c, :, col(b)].astype(f32)

        to_x[c % 3] = rounded(total(1 - b0))
        copy(c, 3).start()
        acc[c] = total(b0)

    def z_half(c):
        arrived(c, 3)
        acc[c] += from_x[c].astype(f32)
        to_z[c] = rounded(acc[c, row2(1 - b1), :])
        copy(c, 4).start()

    def z_quarter(c):
        arrived(c, 4)
        acc[c, row2(b1), :] += from_z[c].astype(f32)
        to_w[c] = rounded(acc[c, row4(b1, 1 - b2), :])
        copy(c, 5).start()

    def settle(c):
        arrived(c, 5)
        total = acc[c, row4(b1, b2), :] + from_w[c].astype(f32)
        for m in range(len(far)):
            more_to[c, m] = rounded(total)
            copy(c, 9 + m).start()
            arrived(c, 9 + m)
            total = rounded(total).astype(f32) + more_from[c, m].astype(f32)
        sum_ref[c, row4(b1, b2), col(b0)] = rounded(total)
        copy(c, 6).start()

    def z_share(c):
        arrived(c, 6, sum_ref.at[c, row4(b1, 1 - b2), col(b0)])
        copy(c, 7).start()

    def x_share(c):
        arrived(c, 7, sum_ref.at[c, row2(1 - b1), col(b0)])
        copy(c, 8).start()

    def end(c):
        arrived(c, 8, sum_ref.at[c, :, col(1 - b0)])

    stages = (pair, to_chip, x_half, z_half, z_quarter, settle, z_share, x_share, end)

    def turn(at):
        for s in range(len(stages)):
            c = at - s

            @pl.when((c >= 0) & (c < n))
            def _():
                stages[s](c)

    rows = packed_ref.shape[0]
    heads = packed_ref.shape[1] // (3 * HEAD_DIM)
    own_rows = datt_ref.shape[1]
    width = h1_ref.shape[1]
    ends = seq_bounds(len_ref)
    scale = jnp.bfloat16(0.125)
    load = pltpu.make_async_copy(packed_ref, pq, load_sem.at[0])
    load.start()
    greet(steps, cross)

    def a2a(k, peer):
        return pltpu.make_async_remote_copy(
            src_ref=datt_ref.at[peer],
            dst_ref=do_s.at[me],
            send_sem=a2a_send.at[k],
            recv_sem=a2a_recv.at[k],
            device_id={"tensor": peer},
            device_id_type=MESH,
        )

    moves = [a2a(k, peer) for k, peer in reversed(list(enumerate((core, chip, cross))))]
    for move in moves:
        move.start()
    keep_own = pltpu.make_async_copy(datt_ref.at[me], do_s.at[me], a2a_local)
    keep_own.start()
    turn(jnp.int32(0))
    load.wait()

    def attention(kv_s, q_s, g_s, qt_s, gt_s, kt_s, d_s, dqt_s, acc_kv):
        def stage_qkv(i, _):
            at = pl.ds(pl.multiple_of(i * 256, 256), 256)
            x = pq[at, :]
            blank = jnp.zeros((256, HEAD_DIM), bf16)
            blank_t = jnp.zeros((HEAD_DIM, 256), bf16)
            for h in range(heads):
                base = h * 3 * HEAD_DIM
                q = x[:, base : base + HEAD_DIM] * scale
                k = x[:, base + HEAD_DIM : base + 2 * HEAD_DIM]
                v = x[:, base + 2 * HEAD_DIM : base + 3 * HEAD_DIM]
                kv_s[h, at, :] = jnp.concatenate([k, v], axis=1)
                q_s[h, at, :] = jnp.concatenate([q, blank], axis=1)
                qt_s[h, :HEAD_DIM, at] = q.T
                qt_s[h, HEAD_DIM:, at] = blank_t
                kt_s[h, :, at] = (k * scale).T
                dqt_s[h, :, at] = jnp.zeros((HEAD_DIM, 256), f32)
                acc_kv[h, at, :] = jnp.zeros((256, 2 * HEAD_DIM), f32)
            return 0

        lax.fori_loop(0, rows // 256, stage_qkv, 0)
        keep_own.wait()
        for move in moves:
            move.wait()
        piece = own_rows // 5

        def stage_grad(i, _):
            owner, part = i // 5, i % 5
            inner = pl.ds(pl.multiple_of(part * piece, piece), piece)
            at = pl.ds(pl.multiple_of(owner * own_rows + part * piece, piece), piece)
            g = do_s[owner, inner, :]
            prod = g.astype(f32) * att_ref[at, :].astype(f32)
            blank = jnp.zeros((piece, HEAD_DIM), bf16)
            blank_t = jnp.zeros((HEAD_DIM, piece), bf16)
            for h in range(heads):
                d = g[:, h * HEAD_DIM : (h + 1) * HEAD_DIM]
                g_s[h, at, :] = jnp.concatenate([blank, d], axis=1)
                gt_s[h, HEAD_DIM:, at] = d.T
                gt_s[h, :HEAD_DIM, at] = blank_t
                d_s[h, :, at] = jnp.sum(prod[:, h * HEAD_DIM : (h + 1) * HEAD_DIM].T, axis=0, keepdims=True)
            return 0

        lax.fori_loop(0, rows // piece, stage_grad, 0)

        def body(i, j):
            q0 = pl.multiple_of(i * block, block)
            k0 = pl.multiple_of(j * block, block)
            at, kat = pl.ds(q0, block), pl.ds(k0, block)
            q_pos = q0 + lax.broadcasted_iota(jnp.int32, (1, block), 1)
            q_start = start_of(ends, q_pos)
            k_pos = k0 + lax.broadcasted_iota(jnp.int32, (block, 1), 0)
            keep = (k_pos <= q_pos) & (k_pos >= q_start)
            for h in range(heads):
                kv = kv_s[h, kat, :]
                s = dot(kv, qt_s[h, :, at]) - lse_ref[h : h + 1, at]
                p = jnp.exp(jnp.where(keep, s, NEG))
                dp_t = dot(kv, gt_s[h, :, at])
                ds = (p * (dp_t - d_s[h, :, at])).astype(bf16)
                acc_kv[h, kat, :] += dot(p.astype(bf16), g_s[h, at, :]) + dot(ds, q_s[h, at, :])
                dqt_s[h, :, at] += dot(kt_s[h, :, kat], ds)

        count = rows // block
        done = 0
        for g in range(count // 2 + 1):
            length = count - g

            def one(p, _, length=length, g=g, done=done):
                wrap = p // length
                i = (length - 1) - wrap * (length - g)
                j = p - wrap * length
                body(i, j)
                b = p + done

                @pl.when(b % 2 == 1)
                def _():
                    turn((b + 1) // 2)

                return 0

            lax.fori_loop(0, count, one, 0)
            done += count

        def finish(i, _):
            at = pl.ds(pl.multiple_of(i * 256, 256), 256)
            parts_of = []
            for h in range(heads):
                parts_of += [dqt_s[h, :, at].T, acc_kv[h, at, :]]
            pq[at, :] = jnp.concatenate(parts_of, axis=1).astype(bf16)
            return 0

        lax.fori_loop(0, rows // 256, finish, 0)

    wide = 2 * HEAD_DIM
    pl.run_scoped(
        attention,
        pltpu.VMEM((heads, rows, wide), bf16),
        pltpu.VMEM((heads, rows, wide), bf16),
        pltpu.VMEM((heads, rows, wide), bf16),
        pltpu.VMEM((heads, wide, rows), bf16),
        pltpu.VMEM((heads, wide, rows), bf16),
        pltpu.VMEM((heads, HEAD_DIM, rows), bf16),
        pltpu.VMEM((heads, 1, rows), f32),
        pltpu.VMEM((heads, HEAD_DIM, rows), f32),
        pltpu.VMEM((heads, rows, wide), f32),
    )
    bodies = (rows // block) * (rows // block + 1) // 2
    next_turn = bodies // 2 + 1
    piece = own_rows // pieces
    parts = rows // own_rows
    qrows, qcols = w_ref.shape
    part = qrows // split
    r2, r4, r8 = part // 2, part // 4, part // 8

    def closing(h1_s, d1_s, d_to, gq, qacc, q_to_x, q_to_z, q_to_w, q_more_to):
        flight, sends = {}, []

        def go(key, src, dst, ssem, rsem, axis, bit):
            flight[key] = remote(src, dst, ssem, rsem, axis, bit)
            sends.append(flight[key])

        def owned(owner):
            return pl.ds(pl.multiple_of(owner * own_rows, own_rows), own_rows)

        fetch = [
            pltpu.make_async_copy(h1_ref.at[pl.ds(t * own_rows, own_rows), :], h1_s.at[t], load_sem.at[1 + t])
            for t in range(parts)
        ]
        for t in fetch:
            t.start()

        def span(c):
            return pl.ds(c * piece, piece)

        def product(slot, owner):
            d1_s[slot] = rounded(dot_nt(pq[owned(owner), :], w_ref[...]))

        def pair_rows(c):
            go(("d", c, 1), d1_s.at[0, span(c)], d_first.at[1, span(c)], d_send.at[c, 1], d_recv.at[c, 1], "tensor", 1)
            go(("d", c, 0), d1_s.at[1, span(c)], d_first.at[0, span(c)], d_send.at[c, 0], d_recv.at[c, 0], "tensor", 1)

        def across(c):
            flight["d", c, 1].wait_recv()
            d_to[span(c)] = rounded(d1_s[2, span(c), :].astype(f32) + d_first[1, span(c), :].astype(f32))
            go(("d", c, 2), d_to.at[span(c)], d_second.at[span(c)], d_send.at[c, 2], d_recv.at[c, 2], "tensor", 2)

        def settle_rows(c):
            flight["d", c, 0].wait_recv()
            flight["d", c, 2].wait_recv()
            near = d1_s[3, span(c), :].astype(f32) + d_first[0, span(c), :].astype(f32)
            in_sum[span(c)] = near + d_second[span(c)].astype(f32)

        def row(c, *bits):
            at, size = c * part, part
            for b in bits:
                size = size // 2
                at = at + b * size
            return pl.ds(pl.multiple_of(at, 16), size)

        def q_go(c, s, src, dst, axis, bit):
            go(("q", c, s), src, dst, q_send.at[c, s], q_recv.at[c, s], axis, bit)

        def q_x(c):
            q_to_x[c] = rounded(gq[row(c, 1 - b0), :])
            q_go(c, 0, q_to_x.at[c], q_from_x.at[c], "dp", 1)

        def q_z(c):
            flight["q", c, 0].wait_recv()
            qacc[c] = gq[row(c, b0), :] + q_from_x[c].astype(f32)
            q_to_z[c] = rounded(qacc[c, pl.ds(pl.multiple_of((1 - b1) * r4, 16), r4), :])
            q_go(c, 1, q_to_z.at[c], q_from_z.at[c], "dp", 2)

        def q_w(c):
            flight["q", c, 1].wait_recv()
            low = pl.ds(pl.multiple_of(b1 * r4, 16), r4)
            qacc[c, low, :] += q_from_z[c].astype(f32)
            q_to_w[c] = rounded(qacc[c, pl.ds(pl.multiple_of(b1 * r4 + (1 - b2) * r8, 16), r8), :])
            q_go(c, 2, q_to_w.at[c], q_from_w.at[c], "dp", 4)

        def q_settle(c):
            flight["q", c, 2].wait_recv()
            total = qacc[c, pl.ds(pl.multiple_of(b1 * r4 + b2 * r8, 16), r8), :] + q_from_w[c].astype(f32)
            for m, (axis, bit) in enumerate(far):
                q_more_to[c, m] = rounded(total)
                q_go(c, 6 + m, q_more_to.at[c, m], q_more_from.at[c, m], axis, bit)
                flight["q", c, 6 + m].wait_recv()
                total = rounded(total).astype(f32) + q_more_from[c, m].astype(f32)
            qkv_sum[row(c, b0, b1, b2), :] = rounded(total)
            spot = qkv_sum.at[row(c, b0, b1, b2), :]
            q_go(c, 3, spot, spot, "dp", 4)

        def q_share(c):
            flight["q", c, 3].wait_recv()
            spot = qkv_sum.at[row(c, b0, b1), :]
            q_go(c, 4, spot, spot, "dp", 2)

        def q_more(c):
            flight["q", c, 4].wait_recv()
            spot = qkv_sum.at[row(c, b0), :]
            q_go(c, 5, spot, spot, "dp", 1)

        def q_end(c):
            flight["q", c, 5].wait_recv()

        def gain_start(m):
            axis, bit = steps[m]
            go(("g", m), gain_at.at[0, m], gain_at.at[1, m], gain_send.at[m], gain_recv.at[m], axis, bit)

        def gain_step(m):
            flight["g", m].wait_recv()
            now = gain_at[0, m] + gain_at[1, m]
            if m + 1 < len(steps):
                gain_at[0, m + 1] = now
                gain_start(m + 1)
            else:
                gains_sum[...] = now

        last = n + len(stages) - 1
        turns = iter(range(next_turn, last))

        def main_turn():
            at = next(turns, None)
            if at is not None:
                turn(jnp.int32(at))

        main_turn()
        product(0, cross)
        product(1, core)
        for c in range(pieces):
            pair_rows(c)
        product(2, chip)
        product(3, me)
        main_turn()
        for t in fetch:
            t.wait()
        gq[...] = dot_tn(h1_s[0], pq[owned(0), :])
        for c in range(pieces):
            across(c)
        for t in range(1, parts):
            gq[...] += dot_tn(h1_s[t], pq[owned(t), :])
        for c in range(split):
            q_x(c)
        main_turn()
        gain_at[0, 0] = gains_ref[...]
        column = jnp.sum(w_ref[...].astype(f32) * gq[...], axis=1, keepdims=True)
        line = jnp.broadcast_to(column, (qrows, 128)).T
        gain_at[0, 0, 2 + parts : 3 + parts, :] = line[0:1, :] / in_gain_ref[...]
        gain_start(0)
        q_stages = (q_z, q_w, q_settle, q_share, q_more, q_end)
        settled = gained = 0
        for stage in q_stages:
            for c in range(split):
                stage(c)
            main_turn()
            if settled < pieces:
                settle_rows(settled)
                settled += 1
            if gained < len(steps):
                gain_step(gained)
                gained += 1
        while settled < pieces:
            settle_rows(settled)
            settled += 1
        while gained < len(steps):
            gain_step(gained)
            gained += 1
        for at in turns:
            turn(jnp.int32(at))
        for each in sends:
            each.wait_send()

    pl.run_scoped(
        closing,
        pltpu.VMEM((parts, own_rows, width), bf16),
        pltpu.VMEM((parts, own_rows, width), bf16),
        pltpu.VMEM((own_rows, width), bf16),
        pltpu.VMEM((qrows, qcols), f32),
        pltpu.VMEM((split, r2, qcols), f32),
        pltpu.VMEM((split, r2, qcols), bf16),
        pltpu.VMEM((split, r4, qcols), bf16),
        pltpu.VMEM((split, r8, qcols), bf16),
        pltpu.VMEM((split, max(len(far), 1), r8, qcols), bf16),
    )

    def sent(c, _):
        for s in range(9 + len(far)):
            if s in (2, 3):

                @pl.when(c >= n - 3)
                def _():
                    copy(c, s).wait_send()

            else:
                copy(c, s).wait_send()
        return 0

    lax.fori_loop(0, n, sent, 0)


def back_pass(groups, lengths, grad_att, packed, att, lse, grads, h1, weight, gains, in_gain,
              chunk=192, block=512, pieces=5, split=3):
    rows = packed.shape[0]
    parts, own_rows, head_width = grad_att.shape
    heads = head_width // HEAD_DIM
    width = grads.shape[2]
    n = grads.shape[1] // chunk
    steps = len(peers_of(4, groups))
    extra = max(steps - 5, 1)
    qrows, qcols = weight.shape
    part = qrows // split
    bf16 = lambda *shape: pltpu.VMEM(shape, jnp.bfloat16)
    f32 = lambda *shape: pltpu.VMEM(shape, jnp.float32)
    vmem, anywhere = pl.BlockSpec(memory_space=pltpu.VMEM), pl.BlockSpec(memory_space=pl.ANY)
    sems = pltpu.SemaphoreType.DMA
    return pl.pallas_call(
        partial(back_kernel, groups, chunk, block, pieces, split),
        out_shape=(
            jax.ShapeDtypeStruct((n, chunk, width), jnp.bfloat16),
            jax.ShapeDtypeStruct((own_rows, width), jnp.float32),
            jax.ShapeDtypeStruct((qrows, qcols), jnp.bfloat16),
            jax.ShapeDtypeStruct(gains.shape, jnp.float32),
        ),
        in_specs=[pl.BlockSpec(memory_space=pltpu.SMEM), anywhere, anywhere, vmem, vmem, anywhere,
                  anywhere, vmem, vmem, vmem],
        out_specs=[vmem] * 4,
        scratch_shapes=[
            bf16(rows, packed.shape[1]),
            bf16(parts, own_rows, head_width),
            bf16(3, 2, chunk, width),
            bf16(n, 2, chunk, width),
            bf16(n, chunk, width),
            f32(n, chunk, width // 2),
            bf16(3, chunk, width),
            bf16(3, chunk, width // 2),
            bf16(n, chunk, width // 2),
            bf16(n, chunk // 2, width // 2),
            bf16(n, chunk // 2, width // 2),
            bf16(n, chunk // 4, width // 2),
            bf16(n, chunk // 4, width // 2),
            bf16(n, extra, chunk // 4, width // 2),
            bf16(n, extra, chunk // 4, width // 2),
            sems((n, 9 + extra)),
            sems((n, 9 + extra)),
            sems((3, 2)),
            sems((3,)),
            sems((3,)),
            sems,
            bf16(2, own_rows, width),
            bf16(own_rows, width),
            sems((pieces, 3)),
            sems((pieces, 3)),
            bf16(split, part // 2, qcols),
            bf16(split, part // 4, qcols),
            bf16(split, part // 8, qcols),
            bf16(split, extra, part // 8, qcols),
            sems((split, 6 + extra)),
            sems((split, 6 + extra)),
            pltpu.VMEM((2, steps) + gains.shape, jnp.float32),
            sems((steps,)),
            sems((steps,)),
            sems((1 + parts,)),
        ],
        compiler_params=pltpu.CompilerParams(
            collective_id=0, has_side_effects=True, vmem_limit_bytes=60 << 20
        ),
        name="back_pass",
    )(lengths, grad_att, packed, att, lse, grads, h1, weight, gains, in_gain.reshape(1, -1))


def local(
    tokens,
    lengths,
    in_gain,
    qkv_weight,
    attn_gain,
    out_weight,
    ffn_gain,
    up_weight,
    hidden_gain,
    down_weight,
    out_grad,
):
    parts = lax.axis_size("tensor")
    own_rows, width = tokens.shape
    head_width, hidden = attn_gain.shape[0], hidden_gain.shape[0]

    pad = -(head_width + hidden) % 1024
    own_gains = jnp.concatenate((attn_gain, hidden_gain, jnp.zeros((pad,), jnp.float32)))
    groups = lax.axis_size("dp")
    gathered_in, packed, gains, attended, own_att, log_total, weights = front_pass(
        groups,
        lengths,
        tokens,
        in_gain,
        qkv_weight,
        own_gains.reshape(8, -1),
        down_weight,
        up_weight,
        out_weight,
    )
    gathered_in = gathered_in.reshape(parts * own_rows, width)
    packed = packed.reshape(parts * own_rows, -1)
    attended = attended.reshape(parts * own_rows, head_width)
    gains = gains.reshape(parts, -1)
    full_attn_gain = gains[:, :head_width].reshape(-1)
    full_hidden_gain = gains[:, head_width : head_width + hidden].reshape(-1)

    result, grad_middle, grad_att, grads, gain_parts = rows_pass(
        own_att,
        tokens,
        out_grad,
        full_attn_gain,
        ffn_gain,
        full_hidden_gain,
        weights,
        own_rows,
    )
    sums, grad_in_normed, qkv_sum, gains = back_pass(
        groups,
        lengths,
        grad_att,
        packed,
        attended,
        log_total,
        grads,
        gathered_in,
        qkv_weight,
        gain_parts,
        in_gain,
    )

    residual = tokens.astype(jnp.float32)
    mean = jnp.mean(residual, axis=1, keepdims=True)
    square = jnp.mean(residual * residual, axis=1, keepdims=True)
    scale = lax.rsqrt(square - mean * mean + EPS)
    unit = (residual - mean) * scale
    weighted = grad_in_normed * in_gain
    first = jnp.mean(weighted, axis=1, keepdims=True)
    second = jnp.mean(weighted * unit, axis=1, keepdims=True)
    in_grad = grad_middle + scale * (weighted - first - unit * second)

    me = lax.axis_index("tensor")
    sums = sums.reshape(-1, width).astype(jnp.float32)
    return (
        result,
        in_grad,
        gains[2 + parts],
        qkv_sum.astype(jnp.float32),
        lax.dynamic_slice_in_dim(gains[1], me * head_width, head_width),
        sums[hidden + width : hidden + width + head_width],
        gains[0],
        sums[hidden : hidden + width],
        lax.dynamic_index_in_dim(gains, 2 + me, 0, keepdims=False),
        sums[:hidden],
    )


def solution(mesh):
    return jax.shard_map(
        local,
        mesh=mesh,
        in_specs=(
            P(("dp", "tensor"), None),
            P("dp", None),
            P(),
            P(None, "tensor"),
            P("tensor"),
            P("tensor", None),
            P(),
            P(None, "tensor"),
            P("tensor"),
            P("tensor", None),
            P(("dp", "tensor"), None),
        ),
        out_specs=(
            P(("dp", "tensor"), None),
            P(("dp", "tensor"), None),
            P(),
            P(None, "tensor"),
            P("tensor"),
            P("tensor", None),
            P(),
            P(None, "tensor"),
            P("tensor"),
            P("tensor", None),
        ),
        check_vma=False,
    )
```

```python
from functools import partial

import jax
import jax.numpy as jnp
from jax import lax
from jax.experimental import pallas as pl
from jax.experimental.pallas import tpu as pltpu
from jax.sharding import PartitionSpec as P

HEAD_DIM = 64
UNIT = 64
EPS = 1e-05


def contract_rows(left, right):
    return lax.dot_general(
        left, right, (((0,), (0,)), ((), ())), preferred_element_type=jnp.float32
    )


def contract_cols(left, right):
    return lax.dot_general(
        left, right, (((1,), (1,)), ((), ())), preferred_element_type=jnp.float32
    )


NEG = -1e30


def seq_bounds(len_ref):
    ends, total = [], 0
    for s in range(len_ref.shape[1]):
        total = total + len_ref[0, s] * UNIT
        ends.append(total)
    return ends


def start_of(ends, row):
    at = 0
    for end in ends:
        at = jnp.where(row >= end, end, at)
    return at


def end_of(ends, row):
    at = ends[-1]
    for end in reversed(ends):
        at = jnp.where(row < end, end, at)
    return at


def dot(a, b):
    return lax.dot_general(a, b, (((1,), (0,)), ((), ())), preferred_element_type=jnp.float32)


MESH = pl.DeviceIdType.MESH


def flip(index, bit):
    return index + bit - 2 * bit * ((index // bit) % 2)


def peers_of(parts, groups):
    steps, bit = [], 1
    while bit < parts:
        steps.append(("tensor", bit))
        bit *= 2
    bit = 1
    while bit < groups:
        steps.append(("dp", bit))
        bit *= 2
    return steps


def at_peer(axis, bit):
    at, low = lax.axis_index(axis), 1
    while low <= bit:
        if bit & low:
            at = flip(at, low)
        low *= 2
    return {axis: at}


def greet(steps, *more):
    barrier = pltpu.get_barrier_semaphore()
    for axis, bit in steps:
        pl.semaphore_signal(barrier, inc=1, device_id=at_peer(axis, bit), device_id_type=MESH)
    for peer in more:
        pl.semaphore_signal(barrier, inc=1, device_id={"tensor": peer}, device_id_type=MESH)
    pl.semaphore_wait(barrier, len(steps) + len(more))


def remote(src, dst, send, recv, axis, bit):
    copy = pltpu.make_async_remote_copy(
        src_ref=src,
        dst_ref=dst,
        send_sem=send,
        recv_sem=recv,
        device_id=at_peer(axis, bit),
        device_id_type=MESH,
    )
    copy.start()
    return copy


def rounded(values):
    return values.astype(jnp.bfloat16)


def spread(me):
    return flip(me, 1), flip(me, 2), flip(flip(me, 1), 2)


def dot_nt(a, b):
    return lax.dot_general(a, b, (((1,), (1,)), ((), ())), preferred_element_type=jnp.float32)


def dot_tn(a, b):
    return lax.dot_general(a, b, (((0,), (0,)), ((), ())), preferred_element_type=jnp.float32)


GELU_A = 0.7978845608028654
GELU_B = 0.044715


def rows_kernel(tile, att_ref, tok_ref, og_ref, gain_ref, w_hbm,
                res_ref, gm_ref, datt_ref, g_hbm, gsum_ref,
                wout, wup, wdown, x_s, mid_s, low_att, low_mid, act_s, slope_s, wide_s, low_act, big_s, acc_s,
                mu_s, rs_s, mu4_s, rs4_s, one_s, two_s, stage, w_sem, g_sem):
    parts, rows, head_width = att_ref.shape
    width = tok_ref.shape[1]
    hidden = width * parts
    n_tiles = rows // tile
    f32 = jnp.float32

    loads = []
    for t in range(parts):
        loads.append(
            pltpu.make_async_copy(
                w_hbm.at[t, pl.ds(2 * width, head_width), :],
                wout.at[pl.ds(t * head_width, head_width), :],
                w_sem.at[2 * parts + t],
            )
        )
    for t in range(parts):
        loads.append(pltpu.make_async_copy(w_hbm.at[t, pl.ds(width, width), :], wup.at[t], w_sem.at[t]))
    for t in range(parts):
        loads.append(pltpu.make_async_copy(w_hbm.at[t, pl.ds(0, width), :], wdown.at[t], w_sem.at[parts + t]))
    for copy in loads:
        copy.start()

    def at(i):
        return pl.ds(pl.multiple_of(i * tile, tile), tile)

    def fold(v):
        return jnp.sum(v.reshape(tile // 8, 8, width), axis=0)

    def tiles(body, init=0):
        return lax.fori_loop(0, n_tiles, body, init)

    def stats(v, n):
        mu = jnp.sum(v, axis=1, keepdims=True) / n
        ms = jnp.sum(v * v, axis=1, keepdims=True) / n
        return mu, lax.rsqrt(ms - mu * mu + EPS)

    def save(slot, block, shard, row, n):
        copy = pltpu.make_async_copy(
            stage.at[slot, pl.ds(0, n), :], g_hbm.at[shard, pl.ds(row, n), :], g_sem.at[slot]
        )
        return copy

    again = jnp.concatenate([gain_ref[t, 2:3, :head_width] for t in range(parts)], axis=1)
    fgain = gain_ref[0, 1:2, :]

    def first(i, _):
        v = jnp.concatenate([att_ref[t, at(i), :] for t in range(parts)], axis=1).astype(f32)
        x_s[at(i), :] = v
        mu, rs = stats(v, width)
        mu_s[at(i), :] = mu
        rs_s[at(i), :] = rs
        low_att[at(i), :] = ((v - mu) * rs * again).astype(jnp.bfloat16)
        return 0

    tiles(first)
    for copy in loads[:parts]:
        copy.wait()
    big_s[...] = jnp.dot(low_att[...], wout[...], preferred_element_type=f32)

    def second(i, _):
        v = tok_ref[at(i), :].astype(f32) + big_s[at(i), :]
        mid_s[at(i), :] = v
        mu, rs = stats(v, width)
        low_mid[at(i), :] = ((v - mu) * rs * fgain).astype(jnp.bfloat16)
        one_s[at(i), :] = jnp.zeros((tile, 1), f32)
        two_s[at(i), :] = jnp.zeros((tile, 1), f32)
        acc_s[at(i), :] = v
        return 0

    tiles(second)

    for copy in loads[parts:]:
        copy.wait()

    def up_block(t, _):
        big_s[...] = jnp.dot(low_mid[...], wup[t], preferred_element_type=f32)

        def body(i, _):
            v = big_s[at(i), :]
            sq = v * v
            th = jnp.tanh(v * (GELU_A + (GELU_A * GELU_B) * sq))
            half = 0.5 * th + 0.5
            act = v * half
            act_s[t, at(i), :] = act
            slope = half + (0.5 * v) * (1.0 - th * th) * (GELU_A + (3.0 * GELU_A * GELU_B) * sq)
            slope_s[t, at(i), :] = slope.astype(jnp.bfloat16)
            one_s[at(i), :] += jnp.sum(act, axis=1, keepdims=True)
            two_s[at(i), :] += jnp.sum(act * act, axis=1, keepdims=True)
            return 0

        tiles(body)
        return 0

    lax.fori_loop(0, parts, up_block, 0)

    def third(i, _):
        mu = one_s[at(i), :] / hidden
        mu4_s[at(i), :] = mu
        rs4_s[at(i), :] = lax.rsqrt(two_s[at(i), :] / hidden - mu * mu + EPS)
        one_s[at(i), :] = jnp.zeros((tile, 1), f32)
        two_s[at(i), :] = jnp.zeros((tile, 1), f32)
        return 0

    tiles(third)

    def down_block(t, _):
        hg = gain_ref[t, 3:4, :]
        big_s[...] = dot_nt(og_ref[...], wdown[t])

        def body(i, part):
            unit = (act_s[t, at(i), :] - mu4_s[at(i), :]) * rs4_s[at(i), :]
            act_s[t, at(i), :] = unit
            low_act[at(i), :] = (unit * hg).astype(jnp.bfloat16)
            d4 = big_s[at(i), :]
            wide = d4 * hg
            wide_s[t, at(i), :] = wide
            one_s[at(i), :] += jnp.sum(wide, axis=1, keepdims=True)
            two_s[at(i), :] += jnp.sum(wide * unit, axis=1, keepdims=True)
            return part + fold(d4 * unit)

        part = tiles(body, jnp.zeros((8, width), f32))
        gsum_ref[pl.ds(2 + t, 1), :] = jnp.sum(part, axis=0, keepdims=True)
        acc_s[...] += jnp.dot(low_act[...], wdown[t], preferred_element_type=f32)
        slot = t % 2

        @pl.when(t >= 2)
        def _():
            save(slot, None, t, 0, width).wait()

        stage[slot] = dot_tn(low_act[...], og_ref[...]).astype(jnp.bfloat16)
        save(slot, None, t, 0, width).start()
        return 0

    lax.fori_loop(0, parts, down_block, 0)

    def fourth(i, _):
        res_ref[at(i), :] = acc_s[at(i), :].astype(jnp.bfloat16)
        one_s[at(i), :] = one_s[at(i), :] / hidden
        two_s[at(i), :] = two_s[at(i), :] / hidden
        acc_s[at(i), :] = jnp.zeros((tile, width), f32)
        return 0

    tiles(fourth)

    def back_block(t, _):
        def body(i, _):
            d_act = rs4_s[at(i), :] * (wide_s[t, at(i), :] - one_s[at(i), :] - act_s[t, at(i), :] * two_s[at(i), :])
            low_act[at(i), :] = (d_act * slope_s[t, at(i), :].astype(f32)).astype(jnp.bfloat16)
            return 0

        tiles(body)
        acc_s[...] += dot_nt(low_act[...], wup[t])
        slot = t % 2
        save(slot, None, t, 0, width).wait()
        stage[slot] = dot_tn(low_mid[...], low_act[...]).astype(jnp.bfloat16)
        save(slot, None, t, width, width).start()
        return 0

    lax.fori_loop(0, parts, back_block, 0)

    def fifth(i, part):
        v = mid_s[at(i), :]
        mu, rs = stats(v, width)
        unit = (v - mu) * rs
        d3 = acc_s[at(i), :]
        wide = d3 * fgain
        m1 = jnp.sum(wide, axis=1, keepdims=True) / width
        m2 = jnp.sum(wide * unit, axis=1, keepdims=True) / width
        d_mid = og_ref[at(i), :].astype(f32) + rs * (wide - m1 - unit * m2)
        gm_ref[at(i), :] = d_mid
        low_act[at(i), :] = d_mid.astype(jnp.bfloat16)
        return part + fold(d3 * unit)

    part = tiles(fifth, jnp.zeros((8, width), f32))
    gsum_ref[0:1, :] = jnp.sum(part, axis=0, keepdims=True)
    big_s[...] = dot_nt(low_act[...], wout[...])
    for slot in range(2):
        save(slot, None, slot, width, width).wait()
    stage[0] = dot_tn(low_att[...], low_act[...]).astype(jnp.bfloat16)
    last = []
    for t in range(parts):
        copy = pltpu.make_async_copy(
            stage.at[0, pl.ds(t * head_width, head_width), :],
            g_hbm.at[t, pl.ds(2 * width, head_width), :],
            w_sem.at[t],
        )
        copy.start()
        last.append(copy)

    def sixth(i, part):
        mu, rs = mu_s[at(i), :], rs_s[at(i), :]
        unit = (x_s[at(i), :] - mu) * rs
        d2 = big_s[at(i), :]
        wide = d2 * again
        m1 = jnp.sum(wide, axis=1, keepdims=True) / width
        m2 = jnp.sum(wide * unit, axis=1, keepdims=True) / width
        d_att = (rs * (wide - m1 - unit * m2)).astype(jnp.bfloat16)
        for t in range(parts):
            datt_ref[t, at(i), :] = d_att[:, t * head_width : (t + 1) * head_width]
        return part + fold(d2 * unit)

    part = tiles(sixth, jnp.zeros((8, width), f32))
    gsum_ref[1:2, :] = jnp.sum(part, axis=0, keepdims=True)
    gsum_ref[pl.ds(2 + parts, 8 - 2 - parts), :] = jnp.zeros((8 - 2 - parts, width), f32)
    for copy in last:
        copy.wait()


def rows_pass(att, tokens, out_grad, gains, weights, tile):
    parts, rows, head_width = att.shape
    width = tokens.shape[1]
    bf16, f32 = jnp.bfloat16, jnp.float32
    vmem = pl.BlockSpec(memory_space=pltpu.VMEM)
    anywhere = pl.BlockSpec(memory_space=pl.ANY)
    column = pltpu.VMEM((rows, 1), f32)
    return pl.pallas_call(
        partial(rows_kernel, tile),
        out_shape=(
            jax.ShapeDtypeStruct((rows, width), bf16),
            jax.ShapeDtypeStruct((rows, width), f32),
            jax.ShapeDtypeStruct(att.shape, bf16),
            jax.ShapeDtypeStruct((parts, 2 * width + head_width, width), bf16),
            jax.ShapeDtypeStruct((8, width), f32),
        ),
        in_specs=[vmem] * 4 + [anywhere],
        out_specs=[vmem] * 3 + [anywhere, vmem],
        scratch_shapes=[
            pltpu.VMEM((width, width), bf16),
            pltpu.VMEM((parts, width, width), bf16),
            pltpu.VMEM((parts, width, width), bf16),
            pltpu.VMEM((rows, width), f32),
            pltpu.VMEM((rows, width), f32),
            pltpu.VMEM((rows, width), bf16),
            pltpu.VMEM((rows, width), bf16),
            pltpu.VMEM((parts, rows, width), f32),
            pltpu.VMEM((parts, rows, width), bf16),
            pltpu.VMEM((parts, rows, width), f32),
            pltpu.VMEM((rows, width), bf16),
            pltpu.VMEM((rows, width), f32),
            pltpu.VMEM((rows, width), f32),
        ] + [column] * 6 + [
            pltpu.VMEM((2, width, width), bf16),
            pltpu.SemaphoreType.DMA((3 * parts,)),
            pltpu.SemaphoreType.DMA((2,)),
        ],
        compiler_params=pltpu.CompilerParams(vmem_limit_bytes=60 << 20),
        cost_estimate=pl.CostEstimate(flops=20 * 10**9, bytes_accessed=40 << 20, transcendentals=2 * 10**6),
        name="rows_pass",
    )(att, tokens, out_grad, gains, weights)


def front_kernel(groups, pieces, chunk, len_ref, tok_ref, w_ref, own_gain_ref, down_ref, up_ref, out_ref,
                 all_ref, packed_ref, gains_ref, att_ref, own_ref, lse_ref, full_ref,
                 k_s, qt_s, vt_s, acc_s, m_s, shard_s,
                 send, recv, gain_send, gain_recv, w_send, w_recv, w_load, w_local, a_send, a_recv, a_local):
    f32, bf16 = jnp.float32, jnp.bfloat16
    me, dp = lax.axis_index("tensor"), lax.axis_index("dp")
    core, chip, cross = spread(me)
    b0, b1, b2 = dp % 2, (dp // 2) % 2, (dp // 4) % 2
    rows, width = tok_ref.shape
    heads = k_s.shape[0]
    parts = all_ref.shape[0]
    piece = rows // pieces
    ends = seq_bounds(len_ref)
    half, rows2, rows4 = width // 2, chunk // 2, chunk // 4

    chunks = []
    for ref in (down_ref, up_ref, out_ref):
        for at in range(0, ref.shape[0], chunk):
            chunks.append((ref, at, len(chunks) * chunk))
    n = len(chunks)

    def load_weight(c):
        ref, at, _ = chunks[c]
        return pltpu.make_async_copy(ref.at[pl.ds(at, chunk), :], shard_s.at[c], w_load.at[c])

    for c in range(n):
        load_weight(c).start()
    values = tok_ref[...].astype(f32)
    mu = jnp.sum(values, axis=1, keepdims=True) / width
    ms = jnp.sum(values * values, axis=1, keepdims=True) / width
    all_ref[me] = ((values - mu) * lax.rsqrt(ms - mu * mu + EPS) * own_gain_ref[0:1, :]).astype(bf16)
    gains_ref[me] = own_gain_ref[...]
    greet([("dp", 1), ("dp", 2), ("dp", 4)], core, chip, cross)

    def to_peer(src, dst, ssem, rsem, where):
        return pltpu.make_async_remote_copy(
            src_ref=src, dst_ref=dst, send_sem=ssem, recv_sem=rsem, device_id=where, device_id_type=MESH
        )

    def block(c, owner):
        return all_ref.at[owner, pl.ds(pl.multiple_of(c * piece, piece), piece), :]

    def to_chip(c):
        return to_peer(block(c, me), block(c, me), send.at[c], recv.at[c], {"tensor": chip})

    def to_far(c):
        return to_peer(block(c, chip), block(c, chip), send.at[pieces + c], recv.at[pieces + c], {"tensor": core})

    def to_core():
        return to_peer(all_ref.at[me], all_ref.at[me], send.at[2 * pieces], recv.at[2 * pieces], {"tensor": core})

    def gain_copy(k):
        owner, peer = ((me, chip), (me, core), (chip, core))[k]
        return to_peer(gains_ref.at[owner], gains_ref.at[owner], gain_send.at[k], gain_recv.at[k], {"tensor": peer})

    to_core().start()
    gain_copy(0).start()
    gain_copy(1).start()

    def spot(shard, c, row0, size, col0, span):
        row = chunks[c][2] + row0
        return full_ref.at[shard, pl.ds(pl.multiple_of(row, 16), size), pl.ds(pl.multiple_of(col0, 128), span)]

    def weight_copy(c, s):
        row4, row2, col = b1 * rows2 + b2 * rows4, b1 * rows2, b0 * half
        if s == 0:
            src = shard_s.at[c, pl.ds(pl.multiple_of(row4, 16), rows4), pl.ds(pl.multiple_of(col, 128), half)]
            dst, where = spot(me, c, row4, rows4, col, half), {"tensor": chip}
        elif s == 1:
            src = dst = spot(chip, c, row4, rows4, col, half)
            where = at_peer("dp", 4)
        elif s == 2:
            src = dst = spot(chip, c, row2, rows2, col, half)
            where = at_peer("dp", 2)
        elif s == 3:
            src = dst = spot(chip, c, 0, chunk, col, half)
            where = at_peer("dp", 1)
        elif s == 4:
            src = dst = spot(chip, c, 0, chunk, 0, width)
            where = {"tensor": core}
        else:
            src = shard_s.at[c]
            dst, where = spot(me, c, 0, chunk, 0, width), {"tensor": core}
        return to_peer(src, dst, w_send.at[c, s], w_recv.at[c, s], where)

    def own_weight(c):
        return pltpu.make_async_copy(shard_s.at[c], spot(me, c, 0, chunk, 0, width), w_local.at[c])

    order = list(reversed(range(n)))
    batches = [order[: n // 3], order[n // 3 : 2 * n // 3], order[2 * n // 3 :]]

    def weights(batch, s):
        for c in batches[batch]:
            if s:
                weight_copy(c, s - 1).wait_recv()
            if s < 5:
                weight_copy(c, s).start()

    scale = jnp.bfloat16(0.125)
    ones = (lax.broadcasted_iota(jnp.int32, (16, piece), 0) == 0).astype(f32).astype(bf16)

    def project(owner, c):
        span = pl.ds(pl.multiple_of(c * piece, piece), piece)
        at = pl.ds(pl.multiple_of(owner * rows + c * piece, piece), piece)
        x = dot_nt(all_ref[owner, span, :], w_ref[...]).astype(bf16)
        packed_ref[owner, span, :] = x
        for h in range(heads):
            base = h * 3 * HEAD_DIM
            qt_s[h, :, at] = (x[:, base : base + HEAD_DIM] * scale).T
            k_s[h, at, :] = x[:, base + HEAD_DIM : base + 2 * HEAD_DIM]
            vt_s[h, :HEAD_DIM, at] = x[:, base + 2 * HEAD_DIM : base + 3 * HEAD_DIM].T
            vt_s[h, HEAD_DIM:, at] = ones

    def loop(body):
        def one(c, _):
            body(c)
            return 0

        lax.fori_loop(0, pieces, one, 0)

    for c in range(n):
        load_weight(c).wait()
    weights(0, 0)
    to_chip(0).start()
    to_chip(1).start()
    weights(1, 0)
    for c in range(2, pieces):
        to_chip(c).start()
    weights(2, 0)
    loop(lambda c: project(me, c))
    to_core().wait_recv()
    loop(lambda c: project(core, c))
    for c in order:
        weight_copy(c, 5).start()
        own_weight(c).start()

    early = ([(0, 1)], [(0, 2)], [(1, 1), (0, 3)], [(1, 2)], [(1, 3), (0, 4)])
    for c in range(pieces):
        to_chip(c).wait_recv()
        to_far(c).start()
        project(chip, c)
        for event in early[c] if c < len(early) else ():
            weights(*event)
    gain_copy(0).wait_recv()
    gain_copy(2).start()

    def from_far(c):
        to_far(c).wait_recv()
        project(cross, c)

    loop(from_far)
    weights(2, 1)

    def attend(o, later):
        first = o * rows
        at = pl.ds(first, rows)
        q_pos = first + lax.broadcasted_iota(jnp.int32, (1, rows), 1)
        q_start = start_of(ends, q_pos)
        for h in range(heads):
            acc_s[h] = jnp.zeros_like(acc_s[h])
            m_s[h] = jnp.full_like(m_s[h], NEG)

        def step(j, _):
            k0 = pl.multiple_of(j * rows, rows)
            kat = pl.ds(k0, rows)
            k_pos = k0 + lax.broadcasted_iota(jnp.int32, (rows, 1), 0)
            keep = (k_pos <= q_pos) & (k_pos >= q_start)
            for h in range(heads):
                s = jnp.where(keep, dot(k_s[h, kat, :], qt_s[h, :, at]), NEG)
                old = m_s[h]
                new = jnp.maximum(old, jnp.max(s, axis=0, keepdims=True))
                p = jnp.exp(s - new).astype(bf16)
                m_s[h] = new
                acc_s[h] = acc_s[h] * jnp.exp(old - new) + dot(vt_s[h, :, kat], p)
            return 0

        done = 0
        for stop, events in later:
            if stop > done:
                lax.fori_loop(done, stop, step, 0)
            for event in events:
                weights(*event)
            done = stop
        lax.fori_loop(done, o + 1, step, 0)
        outs = []
        for h in range(heads):
            acc = acc_s[h]
            total = acc[HEAD_DIM : HEAD_DIM + 1, :]
            outs.append((acc[:HEAD_DIM, :] / total).T)
            lse_ref[h : h + 1, at] = m_s[h] + jnp.log(total)
        att_ref[o] = jnp.concatenate(outs, axis=1).astype(bf16)

    def give(k):
        peer = (core, chip, cross)[k]
        return to_peer(att_ref.at[peer], own_ref.at[me], a_send.at[k], a_recv.at[k], {"tensor": peer})

    def keep_own():
        return pltpu.make_async_copy(att_ref.at[me], own_ref.at[me], a_local)

    plans = ([], [(0, [(2, 2)]), (1, [(1, 4), (2, 3)])], [(2, [(2, 4)])], [])
    for o in range(parts):
        attend(o, plans[o])

        for k, peer in enumerate((core, chip, cross)):

            @pl.when(peer == o)
            def _(k=k):
                give(k).start()

        @pl.when(me == o)
        def _():
            keep_own().start()

    gain_copy(1).wait_recv()
    gain_copy(2).wait_recv()
    for batch in range(3):
        weights(batch, 5)
    for c in order:
        weight_copy(c, 5).wait_recv()
        own_weight(c).wait()
    keep_own().wait()
    for k in range(3):
        give(k).wait()
    for c in range(pieces):
        to_chip(c).wait_send()
        to_far(c).wait_send()
    to_core().wait_send()
    for k in range(3):
        gain_copy(k).wait_send()
    for c in order:
        for s in range(6):
            weight_copy(c, s).wait_send()


def front_pass(groups, lengths, tokens, weight, own_gains, w_down, w_up, w_out, pieces=5, chunk=192):
    rows, width = tokens.shape
    heads = weight.shape[0] // (3 * HEAD_DIM)
    parts = 4
    total = parts * rows
    n = (w_down.shape[0] + w_up.shape[0] + w_out.shape[0]) // chunk
    bf16, f32 = jnp.bfloat16, jnp.float32
    vmem, anywhere = pl.BlockSpec(memory_space=pltpu.VMEM), pl.BlockSpec(memory_space=pl.ANY)
    sems = pltpu.SemaphoreType.DMA
    shape = jax.ShapeDtypeStruct
    return pl.pallas_call(
        partial(front_kernel, groups, pieces, chunk),
        out_shape=(
            shape((parts, rows, width), bf16),
            shape((parts, rows, weight.shape[0]), bf16),
            shape((parts,) + own_gains.shape, f32),
            shape((parts, rows, heads * HEAD_DIM), bf16),
            shape((parts, rows, heads * HEAD_DIM), bf16),
            shape((8, total), f32),
            shape((parts, n * chunk, width), bf16),
        ),
        in_specs=[pl.BlockSpec(memory_space=pltpu.SMEM)] + [vmem] * 3 + [anywhere] * 3,
        out_specs=[vmem] * 6 + [anywhere],
        scratch_shapes=[
            pltpu.VMEM((heads, total, HEAD_DIM), bf16),
            pltpu.VMEM((heads, HEAD_DIM, total), bf16),
            pltpu.VMEM((heads, HEAD_DIM + 16, total), bf16),
            pltpu.VMEM((heads, HEAD_DIM + 16, rows), f32),
            pltpu.VMEM((heads, 1, rows), f32),
            pltpu.VMEM((n, chunk, width), bf16),
            sems((2 * pieces + 1,)),
            sems((2 * pieces + 1,)),
            sems((3,)),
            sems((3,)),
            sems((n, 6)),
            sems((n, 6)),
            sems((n,)),
            sems((n,)),
            sems((3,)),
            sems((3,)),
            sems,
        ],
        compiler_params=pltpu.CompilerParams(
            collective_id=1, has_side_effects=True, vmem_limit_bytes=56 << 20
        ),
        name="front_pass",
    )(lengths, tokens, weight, own_gains, w_down, w_up, w_out)


def chunk_copy(c, s, src, dst, send, recv, axis, bit):
    return pltpu.make_async_remote_copy(
        src_ref=src,
        dst_ref=dst,
        send_sem=send.at[c, s],
        recv_sem=recv.at[c, s],
        device_id=at_peer(axis, bit),
        device_id_type=MESH,
    )


def back_kernel(groups, chunk, block, pieces, len_ref, datt_ref, packed_ref, att_ref, lse_ref, grads_ref,
                h1_ref, w_ref, gains_ref, gain_ref,
                sum_ref, in_sum, gains_sum,
                pq, do_s, own, first, second, acc, to_y, to_x, from_x, to_z, from_z, more_to, more_from,
                send, recv, local_sem, a2a_send, a2a_recv, a2a_local,
                d_first, d_second, d_send, d_recv, gain_at, gain_send, gain_recv, load_sem):
    f32, bf16 = jnp.float32, jnp.bfloat16
    steps = peers_of(4, groups)
    far = steps[5:]
    me, dp = lax.axis_index("tensor"), lax.axis_index("dp")
    core, chip, cross = spread(me)
    cols = grads_ref.shape[2]
    half, rows2, rows4 = cols // 2, chunk // 2, chunk // 4
    b0, b1, b2 = dp % 2, (dp // 2) % 2, (dp // 4) % 2
    n = grads_ref.shape[1] // chunk

    def take(c, shard):
        return grads_ref.at[shard, pl.ds(pl.multiple_of(c * chunk, 16), chunk), :]

    def col(b):
        return pl.ds(pl.multiple_of(b * half, 128), half)

    def row2(b):
        return pl.ds(pl.multiple_of(b * rows2, 16), rows2)

    def row4(b, bb):
        return pl.ds(pl.multiple_of(b * rows2 + bb * rows4, 16), rows4)

    def copy(c, s):
        if s == 0:
            return chunk_copy(c, 0, take(c, core), first.at[c, 0], send, recv, "tensor", 1)
        if s == 1:
            return chunk_copy(c, 1, take(c, cross), first.at[c, 1], send, recv, "tensor", 1)
        if s == 2:
            return chunk_copy(c, 2, to_y.at[c % 3], second.at[c], send, recv, "tensor", 2)
        if s == 3:
            slot = 3 + c - n if isinstance(c, int) and c >= n else c % 3
            return chunk_copy(c, 3, to_x.at[slot], from_x.at[c], send, recv, "dp", 1)
        if s in (4, 5, 6):
            return chunk_copy(c, s, to_z.at[c, s - 4], from_z.at[c, s - 4], send, recv, "dp", 2 * (s - 3))
        if s in (7, 8, 9):
            piece = sum_ref.at[c, row4(b1, b2), col(b0)]
            return chunk_copy(c, s, piece, piece, send, recv, "dp", 2 * (s - 6))
        if s == 10:
            piece = sum_ref.at[c, :, col(b0)]
            return chunk_copy(c, 10, piece, piece, send, recv, "dp", 1)
        axis, bit = far[s - 11]
        return chunk_copy(c, s, more_to.at[c, s - 11], more_from.at[c, s - 11], send, recv, axis, bit)

    def other4(m):
        return row4(b1 + (m % 2) * (1 - 2 * b1), b2 + (m // 2) * (1 - 2 * b2))

    def arrived(c, s, piece=None):
        if piece is None:
            copy(c, s).wait_recv()
        else:
            bit = 1 if s == 10 else 2 * (s - 6)
            chunk_copy(c, s, piece, piece, send, recv, "dp", bit).wait_recv()

    def mine(c, k):
        shard = (me, chip)[k]
        return pltpu.make_async_copy(take(c, shard), own.at[c % 3, k], local_sem.at[c % 3, k])

    def pair(c):
        copy(c, 1).start()
        copy(c, 0).start()
        mine(c, 1).start()
        mine(c, 0).start()

    def to_chip(c):
        @pl.when(c >= 3)
        def _():
            copy(c - 3, 2).wait_send()

        mine(c, 1).wait()
        arrived(c, 1)
        to_y[c % 3] = rounded(own[c % 3, 1].astype(f32) + first[c, 1].astype(f32))
        copy(c, 2).start()

    def x_half(c):
        @pl.when(c >= 3)
        def _():
            copy(c - 3, 3).wait_send()

        mine(c, 0).wait()
        arrived(c, 0)
        arrived(c, 2)

        def total(b):
            whole = own[c % 3, 0, :, col(b)].astype(f32) + first[c, 0, :, col(b)].astype(f32)
            return whole + second[c, :, col(b)].astype(f32)

        to_x[c % 3] = rounded(total(1 - b0))
        copy(c, 3).start()
        acc[c] = total(b0)

    def z_all(c):
        arrived(c, 3)
        acc[c] += from_x[c].astype(f32)
        for m in (3, 1, 2):
            to_z[c, m - 1] = rounded(acc[c, other4(m), :])
            copy(c, 3 + m).start()

    def settle(c):
        total = acc[c, row4(b1, b2), :]
        for m in (1, 2, 3):
            arrived(c, 3 + m)
            total = total + from_z[c, m - 1].astype(f32)
        for m in range(len(far)):
            more_to[c, m] = rounded(total)
            copy(c, 11 + m).start()
            arrived(c, 11 + m)
            total = rounded(total).astype(f32) + more_from[c, m].astype(f32)
        sum_ref[c, row4(b1, b2), col(b0)] = rounded(total)
        for m in (3, 1, 2):
            copy(c, 6 + m).start()

    def x_share(c):
        for m in (1, 2, 3):
            arrived(c, 6 + m, sum_ref.at[c, other4(m), col(b0)])
        copy(c, 10).start()

    def end(c):
        arrived(c, 10, sum_ref.at[c, :, col(1 - b0)])

    stages = (pair, to_chip, x_half, z_all, settle, x_share, end)

    def turn(at):
        for s in range(len(stages)):
            c = at - s

            @pl.when((c >= 0) & (c < n))
            def _():
                stages[s](c)

    rows = packed_ref.shape[0]
    heads = packed_ref.shape[1] // (3 * HEAD_DIM)
    own_rows = datt_ref.shape[1]
    width = h1_ref.shape[1]
    ends = seq_bounds(len_ref)
    scale = jnp.bfloat16(0.125)
    load = pltpu.make_async_copy(packed_ref, pq, load_sem.at[0])
    load.start()
    greet(steps + [("dp", 6)], cross)

    def a2a(k, peer):
        return pltpu.make_async_remote_copy(
            src_ref=datt_ref.at[peer],
            dst_ref=do_s.at[me],
            send_sem=a2a_send.at[k],
            recv_sem=a2a_recv.at[k],
            device_id={"tensor": peer},
            device_id_type=MESH,
        )

    moves = [a2a(k, peer) for k, peer in reversed(list(enumerate((core, chip, cross))))]
    for move in moves:
        move.start()
    keep_own = pltpu.make_async_copy(datt_ref.at[me], do_s.at[me], a2a_local)
    keep_own.start()
    turn(jnp.int32(0))
    load.wait()

    def attention(kv_s, q_s, g_s, qt_s, gt_s, kt_s, d_s, dqt_s, acc_kv):
        def stage_qkv(i, _):
            at = pl.ds(pl.multiple_of(i * 256, 256), 256)
            x = pq[at, :]
            blank = jnp.zeros((256, HEAD_DIM), bf16)
            blank_t = jnp.zeros((HEAD_DIM, 256), bf16)
            for h in range(heads):
                base = h * 3 * HEAD_DIM
                q = x[:, base : base + HEAD_DIM] * scale
                k = x[:, base + HEAD_DIM : base + 2 * HEAD_DIM]
                v = x[:, base + 2 * HEAD_DIM : base + 3 * HEAD_DIM]
                kv_s[h, at, :] = jnp.concatenate([k, v], axis=1)
                q_s[h, at, :] = jnp.concatenate([q, blank], axis=1)
                qt_s[h, :HEAD_DIM, at] = q.T
                qt_s[h, HEAD_DIM:, at] = blank_t
                kt_s[h, :, at] = (k * scale).T
                dqt_s[h, :, at] = jnp.zeros((HEAD_DIM, 256), f32)
                acc_kv[h, at, :] = jnp.zeros((256, 2 * HEAD_DIM), f32)
            return 0

        lax.fori_loop(0, rows // 256, stage_qkv, 0)
        keep_own.wait()
        for move in moves:
            move.wait()
        piece = own_rows // 5

        def stage_grad(i, _):
            owner, part = i // 5, i % 5
            inner = pl.ds(pl.multiple_of(part * piece, piece), piece)
            at = pl.ds(pl.multiple_of(owner * own_rows + part * piece, piece), piece)
            g = do_s[owner, inner, :]
            prod = g.astype(f32) * att_ref[at, :].astype(f32)
            blank = jnp.zeros((piece, HEAD_DIM), bf16)
            blank_t = jnp.zeros((HEAD_DIM, piece), bf16)
            for h in range(heads):
                d = g[:, h * HEAD_DIM : (h + 1) * HEAD_DIM]
                g_s[h, at, :] = jnp.concatenate([blank, d], axis=1)
                gt_s[h, HEAD_DIM:, at] = d.T
                gt_s[h, :HEAD_DIM, at] = blank_t
                d_s[h, :, at] = jnp.sum(prod[:, h * HEAD_DIM : (h + 1) * HEAD_DIM].T, axis=0, keepdims=True)
            return 0

        lax.fori_loop(0, rows // piece, stage_grad, 0)

        def body(i, j):
            q0 = pl.multiple_of(i * block, block)
            k0 = pl.multiple_of(j * block, block)
            at, kat = pl.ds(q0, block), pl.ds(k0, block)
            q_pos = q0 + lax.broadcasted_iota(jnp.int32, (1, block), 1)
            q_start = start_of(ends, q_pos)
            k_pos = k0 + lax.broadcasted_iota(jnp.int32, (block, 1), 0)
            keep = (k_pos <= q_pos) & (k_pos >= q_start)
            for h in range(heads):
                kv = kv_s[h, kat, :]
                s = dot(kv, qt_s[h, :, at]) - lse_ref[h : h + 1, at]
                p = jnp.exp(jnp.where(keep, s, NEG))
                dp_t = dot(kv, gt_s[h, :, at])
                ds = (p * (dp_t - d_s[h, :, at])).astype(bf16)
                acc_kv[h, kat, :] += dot(p.astype(bf16), g_s[h, at, :]) + dot(ds, q_s[h, at, :])
                dqt_s[h, :, at] += dot(kt_s[h, :, kat], ds)

        count = rows // block
        done = 0
        for g in range(count // 2 + 1):
            length = count - g

            def one(p, _, length=length, g=g, done=done):
                wrap = p // length
                i = (length - 1) - wrap * (length - g)
                j = p - wrap * length
                body(i, j)
                b = p + done

                @pl.when(b % 2 == 1)
                def _():
                    turn((b + 1) // 2)

                return 0

            lax.fori_loop(0, count, one, 0)
            done += count

        def finish(i, _):
            at = pl.ds(pl.multiple_of(i * 256, 256), 256)
            parts_of = []
            for h in range(heads):
                parts_of += [dqt_s[h, :, at].T, acc_kv[h, at, :]]
            pq[at, :] = jnp.concatenate(parts_of, axis=1).astype(bf16)
            return 0

        lax.fori_loop(0, rows // 256, finish, 0)

    wide = 2 * HEAD_DIM
    pl.run_scoped(
        attention,
        pltpu.VMEM((heads, rows, wide), bf16),
        pltpu.VMEM((heads, rows, wide), bf16),
        pltpu.VMEM((heads, rows, wide), bf16),
        pltpu.VMEM((heads, wide, rows), bf16),
        pltpu.VMEM((heads, wide, rows), bf16),
        pltpu.VMEM((heads, HEAD_DIM, rows), bf16),
        pltpu.VMEM((heads, 1, rows), f32),
        pltpu.VMEM((heads, HEAD_DIM, rows), f32),
        pltpu.VMEM((heads, rows, wide), f32),
    )
    bodies = (rows // block) * (rows // block + 1) // 2
    next_turn = bodies // 2 + 1
    piece = own_rows // pieces
    parts = rows // own_rows
    extra_chunks = w_ref.shape[0] // chunk

    def closing(h1_s, d1_s, d_to, gq):
        flight, sends = {}, []

        def go(key, src, dst, ssem, rsem, axis, bit):
            flight[key] = remote(src, dst, ssem, rsem, axis, bit)
            sends.append(flight[key])

        def owned(owner):
            return pl.ds(pl.multiple_of(owner * own_rows, own_rows), own_rows)

        fetch = [
            pltpu.make_async_copy(h1_ref.at[pl.ds(t * own_rows, own_rows), :], h1_s.at[t], load_sem.at[1 + t])
            for t in range(parts)
        ]
        for t in fetch:
            t.start()

        def span(c):
            return pl.ds(c * piece, piece)

        def product(slot, owner):
            d1_s[slot] = rounded(dot(pq[owned(owner), :], w_ref[...]))

        def pair_rows(c):
            go(("d", c, 1), d1_s.at[0, span(c)], d_first.at[1, span(c)], d_send.at[c, 1], d_recv.at[c, 1], "tensor", 1)
            go(("d", c, 0), d1_s.at[1, span(c)], d_first.at[0, span(c)], d_send.at[c, 0], d_recv.at[c, 0], "tensor", 1)

        def across(c):
            flight["d", c, 1].wait_recv()
            d_to[span(c)] = rounded(d1_s[2, span(c), :].astype(f32) + d_first[1, span(c), :].astype(f32))
            go(("d", c, 2), d_to.at[span(c)], d_second.at[span(c)], d_send.at[c, 2], d_recv.at[c, 2], "tensor", 2)

        def settle_rows(c):
            flight["d", c, 0].wait_recv()
            flight["d", c, 2].wait_recv()
            near = d1_s[3, span(c), :].astype(f32) + d_first[0, span(c), :].astype(f32)
            in_sum[span(c)] = near + d_second[span(c)].astype(f32)

        def q_x(i):
            rows_of = pl.ds(i * chunk, chunk)
            to_x[3 + i] = rounded(gq[rows_of, col(1 - b0)])
            copy(n + i, 3).start()
            acc[n + i] = gq[rows_of, col(b0)]

        def gain_start(m):
            axis, bit = steps[m]
            go(("g", m), gain_at.at[0, m], gain_at.at[1, m], gain_send.at[m], gain_recv.at[m], axis, bit)

        def gain_step(m):
            flight["g", m].wait_recv()
            now = gain_at[0, m] + gain_at[1, m]
            if m + 1 < len(steps):
                gain_at[0, m + 1] = now
                gain_start(m + 1)
            else:
                gains_sum[...] = now

        last = n + len(stages) - 1
        turns = iter(range(next_turn, last))

        def main_turn():
            at = next(turns, None)
            if at is not None:
                turn(jnp.int32(at))

        main_turn()
        product(0, cross)
        product(1, core)
        for c in range(pieces):
            pair_rows(c)
        product(2, chip)
        product(3, me)
        main_turn()
        for t in fetch:
            t.wait()
        gq[...] = dot_tn(pq[owned(0), :], h1_s[0])
        for c in range(pieces):
            across(c)
        for t in range(1, parts):
            gq[...] += dot_tn(pq[owned(t), :], h1_s[t])
        for i in range(extra_chunks):
            q_x(i)
        main_turn()
        gain_at[0, 0] = gains_ref[...]
        line = jnp.sum(w_ref[...].astype(f32) * gq[...], axis=0, keepdims=True)
        gain_at[0, 0, 2 + parts : 3 + parts, :] = line / gain_ref[0, 0:1, :]
        gain_start(0)
        q_stages = (z_all, settle, x_share, end)
        settled = gained = 0
        for stage in q_stages:
            for i in range(extra_chunks):
                stage(n + i)
            main_turn()
            if settled < pieces:
                settle_rows(settled)
                settled += 1
            if gained < len(steps):
                gain_step(gained)
                gained += 1
        while settled < pieces:
            settle_rows(settled)
            settled += 1
        while gained < len(steps):
            gain_step(gained)
            gained += 1
        for at in turns:
            turn(jnp.int32(at))
        for each in sends:
            each.wait_send()

    pl.run_scoped(
        closing,
        pltpu.VMEM((parts, own_rows, width), bf16),
        pltpu.VMEM((parts, own_rows, width), bf16),
        pltpu.VMEM((own_rows, width), bf16),
        pltpu.VMEM(w_ref.shape, f32),
    )

    def sent(c, _):
        for s in range(11 + len(far)):
            if s in (2, 3):

                @pl.when(c >= n - 3)
                def _():
                    copy(c, s).wait_send()

            else:
                copy(c, s).wait_send()
        return 0

    lax.fori_loop(0, n, sent, 0)
    for i in range(extra_chunks):
        for s in range(3, 11 + len(far)):
            copy(n + i, s).wait_send()


def back_pass(groups, lengths, grad_att, packed, att, lse, grads, h1, weight, sums, gains,
              chunk=192, block=512, pieces=5):
    rows = packed.shape[0]
    parts, own_rows, head_width = grad_att.shape
    width = grads.shape[2]
    n = grads.shape[1] // chunk
    more = weight.shape[0] // chunk
    steps = len(peers_of(4, groups))
    extra = max(steps - 5, 1)
    bf16 = lambda *shape: pltpu.VMEM(shape, jnp.bfloat16)
    f32 = lambda *shape: pltpu.VMEM(shape, jnp.float32)
    vmem, anywhere = pl.BlockSpec(memory_space=pltpu.VMEM), pl.BlockSpec(memory_space=pl.ANY)
    sems = pltpu.SemaphoreType.DMA
    return pl.pallas_call(
        partial(back_kernel, groups, chunk, block, pieces),
        out_shape=(
            jax.ShapeDtypeStruct((n + more, chunk, width), jnp.bfloat16),
            jax.ShapeDtypeStruct((own_rows, width), jnp.float32),
            jax.ShapeDtypeStruct(sums.shape, jnp.float32),
        ),
        in_specs=[pl.BlockSpec(memory_space=pltpu.SMEM), anywhere, anywhere, vmem, vmem, anywhere,
                  anywhere, vmem, vmem, vmem],
        out_specs=[vmem] * 3,
        scratch_shapes=[
            bf16(rows, packed.shape[1]),
            bf16(parts, own_rows, head_width),
            bf16(3, 2, chunk, width),
            bf16(n, 2, chunk, width),
            bf16(n, chunk, width),
            f32(n + more, chunk, width // 2),
            bf16(3, chunk, width),
            bf16(3 + more, chunk, width // 2),
            bf16(n + more, chunk, width // 2),
            bf16(n + more, 3, chunk // 4, width // 2),
            bf16(n + more, 3, chunk // 4, width // 2),
            bf16(n + more, extra, chunk // 4, width // 2),
            bf16(n + more, extra, chunk // 4, width // 2),
            sems((n + more, 11 + extra)),
            sems((n + more, 11 + extra)),
            sems((3, 2)),
            sems((3,)),
            sems((3,)),
            sems,
            bf16(2, own_rows, width),
            bf16(own_rows, width),
            sems((pieces, 3)),
            sems((pieces, 3)),
            pltpu.VMEM((2, steps) + sums.shape, jnp.float32),
            sems((steps,)),
            sems((steps,)),
            sems((1 + parts,)),
        ],
        compiler_params=pltpu.CompilerParams(
            collective_id=0, has_side_effects=True, vmem_limit_bytes=60 << 20
        ),
        name="back_pass",
    )(lengths, grad_att, packed, att, lse, grads, h1, weight, sums, gains)


def local(
    tokens,
    lengths,
    in_gain,
    qkv_weight,
    attn_gain,
    out_weight,
    ffn_gain,
    up_weight,
    hidden_gain,
    down_weight,
    out_grad,
):
    parts = lax.axis_size("tensor")
    own_rows, width = tokens.shape
    head_width, hidden = attn_gain.shape[0], hidden_gain.shape[0]

    filler = jnp.zeros((width - head_width,), jnp.float32)
    rest = jnp.zeros((4 * width,), jnp.float32)
    own_gains = jnp.concatenate((in_gain, ffn_gain, attn_gain, filler, hidden_gain, rest)).reshape(8, width)
    weight_t = qkv_weight.T
    groups = lax.axis_size("dp")
    gathered_in, packed, gains, attended, own_att, log_total, weights = front_pass(
        groups,
        lengths,
        tokens,
        weight_t,
        own_gains,
        down_weight,
        up_weight,
        out_weight,
    )
    gathered_in = gathered_in.reshape(parts * own_rows, width)
    packed = packed.reshape(parts * own_rows, -1)
    attended = attended.reshape(parts * own_rows, head_width)
    result, grad_middle, grad_att, grads, gain_parts = rows_pass(
        own_att,
        tokens,
        out_grad,
        gains,
        weights,
        own_rows,
    )
    sums, grad_in_normed, gains = back_pass(
        groups,
        lengths,
        grad_att,
        packed,
        attended,
        log_total,
        grads,
        gathered_in,
        weight_t,
        gain_parts,
        gains,
    )

    residual = tokens.astype(jnp.float32)
    mean = jnp.mean(residual, axis=1, keepdims=True)
    square = jnp.mean(residual * residual, axis=1, keepdims=True)
    scale = lax.rsqrt(square - mean * mean + EPS)
    unit = (residual - mean) * scale
    weighted = grad_in_normed * in_gain
    first = jnp.mean(weighted, axis=1, keepdims=True)
    second = jnp.mean(weighted * unit, axis=1, keepdims=True)
    in_grad = grad_middle + scale * (weighted - first - unit * second)

    me = lax.axis_index("tensor")
    sums = sums.reshape(-1, width).astype(jnp.float32)
    return (
        result,
        in_grad,
        gains[2 + parts],
        sums[hidden + width + head_width :].T,
        lax.dynamic_slice_in_dim(gains[1], me * head_width, head_width),
        sums[hidden + width : hidden + width + head_width],
        gains[0],
        sums[hidden : hidden + width],
        lax.dynamic_index_in_dim(gains, 2 + me, 0, keepdims=False),
        sums[:hidden],
    )


def solution(mesh):
    return jax.shard_map(
        local,
        mesh=mesh,
        in_specs=(
            P(("dp", "tensor"), None),
            P("dp", None),
            P(),
            P(None, "tensor"),
            P("tensor"),
            P("tensor", None),
            P(),
            P(None, "tensor"),
            P("tensor"),
            P("tensor", None),
            P(("dp", "tensor"), None),
        ),
        out_specs=(
            P(("dp", "tensor"), None),
            P(("dp", "tensor"), None),
            P(),
            P(None, "tensor"),
            P("tensor"),
            P("tensor", None),
            P(),
            P(None, "tensor"),
            P("tensor"),
            P("tensor", None),
        ),
        check_vma=False,
    )
```

```python
from functools import partial

import jax
import jax.numpy as jnp
from jax import lax
from jax.experimental import pallas as pl
from jax.experimental.pallas import tpu as pltpu
from jax.sharding import PartitionSpec as P

HEAD_DIM = 64
UNIT = 64
EPS = 1e-05


def contract_rows(left, right):
    return lax.dot_general(
        left, right, (((0,), (0,)), ((), ())), preferred_element_type=jnp.float32
    )


def contract_cols(left, right):
    return lax.dot_general(
        left, right, (((1,), (1,)), ((), ())), preferred_element_type=jnp.float32
    )


NEG = -1e30


def seq_bounds(len_ref):
    ends, total = [], 0
    for s in range(len_ref.shape[1]):
        total = total + len_ref[0, s] * UNIT
        ends.append(total)
    return ends


def start_of(ends, row):
    at = 0
    for end in ends:
        at = jnp.where(row >= end, end, at)
    return at


def end_of(ends, row):
    at = ends[-1]
    for end in reversed(ends):
        at = jnp.where(row < end, end, at)
    return at


def dot(a, b):
    return lax.dot_general(a, b, (((1,), (0,)), ((), ())), preferred_element_type=jnp.float32)


MESH = pl.DeviceIdType.MESH


def flip(index, bit):
    return index + bit - 2 * bit * ((index // bit) % 2)


def peers_of(parts, groups):
    steps, bit = [], 1
    while bit < parts:
        steps.append(("tensor", bit))
        bit *= 2
    bit = 1
    while bit < groups:
        steps.append(("dp", bit))
        bit *= 2
    return steps


def at_peer(axis, bit):
    at, low = lax.axis_index(axis), 1
    while low <= bit:
        if bit & low:
            at = flip(at, low)
        low *= 2
    return {axis: at}


def greet(steps, *more):
    barrier = pltpu.get_barrier_semaphore()
    for axis, bit in steps:
        pl.semaphore_signal(barrier, inc=1, device_id=at_peer(axis, bit), device_id_type=MESH)
    for peer in more:
        pl.semaphore_signal(barrier, inc=1, device_id={"tensor": peer}, device_id_type=MESH)
    pl.semaphore_wait(barrier, len(steps) + len(more))


def remote(src, dst, send, recv, axis, bit):
    copy = pltpu.make_async_remote_copy(
        src_ref=src,
        dst_ref=dst,
        send_sem=send,
        recv_sem=recv,
        device_id=at_peer(axis, bit),
        device_id_type=MESH,
    )
    copy.start()
    return copy


def rounded(values):
    return values.astype(jnp.bfloat16)


def spread(me):
    return flip(me, 1), flip(me, 2), flip(flip(me, 1), 2)


def dot_nt(a, b):
    return lax.dot_general(a, b, (((1,), (1,)), ((), ())), preferred_element_type=jnp.float32)


def dot_tn(a, b):
    return lax.dot_general(a, b, (((0,), (0,)), ((), ())), preferred_element_type=jnp.float32)


GELU_A = 0.7978845608028654
GELU_B = 0.044715


def rows_kernel(tile, att_ref, tok_ref, og_ref, gain_ref, w_hbm,
                res_ref, gm_ref, datt_ref, g_hbm, gsum_ref,
                wout, wup, wdown, x_s, mid_s, low_att, low_mid, act_s, slope_s, wide_s, low_act, big_s, acc_s,
                mu_s, rs_s, mu4_s, rs4_s, one_s, two_s, stage, w_sem, g_sem):
    parts, rows, head_width = att_ref.shape
    width = tok_ref.shape[1]
    hidden = width * parts
    n_tiles = rows // tile
    f32 = jnp.float32

    loads = []
    for t in range(parts):
        loads.append(
            pltpu.make_async_copy(
                w_hbm.at[t, pl.ds(2 * width, head_width), :],
                wout.at[pl.ds(t * head_width, head_width), :],
                w_sem.at[2 * parts + t],
            )
        )
    for t in range(parts):
        loads.append(pltpu.make_async_copy(w_hbm.at[t, pl.ds(width, width), :], wup.at[t], w_sem.at[t]))
    for t in range(parts):
        loads.append(pltpu.make_async_copy(w_hbm.at[t, pl.ds(0, width), :], wdown.at[t], w_sem.at[parts + t]))
    for copy in loads:
        copy.start()

    def at(i):
        return pl.ds(pl.multiple_of(i * tile, tile), tile)

    def fold(v):
        return jnp.sum(v.reshape(tile // 8, 8, width), axis=0)

    def tiles(body, init=0):
        return lax.fori_loop(0, n_tiles, body, init)

    def stats(v, n):
        mu = jnp.sum(v, axis=1, keepdims=True) / n
        ms = jnp.sum(v * v, axis=1, keepdims=True) / n
        return mu, lax.rsqrt(ms - mu * mu + EPS)

    def save(slot, block, shard, row, n):
        copy = pltpu.make_async_copy(
            stage.at[slot, pl.ds(0, n), :], g_hbm.at[shard, pl.ds(row, n), :], g_sem.at[slot]
        )
        return copy

    again = jnp.concatenate([gain_ref[t, 2:3, :head_width] for t in range(parts)], axis=1)
    fgain = gain_ref[0, 1:2, :]

    def first(i, _):
        v = jnp.concatenate([att_ref[t, at(i), :] for t in range(parts)], axis=1).astype(f32)
        x_s[at(i), :] = v
        mu, rs = stats(v, width)
        mu_s[at(i), :] = mu
        rs_s[at(i), :] = rs
        low_att[at(i), :] = ((v - mu) * rs * again).astype(jnp.bfloat16)
        return 0

    tiles(first)
    for copy in loads[:parts]:
        copy.wait()
    big_s[...] = jnp.dot(low_att[...], wout[...], preferred_element_type=f32)

    def second(i, _):
        v = tok_ref[at(i), :].astype(f32) + big_s[at(i), :]
        mid_s[at(i), :] = v
        mu, rs = stats(v, width)
        low_mid[at(i), :] = ((v - mu) * rs * fgain).astype(jnp.bfloat16)
        one_s[at(i), :] = jnp.zeros((tile, 1), f32)
        two_s[at(i), :] = jnp.zeros((tile, 1), f32)
        acc_s[at(i), :] = v
        return 0

    tiles(second)

    for copy in loads[parts:]:
        copy.wait()

    def up_block(t, _):
        big_s[...] = jnp.dot(low_mid[...], wup[t], preferred_element_type=f32)

        def body(i, _):
            v = big_s[at(i), :]
            sq = v * v
            th = jnp.tanh(v * (GELU_A + (GELU_A * GELU_B) * sq))
            half = 0.5 * th + 0.5
            act = v * half
            act_s[t, at(i), :] = act
            slope = half + (0.5 * v) * (1.0 - th * th) * (GELU_A + (3.0 * GELU_A * GELU_B) * sq)
            slope_s[t, at(i), :] = slope.astype(jnp.bfloat16)
            one_s[at(i), :] += jnp.sum(act, axis=1, keepdims=True)
            two_s[at(i), :] += jnp.sum(act * act, axis=1, keepdims=True)
            return 0

        tiles(body)
        return 0

    lax.fori_loop(0, parts, up_block, 0)

    def third(i, _):
        mu = one_s[at(i), :] / hidden
        mu4_s[at(i), :] = mu
        rs4_s[at(i), :] = lax.rsqrt(two_s[at(i), :] / hidden - mu * mu + EPS)
        one_s[at(i), :] = jnp.zeros((tile, 1), f32)
        two_s[at(i), :] = jnp.zeros((tile, 1), f32)
        return 0

    tiles(third)

    def down_block(t, _):
        hg = gain_ref[t, 3:4, :]
        big_s[...] = dot_nt(og_ref[...], wdown[t])

        def body(i, part):
            unit = (act_s[t, at(i), :] - mu4_s[at(i), :]) * rs4_s[at(i), :]
            act_s[t, at(i), :] = unit
            low_act[at(i), :] = (unit * hg).astype(jnp.bfloat16)
            d4 = big_s[at(i), :]
            wide = d4 * hg
            wide_s[t, at(i), :] = wide
            one_s[at(i), :] += jnp.sum(wide, axis=1, keepdims=True)
            two_s[at(i), :] += jnp.sum(wide * unit, axis=1, keepdims=True)
            return part + fold(d4 * unit)

        part = tiles(body, jnp.zeros((8, width), f32))
        gsum_ref[pl.ds(2 + t, 1), :] = jnp.sum(part, axis=0, keepdims=True)
        acc_s[...] += jnp.dot(low_act[...], wdown[t], preferred_element_type=f32)
        slot = t % 2

        @pl.when(t >= 2)
        def _():
            save(slot, None, t, 0, width).wait()

        stage[slot] = dot_tn(low_act[...], og_ref[...]).astype(jnp.bfloat16)
        save(slot, None, t, 0, width).start()
        return 0

    lax.fori_loop(0, parts, down_block, 0)

    def fourth(i, _):
        res_ref[at(i), :] = acc_s[at(i), :].astype(jnp.bfloat16)
        one_s[at(i), :] = one_s[at(i), :] / hidden
        two_s[at(i), :] = two_s[at(i), :] / hidden
        acc_s[at(i), :] = jnp.zeros((tile, width), f32)
        return 0

    tiles(fourth)

    def back_block(t, _):
        def body(i, _):
            d_act = rs4_s[at(i), :] * (wide_s[t, at(i), :] - one_s[at(i), :] - act_s[t, at(i), :] * two_s[at(i), :])
            low_act[at(i), :] = (d_act * slope_s[t, at(i), :].astype(f32)).astype(jnp.bfloat16)
            return 0

        tiles(body)
        acc_s[...] += dot_nt(low_act[...], wup[t])
        slot = t % 2
        save(slot, None, t, 0, width).wait()
        stage[slot] = dot_tn(low_mid[...], low_act[...]).astype(jnp.bfloat16)
        save(slot, None, t, width, width).start()
        return 0

    lax.fori_loop(0, parts, back_block, 0)

    def fifth(i, part):
        v = mid_s[at(i), :]
        mu, rs = stats(v, width)
        unit = (v - mu) * rs
        d3 = acc_s[at(i), :]
        wide = d3 * fgain
        m1 = jnp.sum(wide, axis=1, keepdims=True) / width
        m2 = jnp.sum(wide * unit, axis=1, keepdims=True) / width
        d_mid = og_ref[at(i), :].astype(f32) + rs * (wide - m1 - unit * m2)
        gm_ref[at(i), :] = d_mid
        low_act[at(i), :] = d_mid.astype(jnp.bfloat16)
        return part + fold(d3 * unit)

    part = tiles(fifth, jnp.zeros((8, width), f32))
    gsum_ref[0:1, :] = jnp.sum(part, axis=0, keepdims=True)
    big_s[...] = dot_nt(low_act[...], wout[...])
    for slot in range(2):
        save(slot, None, slot, width, width).wait()
    stage[0] = dot_tn(low_att[...], low_act[...]).astype(jnp.bfloat16)
    last = []
    for t in range(parts):
        copy = pltpu.make_async_copy(
            stage.at[0, pl.ds(t * head_width, head_width), :],
            g_hbm.at[t, pl.ds(2 * width, head_width), :],
            w_sem.at[t],
        )
        copy.start()
        last.append(copy)

    def sixth(i, part):
        mu, rs = mu_s[at(i), :], rs_s[at(i), :]
        unit = (x_s[at(i), :] - mu) * rs
        d2 = big_s[at(i), :]
        wide = d2 * again
        m1 = jnp.sum(wide, axis=1, keepdims=True) / width
        m2 = jnp.sum(wide * unit, axis=1, keepdims=True) / width
        d_att = (rs * (wide - m1 - unit * m2)).astype(jnp.bfloat16)
        for t in range(parts):
            datt_ref[t, at(i), :] = d_att[:, t * head_width : (t + 1) * head_width]
        return part + fold(d2 * unit)

    part = tiles(sixth, jnp.zeros((8, width), f32))
    gsum_ref[1:2, :] = jnp.sum(part, axis=0, keepdims=True)
    gsum_ref[pl.ds(2 + parts, 8 - 2 - parts), :] = jnp.zeros((8 - 2 - parts, width), f32)
    for copy in last:
        copy.wait()


def rows_pass(att, tokens, out_grad, gains, weights, tile):
    parts, rows, head_width = att.shape
    width = tokens.shape[1]
    bf16, f32 = jnp.bfloat16, jnp.float32
    vmem = pl.BlockSpec(memory_space=pltpu.VMEM)
    anywhere = pl.BlockSpec(memory_space=pl.ANY)
    column = pltpu.VMEM((rows, 1), f32)
    return pl.pallas_call(
        partial(rows_kernel, tile),
        out_shape=(
            jax.ShapeDtypeStruct((rows, width), bf16),
            jax.ShapeDtypeStruct((rows, width), f32),
            jax.ShapeDtypeStruct(att.shape, bf16),
            jax.ShapeDtypeStruct((parts, 2 * width + head_width, width), bf16),
            jax.ShapeDtypeStruct((8, width), f32),
        ),
        in_specs=[vmem] * 4 + [anywhere],
        out_specs=[vmem] * 3 + [anywhere, vmem],
        scratch_shapes=[
            pltpu.VMEM((width, width), bf16),
            pltpu.VMEM((parts, width, width), bf16),
            pltpu.VMEM((parts, width, width), bf16),
            pltpu.VMEM((rows, width), f32),
            pltpu.VMEM((rows, width), f32),
            pltpu.VMEM((rows, width), bf16),
            pltpu.VMEM((rows, width), bf16),
            pltpu.VMEM((parts, rows, width), f32),
            pltpu.VMEM((parts, rows, width), bf16),
            pltpu.VMEM((parts, rows, width), f32),
            pltpu.VMEM((rows, width), bf16),
            pltpu.VMEM((rows, width), f32),
            pltpu.VMEM((rows, width), f32),
        ] + [column] * 6 + [
            pltpu.VMEM((2, width, width), bf16),
            pltpu.SemaphoreType.DMA((3 * parts,)),
            pltpu.SemaphoreType.DMA((2,)),
        ],
        compiler_params=pltpu.CompilerParams(vmem_limit_bytes=60 << 20),
        cost_estimate=pl.CostEstimate(flops=20 * 10**9, bytes_accessed=40 << 20, transcendentals=2 * 10**6),
        name="rows_pass",
    )(att, tokens, out_grad, gains, weights)


def front_kernel(groups, pieces, chunk, len_ref, tok_ref, w_ref, own_gain_ref, down_ref, up_ref, out_ref,
                 all_ref, packed_ref, gains_ref, att_ref, own_ref, lse_ref, full_ref,
                 k_s, qt_s, vt_s, acc_s, m_s, shard_s,
                 send, recv, gain_send, gain_recv, w_send, w_recv, w_load, w_local, a_send, a_recv, a_local):
    f32, bf16 = jnp.float32, jnp.bfloat16
    me, dp = lax.axis_index("tensor"), lax.axis_index("dp")
    core, chip, cross = spread(me)
    b0, b1, b2 = dp % 2, (dp // 2) % 2, (dp // 4) % 2
    rows, width = tok_ref.shape
    heads = k_s.shape[0]
    parts = all_ref.shape[0]
    piece = rows // pieces
    ends = seq_bounds(len_ref)
    half, rows2, rows4 = width // 2, chunk // 2, chunk // 4

    chunks = []
    for ref in (down_ref, up_ref, out_ref):
        for at in range(0, ref.shape[0], chunk):
            chunks.append((ref, at, len(chunks) * chunk))
    n = len(chunks)

    def load_weight(c):
        ref, at, _ = chunks[c]
        return pltpu.make_async_copy(ref.at[pl.ds(at, chunk), :], shard_s.at[c], w_load.at[c])

    for c in range(n):
        load_weight(c).start()
    values = tok_ref[...].astype(f32)
    mu = jnp.sum(values, axis=1, keepdims=True) / width
    ms = jnp.sum(values * values, axis=1, keepdims=True) / width
    all_ref[me] = ((values - mu) * lax.rsqrt(ms - mu * mu + EPS) * own_gain_ref[0:1, :]).astype(bf16)
    gains_ref[me] = own_gain_ref[...]
    greet([("dp", 1), ("dp", 2), ("dp", 4)], core, chip, cross)

    def to_peer(src, dst, ssem, rsem, where):
        return pltpu.make_async_remote_copy(
            src_ref=src, dst_ref=dst, send_sem=ssem, recv_sem=rsem, device_id=where, device_id_type=MESH
        )

    def block(c, owner):
        return all_ref.at[owner, pl.ds(pl.multiple_of(c * piece, piece), piece), :]

    def to_chip(c):
        return to_peer(block(c, me), block(c, me), send.at[c], recv.at[c], {"tensor": chip})

    def to_far(c):
        return to_peer(block(c, chip), block(c, chip), send.at[pieces + c], recv.at[pieces + c], {"tensor": core})

    def to_core():
        return to_peer(all_ref.at[me], all_ref.at[me], send.at[2 * pieces], recv.at[2 * pieces], {"tensor": core})

    def gain_copy(k):
        owner, peer = ((me, chip), (me, core), (chip, core))[k]
        return to_peer(gains_ref.at[owner], gains_ref.at[owner], gain_send.at[k], gain_recv.at[k], {"tensor": peer})

    to_core().start()
    gain_copy(0).start()
    gain_copy(1).start()

    def spot(shard, c, row0, size, col0, span):
        row = chunks[c][2] + row0
        return full_ref.at[shard, pl.ds(pl.multiple_of(row, 16), size), pl.ds(pl.multiple_of(col0, 128), span)]

    def weight_copy(c, s):
        row4, row2, col = b1 * rows2 + b2 * rows4, b1 * rows2, b0 * half
        if s == 0:
            src = shard_s.at[c, pl.ds(pl.multiple_of(row4, 16), rows4), pl.ds(pl.multiple_of(col, 128), half)]
            dst, where = spot(me, c, row4, rows4, col, half), {"tensor": chip}
        elif s == 1:
            src = dst = spot(chip, c, row4, rows4, col, half)
            where = at_peer("dp", 4)
        elif s == 2:
            src = dst = spot(chip, c, row2, rows2, col, half)
            where = at_peer("dp", 2)
        elif s == 3:
            src = dst = spot(chip, c, 0, chunk, col, half)
            where = at_peer("dp", 1)
        elif s == 4:
            src = dst = spot(chip, c, 0, chunk, 0, width)
            where = {"tensor": core}
        else:
            src = shard_s.at[c]
            dst, where = spot(me, c, 0, chunk, 0, width), {"tensor": core}
        return to_peer(src, dst, w_send.at[c, s], w_recv.at[c, s], where)

    def own_weight(c):
        return pltpu.make_async_copy(shard_s.at[c], spot(me, c, 0, chunk, 0, width), w_local.at[c])

    order = list(reversed(range(n)))
    batches = [order[: n // 3], order[n // 3 : 2 * n // 3], order[2 * n // 3 :]]

    def weights(batch, s):
        for c in batches[batch]:
            if s:
                weight_copy(c, s - 1).wait_recv()
            if s < 5:
                weight_copy(c, s).start()

    scale = jnp.bfloat16(0.125)
    ones = (lax.broadcasted_iota(jnp.int32, (16, piece), 0) == 0).astype(f32).astype(bf16)

    def project(owner, c):
        span = pl.ds(pl.multiple_of(c * piece, piece), piece)
        at = pl.ds(pl.multiple_of(owner * rows + c * piece, piece), piece)
        x = dot_nt(all_ref[owner, span, :], w_ref[...]).astype(bf16)
        packed_ref[owner, span, :] = x
        for h in range(heads):
            base = h * 3 * HEAD_DIM
            qt_s[h, :, at] = (x[:, base : base + HEAD_DIM] * scale).T
            k_s[h, at, :] = x[:, base + HEAD_DIM : base + 2 * HEAD_DIM]
            vt_s[h, :HEAD_DIM, at] = x[:, base + 2 * HEAD_DIM : base + 3 * HEAD_DIM].T
            vt_s[h, HEAD_DIM:, at] = ones

    def loop(body):
        def one(c, _):
            body(c)
            return 0

        lax.fori_loop(0, pieces, one, 0)

    for c in range(n):
        load_weight(c).wait()
    weights(0, 0)
    to_chip(0).start()
    to_chip(1).start()
    weights(1, 0)
    for c in range(2, pieces):
        to_chip(c).start()
    weights(2, 0)
    loop(lambda c: project(me, c))
    to_core().wait_recv()
    loop(lambda c: project(core, c))
    for c in order:
        weight_copy(c, 5).start()
        own_weight(c).start()

    early = ([(0, 1)], [(0, 2)], [(1, 1), (0, 3)], [(1, 2)], [(1, 3), (0, 4)])
    for c in range(pieces):
        to_chip(c).wait_recv()
        to_far(c).start()
        project(chip, c)
        for event in early[c] if c < len(early) else ():
            weights(*event)
    gain_copy(0).wait_recv()
    gain_copy(2).start()

    def from_far(c):
        to_far(c).wait_recv()
        project(cross, c)

    loop(from_far)
    weights(2, 1)

    def attend(o, later):
        first = o * rows
        at = pl.ds(first, rows)
        q_pos = first + lax.broadcasted_iota(jnp.int32, (1, rows), 1)
        q_start = start_of(ends, q_pos)
        for h in range(heads):
            acc_s[h] = jnp.zeros_like(acc_s[h])
            m_s[h] = jnp.full_like(m_s[h], NEG)

        def step(j, _):
            k0 = pl.multiple_of(j * rows, rows)
            kat = pl.ds(k0, rows)
            k_pos = k0 + lax.broadcasted_iota(jnp.int32, (rows, 1), 0)
            keep = (k_pos <= q_pos) & (k_pos >= q_start)
            for h in range(heads):
                s = jnp.where(keep, dot(k_s[h, kat, :], qt_s[h, :, at]), NEG)
                old = m_s[h]
                new = jnp.maximum(old, jnp.max(s, axis=0, keepdims=True))
                p = jnp.exp(s - new).astype(bf16)
                m_s[h] = new
                acc_s[h] = acc_s[h] * jnp.exp(old - new) + dot(vt_s[h, :, kat], p)
            return 0

        done = 0
        for stop, events in later:
            if stop > done:
                lax.fori_loop(done, stop, step, 0)
            for event in events:
                weights(*event)
            done = stop
        lax.fori_loop(done, o + 1, step, 0)
        outs = []
        for h in range(heads):
            acc = acc_s[h]
            total = acc[HEAD_DIM : HEAD_DIM + 1, :]
            outs.append((acc[:HEAD_DIM, :] / total).T)
            lse_ref[h : h + 1, at] = m_s[h] + jnp.log(total)
        att_ref[o] = jnp.concatenate(outs, axis=1).astype(bf16)

    def give(k):
        peer = (core, chip, cross)[k]
        return to_peer(att_ref.at[peer], own_ref.at[me], a_send.at[k], a_recv.at[k], {"tensor": peer})

    def keep_own():
        return pltpu.make_async_copy(att_ref.at[me], own_ref.at[me], a_local)

    plans = ([], [(0, [(2, 2)]), (1, [(1, 4), (2, 3)])], [(2, [(2, 4)])], [])
    for o in range(parts):
        attend(o, plans[o])

        for k, peer in enumerate((core, chip, cross)):

            @pl.when(peer == o)
            def _(k=k):
                give(k).start()

        @pl.when(me == o)
        def _():
            keep_own().start()

    gain_copy(1).wait_recv()
    gain_copy(2).wait_recv()
    for batch in range(3):
        weights(batch, 5)
    for c in order:
        weight_copy(c, 5).wait_recv()
        own_weight(c).wait()
    keep_own().wait()
    for k in range(3):
        give(k).wait()
    for c in range(pieces):
        to_chip(c).wait_send()
        to_far(c).wait_send()
    to_core().wait_send()
    for k in range(3):
        gain_copy(k).wait_send()
    for c in order:
        for s in range(6):
            weight_copy(c, s).wait_send()


def front_pass(groups, lengths, tokens, weight, own_gains, w_down, w_up, w_out, pieces=5, chunk=192):
    rows, width = tokens.shape
    heads = weight.shape[0] // (3 * HEAD_DIM)
    parts = 4
    total = parts * rows
    n = (w_down.shape[0] + w_up.shape[0] + w_out.shape[0]) // chunk
    bf16, f32 = jnp.bfloat16, jnp.float32
    vmem, anywhere = pl.BlockSpec(memory_space=pltpu.VMEM), pl.BlockSpec(memory_space=pl.ANY)
    sems = pltpu.SemaphoreType.DMA
    shape = jax.ShapeDtypeStruct
    return pl.pallas_call(
        partial(front_kernel, groups, pieces, chunk),
        out_shape=(
            shape((parts, rows, width), bf16),
            shape((parts, rows, weight.shape[0]), bf16),
            shape((parts,) + own_gains.shape, f32),
            shape((parts, rows, heads * HEAD_DIM), bf16),
            shape((parts, rows, heads * HEAD_DIM), bf16),
            shape((8, total), f32),
            shape((parts, n * chunk, width), bf16),
        ),
        in_specs=[pl.BlockSpec(memory_space=pltpu.SMEM)] + [vmem] * 3 + [anywhere] * 3,
        out_specs=[vmem] * 6 + [anywhere],
        scratch_shapes=[
            pltpu.VMEM((heads, total, HEAD_DIM), bf16),
            pltpu.VMEM((heads, HEAD_DIM, total), bf16),
            pltpu.VMEM((heads, HEAD_DIM + 16, total), bf16),
            pltpu.VMEM((heads, HEAD_DIM + 16, rows), f32),
            pltpu.VMEM((heads, 1, rows), f32),
            pltpu.VMEM((n, chunk, width), bf16),
            sems((2 * pieces + 1,)),
            sems((2 * pieces + 1,)),
            sems((3,)),
            sems((3,)),
            sems((n, 6)),
            sems((n, 6)),
            sems((n,)),
            sems((n,)),
            sems((3,)),
            sems((3,)),
            sems,
        ],
        compiler_params=pltpu.CompilerParams(
            collective_id=1, has_side_effects=True, vmem_limit_bytes=56 << 20
        ),
        name="front_pass",
    )(lengths, tokens, weight, own_gains, w_down, w_up, w_out)


def chunk_copy(c, s, src, dst, send, recv, axis, bit):
    return pltpu.make_async_remote_copy(
        src_ref=src,
        dst_ref=dst,
        send_sem=send.at[c, s],
        recv_sem=recv.at[c, s],
        device_id=at_peer(axis, bit),
        device_id_type=MESH,
    )


def back_kernel(groups, chunk, block, pieces, len_ref, datt_ref, packed_ref, att_ref, lse_ref, grads_ref,
                h1_ref, w_ref, gains_ref, gain_ref,
                sum_ref, in_sum, gains_sum,
                pq, do_s, own, first, second, acc, to_y, to_x, from_x, to_z, from_z, more_to, more_from,
                send, recv, local_sem, a2a_send, a2a_recv, a2a_local,
                d_first, d_second, d_send, d_recv, gain_at, gain_send, gain_recv, load_sem):
    f32, bf16 = jnp.float32, jnp.bfloat16
    steps = peers_of(4, groups)
    far = steps[5:]
    me, dp = lax.axis_index("tensor"), lax.axis_index("dp")
    core, chip, cross = spread(me)
    cols = grads_ref.shape[2]
    half, rows2, rows4 = cols // 2, chunk // 2, chunk // 4
    b0, b1, b2 = dp % 2, (dp // 2) % 2, (dp // 4) % 2
    n = grads_ref.shape[1] // chunk

    def take(c, shard):
        return grads_ref.at[shard, pl.ds(pl.multiple_of(c * chunk, 16), chunk), :]

    def col(b):
        return pl.ds(pl.multiple_of(b * half, 128), half)

    def row2(b):
        return pl.ds(pl.multiple_of(b * rows2, 16), rows2)

    def row4(b, bb):
        return pl.ds(pl.multiple_of(b * rows2 + bb * rows4, 16), rows4)

    def copy(c, s):
        if s == 0:
            return chunk_copy(c, 0, take(c, core), first.at[c, 0], send, recv, "tensor", 1)
        if s == 1:
            return chunk_copy(c, 1, take(c, cross), first.at[c, 1], send, recv, "tensor", 1)
        if s == 2:
            return chunk_copy(c, 2, to_y.at[c % 3], second.at[c], send, recv, "tensor", 2)
        if s == 3:
            slot = 3 + c - n if isinstance(c, int) and c >= n else c % 3
            return chunk_copy(c, 3, to_x.at[slot], from_x.at[c], send, recv, "dp", 1)
        if s in (4, 5, 6):
            return chunk_copy(c, s, to_z.at[c, s - 4], from_z.at[c, s - 4], send, recv, "dp", 2 * (s - 3))
        if s in (7, 8, 9):
            piece = sum_ref.at[c, row4(b1, b2), col(b0)]
            return chunk_copy(c, s, piece, piece, send, recv, "dp", 2 * (s - 6))
        if s == 10:
            piece = sum_ref.at[c, :, col(b0)]
            return chunk_copy(c, 10, piece, piece, send, recv, "dp", 1)
        axis, bit = far[s - 11]
        return chunk_copy(c, s, more_to.at[c, s - 11], more_from.at[c, s - 11], send, recv, axis, bit)

    def other4(m):
        return row4(b1 + (m % 2) * (1 - 2 * b1), b2 + (m // 2) * (1 - 2 * b2))

    def arrived(c, s, piece=None):
        if piece is None:
            copy(c, s).wait_recv()
        else:
            bit = 1 if s == 10 else 2 * (s - 6)
            chunk_copy(c, s, piece, piece, send, recv, "dp", bit).wait_recv()

    def mine(c, k):
        shard = (me, chip)[k]
        return pltpu.make_async_copy(take(c, shard), own.at[c % 4, k], local_sem.at[c % 4, k])

    def pair(c):
        copy(c, 1).start()
        copy(c, 0).start()
        mine(c, 1).start()
        mine(c, 0).start()

    def to_chip(c):
        @pl.when(c >= 3)
        def _():
            copy(c - 3, 2).wait_send()

        mine(c, 1).wait()
        arrived(c, 1)
        to_y[c % 3] = rounded(own[c % 4, 1].astype(f32) + first[c, 1].astype(f32))
        copy(c, 2).start()

    def x_half(c):
        @pl.when(c >= 3)
        def _():
            copy(c - 3, 3).wait_send()

        mine(c, 0).wait()
        arrived(c, 0)
        arrived(c, 2)

        def total(b):
            whole = own[c % 4, 0, :, col(b)].astype(f32) + first[c, 0, :, col(b)].astype(f32)
            return whole + second[c, :, col(b)].astype(f32)

        to_x[c % 3] = rounded(total(1 - b0))
        copy(c, 3).start()
        acc[c] = total(b0)

    def z_all(c):
        arrived(c, 3)
        acc[c] += from_x[c].astype(f32)
        for m in (3, 1, 2):
            to_z[c, m - 1] = rounded(acc[c, other4(m), :])
            copy(c, 3 + m).start()

    def settle(c):
        total = acc[c, row4(b1, b2), :]
        for m in (1, 2, 3):
            arrived(c, 3 + m)
            total = total + from_z[c, m - 1].astype(f32)
        for m in range(len(far)):
            more_to[c, m] = rounded(total)
            copy(c, 11 + m).start()
            arrived(c, 11 + m)
            total = rounded(total).astype(f32) + more_from[c, m].astype(f32)
        sum_ref[c, row4(b1, b2), col(b0)] = rounded(total)
        for m in (3, 1, 2):
            copy(c, 6 + m).start()

    def x_share(c):
        for m in (1, 2, 3):
            arrived(c, 6 + m, sum_ref.at[c, other4(m), col(b0)])
        copy(c, 10).start()

    def end(c):
        arrived(c, 10, sum_ref.at[c, :, col(1 - b0)])

    stages = (pair, to_chip, x_half, z_all, settle, x_share, end)
    lags = (0, 1, 3, 4, 5, 6, 7)

    def turn(at):
        for s, lag in enumerate(lags):
            c = at - lag

            @pl.when((c >= 0) & (c < n))
            def _():
                stages[s](c)

    rows = packed_ref.shape[0]
    heads = packed_ref.shape[1] // (3 * HEAD_DIM)
    own_rows = datt_ref.shape[1]
    width = h1_ref.shape[1]
    ends = seq_bounds(len_ref)
    scale = jnp.bfloat16(0.125)
    load = pltpu.make_async_copy(packed_ref, pq, load_sem.at[0])
    load.start()
    greet(steps + [("dp", 6)], cross)

    def a2a(k, peer):
        return pltpu.make_async_remote_copy(
            src_ref=datt_ref.at[peer],
            dst_ref=do_s.at[me],
            send_sem=a2a_send.at[k],
            recv_sem=a2a_recv.at[k],
            device_id={"tensor": peer},
            device_id_type=MESH,
        )

    moves = [a2a(k, peer) for k, peer in reversed(list(enumerate((core, chip, cross))))]
    for move in moves:
        move.start()
    keep_own = pltpu.make_async_copy(datt_ref.at[me], do_s.at[me], a2a_local)
    keep_own.start()
    turn(jnp.int32(0))
    load.wait()

    def attention(kv_s, q_s, g_s, qt_s, gt_s, kt_s, d_s, dqt_s, acc_kv):
        def stage_qkv(i, _):
            at = pl.ds(pl.multiple_of(i * 256, 256), 256)
            x = pq[at, :]
            blank = jnp.zeros((256, HEAD_DIM), bf16)
            blank_t = jnp.zeros((HEAD_DIM, 256), bf16)
            for h in range(heads):
                base = h * 3 * HEAD_DIM
                q = x[:, base : base + HEAD_DIM] * scale
                k = x[:, base + HEAD_DIM : base + 2 * HEAD_DIM]
                v = x[:, base + 2 * HEAD_DIM : base + 3 * HEAD_DIM]
                kv_s[h, at, :] = jnp.concatenate([k, v], axis=1)
                q_s[h, at, :] = jnp.concatenate([q, blank], axis=1)
                qt_s[h, :HEAD_DIM, at] = q.T
                qt_s[h, HEAD_DIM:, at] = blank_t
                kt_s[h, :, at] = (k * scale).T
                dqt_s[h, :, at] = jnp.zeros((HEAD_DIM, 256), f32)
                acc_kv[h, at, :] = jnp.zeros((256, 2 * HEAD_DIM), f32)
            return 0

        lax.fori_loop(0, rows // 256, stage_qkv, 0)
        keep_own.wait()
        for move in moves:
            move.wait()
        piece = own_rows // 5

        def stage_grad(i, _):
            owner, part = i // 5, i % 5
            inner = pl.ds(pl.multiple_of(part * piece, piece), piece)
            at = pl.ds(pl.multiple_of(owner * own_rows + part * piece, piece), piece)
            g = do_s[owner, inner, :]
            prod = g.astype(f32) * att_ref[at, :].astype(f32)
            blank = jnp.zeros((piece, HEAD_DIM), bf16)
            blank_t = jnp.zeros((HEAD_DIM, piece), bf16)
            for h in range(heads):
                d = g[:, h * HEAD_DIM : (h + 1) * HEAD_DIM]
                g_s[h, at, :] = jnp.concatenate([blank, d], axis=1)
                gt_s[h, HEAD_DIM:, at] = d.T
                gt_s[h, :HEAD_DIM, at] = blank_t
                d_s[h, :, at] = jnp.sum(prod[:, h * HEAD_DIM : (h + 1) * HEAD_DIM].T, axis=0, keepdims=True)
            return 0

        lax.fori_loop(0, rows // piece, stage_grad, 0)

        def body(i, j):
            q0 = pl.multiple_of(i * block, block)
            k0 = pl.multiple_of(j * block, block)
            at, kat = pl.ds(q0, block), pl.ds(k0, block)
            q_pos = q0 + lax.broadcasted_iota(jnp.int32, (1, block), 1)
            q_start = start_of(ends, q_pos)
            k_pos = k0 + lax.broadcasted_iota(jnp.int32, (block, 1), 0)
            keep = (k_pos <= q_pos) & (k_pos >= q_start)
            for h in range(heads):
                kv = kv_s[h, kat, :]
                s = dot(kv, qt_s[h, :, at]) - lse_ref[h : h + 1, at]
                p = jnp.exp(jnp.where(keep, s, NEG))
                dp_t = dot(kv, gt_s[h, :, at])
                ds = (p * (dp_t - d_s[h, :, at])).astype(bf16)
                acc_kv[h, kat, :] += dot(p.astype(bf16), g_s[h, at, :]) + dot(ds, q_s[h, at, :])
                dqt_s[h, :, at] += dot(kt_s[h, :, kat], ds)

        count = rows // block
        done = 0
        for g in range(count // 2 + 1):
            length = count - g

            def one(p, _, length=length, g=g, done=done):
                wrap = p // length
                i = (length - 1) - wrap * (length - g)
                j = p - wrap * length
                body(i, j)
                b = p + done

                @pl.when(b % 2 == 1)
                def _():
                    turn((b + 1) // 2)

                return 0

            lax.fori_loop(0, count, one, 0)
            done += count

        def finish(i, _):
            at = pl.ds(pl.multiple_of(i * 256, 256), 256)
            parts_of = []
            for h in range(heads):
                parts_of += [dqt_s[h, :, at].T, acc_kv[h, at, :]]
            pq[at, :] = jnp.concatenate(parts_of, axis=1).astype(bf16)
            return 0

        lax.fori_loop(0, rows // 256, finish, 0)

    wide = 2 * HEAD_DIM
    pl.run_scoped(
        attention,
        pltpu.VMEM((heads, rows, wide), bf16),
        pltpu.VMEM((heads, rows, wide), bf16),
        pltpu.VMEM((heads, rows, wide), bf16),
        pltpu.VMEM((heads, wide, rows), bf16),
        pltpu.VMEM((heads, wide, rows), bf16),
        pltpu.VMEM((heads, HEAD_DIM, rows), bf16),
        pltpu.VMEM((heads, 1, rows), f32),
        pltpu.VMEM((heads, HEAD_DIM, rows), f32),
        pltpu.VMEM((heads, rows, wide), f32),
    )
    bodies = (rows // block) * (rows // block + 1) // 2
    next_turn = bodies // 2 + 1
    piece = own_rows // pieces
    parts = rows // own_rows
    extra_chunks = w_ref.shape[0] // chunk

    def closing(h1_s, d1_s, d_to, gq):
        flight, sends = {}, []

        def go(key, src, dst, ssem, rsem, axis, bit):
            flight[key] = remote(src, dst, ssem, rsem, axis, bit)
            sends.append(flight[key])

        def owned(owner):
            return pl.ds(pl.multiple_of(owner * own_rows, own_rows), own_rows)

        fetch = [
            pltpu.make_async_copy(h1_ref.at[pl.ds(t * own_rows, own_rows), :], h1_s.at[t], load_sem.at[1 + t])
            for t in range(parts)
        ]
        for t in fetch:
            t.start()

        def span(c):
            return pl.ds(c * piece, piece)

        def product(slot, owner):
            d1_s[slot] = rounded(dot(pq[owned(owner), :], w_ref[...]))

        def pair_rows(c):
            go(("d", c, 1), d1_s.at[0, span(c)], d_first.at[1, span(c)], d_send.at[c, 1], d_recv.at[c, 1], "tensor", 1)
            go(("d", c, 0), d1_s.at[1, span(c)], d_first.at[0, span(c)], d_send.at[c, 0], d_recv.at[c, 0], "tensor", 1)

        def across(c):
            flight["d", c, 1].wait_recv()
            d_to[span(c)] = rounded(d1_s[2, span(c), :].astype(f32) + d_first[1, span(c), :].astype(f32))
            go(("d", c, 2), d_to.at[span(c)], d_second.at[span(c)], d_send.at[c, 2], d_recv.at[c, 2], "tensor", 2)

        def settle_rows(c):
            flight["d", c, 0].wait_recv()
            flight["d", c, 2].wait_recv()
            near = d1_s[3, span(c), :].astype(f32) + d_first[0, span(c), :].astype(f32)
            in_sum[span(c)] = near + d_second[span(c)].astype(f32)

        def q_x(i):
            rows_of = pl.ds(i * chunk, chunk)
            to_x[3 + i] = rounded(gq[rows_of, col(1 - b0)])
            copy(n + i, 3).start()
            acc[n + i] = gq[rows_of, col(b0)]

        def gain_start(m):
            axis, bit = steps[m]
            go(("g", m), gain_at.at[0, m], gain_at.at[1, m], gain_send.at[m], gain_recv.at[m], axis, bit)

        def gain_step(m):
            flight["g", m].wait_recv()
            now = gain_at[0, m] + gain_at[1, m]
            if m + 1 < len(steps):
                gain_at[0, m + 1] = now
                gain_start(m + 1)
            else:
                gains_sum[...] = now

        last = n + lags[-1]
        turns = iter(range(next_turn, last))

        def main_turn():
            at = next(turns, None)
            if at is not None:
                turn(jnp.int32(at))

        main_turn()
        product(0, cross)
        product(1, core)
        for c in range(pieces):
            pair_rows(c)
        product(2, chip)
        product(3, me)
        main_turn()
        for t in fetch:
            t.wait()
        gq[...] = dot_tn(pq[owned(0), :], h1_s[0])
        for c in range(pieces):
            across(c)
        for t in range(1, parts):
            gq[...] += dot_tn(pq[owned(t), :], h1_s[t])
        for i in range(extra_chunks):
            q_x(i)
        main_turn()
        gain_at[0, 0] = gains_ref[...]
        line = jnp.sum(w_ref[...].astype(f32) * gq[...], axis=0, keepdims=True)
        gain_at[0, 0, 2 + parts : 3 + parts, :] = line / gain_ref[0, 0:1, :]
        gain_start(0)
        q_stages = (z_all, settle, x_share, end)
        settled = gained = 0
        for stage in q_stages:
            for i in range(extra_chunks):
                stage(n + i)
            main_turn()
            if settled < pieces:
                settle_rows(settled)
                settled += 1
            if gained < len(steps):
                gain_step(gained)
                gained += 1
        while settled < pieces:
            settle_rows(settled)
            settled += 1
        while gained < len(steps):
            gain_step(gained)
            gained += 1
        for at in turns:
            turn(jnp.int32(at))
        for each in sends:
            each.wait_send()

    pl.run_scoped(
        closing,
        pltpu.VMEM((parts, own_rows, width), bf16),
        pltpu.VMEM((parts, own_rows, width), bf16),
        pltpu.VMEM((own_rows, width), bf16),
        pltpu.VMEM(w_ref.shape, f32),
    )

    def sent(c, _):
        for s in range(11 + len(far)):
            if s in (2, 3):

                @pl.when(c >= n - 3)
                def _():
                    copy(c, s).wait_send()

            else:
                copy(c, s).wait_send()
        return 0

    lax.fori_loop(0, n, sent, 0)
    for i in range(extra_chunks):
        for s in range(3, 11 + len(far)):
            copy(n + i, s).wait_send()


def back_pass(groups, lengths, grad_att, packed, att, lse, grads, h1, weight, sums, gains,
              chunk=192, block=512, pieces=5):
    rows = packed.shape[0]
    parts, own_rows, head_width = grad_att.shape
    width = grads.shape[2]
    n = grads.shape[1] // chunk
    more = weight.shape[0] // chunk
    steps = len(peers_of(4, groups))
    extra = max(steps - 5, 1)
    bf16 = lambda *shape: pltpu.VMEM(shape, jnp.bfloat16)
    f32 = lambda *shape: pltpu.VMEM(shape, jnp.float32)
    vmem, anywhere = pl.BlockSpec(memory_space=pltpu.VMEM), pl.BlockSpec(memory_space=pl.ANY)
    sems = pltpu.SemaphoreType.DMA
    return pl.pallas_call(
        partial(back_kernel, groups, chunk, block, pieces),
        out_shape=(
            jax.ShapeDtypeStruct((n + more, chunk, width), jnp.bfloat16),
            jax.ShapeDtypeStruct((own_rows, width), jnp.float32),
            jax.ShapeDtypeStruct(sums.shape, jnp.float32),
        ),
        in_specs=[pl.BlockSpec(memory_space=pltpu.SMEM), anywhere, anywhere, vmem, vmem, anywhere,
                  anywhere, vmem, vmem, vmem],
        out_specs=[vmem] * 3,
        scratch_shapes=[
            bf16(rows, packed.shape[1]),
            bf16(parts, own_rows, head_width),
            bf16(4, 2, chunk, width),
            bf16(n, 2, chunk, width),
            bf16(n, chunk, width),
            f32(n + more, chunk, width // 2),
            bf16(3, chunk, width),
            bf16(3 + more, chunk, width // 2),
            bf16(n + more, chunk, width // 2),
            bf16(n + more, 3, chunk // 4, width // 2),
            bf16(n + more, 3, chunk // 4, width // 2),
            bf16(n + more, extra, chunk // 4, width // 2),
            bf16(n + more, extra, chunk // 4, width // 2),
            sems((n + more, 11 + extra)),
            sems((n + more, 11 + extra)),
            sems((4, 2)),
            sems((3,)),
            sems((3,)),
            sems,
            bf16(2, own_rows, width),
            bf16(own_rows, width),
            sems((pieces, 3)),
            sems((pieces, 3)),
            pltpu.VMEM((2, steps) + sums.shape, jnp.float32),
            sems((steps,)),
            sems((steps,)),
            sems((1 + parts,)),
        ],
        compiler_params=pltpu.CompilerParams(
            collective_id=0, has_side_effects=True, vmem_limit_bytes=60 << 20
        ),
        name="back_pass",
    )(lengths, grad_att, packed, att, lse, grads, h1, weight, sums, gains)


def local(
    tokens,
    lengths,
    in_gain,
    qkv_weight,
    attn_gain,
    out_weight,
    ffn_gain,
    up_weight,
    hidden_gain,
    down_weight,
    out_grad,
):
    parts = lax.axis_size("tensor")
    own_rows, width = tokens.shape
    head_width, hidden = attn_gain.shape[0], hidden_gain.shape[0]

    filler = jnp.zeros((width - head_width,), jnp.float32)
    rest = jnp.zeros((4 * width,), jnp.float32)
    own_gains = jnp.concatenate((in_gain, ffn_gain, attn_gain, filler, hidden_gain, rest)).reshape(8, width)
    weight_t = qkv_weight.T
    groups = lax.axis_size("dp")
    gathered_in, packed, gains, attended, own_att, log_total, weights = front_pass(
        groups,
        lengths,
        tokens,
        weight_t,
        own_gains,
        down_weight,
        up_weight,
        out_weight,
    )
    gathered_in = gathered_in.reshape(parts * own_rows, width)
    packed = packed.reshape(parts * own_rows, -1)
    attended = attended.reshape(parts * own_rows, head_width)
    result, grad_middle, grad_att, grads, gain_parts = rows_pass(
        own_att,
        tokens,
        out_grad,
        gains,
        weights,
        own_rows,
    )
    sums, grad_in_normed, gains = back_pass(
        groups,
        lengths,
        grad_att,
        packed,
        attended,
        log_total,
        grads,
        gathered_in,
        weight_t,
        gain_parts,
        gains,
    )

    residual = tokens.astype(jnp.float32)
    mean = jnp.mean(residual, axis=1, keepdims=True)
    square = jnp.mean(residual * residual, axis=1, keepdims=True)
    scale = lax.rsqrt(square - mean * mean + EPS)
    unit = (residual - mean) * scale
    weighted = grad_in_normed * in_gain
    first = jnp.mean(weighted, axis=1, keepdims=True)
    second = jnp.mean(weighted * unit, axis=1, keepdims=True)
    in_grad = grad_middle + scale * (weighted - first - unit * second)

    me = lax.axis_index("tensor")
    sums = sums.reshape(-1, width).astype(jnp.float32)
    return (
        result,
        in_grad,
        gains[2 + parts],
        sums[hidden + width + head_width :].T,
        lax.dynamic_slice_in_dim(gains[1], me * head_width, head_width),
        sums[hidden + width : hidden + width + head_width],
        gains[0],
        sums[hidden : hidden + width],
        lax.dynamic_index_in_dim(gains, 2 + me, 0, keepdims=False),
        sums[:hidden],
    )


def solution(mesh):
    return jax.shard_map(
        local,
        mesh=mesh,
        in_specs=(
            P(("dp", "tensor"), None),
            P("dp", None),
            P(),
            P(None, "tensor"),
            P("tensor"),
            P("tensor", None),
            P(),
            P(None, "tensor"),
            P("tensor"),
            P("tensor", None),
            P(("dp", "tensor"), None),
        ),
        out_specs=(
            P(("dp", "tensor"), None),
            P(("dp", "tensor"), None),
            P(),
            P(None, "tensor"),
            P("tensor"),
            P("tensor", None),
            P(),
            P(None, "tensor"),
            P("tensor"),
            P("tensor", None),
        ),
        check_vma=False,
    )
```

```python
from functools import partial

import jax
import jax.numpy as jnp
from jax import lax
from jax.experimental import pallas as pl
from jax.experimental.pallas import tpu as pltpu
from jax.sharding import PartitionSpec as P

HEAD_DIM = 64
UNIT = 64
EPS = 1e-05


def contract_rows(left, right):
    return lax.dot_general(
        left, right, (((0,), (0,)), ((), ())), preferred_element_type=jnp.float32
    )


def contract_cols(left, right):
    return lax.dot_general(
        left, right, (((1,), (1,)), ((), ())), preferred_element_type=jnp.float32
    )


NEG = -1e30


def seq_bounds(len_ref):
    ends, total = [], 0
    for s in range(len_ref.shape[1]):
        total = total + len_ref[0, s] * UNIT
        ends.append(total)
    return ends


def start_of(ends, row):
    at = 0
    for end in ends:
        at = jnp.where(row >= end, end, at)
    return at


def end_of(ends, row):
    at = ends[-1]
    for end in reversed(ends):
        at = jnp.where(row < end, end, at)
    return at


def dot(a, b):
    return lax.dot_general(a, b, (((1,), (0,)), ((), ())), preferred_element_type=jnp.float32)


MESH = pl.DeviceIdType.MESH


def flip(index, bit):
    return index + bit - 2 * bit * ((index // bit) % 2)


def peers_of(parts, groups):
    steps, bit = [], 1
    while bit < parts:
        steps.append(("tensor", bit))
        bit *= 2
    bit = 1
    while bit < groups:
        steps.append(("dp", bit))
        bit *= 2
    return steps


def at_peer(axis, bit):
    at, low = lax.axis_index(axis), 1
    while low <= bit:
        if bit & low:
            at = flip(at, low)
        low *= 2
    return {axis: at}


def greet(steps, *more):
    barrier = pltpu.get_barrier_semaphore()
    for axis, bit in steps:
        pl.semaphore_signal(barrier, inc=1, device_id=at_peer(axis, bit), device_id_type=MESH)
    for peer in more:
        pl.semaphore_signal(barrier, inc=1, device_id={"tensor": peer}, device_id_type=MESH)
    pl.semaphore_wait(barrier, len(steps) + len(more))


def remote(src, dst, send, recv, axis, bit):
    copy = pltpu.make_async_remote_copy(
        src_ref=src,
        dst_ref=dst,
        send_sem=send,
        recv_sem=recv,
        device_id=at_peer(axis, bit),
        device_id_type=MESH,
    )
    copy.start()
    return copy


def rounded(values):
    return values.astype(jnp.bfloat16)


def spread(me):
    return flip(me, 1), flip(me, 2), flip(flip(me, 1), 2)


def dot_nt(a, b):
    return lax.dot_general(a, b, (((1,), (1,)), ((), ())), preferred_element_type=jnp.float32)


def dot_tn(a, b):
    return lax.dot_general(a, b, (((0,), (0,)), ((), ())), preferred_element_type=jnp.float32)


GELU_A = 0.7978845608028654
GELU_B = 0.044715


def rows_kernel(tile, att_ref, tok_ref, og_ref, gain_ref, w_hbm,
                res_ref, gm_ref, datt_ref, g_hbm, gsum_ref,
                wout, wup, wdown, x_s, mid_s, low_att, low_mid, act_s, slope_s, wide_s, low_act, big_s, acc_s,
                mu_s, rs_s, mu4_s, rs4_s, one_s, two_s, stage, w_sem, g_sem):
    parts, rows, head_width = att_ref.shape
    width = tok_ref.shape[1]
    hidden = width * parts
    n_tiles = rows // tile
    f32 = jnp.float32

    loads = []
    for t in range(parts):
        loads.append(
            pltpu.make_async_copy(
                w_hbm.at[t, pl.ds(2 * width, head_width), :],
                wout.at[pl.ds(t * head_width, head_width), :],
                w_sem.at[2 * parts + t],
            )
        )
    for t in range(parts):
        loads.append(pltpu.make_async_copy(w_hbm.at[t, pl.ds(width, width), :], wup.at[t], w_sem.at[t]))
    for t in range(parts):
        loads.append(pltpu.make_async_copy(w_hbm.at[t, pl.ds(0, width), :], wdown.at[t], w_sem.at[parts + t]))
    for copy in loads:
        copy.start()

    def at(i):
        return pl.ds(pl.multiple_of(i * tile, tile), tile)

    def fold(v):
        return jnp.sum(v.reshape(tile // 8, 8, width), axis=0)

    def tiles(body, init=0):
        return lax.fori_loop(0, n_tiles, body, init)

    def stats(v, n):
        mu = jnp.sum(v, axis=1, keepdims=True) / n
        ms = jnp.sum(v * v, axis=1, keepdims=True) / n
        return mu, lax.rsqrt(ms - mu * mu + EPS)

    def save(slot, block, shard, row, n):
        copy = pltpu.make_async_copy(
            stage.at[slot, pl.ds(0, n), :], g_hbm.at[shard, pl.ds(row, n), :], g_sem.at[slot]
        )
        return copy

    again = jnp.concatenate([gain_ref[t, 2:3, :head_width] for t in range(parts)], axis=1)
    fgain = gain_ref[0, 1:2, :]

    def first(i, _):
        v = jnp.concatenate([att_ref[t, at(i), :] for t in range(parts)], axis=1).astype(f32)
        x_s[at(i), :] = v
        mu, rs = stats(v, width)
        mu_s[at(i), :] = mu
        rs_s[at(i), :] = rs
        low_att[at(i), :] = ((v - mu) * rs * again).astype(jnp.bfloat16)
        return 0

    tiles(first)
    for copy in loads[:parts]:
        copy.wait()
    big_s[...] = jnp.dot(low_att[...], wout[...], preferred_element_type=f32)

    def second(i, _):
        v = tok_ref[at(i), :].astype(f32) + big_s[at(i), :]
        mid_s[at(i), :] = v
        mu, rs = stats(v, width)
        low_mid[at(i), :] = ((v - mu) * rs * fgain).astype(jnp.bfloat16)
        one_s[at(i), :] = jnp.zeros((tile, 1), f32)
        two_s[at(i), :] = jnp.zeros((tile, 1), f32)
        acc_s[at(i), :] = v
        return 0

    tiles(second)

    for copy in loads[parts:]:
        copy.wait()

    def up_block(t, _):
        big_s[...] = jnp.dot(low_mid[...], wup[t], preferred_element_type=f32)

        def body(i, _):
            v = big_s[at(i), :]
            sq = v * v
            th = jnp.tanh(v * (GELU_A + (GELU_A * GELU_B) * sq))
            half = 0.5 * th + 0.5
            act = v * half
            act_s[t, at(i), :] = act
            slope = half + (0.5 * v) * (1.0 - th * th) * (GELU_A + (3.0 * GELU_A * GELU_B) * sq)
            slope_s[t, at(i), :] = slope.astype(jnp.bfloat16)
            one_s[at(i), :] += jnp.sum(act, axis=1, keepdims=True)
            two_s[at(i), :] += jnp.sum(act * act, axis=1, keepdims=True)
            return 0

        tiles(body)
        return 0

    lax.fori_loop(0, parts, up_block, 0)

    def third(i, _):
        mu = one_s[at(i), :] / hidden
        mu4_s[at(i), :] = mu
        rs4_s[at(i), :] = lax.rsqrt(two_s[at(i), :] / hidden - mu * mu + EPS)
        one_s[at(i), :] = jnp.zeros((tile, 1), f32)
        two_s[at(i), :] = jnp.zeros((tile, 1), f32)
        return 0

    tiles(third)

    def down_block(t, _):
        hg = gain_ref[t, 3:4, :]
        big_s[...] = dot_nt(og_ref[...], wdown[t])

        def body(i, part):
            unit = (act_s[t, at(i), :] - mu4_s[at(i), :]) * rs4_s[at(i), :]
            act_s[t, at(i), :] = unit
            low_act[at(i), :] = (unit * hg).astype(jnp.bfloat16)
            d4 = big_s[at(i), :]
            wide = d4 * hg
            wide_s[t, at(i), :] = wide
            one_s[at(i), :] += jnp.sum(wide, axis=1, keepdims=True)
            two_s[at(i), :] += jnp.sum(wide * unit, axis=1, keepdims=True)
            return part + fold(d4 * unit)

        part = tiles(body, jnp.zeros((8, width), f32))
        gsum_ref[pl.ds(2 + t, 1), :] = jnp.sum(part, axis=0, keepdims=True)
        acc_s[...] += jnp.dot(low_act[...], wdown[t], preferred_element_type=f32)
        slot = t % 2

        @pl.when(t >= 2)
        def _():
            save(slot, None, t, 0, width).wait()

        stage[slot] = dot_tn(low_act[...], og_ref[...]).astype(jnp.bfloat16)
        save(slot, None, t, 0, width).start()
        return 0

    lax.fori_loop(0, parts, down_block, 0)

    def fourth(i, _):
        res_ref[at(i), :] = acc_s[at(i), :].astype(jnp.bfloat16)
        one_s[at(i), :] = one_s[at(i), :] / hidden
        two_s[at(i), :] = two_s[at(i), :] / hidden
        acc_s[at(i), :] = jnp.zeros((tile, width), f32)
        return 0

    tiles(fourth)

    def back_block(t, _):
        def body(i, _):
            d_act = rs4_s[at(i), :] * (wide_s[t, at(i), :] - one_s[at(i), :] - act_s[t, at(i), :] * two_s[at(i), :])
            low_act[at(i), :] = (d_act * slope_s[t, at(i), :].astype(f32)).astype(jnp.bfloat16)
            return 0

        tiles(body)
        acc_s[...] += dot_nt(low_act[...], wup[t])
        slot = t % 2
        save(slot, None, t, 0, width).wait()
        stage[slot] = dot_tn(low_mid[...], low_act[...]).astype(jnp.bfloat16)
        save(slot, None, t, width, width).start()
        return 0

    lax.fori_loop(0, parts, back_block, 0)

    def fifth(i, part):
        v = mid_s[at(i), :]
        mu, rs = stats(v, width)
        unit = (v - mu) * rs
        d3 = acc_s[at(i), :]
        wide = d3 * fgain
        m1 = jnp.sum(wide, axis=1, keepdims=True) / width
        m2 = jnp.sum(wide * unit, axis=1, keepdims=True) / width
        d_mid = og_ref[at(i), :].astype(f32) + rs * (wide - m1 - unit * m2)
        gm_ref[at(i), :] = d_mid
        low_act[at(i), :] = d_mid.astype(jnp.bfloat16)
        return part + fold(d3 * unit)

    part = tiles(fifth, jnp.zeros((8, width), f32))
    gsum_ref[0:1, :] = jnp.sum(part, axis=0, keepdims=True)
    big_s[...] = dot_nt(low_act[...], wout[...])
    for slot in range(2):
        save(slot, None, slot, width, width).wait()
    stage[0] = dot_tn(low_att[...], low_act[...]).astype(jnp.bfloat16)
    last = []
    for t in range(parts):
        copy = pltpu.make_async_copy(
            stage.at[0, pl.ds(t * head_width, head_width), :],
            g_hbm.at[t, pl.ds(2 * width, head_width), :],
            w_sem.at[t],
        )
        copy.start()
        last.append(copy)

    def sixth(i, part):
        mu, rs = mu_s[at(i), :], rs_s[at(i), :]
        unit = (x_s[at(i), :] - mu) * rs
        d2 = big_s[at(i), :]
        wide = d2 * again
        m1 = jnp.sum(wide, axis=1, keepdims=True) / width
        m2 = jnp.sum(wide * unit, axis=1, keepdims=True) / width
        d_att = (rs * (wide - m1 - unit * m2)).astype(jnp.bfloat16)
        for t in range(parts):
            datt_ref[t, at(i), :] = d_att[:, t * head_width : (t + 1) * head_width]
        return part + fold(d2 * unit)

    part = tiles(sixth, jnp.zeros((8, width), f32))
    gsum_ref[1:2, :] = jnp.sum(part, axis=0, keepdims=True)
    gsum_ref[pl.ds(2 + parts, 8 - 2 - parts), :] = jnp.zeros((8 - 2 - parts, width), f32)
    for copy in last:
        copy.wait()


def rows_pass(att, tokens, out_grad, gains, weights, tile):
    parts, rows, head_width = att.shape
    width = tokens.shape[1]
    bf16, f32 = jnp.bfloat16, jnp.float32
    vmem = pl.BlockSpec(memory_space=pltpu.VMEM)
    anywhere = pl.BlockSpec(memory_space=pl.ANY)
    column = pltpu.VMEM((rows, 1), f32)
    return pl.pallas_call(
        partial(rows_kernel, tile),
        out_shape=(
            jax.ShapeDtypeStruct((rows, width), bf16),
            jax.ShapeDtypeStruct((rows, width), f32),
            jax.ShapeDtypeStruct(att.shape, bf16),
            jax.ShapeDtypeStruct((parts, 2 * width + head_width, width), bf16),
            jax.ShapeDtypeStruct((8, width), f32),
        ),
        in_specs=[vmem] * 4 + [anywhere],
        out_specs=[vmem] * 3 + [anywhere, vmem],
        scratch_shapes=[
            pltpu.VMEM((width, width), bf16),
            pltpu.VMEM((parts, width, width), bf16),
            pltpu.VMEM((parts, width, width), bf16),
            pltpu.VMEM((rows, width), f32),
            pltpu.VMEM((rows, width), f32),
            pltpu.VMEM((rows, width), bf16),
            pltpu.VMEM((rows, width), bf16),
            pltpu.VMEM((parts, rows, width), f32),
            pltpu.VMEM((parts, rows, width), bf16),
            pltpu.VMEM((parts, rows, width), f32),
            pltpu.VMEM((rows, width), bf16),
            pltpu.VMEM((rows, width), f32),
            pltpu.VMEM((rows, width), f32),
        ] + [column] * 6 + [
            pltpu.VMEM((2, width, width), bf16),
            pltpu.SemaphoreType.DMA((3 * parts,)),
            pltpu.SemaphoreType.DMA((2,)),
        ],
        compiler_params=pltpu.CompilerParams(vmem_limit_bytes=60 << 20),
        cost_estimate=pl.CostEstimate(flops=20 * 10**9, bytes_accessed=40 << 20, transcendentals=2 * 10**6),
        name="rows_pass",
    )(att, tokens, out_grad, gains, weights)


def front_kernel(groups, pieces, chunk, len_ref, tok_ref, w_ref, own_gain_ref, down_ref, up_ref, out_ref,
                 all_ref, packed_ref, gains_ref, att_ref, own_ref, lse_ref, full_ref,
                 k_s, qt_s, vt_s, acc_s, m_s, shard_s,
                 send, recv, gain_send, gain_recv, w_send, w_recv, w_load, w_local, a_send, a_recv, a_local):
    f32, bf16 = jnp.float32, jnp.bfloat16
    me, dp = lax.axis_index("tensor"), lax.axis_index("dp")
    core, chip, cross = spread(me)
    b0, b1, b2 = dp % 2, (dp // 2) % 2, (dp // 4) % 2
    rows, width = tok_ref.shape
    heads = k_s.shape[0]
    parts = all_ref.shape[0]
    piece = rows // pieces
    ends = seq_bounds(len_ref)
    half, rows2, rows4 = width // 2, chunk // 2, chunk // 4

    chunks = []
    for ref in (down_ref, up_ref, out_ref):
        for at in range(0, ref.shape[0], chunk):
            chunks.append((ref, at, len(chunks) * chunk))
    n = len(chunks)

    def load_weight(c):
        ref, at, _ = chunks[c]
        return pltpu.make_async_copy(ref.at[pl.ds(at, chunk), :], shard_s.at[c], w_load.at[c])

    for c in range(n):
        load_weight(c).start()
    values = tok_ref[...].astype(f32)
    mu = jnp.sum(values, axis=1, keepdims=True) / width
    ms = jnp.sum(values * values, axis=1, keepdims=True) / width
    all_ref[me] = ((values - mu) * lax.rsqrt(ms - mu * mu + EPS) * own_gain_ref[0:1, :]).astype(bf16)
    gains_ref[me] = own_gain_ref[...]
    greet([("dp", 1), ("dp", 2), ("dp", 4)], core, chip, cross)

    def to_peer(src, dst, ssem, rsem, where):
        return pltpu.make_async_remote_copy(
            src_ref=src, dst_ref=dst, send_sem=ssem, recv_sem=rsem, device_id=where, device_id_type=MESH
        )

    def block(c, owner):
        return all_ref.at[owner, pl.ds(pl.multiple_of(c * piece, piece), piece), :]

    def to_chip(c):
        return to_peer(block(c, me), block(c, me), send.at[c], recv.at[c], {"tensor": chip})

    def to_far(c):
        return to_peer(block(c, chip), block(c, chip), send.at[pieces + c], recv.at[pieces + c], {"tensor": core})

    def to_core():
        return to_peer(all_ref.at[me], all_ref.at[me], send.at[2 * pieces], recv.at[2 * pieces], {"tensor": core})

    def gain_copy(k):
        owner, peer = ((me, chip), (me, core), (chip, core))[k]
        return to_peer(gains_ref.at[owner], gains_ref.at[owner], gain_send.at[k], gain_recv.at[k], {"tensor": peer})

    to_core().start()
    gain_copy(0).start()
    gain_copy(1).start()

    def spot(shard, c, row0, size, col0, span):
        row = chunks[c][2] + row0
        return full_ref.at[shard, pl.ds(pl.multiple_of(row, 16), size), pl.ds(pl.multiple_of(col0, 128), span)]

    def weight_copy(c, s):
        row4, row2, col = b1 * rows2 + b2 * rows4, b1 * rows2, b0 * half
        if s == 0:
            src = shard_s.at[c, pl.ds(pl.multiple_of(row4, 16), rows4), pl.ds(pl.multiple_of(col, 128), half)]
            dst, where = spot(me, c, row4, rows4, col, half), {"tensor": chip}
        elif s == 1:
            src = dst = spot(chip, c, row4, rows4, col, half)
            where = at_peer("dp", 4)
        elif s == 2:
            src = dst = spot(chip, c, row2, rows2, col, half)
            where = at_peer("dp", 2)
        elif s == 3:
            src = dst = spot(chip, c, 0, chunk, col, half)
            where = at_peer("dp", 1)
        elif s == 4:
            src = dst = spot(chip, c, 0, chunk, 0, width)
            where = {"tensor": core}
        else:
            src = shard_s.at[c]
            dst, where = spot(me, c, 0, chunk, 0, width), {"tensor": core}
        return to_peer(src, dst, w_send.at[c, s], w_recv.at[c, s], where)

    def own_weight(c):
        return pltpu.make_async_copy(shard_s.at[c], spot(me, c, 0, chunk, 0, width), w_local.at[c])

    order = list(reversed(range(n)))
    batches = [order[: n // 3], order[n // 3 : 2 * n // 3], order[2 * n // 3 :]]

    def weights(batch, s):
        for c in batches[batch]:
            if s:
                weight_copy(c, s - 1).wait_recv()
            if s < 5:
                weight_copy(c, s).start()

    scale = jnp.bfloat16(0.125)
    ones = (lax.broadcasted_iota(jnp.int32, (16, piece), 0) == 0).astype(f32).astype(bf16)

    def project(owner, c):
        span = pl.ds(pl.multiple_of(c * piece, piece), piece)
        at = pl.ds(pl.multiple_of(owner * rows + c * piece, piece), piece)
        x = dot_nt(all_ref[owner, span, :], w_ref[...]).astype(bf16)
        packed_ref[owner, span, :] = x
        for h in range(heads):
            base = h * 3 * HEAD_DIM
            qt_s[h, :, at] = (x[:, base : base + HEAD_DIM] * scale).T
            k_s[h, at, :] = x[:, base + HEAD_DIM : base + 2 * HEAD_DIM]
            vt_s[h, :HEAD_DIM, at] = x[:, base + 2 * HEAD_DIM : base + 3 * HEAD_DIM].T
            vt_s[h, HEAD_DIM:, at] = ones

    def loop(body):
        def one(c, _):
            body(c)
            return 0

        lax.fori_loop(0, pieces, one, 0)

    for c in range(n):
        load_weight(c).wait()
    weights(0, 0)
    to_chip(0).start()
    to_chip(1).start()
    weights(1, 0)
    for c in range(2, pieces):
        to_chip(c).start()
    weights(2, 0)
    loop(lambda c: project(me, c))
    to_core().wait_recv()
    loop(lambda c: project(core, c))
    for c in order:
        weight_copy(c, 5).start()
        own_weight(c).start()

    early = ([(0, 1)], [(0, 2)], [(1, 1), (0, 3)], [(1, 2)], [(1, 3), (0, 4)])
    for c in range(pieces):
        to_chip(c).wait_recv()
        to_far(c).start()
        project(chip, c)
        for event in early[c] if c < len(early) else ():
            weights(*event)
    gain_copy(0).wait_recv()
    gain_copy(2).start()

    def from_far(c):
        to_far(c).wait_recv()
        project(cross, c)

    loop(from_far)
    weights(2, 1)

    def attend(o, later):
        first = o * rows
        at = pl.ds(first, rows)
        q_pos = first + lax.broadcasted_iota(jnp.int32, (1, rows), 1)
        q_start = start_of(ends, q_pos)
        for h in range(heads):
            acc_s[h] = jnp.zeros_like(acc_s[h])
            m_s[h] = jnp.full_like(m_s[h], NEG)

        def step(j, _):
            k0 = pl.multiple_of(j * rows, rows)
            kat = pl.ds(k0, rows)
            k_pos = k0 + lax.broadcasted_iota(jnp.int32, (rows, 1), 0)
            keep = (k_pos <= q_pos) & (k_pos >= q_start)
            for h in range(heads):
                s = jnp.where(keep, dot(k_s[h, kat, :], qt_s[h, :, at]), NEG)
                old = m_s[h]
                new = jnp.maximum(old, jnp.max(s, axis=0, keepdims=True))
                p = jnp.exp(s - new).astype(bf16)
                m_s[h] = new
                acc_s[h] = acc_s[h] * jnp.exp(old - new) + dot(vt_s[h, :, kat], p)
            return 0

        done = 0
        for stop, events in later:
            if stop > done:
                lax.fori_loop(done, stop, step, 0)
            for event in events:
                weights(*event)
            done = stop
        lax.fori_loop(done, o + 1, step, 0)
        outs = []
        for h in range(heads):
            acc = acc_s[h]
            total = acc[HEAD_DIM : HEAD_DIM + 1, :]
            outs.append((acc[:HEAD_DIM, :] / total).T)
            lse_ref[h : h + 1, at] = m_s[h] + jnp.log(total)
        att_ref[o] = jnp.concatenate(outs, axis=1).astype(bf16)

    def give(k):
        peer = (core, chip, cross)[k]
        return to_peer(att_ref.at[peer], own_ref.at[me], a_send.at[k], a_recv.at[k], {"tensor": peer})

    def keep_own():
        return pltpu.make_async_copy(att_ref.at[me], own_ref.at[me], a_local)

    plans = ([], [(0, [(2, 2)]), (1, [(1, 4), (2, 3)])], [(2, [(2, 4)])], [])
    for o in range(parts):
        attend(o, plans[o])

        for k, peer in enumerate((core, chip, cross)):

            @pl.when(peer == o)
            def _(k=k):
                give(k).start()

        @pl.when(me == o)
        def _():
            keep_own().start()

    gain_copy(1).wait_recv()
    gain_copy(2).wait_recv()
    for batch in range(3):
        weights(batch, 5)
    for c in order:
        weight_copy(c, 5).wait_recv()
        own_weight(c).wait()
    keep_own().wait()
    for k in range(3):
        give(k).wait()
    for c in range(pieces):
        to_chip(c).wait_send()
        to_far(c).wait_send()
    to_core().wait_send()
    for k in range(3):
        gain_copy(k).wait_send()
    for c in order:
        for s in range(6):
            weight_copy(c, s).wait_send()


def front_pass(groups, lengths, tokens, weight, own_gains, w_down, w_up, w_out, pieces=5, chunk=192):
    rows, width = tokens.shape
    heads = weight.shape[0] // (3 * HEAD_DIM)
    parts = 4
    total = parts * rows
    n = (w_down.shape[0] + w_up.shape[0] + w_out.shape[0]) // chunk
    bf16, f32 = jnp.bfloat16, jnp.float32
    vmem, anywhere = pl.BlockSpec(memory_space=pltpu.VMEM), pl.BlockSpec(memory_space=pl.ANY)
    sems = pltpu.SemaphoreType.DMA
    shape = jax.ShapeDtypeStruct
    return pl.pallas_call(
        partial(front_kernel, groups, pieces, chunk),
        out_shape=(
            shape((parts, rows, width), bf16),
            shape((parts, rows, weight.shape[0]), bf16),
            shape((parts,) + own_gains.shape, f32),
            shape((parts, rows, heads * HEAD_DIM), bf16),
            shape((parts, rows, heads * HEAD_DIM), bf16),
            shape((8, total), f32),
            shape((parts, n * chunk, width), bf16),
        ),
        in_specs=[pl.BlockSpec(memory_space=pltpu.SMEM)] + [vmem] * 3 + [anywhere] * 3,
        out_specs=[vmem] * 6 + [anywhere],
        scratch_shapes=[
            pltpu.VMEM((heads, total, HEAD_DIM), bf16),
            pltpu.VMEM((heads, HEAD_DIM, total), bf16),
            pltpu.VMEM((heads, HEAD_DIM + 16, total), bf16),
            pltpu.VMEM((heads, HEAD_DIM + 16, rows), f32),
            pltpu.VMEM((heads, 1, rows), f32),
            pltpu.VMEM((n, chunk, width), bf16),
            sems((2 * pieces + 1,)),
            sems((2 * pieces + 1,)),
            sems((3,)),
            sems((3,)),
            sems((n, 6)),
            sems((n, 6)),
            sems((n,)),
            sems((n,)),
            sems((3,)),
            sems((3,)),
            sems,
        ],
        compiler_params=pltpu.CompilerParams(
            collective_id=1, has_side_effects=True, vmem_limit_bytes=56 << 20
        ),
        name="front_pass",
    )(lengths, tokens, weight, own_gains, w_down, w_up, w_out)


def chunk_copy(c, s, src, dst, send, recv, axis, bit):
    return pltpu.make_async_remote_copy(
        src_ref=src,
        dst_ref=dst,
        send_sem=send.at[c, s],
        recv_sem=recv.at[c, s],
        device_id=at_peer(axis, bit),
        device_id_type=MESH,
    )


def back_kernel(groups, chunk, block, pieces, len_ref, datt_ref, packed_ref, att_ref, lse_ref, grads_ref,
                h1_ref, w_ref, gains_ref, gain_ref,
                sum_ref, in_sum, gains_sum,
                pq, do_s, own, first, second, acc, to_y, to_x, from_x, to_z, from_z, more_to, more_from,
                send, recv, local_sem, a2a_send, a2a_recv, a2a_local,
                d_first, d_second, d_send, d_recv, gain_at, gain_send, gain_recv, load_sem):
    f32, bf16 = jnp.float32, jnp.bfloat16
    steps = peers_of(4, groups)
    far = steps[5:]
    me, dp = lax.axis_index("tensor"), lax.axis_index("dp")
    core, chip, cross = spread(me)
    cols = grads_ref.shape[2]
    half, rows2, rows4 = cols // 2, chunk // 2, chunk // 4
    b0, b1, b2 = dp % 2, (dp // 2) % 2, (dp // 4) % 2
    n = grads_ref.shape[1] // chunk

    def take(c, shard):
        return grads_ref.at[shard, pl.ds(pl.multiple_of(c * chunk, 16), chunk), :]

    def col(b):
        return pl.ds(pl.multiple_of(b * half, 128), half)

    def row2(b):
        return pl.ds(pl.multiple_of(b * rows2, 16), rows2)

    def row4(b, bb):
        return pl.ds(pl.multiple_of(b * rows2 + bb * rows4, 16), rows4)

    def copy(c, s):
        if s == 0:
            return chunk_copy(c, 0, take(c, core), first.at[c, 0], send, recv, "tensor", 1)
        if s == 1:
            return chunk_copy(c, 1, take(c, cross), first.at[c, 1], send, recv, "tensor", 1)
        if s == 2:
            return chunk_copy(c, 2, to_y.at[c % 3], second.at[c], send, recv, "tensor", 2)
        if s == 3:
            slot = 3 + c - n if isinstance(c, int) and c >= n else c % 3
            return chunk_copy(c, 3, to_x.at[slot], from_x.at[c], send, recv, "dp", 1)
        if s in (4, 5, 6):
            return chunk_copy(c, s, to_z.at[c, s - 4], from_z.at[c, s - 4], send, recv, "dp", 2 * (s - 3))
        if s in (7, 8, 9):
            piece = sum_ref.at[c, row4(b1, b2), col(b0)]
            return chunk_copy(c, s, piece, piece, send, recv, "dp", 2 * (s - 6))
        if s == 10:
            piece = sum_ref.at[c, :, col(b0)]
            return chunk_copy(c, 10, piece, piece, send, recv, "dp", 1)
        axis, bit = far[s - 11]
        return chunk_copy(c, s, more_to.at[c, s - 11], more_from.at[c, s - 11], send, recv, axis, bit)

    def other4(m):
        return row4(b1 + (m % 2) * (1 - 2 * b1), b2 + (m // 2) * (1 - 2 * b2))

    def arrived(c, s, piece=None):
        if piece is None:
            copy(c, s).wait_recv()
        else:
            bit = 1 if s == 10 else 2 * (s - 6)
            chunk_copy(c, s, piece, piece, send, recv, "dp", bit).wait_recv()

    def mine(c, k):
        shard = (me, chip)[k]
        return pltpu.make_async_copy(take(c, shard), own.at[c % 4, k], local_sem.at[c % 4, k])

    def pair(c):
        copy(c, 1).start()
        copy(c, 0).start()
        mine(c, 1).start()
        mine(c, 0).start()

    def to_chip(c):
        @pl.when(c >= 3)
        def _():
            copy(c - 3, 2).wait_send()

        mine(c, 1).wait()
        arrived(c, 1)
        to_y[c % 3] = rounded(own[c % 4, 1].astype(f32) + first[c, 1].astype(f32))
        copy(c, 2).start()

    def x_half(c):
        @pl.when(c >= 3)
        def _():
            copy(c - 3, 3).wait_send()

        mine(c, 0).wait()
        arrived(c, 0)
        arrived(c, 2)

        def total(b):
            whole = own[c % 4, 0, :, col(b)].astype(f32) + first[c, 0, :, col(b)].astype(f32)
            return whole + second[c, :, col(b)].astype(f32)

        to_x[c % 3] = rounded(total(1 - b0))
        copy(c, 3).start()
        acc[c] = total(b0)

    def z_all(c):
        arrived(c, 3)
        acc[c] += from_x[c].astype(f32)
        for m in (3, 1, 2):
            to_z[c, m - 1] = rounded(acc[c, other4(m), :])
            copy(c, 3 + m).start()

    def settle(c):
        total = acc[c, row4(b1, b2), :]
        for m in (1, 2, 3):
            arrived(c, 3 + m)
            total = total + from_z[c, m - 1].astype(f32)
        for m in range(len(far)):
            more_to[c, m] = rounded(total)
            copy(c, 11 + m).start()
            arrived(c, 11 + m)
            total = rounded(total).astype(f32) + more_from[c, m].astype(f32)
        sum_ref[c, row4(b1, b2), col(b0)] = rounded(total)
        for m in (3, 1, 2):
            copy(c, 6 + m).start()

    def x_share(c):
        for m in (1, 2, 3):
            arrived(c, 6 + m, sum_ref.at[c, other4(m), col(b0)])
        copy(c, 10).start()

    def end(c):
        arrived(c, 10, sum_ref.at[c, :, col(1 - b0)])

    stages = (pair, to_chip, x_half, z_all, settle, x_share, end)
    lags = (0, 1, 3, 5, 6, 7, 8)

    def turn(at):
        for s, lag in enumerate(lags):
            c = at - lag

            @pl.when((c >= 0) & (c < n))
            def _():
                stages[s](c)

    rows = packed_ref.shape[0]
    heads = packed_ref.shape[1] // (3 * HEAD_DIM)
    own_rows = datt_ref.shape[1]
    width = h1_ref.shape[1]
    ends = seq_bounds(len_ref)
    scale = jnp.bfloat16(0.125)
    load = pltpu.make_async_copy(packed_ref, pq, load_sem.at[0])
    load.start()
    greet(steps + [("dp", 6)], cross)

    def a2a(k, peer):
        return pltpu.make_async_remote_copy(
            src_ref=datt_ref.at[peer],
            dst_ref=do_s.at[me],
            send_sem=a2a_send.at[k],
            recv_sem=a2a_recv.at[k],
            device_id={"tensor": peer},
            device_id_type=MESH,
        )

    moves = [a2a(k, peer) for k, peer in reversed(list(enumerate((core, chip, cross))))]
    for move in moves:
        move.start()
    keep_own = pltpu.make_async_copy(datt_ref.at[me], do_s.at[me], a2a_local)
    keep_own.start()
    turn(jnp.int32(0))
    load.wait()

    def attention(kv_s, q_s, g_s, qt_s, gt_s, kt_s, d_s, dqt_s, acc_kv):
        def stage_qkv(i, _):
            at = pl.ds(pl.multiple_of(i * 256, 256), 256)
            x = pq[at, :]
            blank = jnp.zeros((256, HEAD_DIM), bf16)
            blank_t = jnp.zeros((HEAD_DIM, 256), bf16)
            for h in range(heads):
                base = h * 3 * HEAD_DIM
                q = x[:, base : base + HEAD_DIM] * scale
                k = x[:, base + HEAD_DIM : base + 2 * HEAD_DIM]
                v = x[:, base + 2 * HEAD_DIM : base + 3 * HEAD_DIM]
                kv_s[h, at, :] = jnp.concatenate([k, v], axis=1)
                q_s[h, at, :] = jnp.concatenate([q, blank], axis=1)
                qt_s[h, :HEAD_DIM, at] = q.T
                qt_s[h, HEAD_DIM:, at] = blank_t
                kt_s[h, :, at] = (k * scale).T
                dqt_s[h, :, at] = jnp.zeros((HEAD_DIM, 256), f32)
                acc_kv[h, at, :] = jnp.zeros((256, 2 * HEAD_DIM), f32)
            return 0

        lax.fori_loop(0, rows // 256, stage_qkv, 0)
        keep_own.wait()
        for move in moves:
            move.wait()
        piece = own_rows // 5

        def stage_grad(i, _):
            owner, part = i // 5, i % 5
            inner = pl.ds(pl.multiple_of(part * piece, piece), piece)
            at = pl.ds(pl.multiple_of(owner * own_rows + part * piece, piece), piece)
            g = do_s[owner, inner, :]
            prod = g.astype(f32) * att_ref[at, :].astype(f32)
            blank = jnp.zeros((piece, HEAD_DIM), bf16)
            blank_t = jnp.zeros((HEAD_DIM, piece), bf16)
            for h in range(heads):
                d = g[:, h * HEAD_DIM : (h + 1) * HEAD_DIM]
                g_s[h, at, :] = jnp.concatenate([blank, d], axis=1)
                gt_s[h, HEAD_DIM:, at] = d.T
                gt_s[h, :HEAD_DIM, at] = blank_t
                d_s[h, :, at] = jnp.sum(prod[:, h * HEAD_DIM : (h + 1) * HEAD_DIM].T, axis=0, keepdims=True)
            return 0

        lax.fori_loop(0, rows // piece, stage_grad, 0)

        def body(i, j):
            q0 = pl.multiple_of(i * block, block)
            k0 = pl.multiple_of(j * block, block)
            at, kat = pl.ds(q0, block), pl.ds(k0, block)
            q_pos = q0 + lax.broadcasted_iota(jnp.int32, (1, block), 1)
            q_start = start_of(ends, q_pos)
            k_pos = k0 + lax.broadcasted_iota(jnp.int32, (block, 1), 0)
            keep = (k_pos <= q_pos) & (k_pos >= q_start)
            for h in range(heads):
                kv = kv_s[h, kat, :]
                s = dot(kv, qt_s[h, :, at]) - lse_ref[h : h + 1, at]
                p = jnp.exp(jnp.where(keep, s, NEG))
                dp_t = dot(kv, gt_s[h, :, at])
                ds = (p * (dp_t - d_s[h, :, at])).astype(bf16)
                acc_kv[h, kat, :] += dot(p.astype(bf16), g_s[h, at, :]) + dot(ds, q_s[h, at, :])
                dqt_s[h, :, at] += dot(kt_s[h, :, kat], ds)

        count = rows // block
        done = 0
        for g in range(count // 2 + 1):
            length = count - g

            def one(p, _, length=length, g=g, done=done):
                wrap = p // length
                i = (length - 1) - wrap * (length - g)
                j = p - wrap * length
                body(i, j)
                b = p + done

                @pl.when(b % 2 == 1)
                def _():
                    turn((b + 1) // 2)

                return 0

            lax.fori_loop(0, count, one, 0)
            done += count

        def finish(i, _):
            at = pl.ds(pl.multiple_of(i * 256, 256), 256)
            parts_of = []
            for h in range(heads):
                parts_of += [dqt_s[h, :, at].T, acc_kv[h, at, :]]
            pq[at, :] = jnp.concatenate(parts_of, axis=1).astype(bf16)
            return 0

        lax.fori_loop(0, rows // 256, finish, 0)

    wide = 2 * HEAD_DIM
    pl.run_scoped(
        attention,
        pltpu.VMEM((heads, rows, wide), bf16),
        pltpu.VMEM((heads, rows, wide), bf16),
        pltpu.VMEM((heads, rows, wide), bf16),
        pltpu.VMEM((heads, wide, rows), bf16),
        pltpu.VMEM((heads, wide, rows), bf16),
        pltpu.VMEM((heads, HEAD_DIM, rows), bf16),
        pltpu.VMEM((heads, 1, rows), f32),
        pltpu.VMEM((heads, HEAD_DIM, rows), f32),
        pltpu.VMEM((heads, rows, wide), f32),
    )
    bodies = (rows // block) * (rows // block + 1) // 2
    next_turn = bodies // 2 + 1
    piece = own_rows // pieces
    parts = rows // own_rows
    extra_chunks = w_ref.shape[0] // chunk

    def closing(h1_s, d1_s, d_to, gq):
        flight, sends = {}, []

        def go(key, src, dst, ssem, rsem, axis, bit):
            flight[key] = remote(src, dst, ssem, rsem, axis, bit)
            sends.append(flight[key])

        def owned(owner):
            return pl.ds(pl.multiple_of(owner * own_rows, own_rows), own_rows)

        fetch = [
            pltpu.make_async_copy(h1_ref.at[pl.ds(t * own_rows, own_rows), :], h1_s.at[t], load_sem.at[1 + t])
            for t in range(parts)
        ]
        for t in fetch:
            t.start()

        def span(c):
            return pl.ds(c * piece, piece)

        def product(slot, owner):
            d1_s[slot] = rounded(dot(pq[owned(owner), :], w_ref[...]))

        def pair_rows(c):
            go(("d", c, 1), d1_s.at[0, span(c)], d_first.at[1, span(c)], d_send.at[c, 1], d_recv.at[c, 1], "tensor", 1)
            go(("d", c, 0), d1_s.at[1, span(c)], d_first.at[0, span(c)], d_send.at[c, 0], d_recv.at[c, 0], "tensor", 1)

        def across(c):
            flight["d", c, 1].wait_recv()
            d_to[span(c)] = rounded(d1_s[2, span(c), :].astype(f32) + d_first[1, span(c), :].astype(f32))
            go(("d", c, 2), d_to.at[span(c)], d_second.at[span(c)], d_send.at[c, 2], d_recv.at[c, 2], "tensor", 2)

        def settle_rows(c):
            flight["d", c, 0].wait_recv()
            flight["d", c, 2].wait_recv()
            near = d1_s[3, span(c), :].astype(f32) + d_first[0, span(c), :].astype(f32)
            in_sum[span(c)] = near + d_second[span(c)].astype(f32)

        def q_x(i):
            rows_of = pl.ds(i * chunk, chunk)
            to_x[3 + i] = rounded(gq[rows_of, col(1 - b0)])
            copy(n + i, 3).start()
            acc[n + i] = gq[rows_of, col(b0)]

        def gain_start(m):
            axis, bit = steps[m]
            go(("g", m), gain_at.at[0, m], gain_at.at[1, m], gain_send.at[m], gain_recv.at[m], axis, bit)

        def gain_step(m):
            flight["g", m].wait_recv()
            now = gain_at[0, m] + gain_at[1, m]
            if m + 1 < len(steps):
                gain_at[0, m + 1] = now
                gain_start(m + 1)
            else:
                gains_sum[...] = now

        last = n + lags[-1]
        turns = iter(range(next_turn, last))

        def main_turn():
            at = next(turns, None)
            if at is not None:
                turn(jnp.int32(at))

        main_turn()
        product(0, cross)
        product(1, core)
        for c in range(pieces):
            pair_rows(c)
        product(2, chip)
        product(3, me)
        main_turn()
        for t in fetch:
            t.wait()
        gq[...] = dot_tn(pq[owned(0), :], h1_s[0])
        for c in range(pieces):
            across(c)
        for t in range(1, parts):
            gq[...] += dot_tn(pq[owned(t), :], h1_s[t])
        for i in range(extra_chunks):
            q_x(i)
        main_turn()
        gain_at[0, 0] = gains_ref[...]
        line = jnp.sum(w_ref[...].astype(f32) * gq[...], axis=0, keepdims=True)
        gain_at[0, 0, 2 + parts : 3 + parts, :] = line / gain_ref[0, 0:1, :]
        gain_start(0)
        q_stages = (z_all, settle, x_share, end)
        settled = gained = 0
        for stage in q_stages:
            for i in range(extra_chunks):
                stage(n + i)
            main_turn()
            if settled < pieces:
                settle_rows(settled)
                settled += 1
            if gained < len(steps):
                gain_step(gained)
                gained += 1
        while settled < pieces:
            settle_rows(settled)
            settled += 1
        while gained < len(steps):
            gain_step(gained)
            gained += 1
        for at in turns:
            turn(jnp.int32(at))
        for each in sends:
            each.wait_send()

    pl.run_scoped(
        closing,
        pltpu.VMEM((parts, own_rows, width), bf16),
        pltpu.VMEM((parts, own_rows, width), bf16),
        pltpu.VMEM((own_rows, width), bf16),
        pltpu.VMEM(w_ref.shape, f32),
    )

    def sent(c, _):
        for s in range(11 + len(far)):
            if s in (2, 3):

                @pl.when(c >= n - 3)
                def _():
                    copy(c, s).wait_send()

            else:
                copy(c, s).wait_send()
        return 0

    lax.fori_loop(0, n, sent, 0)
    for i in range(extra_chunks):
        for s in range(3, 11 + len(far)):
            copy(n + i, s).wait_send()


def back_pass(groups, lengths, grad_att, packed, att, lse, grads, h1, weight, sums, gains,
              chunk=192, block=512, pieces=5):
    rows = packed.shape[0]
    parts, own_rows, head_width = grad_att.shape
    width = grads.shape[2]
    n = grads.shape[1] // chunk
    more = weight.shape[0] // chunk
    steps = len(peers_of(4, groups))
    extra = max(steps - 5, 1)
    bf16 = lambda *shape: pltpu.VMEM(shape, jnp.bfloat16)
    f32 = lambda *shape: pltpu.VMEM(shape, jnp.float32)
    vmem, anywhere = pl.BlockSpec(memory_space=pltpu.VMEM), pl.BlockSpec(memory_space=pl.ANY)
    sems = pltpu.SemaphoreType.DMA
    return pl.pallas_call(
        partial(back_kernel, groups, chunk, block, pieces),
        out_shape=(
            jax.ShapeDtypeStruct((n + more, chunk, width), jnp.bfloat16),
            jax.ShapeDtypeStruct((own_rows, width), jnp.float32),
            jax.ShapeDtypeStruct(sums.shape, jnp.float32),
        ),
        in_specs=[pl.BlockSpec(memory_space=pltpu.SMEM), anywhere, anywhere, vmem, vmem, anywhere,
                  anywhere, vmem, vmem, vmem],
        out_specs=[vmem] * 3,
        scratch_shapes=[
            bf16(rows, packed.shape[1]),
            bf16(parts, own_rows, head_width),
            bf16(4, 2, chunk, width),
            bf16(n, 2, chunk, width),
            bf16(n, chunk, width),
            f32(n + more, chunk, width // 2),
            bf16(3, chunk, width),
            bf16(3 + more, chunk, width // 2),
            bf16(n + more, chunk, width // 2),
            bf16(n + more, 3, chunk // 4, width // 2),
            bf16(n + more, 3, chunk // 4, width // 2),
            bf16(n + more, extra, chunk // 4, width // 2),
            bf16(n + more, extra, chunk // 4, width // 2),
            sems((n + more, 11 + extra)),
            sems((n + more, 11 + extra)),
            sems((4, 2)),
            sems((3,)),
            sems((3,)),
            sems,
            bf16(2, own_rows, width),
            bf16(own_rows, width),
            sems((pieces, 3)),
            sems((pieces, 3)),
            pltpu.VMEM((2, steps) + sums.shape, jnp.float32),
            sems((steps,)),
            sems((steps,)),
            sems((1 + parts,)),
        ],
        compiler_params=pltpu.CompilerParams(
            collective_id=0, has_side_effects=True, vmem_limit_bytes=60 << 20
        ),
        name="back_pass",
    )(lengths, grad_att, packed, att, lse, grads, h1, weight, sums, gains)


def local(
    tokens,
    lengths,
    in_gain,
    qkv_weight,
    attn_gain,
    out_weight,
    ffn_gain,
    up_weight,
    hidden_gain,
    down_weight,
    out_grad,
):
    parts = lax.axis_size("tensor")
    own_rows, width = tokens.shape
    head_width, hidden = attn_gain.shape[0], hidden_gain.shape[0]

    filler = jnp.zeros((width - head_width,), jnp.float32)
    rest = jnp.zeros((4 * width,), jnp.float32)
    own_gains = jnp.concatenate((in_gain, ffn_gain, attn_gain, filler, hidden_gain, rest)).reshape(8, width)
    weight_t = qkv_weight.T
    groups = lax.axis_size("dp")
    gathered_in, packed, gains, attended, own_att, log_total, weights = front_pass(
        groups,
        lengths,
        tokens,
        weight_t,
        own_gains,
        down_weight,
        up_weight,
        out_weight,
    )
    gathered_in = gathered_in.reshape(parts * own_rows, width)
    packed = packed.reshape(parts * own_rows, -1)
    attended = attended.reshape(parts * own_rows, head_width)
    result, grad_middle, grad_att, grads, gain_parts = rows_pass(
        own_att,
        tokens,
        out_grad,
        gains,
        weights,
        own_rows,
    )
    sums, grad_in_normed, gains = back_pass(
        groups,
        lengths,
        grad_att,
        packed,
        attended,
        log_total,
        grads,
        gathered_in,
        weight_t,
        gain_parts,
        gains,
    )

    residual = tokens.astype(jnp.float32)
    mean = jnp.mean(residual, axis=1, keepdims=True)
    square = jnp.mean(residual * residual, axis=1, keepdims=True)
    scale = lax.rsqrt(square - mean * mean + EPS)
    unit = (residual - mean) * scale
    weighted = grad_in_normed * in_gain
    first = jnp.mean(weighted, axis=1, keepdims=True)
    second = jnp.mean(weighted * unit, axis=1, keepdims=True)
    in_grad = grad_middle + scale * (weighted - first - unit * second)

    me = lax.axis_index("tensor")
    sums = sums.reshape(-1, width).astype(jnp.float32)
    return (
        result,
        in_grad,
        gains[2 + parts],
        sums[hidden + width + head_width :].T,
        lax.dynamic_slice_in_dim(gains[1], me * head_width, head_width),
        sums[hidden + width : hidden + width + head_width],
        gains[0],
        sums[hidden : hidden + width],
        lax.dynamic_index_in_dim(gains, 2 + me, 0, keepdims=False),
        sums[:hidden],
    )


def solution(mesh):
    return jax.shard_map(
        local,
        mesh=mesh,
        in_specs=(
            P(("dp", "tensor"), None),
            P("dp", None),
            P(),
            P(None, "tensor"),
            P("tensor"),
            P("tensor", None),
            P(),
            P(None, "tensor"),
            P("tensor"),
            P("tensor", None),
            P(("dp", "tensor"), None),
        ),
        out_specs=(
            P(("dp", "tensor"), None),
            P(("dp", "tensor"), None),
            P(),
            P(None, "tensor"),
            P("tensor"),
            P("tensor", None),
            P(),
            P(None, "tensor"),
            P("tensor"),
            P("tensor", None),
        ),
        check_vma=False,
    )
```
